32 devices in a mesh: dp: 8 (over z, y), head: 4 (over x, core).
Axes of the slice: x: 2, y: 2, z: 4, core: 2. Of those that a mesh axis runs over, the one named last changes fastest.
Arguments:
- tokens: bfloat16 [8, 1024, 768], P('dp', 'head'), may hold values from -6 to 6
- memory: bfloat16 [8, 2048, 768], P('dp', 'head'), may hold values from -6 to 6
- text_length: int32 [8], P('dp'), may hold values from 256 to 1024, as said below
- patch_count: int32 [8], P('dp'), may hold values from 512 to 2048, as said below
- self_gain: bfloat16 [768], P(('dp', 'head')), may hold values from 0.5 to 1.5
- self_query: bfloat16 [768, 768], P(('dp', 'head')), may hold values from -0.21875 to 0.21875
- self_key: bfloat16 [768, 768], P(('dp', 'head')), may hold values from -0.21875 to 0.21875
- self_value: bfloat16 [768, 768], P(('dp', 'head')), may hold values from -0.21875 to 0.21875
- self_out: bfloat16 [768, 768], P(('dp', 'head')), may hold values from -3.5 to 3.5
- cross_gain: bfloat16 [768], P(('dp', 'head')), may hold values from 0.5 to 1.5
- cross_query: bfloat16 [768, 768], P(('dp', 'head')), may hold values from -0.21875 to 0.21875
- cross_key: bfloat16 [768, 768], P(('dp', 'head')), may hold values from -0.21875 to 0.21875
- cross_value: bfloat16 [768, 768], P(('dp', 'head')), may hold values from -0.21875 to 0.21875
- cross_out: bfloat16 [768, 768], P(('dp', 'head')), may hold values from -6 to 6
- mlp_gain: bfloat16 [768], P(('dp', 'head')), may hold values from 0.5 to 1.5
- mlp_gate: bfloat16 [768, 2048], P(('dp', 'head')), may hold values from -0.21875 to 0.21875
- mlp_up: bfloat16 [768, 2048], P(('dp', 'head')), may hold values from -0.21875 to 0.21875
- mlp_down: bfloat16 [2048, 768], P(('dp', 'head')), may hold values from -0.125 to 0.125
- output_grad: bfloat16 [8, 1024, 768], P('dp', 'head'), may hold values from -6 to 6
Outputs:
- output: bfloat16 [8, 1024, 768], P('dp', 'head')
- input_grad: float32 [8, 1024, 768], P('dp', 'head')
- memory_grad: float32 [8, 2048, 768], P('dp', 'head')
- self_dgain: float32 [768], P(('dp', 'head'))
- self_dquery: float32 [768, 768], P(('dp', 'head'))
- self_dkey: float32 [768, 768], P(('dp', 'head'))
- self_dvalue: float32 [768, 768], P(('dp', 'head'))
- self_dout: float32 [768, 768], P(('dp', 'head'))
- cross_dgain: float32 [768], P(('dp', 'head'))
- cross_dquery: float32 [768, 768], P(('dp', 'head'))
- cross_dkey: float32 [768, 768], P(('dp', 'head'))
- cross_dvalue: float32 [768, 768], P(('dp', 'head'))
- cross_dout: float32 [768, 768], P(('dp', 'head'))
- mlp_dgain: float32 [768], P(('dp', 'head'))
- mlp_dgate: float32 [768, 2048], P(('dp', 'head'))
- mlp_dup: float32 [768, 2048], P(('dp', 'head'))
- mlp_ddown: float32 [2048, 768], P(('dp', 'head'))
The draws below stay inside these ranges and needn't reach their ends.
Inputs may be any that keep to these rules, and one draw needn't show every extreme that they name: `text_length`: positions at or past a chart's length are padding; some chart uses all 1024 positions and some only 256. `patch_count`: the valid patches are the first ones of a chart's grid; some chart fills all 2048 and some only 512.
All inputs are finite; a program needn't handle non-finite values.
Results may differ from the reference program's by a relative error of at most 0.02.
Values may be sent and summed in bfloat16 or wider, within the bound.
No kernel may reach another device: no remote copies, remote signals or barrier semaphores. Data moves between devices by JAX's collectives and lax.ppermute only.
A program may use at most 192 MiB of HBM per device.

```python
import math
import jax
import jax.numpy as jnp
from jax import lax

D = 768
HEADS = 12
HEAD_DIM = 64
FF = 2048
LEN = 1024
PATCHES = 2048
CHARTS = 8


def spread_counts(folded, highest):
    drawn = jax.random.randint(folded, (CHARTS,), highest // 4, highest + 1, dtype=jnp.int32)
    ranking = jax.random.permutation(jax.random.fold_in(folded, 1), CHARTS)
    drawn = drawn.at[ranking[0]].set(highest)
    return drawn.at[ranking[1]].set(highest // 4)


def draw_text_length(key, part):
    return spread_counts(jax.random.fold_in(key, 11), LEN)


def draw_patch_count(key, part):
    return spread_counts(jax.random.fold_in(key, 23), PATCHES)


def strengthened(values, own_key, source, target, blocks, factor):
    def block_of(axis_at):
        return (jnp.arange(values.shape[axis_at]) // (values.shape[axis_at] // blocks)).reshape((-1,) + (1,) * (values.ndim - 1 - axis_at))

    first = jax.random.permutation(own_key, blocks)[block_of(target)]
    other_side = (block_of(target) + blocks // 2) % blocks
    return jnp.where((block_of(source) == first) | (block_of(source) == other_side), factor * values, values)


def level_of(rng, shape, cuts, low, high):
    gain = 1.0
    for position, blocks in cuts:
        draws = jax.random.uniform(jax.random.fold_in(jax.random.fold_in(rng, 6), position), (blocks,), jnp.float32, low / len(cuts), high / len(cuts))
        gain = gain * jnp.repeat(jnp.exp(draws), shape[position] // blocks).reshape((-1,) + (1,) * (len(shape) - 1 - position))
    return gain


def bell_draw(own_key, dims, deviation, limit, cuts=(), kind=jnp.bfloat16):
    values = deviation * jax.random.normal(own_key, dims, jnp.float32)
    if cuts:
        values = values * level_of(own_key, dims, cuts, -0.22, 0.18)
    return jnp.clip(values, -limit, limit).astype(kind)


def noise_with(rng, extent, scale, reach, cuts, heavy, held_as=jnp.bfloat16):
    values = scale * jax.random.normal(rng, extent, jnp.float32)
    if cuts:
        values = values * level_of(rng, extent, cuts, -0.22, 0.18)
    return jnp.clip(strengthened(values, jax.random.fold_in(rng, 3), *heavy), -reach, reach).astype(held_as)


def setup_inputs(seed: int = 0) -> dict:
    streams_of = jax.random.split(jax.random.key(seed), 20)
    tokens = noise_with(streams_of[0], (CHARTS, LEN, D), 1.0, 6.0, ((0, 8), (1, 4)), (0, 2, 8, 2.0))
    memory = bell_draw(streams_of[1], (CHARTS, PATCHES, D), 1.0, 6.0, ((0, 8), (1, 4)))
    text_length = draw_text_length(jax.random.fold_in(streams_of[19], 71), 0)
    patch_count = draw_patch_count(jax.random.fold_in(streams_of[19], 71), 0)
    self_gain = jnp.clip(1.0 + 0.1 * jax.random.normal(streams_of[4], (D,), jnp.float32), 0.5, 1.5).astype(jnp.bfloat16)
    self_query = bell_draw(streams_of[5], (D, D), D ** -0.5, 0.21875, ((0, 32),))
    self_key = bell_draw(streams_of[6], (D, D), D ** -0.5, 0.21875, ((0, 32),))
    self_value = bell_draw(streams_of[7], (D, D), D ** -0.5, 0.21875, ((0, 32),))
    self_out = bell_draw(streams_of[8], (D, D), (max(D // (LEN // 4), 1)) ** -0.5, 3.5, ((0, 32),))
    cross_gain = jnp.clip(1.0 + 0.1 * jax.random.normal(streams_of[9], (D,), jnp.float32), 0.5, 1.5).astype(jnp.bfloat16)
    cross_query = bell_draw(streams_of[10], (D, D), D ** -0.5, 0.21875, ((0, 32),))
    cross_key = bell_draw(streams_of[11], (D, D), D ** -0.5, 0.21875, ((0, 32),))
    cross_value = bell_draw(streams_of[12], (D, D), D ** -0.5, 0.21875, ((0, 32),))
    cross_out = bell_draw(streams_of[13], (D, D), (max(D // (PATCHES // 4), 1)) ** -0.5, 6.0, ((0, 32),))
    mlp_gain = jnp.clip(1.0 + 0.1 * jax.random.normal(streams_of[14], (D,), jnp.float32), 0.5, 1.5).astype(jnp.bfloat16)
    mlp_gate = bell_draw(streams_of[15], (D, FF), D ** -0.5, 0.21875, ((0, 32),))
    mlp_up = bell_draw(streams_of[16], (D, FF), D ** -0.5, 0.21875, ((0, 32),))
    mlp_down = bell_draw(streams_of[17], (FF, D), FF ** -0.5, 0.125, ((0, 32),))
    output_grad = bell_draw(streams_of[18], (CHARTS, LEN, D), 1.0, 6.0, ((0, 8), (1, 4)))
    return {"tokens": tokens, "memory": memory, "text_length": text_length, "patch_count": patch_count, "self_gain": self_gain, "self_query": self_query, "self_key": self_key, "self_value": self_value, "self_out": self_out, "cross_gain": cross_gain, "cross_query": cross_query, "cross_key": cross_key, "cross_value": cross_value, "cross_out": cross_out, "mlp_gain": mlp_gain, "mlp_gate": mlp_gate, "mlp_up": mlp_up, "mlp_down": mlp_down, "output_grad": output_grad}


@jax.custom_vjp
def low(v):
    return lax.optimization_barrier(v.astype(jnp.bfloat16)).astype(jnp.float32)

@jax.custom_vjp
def low_back(v):
    return v

def low_keep(v):
    return (low(v), None)

def low_pass(kept, grad):
    return (grad,)

def back_keep(v):
    return (v, None)

def back_low(kept, grad):
    return (low(grad),)
low.defvjp(low_keep, low_pass)
low_back.defvjp(back_keep, back_low)
HIGH = lax.Precision.HIGHEST

def normed(values, gain_vec):
    inverse = lax.rsqrt(lax.optimization_barrier(jnp.mean(values * values, axis=-1, keepdims=True)) + 1e-06)
    return values * inverse * gain_vec

def dense(left_side, right_side):
    return jnp.dot(left_side, right_side, precision=HIGH, preferred_element_type=jnp.float32)

def both_ways(values):
    return low(low_back(values))

def attention(queries, key_rows, value_rows, key_limit, causal):
    length = queries.shape[0]
    block_rows = min(512, length)
    block_count = length // block_rows
    scaling = 1.0 / math.sqrt(HEAD_DIM)
    columns = jnp.arange(key_rows.shape[0], dtype=jnp.int32)

    def one_block(block_pair):
        rows_block, first_row = block_pair
        scores = low_back(jnp.einsum('qhd,khd->hqk', rows_block, key_rows, precision=HIGH) * scaling)
        allowed = jnp.broadcast_to(columns[None, :] < key_limit, (block_rows, key_rows.shape[0]))
        if causal:
            positions = first_row + jnp.arange(block_rows, dtype=jnp.int32)
            allowed = allowed & (columns[None, :] <= positions[:, None])
        masked = jnp.where(allowed[None], scores, -1e+30)
        prob_rows = low(jax.nn.softmax(masked, axis=-1))
        return jnp.einsum('hqk,khd->qhd', prob_rows, value_rows, precision=HIGH)
    starts = jnp.arange(block_count, dtype=jnp.int32) * block_rows
    blocks_out = lax.map(jax.checkpoint(one_block), (queries.reshape(block_count, block_rows, HEADS, HEAD_DIM), starts))
    return blocks_out.reshape(length, HEADS * HEAD_DIM)

def chart_layer(params, text_chart, memory_chart, length_chart, count_chart):
    gain_one, query_one, key_one, value_one, out_one, gain_two, query_two, key_two, value_two, out_two, gain_three, gate_three, up_three, down_three = params
    normed_one = low(normed(text_chart, gain_one))
    queries = both_ways(dense(normed_one, query_one)).reshape(LEN, HEADS, HEAD_DIM)
    key_rows = both_ways(dense(normed_one, key_one)).reshape(LEN, HEADS, HEAD_DIM)
    value_rows = both_ways(dense(normed_one, value_one)).reshape(LEN, HEADS, HEAD_DIM)
    context_one = both_ways(attention(queries, key_rows, value_rows, length_chart, True))
    hidden_one = text_chart + low_back(dense(context_one, out_one))
    normed_two = low(normed(hidden_one, gain_two))
    queries_two = both_ways(dense(normed_two, query_two)).reshape(LEN, HEADS, HEAD_DIM)
    memory_keys = both_ways(dense(memory_chart, key_two)).reshape(PATCHES, HEADS, HEAD_DIM)
    memory_values = both_ways(dense(memory_chart, value_two)).reshape(PATCHES, HEADS, HEAD_DIM)
    context_two = both_ways(attention(queries_two, memory_keys, memory_values, count_chart, False))
    hidden_two = hidden_one + low_back(dense(context_two, out_two))
    normed_three = low(normed(hidden_two, gain_three))
    gate_raw = low_back(dense(normed_three, gate_three))
    up_raw = low_back(dense(normed_three, up_three))
    mixed = low(jax.nn.gelu(gate_raw, approximate=True) * up_raw)
    return hidden_two + low_back(dense(mixed, down_three))

def reference(tokens, memory, text_length, patch_count, self_gain, self_query, self_key, self_value, self_out, cross_gain, cross_query, cross_key, cross_value, cross_out, mlp_gain, mlp_gate, mlp_up, mlp_down, output_grad):
    weights = tuple((matrix.astype(jnp.float32) for matrix in (self_gain, self_query, self_key, self_value, self_out, cross_gain, cross_query, cross_key, cross_value, cross_out, mlp_gain, mlp_gate, mlp_up, mlp_down)))
    text_float = tokens.astype(jnp.float32)
    memory_float = memory.astype(jnp.float32)
    checked_layer = jax.checkpoint(chart_layer)

    def run_all(text_in, memory_in, params):

        def step(carried, pieces):
            return (carried, checked_layer(params, pieces[0], pieces[1], pieces[2], pieces[3]))
        _, stacked = lax.scan(step, jnp.zeros((), jnp.float32), (text_in, memory_in, text_length.astype(jnp.int32), patch_count.astype(jnp.int32)))
        return stacked
    result, pullback = jax.vjp(run_all, text_float, memory_float, weights)
    input_grad, memory_grad, grads = pullback(output_grad.astype(jnp.float32))
    return (result.astype(jnp.bfloat16), input_grad, memory_grad, grads[0], grads[1], grads[2], grads[3], grads[4], grads[5], grads[6], grads[7], grads[8], grads[9], grads[10], grads[11], grads[12], grads[13])
```

```python
import functools
import math

import jax
import jax.numpy as jnp
from jax import lax
from jax.experimental import pallas as pl
from jax.experimental.pallas import tpu as pltpu
from jax.sharding import PartitionSpec as P

HEAD_DIM = 64
PAIR_LANES = 128
NEG_FILL = -1e30
EPS = 1e-06
F32 = jnp.float32
LOW = jnp.bfloat16


NT = (((1,), (1,)), ((), ()))
TN = (((0,), (0,)), ((), ()))


def dot_nt(left, right):
    return lax.dot_general(left, right, NT, preferred_element_type=F32)


def dot_tn(left, right):
    return lax.dot_general(left, right, TN, preferred_element_type=F32)


def dot_nn(left, right):
    return jnp.dot(left, right, preferred_element_type=F32)


def query_limits(info, queries, causal):
    last = info[0] - 1
    if not causal:
        return jnp.full((1, queries), last, jnp.int32), last
    rows = info[1] + lax.broadcasted_iota(jnp.int32, (1, queries), 1)
    return jnp.minimum(rows, last), jnp.minimum(info[1] + queries - 1, last)


def head_lanes(head):
    lanes = lax.broadcasted_iota(jnp.int32, (1, PAIR_LANES), 1)
    return (lanes // HEAD_DIM) == head


def fold(values, op):
    rows, columns = values.shape
    return op(values.reshape(rows // 8, 8, columns), axis=0)


def forward_kernel(causal, chunk, info, q_ref, k_ref, v_ref, c_ref, lse_ref, s_ref, m_ref, l_ref, a_ref):
    queries = q_ref.shape[0]
    chunks = k_ref.shape[0] // chunk
    scaling = 1.0 / math.sqrt(HEAD_DIM)
    limit, latest = query_limits(info, queries, causal)
    q_all = q_ref[...] * jnp.asarray(scaling, q_ref.dtype)
    q_heads = [jnp.where(head_lanes(h), q_all, jnp.zeros_like(q_all)) for h in range(2)]
    m_ref[...] = jnp.full(m_ref.shape, NEG_FILL, F32)
    l_ref[...] = jnp.zeros(l_ref.shape, F32)
    a_ref[...] = jnp.zeros(a_ref.shape, F32)

    @pl.loop(0, chunks)
    def _(j):
        start = info[2 + j]

        @pl.when(start <= latest)
        def _():
            rows = pl.ds(pl.multiple_of(j * chunk, chunk), chunk)
            keys = k_ref[rows, :]
            place = start + lax.broadcasted_iota(jnp.int32, (chunk, queries), 0)
            allowed = place <= limit
            for h in range(2):
                scores = jnp.where(allowed, dot_nt(keys, q_heads[h]), NEG_FILL)
                s_ref[h, rows, :] = scores
                m_ref[h] = jnp.maximum(m_ref[h], fold(scores, jnp.max))

    highest = [jnp.max(m_ref[h], axis=0, keepdims=True) for h in range(2)]

    @pl.loop(0, chunks)
    def _(j):
        @pl.when(info[2 + j] <= latest)
        def _():
            rows = pl.ds(pl.multiple_of(j * chunk, chunk), chunk)
            values = v_ref[rows, :]
            for h in range(2):
                weight = jnp.exp(s_ref[h, rows, :] - highest[h])
                l_ref[h] = l_ref[h] + fold(weight, jnp.sum)
                a_ref[h] = a_ref[h] + dot_tn(values, weight.astype(LOW))

    parts = []
    for h in range(2):
        total = jnp.sum(l_ref[h], axis=0, keepdims=True)
        lse_ref[0, pl.ds(h, 1), :] = highest[h] + jnp.log(total)
        parts.append(a_ref[h, pl.ds(h * HEAD_DIM, HEAD_DIM), :] / total)
    c_ref[...] = jnp.concatenate(parts, axis=0).T.astype(c_ref.dtype)


def backward_kernel(causal, chunk, info, q_ref, k_ref, v_ref, c_ref, g_ref, lse_ref, dq_ref, dk_ref, dv_ref, a_ref):
    queries = q_ref.shape[0]
    chunks = k_ref.shape[0] // chunk
    scaling = 1.0 / math.sqrt(HEAD_DIM)
    limit, latest = query_limits(info, queries, causal)
    q_all = q_ref[...] * jnp.asarray(scaling, q_ref.dtype)
    g_all = g_ref[...]
    q_heads = [jnp.where(head_lanes(h), q_all, jnp.zeros_like(q_all)) for h in range(2)]
    g_heads = [jnp.where(head_lanes(h), g_all, jnp.zeros_like(g_all)) for h in range(2)]
    product = (c_ref[...].astype(F32) * g_all.astype(F32)).T
    centres = [
        jnp.sum(product[h * HEAD_DIM : (h + 1) * HEAD_DIM], axis=0, keepdims=True) for h in range(2)
    ]
    logs = [lse_ref[0, pl.ds(h, 1), :] for h in range(2)]
    a_ref[...] = jnp.zeros(a_ref.shape, F32)

    @pl.loop(0, chunks)
    def _(j):
        start = info[2 + j]
        rows = pl.ds(pl.multiple_of(j * chunk, chunk), chunk)

        @pl.when(start <= latest)
        def _():
            keys = k_ref[rows, :]
            values = v_ref[rows, :]
            place = start + lax.broadcasted_iota(jnp.int32, (chunk, queries), 0)
            allowed = place <= limit
            dk = jnp.zeros((chunk, PAIR_LANES), F32)
            dv = jnp.zeros((chunk, PAIR_LANES), F32)
            for h in range(2):
                scores = jnp.where(allowed, dot_nt(keys, q_heads[h]), NEG_FILL)
                prob = jnp.exp(scores - logs[h])
                dprob = dot_nt(values, g_heads[h])
                dv = dv + dot_nn(prob.astype(LOW), g_heads[h])
                dscore = (prob * (dprob - centres[h])).astype(LOW)
                dk = dk + dot_nn(dscore, q_heads[h])
                a_ref[h] = a_ref[h] + dot_tn(keys, dscore)
            dk_ref[rows, :] = dk.astype(dk_ref.dtype)
            dv_ref[rows, :] = dv.astype(dv_ref.dtype)

        @pl.when(start > latest)
        def _():
            dk_ref[rows, :] = jnp.zeros((chunk, PAIR_LANES), dk_ref.dtype)
            dv_ref[rows, :] = jnp.zeros((chunk, PAIR_LANES), dv_ref.dtype)

    parts = [a_ref[h, pl.ds(h * HEAD_DIM, HEAD_DIM), :] for h in range(2)]
    dq_ref[...] = (jnp.concatenate(parts, axis=0).T * scaling).astype(dq_ref.dtype)


def lane_spec(rows):
    return pl.BlockSpec((rows, PAIR_LANES), lambda i, info: (0, i))


def stat_spec(queries):
    return pl.BlockSpec((1, 2, queries), lambda i, info: (i, 0, 0))


def attention_forward(info, queries, keys, values, causal, chunk):
    rows, features = queries.shape
    key_rows = keys.shape[0]
    pairs = features // PAIR_LANES
    return pl.pallas_call(
        functools.partial(forward_kernel, causal, chunk),
        out_shape=(
            jax.ShapeDtypeStruct((rows, features), LOW),
            jax.ShapeDtypeStruct((pairs, 2, rows), F32),
        ),
        grid_spec=pltpu.PrefetchScalarGridSpec(
            num_scalar_prefetch=1,
            grid=(pairs,),
            in_specs=[lane_spec(rows), lane_spec(key_rows), lane_spec(key_rows)],
            out_specs=[lane_spec(rows), stat_spec(rows)],
            scratch_shapes=[
                pltpu.VMEM((2, key_rows, rows), F32),
                pltpu.VMEM((2, 8, rows), F32),
                pltpu.VMEM((2, 8, rows), F32),
                pltpu.VMEM((2, PAIR_LANES, rows), F32),
            ],
        ),
        compiler_params=pltpu.CompilerParams(vmem_limit_bytes=40 << 20),
        cost_estimate=pl.CostEstimate(
            flops=16 * rows * key_rows * features,
            transcendentals=rows * key_rows * features // HEAD_DIM,
            bytes_accessed=4 * (rows + key_rows) * features,
        ),
    )(info, queries, keys, values)


def attention_backward(info, queries, keys, values, context, grads, lse, causal, chunk):
    rows, features = queries.shape
    key_rows = keys.shape[0]
    pairs = features // PAIR_LANES
    return pl.pallas_call(
        functools.partial(backward_kernel, causal, chunk),
        out_shape=(
            jax.ShapeDtypeStruct((rows, features), LOW),
            jax.ShapeDtypeStruct((key_rows, features), LOW),
            jax.ShapeDtypeStruct((key_rows, features), LOW),
        ),
        grid_spec=pltpu.PrefetchScalarGridSpec(
            num_scalar_prefetch=1,
            grid=(pairs,),
            in_specs=[
                lane_spec(rows),
                lane_spec(key_rows),
                lane_spec(key_rows),
                lane_spec(rows),
                lane_spec(rows),
                stat_spec(rows),
            ],
            out_specs=[lane_spec(rows), lane_spec(key_rows), lane_spec(key_rows)],
            scratch_shapes=[pltpu.VMEM((2, PAIR_LANES, rows), F32)],
        ),
        compiler_params=pltpu.CompilerParams(vmem_limit_bytes=40 << 20),
        cost_estimate=pl.CostEstimate(
            flops=40 * rows * key_rows * features,
            transcendentals=rows * key_rows * features // HEAD_DIM,
            bytes_accessed=8 * (rows + key_rows) * features,
        ),
    )(info, queries, keys, values, context, grads, lse)


def whole_kernel(count, rows, cuts, index, source, *targets):
    for step in range(count):
        at = index[step]
        for cut, target in zip(cuts, targets):
            target[pl.ds(step * rows, rows), :] = source[at, :, pl.ds(cut, target.shape[1])]


def halves_kernel(count, rows, cuts, index, *refs):
    sources, targets = refs[: len(cuts)], refs[len(cuts) :]
    half = count // 2
    for step in range(count):
        at = pl.ds(pl.multiple_of(index[step] * rows, rows), rows)
        for cut, source in zip(cuts, sources):
            targets[step // half][step % half, :, pl.ds(cut, source.shape[1])] = source[at, :]


def cuts_of(widths):
    return [sum(widths[:i]) for i in range(len(widths))]


def vmem_specs(number):
    return [pl.BlockSpec(memory_space=pltpu.VMEM)] * number


def to_whole(blocks, index, widths):
    count, rows, columns = blocks.shape
    cuts = cuts_of(widths)
    if rows % 16:
        whole = jnp.take(blocks, index, axis=0).reshape(count * rows, columns)
        return [whole[:, cut : cut + width] for cut, width in zip(cuts, widths)]
    return pl.pallas_call(
        functools.partial(whole_kernel, count, rows, cuts),
        out_shape=[jax.ShapeDtypeStruct((count * rows, width), blocks.dtype) for width in widths],
        in_specs=[pl.BlockSpec(memory_space=pltpu.SMEM)] + vmem_specs(1),
        out_specs=vmem_specs(len(widths)),
        cost_estimate=pl.CostEstimate(
            flops=0, transcendentals=0, bytes_accessed=4 * count * rows * columns
        ),
    )(index, blocks)


def to_halves(wholes, index, rows):
    widths = [whole.shape[1] for whole in wholes]
    columns = sum(widths)
    count = wholes[0].shape[0] // rows
    half = count // 2
    if rows % 16:
        joined = jnp.concatenate(wholes, axis=1).reshape(count, rows, columns)
        joined = jnp.take(joined, index, axis=0)
        return joined[:half], joined[half:]
    shape = jax.ShapeDtypeStruct((half, rows, columns), wholes[0].dtype)
    return pl.pallas_call(
        functools.partial(halves_kernel, count, rows, cuts_of(widths)),
        out_shape=[shape, shape],
        in_specs=[pl.BlockSpec(memory_space=pltpu.SMEM)] + vmem_specs(len(wholes)),
        out_specs=vmem_specs(2),
        cost_estimate=pl.CostEstimate(
            flops=0, transcendentals=0, bytes_accessed=4 * count * rows * columns
        ),
    )(index, *wholes)


def normalize(values):
    inverse = lax.rsqrt(jnp.mean(values * values, axis=-1, keepdims=True) + EPS)
    return values * inverse, inverse


def norm_back(normed, inverse, gain, grads):
    scaled = grads * gain
    return inverse * (scaled - normed * jnp.mean(scaled * normed, axis=-1, keepdims=True))


def gelu_parts(gate):
    factor = math.sqrt(2.0 / math.pi)
    inner = jnp.tanh(factor * (gate + 0.044715 * gate * gate * gate))
    value = 0.5 * gate * (1.0 + inner)
    slope = 0.5 * (1.0 + inner) + 0.5 * gate * (1.0 - inner * inner) * factor * (
        1.0 + 3.0 * 0.044715 * gate * gate
    )
    return value, slope


class Ring:
    def __init__(self):
        self.heads = lax.axis_size("head")
        self.charts = lax.axis_size("dp")
        self.groups = self.heads // 2
        place = lax.axis_index("head")
        self.second = (place % 2) == 1
        self.half = place % 2
        self.group = place // 2
        self.block = lax.axis_index("dp") * self.groups + self.group
        self.blocks = self.charts * self.groups
        chart_bits = [("dp", 1 << i) for i in range(self.charts.bit_length() - 1)]
        group_bits = [("head", 2 << i) for i in range(self.groups.bit_length() - 1)]
        far = chart_bits[1:]
        near = chart_bits[:1]
        self.group_bits = group_bits
        self.orders = (far + near + group_bits, far + group_bits + near)

    def send(self, values, axis, bit):
        size = self.charts if axis == "dp" else self.heads
        return lax.ppermute(values, axis, [(i, i ^ bit) for i in range(size)])

    def swap(self, values):
        return self.send(values, "head", 1)

    def in_order(self, mine, other):
        return jnp.where(self.second, other, mine), jnp.where(self.second, mine, other)

    def joined(self, mine, other, axis):
        return jnp.concatenate(self.in_order(mine, other), axis=axis)

    def masks(self, order):
        masks = [0]
        for axis, bit in order:
            step = bit * self.groups if axis == "dp" else bit // 2
            masks = masks + [m ^ step for m in masks]
        return masks

    def arrivals(self, order):
        apart = self.block ^ jnp.arange(self.blocks, dtype=jnp.int32)
        index = jnp.zeros((self.blocks,), jnp.int32)
        for place, (axis, bit) in enumerate(order):
            step = bit * self.groups if axis == "dp" else bit // 2
            index = index + jnp.where((apart & step) != 0, 1 << place, 0)
        return index

    def origins(self, order):
        return self.block ^ jnp.asarray(self.masks(order), jnp.int32)

    def gather(self, shard, order, widths):
        blocks = shard[None]
        for axis, bit in order:
            blocks = jnp.concatenate([blocks, self.send(blocks, axis, bit)], axis=0)
        return to_whole(blocks, self.arrivals(order), widths)

    def scatter_sum(self, wholes, order, rows):
        keep, give = to_halves(wholes, self.origins(order), rows)
        for place, (axis, bit) in enumerate(reversed(order)):
            got = self.send(give, axis, bit)
            half = keep.shape[0] // 2
            add = lambda cut: keep[cut].astype(F32) + got[cut].astype(F32)
            if half:
                give = add(slice(half, None)).astype(LOW)
                keep = add(slice(0, half)).astype(LOW)
            else:
                keep = add(slice(None))
        return keep[0]

    def pair_rows(self, mine, axis=0):
        return self.joined(mine, self.swap(mine), axis)

    def across(self, mine):
        rows = mine[None]
        for axis, bit in self.group_bits:
            rows = jnp.concatenate([rows, self.send(rows, axis, bit)], axis=0)
        return rows

    def halves(self, weights):
        first = jnp.concatenate([pair[0] for pair in weights], axis=1)
        later = jnp.concatenate([pair[1] for pair in weights], axis=1)
        mine = jnp.where(self.second, later, first)
        give = jnp.where(self.second, first, later)
        return self.joined(mine, self.swap(give), 0)

    def unhalve(self, pair_block):
        rows = pair_block.shape[0] // 2
        upper, lower = pair_block[:rows], pair_block[rows:]
        mine = jnp.where(self.second, lower, upper)
        give = jnp.where(self.second, upper, lower)
        return self.in_order(mine, self.swap(give))


def column_halves(weight):
    half = weight.shape[1] // 2
    return weight[:, :half], weight[:, half:]


def unit_halves(weight, units):
    rows, columns = weight.shape
    split = weight.reshape(rows, columns // (2 * units), 2, units)
    return split[:, :, 0].reshape(rows, -1), split[:, :, 1].reshape(rows, -1)


def unit_whole(first, later, units):
    rows, columns = first.shape
    pieces = [part.reshape(rows, columns // units, 1, units) for part in (first, later)]
    return jnp.concatenate(pieces, axis=2).reshape(rows, 2 * columns)


def on_device(
    tokens,
    memory,
    text_length,
    patch_count,
    self_gain,
    self_query,
    self_key,
    self_value,
    self_out,
    cross_gain,
    cross_query,
    cross_key,
    cross_value,
    cross_out,
    mlp_gain,
    mlp_gate,
    mlp_up,
    mlp_down,
    output_grad,
):
    ring = Ring()
    order_a, order_b = ring.orders
    width = tokens.shape[-1]
    half = width // 2
    units = mlp_down.shape[0]
    hidden_half = units * ring.blocks
    rows = self_query.shape[0]
    own = tokens.shape[1]
    own_patches = memory.shape[1]
    both = 2 * own

    gain_columns = jnp.stack([self_gain, cross_gain, mlp_gain], axis=1)
    gain_columns = jnp.pad(gain_columns, ((0, 0), (0, PAIR_LANES - 3)))
    first_a = ring.halves([column_halves(self_query), (gain_columns, gain_columns)])
    first_b = ring.halves([column_halves(self_key), column_halves(self_value)])
    token_rows = ring.pair_rows(ring.across(tokens[0]), 1).reshape(-1, width)
    query_one, gains = ring.gather(first_a, order_a, [half, PAIR_LANES])
    key_one, value_one = ring.gather(first_b, order_b, [half, half])
    patch_rows = ring.pair_rows(ring.across(memory[0]), 1).reshape(-1, width)
    next_a = ring.halves(
        [column_halves(self_out), column_halves(cross_query), column_halves(cross_out)]
    )
    next_b = ring.halves([column_halves(cross_key), column_halves(cross_value)])
    out_one_half, query_two, out_two_half = ring.gather(next_a, order_a, [half] * 3)
    key_two, value_two = ring.gather(next_b, order_b, [half] * 2)
    out_one = ring.pair_rows(out_one_half, 1)
    out_two = ring.pair_rows(out_two_half, 1)
    gate_rows = ring.halves([unit_halves(mlp_gate, units)])
    up_rows = ring.halves([unit_halves(mlp_up, units)])
    (gate_three,) = ring.gather(gate_rows, order_a, [hidden_half])
    (up_three,) = ring.gather(up_rows, order_b, [hidden_half])
    (down_left,) = ring.gather(mlp_down[:, :half], order_a, [half])
    (down_right,) = ring.gather(mlp_down[:, half:], order_b, [half])
    down_three = jnp.concatenate([down_left, down_right], axis=1)
    grad_low = ring.pair_rows(output_grad[0])

    gain_rows = gains[:, :3].astype(F32).T
    gain_one, gain_two, gain_three = gain_rows[0:1], gain_rows[1:2], gain_rows[2:3]

    token_chunk = math.gcd(256, both)
    patch_chunk = math.gcd(256, 2 * own_patches)

    def chunk_starts(rows_of_pair, chunk):
        groups = ring.group ^ jnp.arange(ring.groups, dtype=jnp.int32)
        inner = jnp.arange(rows_of_pair // chunk, dtype=jnp.int32) * chunk
        return (groups[:, None] * rows_of_pair + inner[None, :]).reshape(-1)

    first_query = (ring.group * both).astype(jnp.int32)[None]
    info_one = jnp.concatenate([text_length, first_query, chunk_starts(both, token_chunk)])
    info_two = jnp.concatenate(
        [patch_count, first_query, chunk_starts(2 * own_patches, patch_chunk)]
    )

    token_float = token_rows.astype(F32)
    plain_one, inverse_one = normalize(token_float)
    normed_one = (plain_one * gain_one).astype(LOW)
    mine_one = normed_one[:both]
    query_heads = dot_nn(mine_one, query_one).astype(LOW)
    key_heads = dot_nn(normed_one, key_one).astype(LOW)
    value_heads = dot_nn(normed_one, value_one).astype(LOW)
    context_heads, lse_one = attention_forward(
        info_one, query_heads, key_heads, value_heads, True, token_chunk
    )
    context_one = ring.pair_rows(context_heads, 1)
    hidden_one = token_float[:both] + dot_nn(context_one, out_one)
    plain_two, inverse_two = normalize(hidden_one)
    normed_two = (plain_two * gain_two).astype(LOW)
    cross_heads = dot_nn(normed_two, query_two).astype(LOW)
    memory_keys = dot_nn(patch_rows, key_two).astype(LOW)
    memory_values = dot_nn(patch_rows, value_two).astype(LOW)
    cross_context, lse_two = attention_forward(
        info_two, cross_heads, memory_keys, memory_values, False, patch_chunk
    )
    context_two = ring.pair_rows(cross_context, 1)
    hidden_two = hidden_one + dot_nn(context_two, out_two)
    plain_three, inverse_three = normalize(hidden_two)
    normed_three = (plain_three * gain_three).astype(LOW)
    gate = dot_nn(normed_three, gate_three)
    up = dot_nn(normed_three, up_three)
    active, slope = gelu_parts(gate)
    mixed = (active * up).astype(LOW)

    def own_rows(values, count):
        return lax.dynamic_slice_in_dim(values, ring.half * count, count, 0)

    def other_rows(values, count):
        return lax.dynamic_slice_in_dim(values, (1 - ring.half) * count, count, 0)

    down_part = dot_nn(mixed, down_three)
    down_got = ring.swap(other_rows(down_part, own).astype(LOW))
    output = (
        own_rows(hidden_two, own) + own_rows(down_part, own) + down_got.astype(F32)
    ).astype(LOW)

    grad_float = grad_low.astype(F32)
    ddown = dot_tn(mixed, grad_low).astype(LOW)
    grad_mixed = dot_nt(grad_low, down_three)
    gate_low = (grad_mixed * up * slope).astype(LOW)
    up_low = (grad_mixed * active).astype(LOW)
    dgate = dot_tn(normed_three, gate_low).astype(LOW)
    dup = dot_tn(normed_three, up_low).astype(LOW)
    part_three = dot_nt(gate_low, gate_three) + dot_nt(up_low, up_three)
    mlp_dgain = jnp.sum(part_three * plain_three, axis=0)
    part_low = part_three.astype(LOW)
    dnormed_three = part_low.astype(F32) + ring.swap(part_low).astype(F32)
    dhidden_two = grad_float + norm_back(plain_three, inverse_three, gain_three, dnormed_three)
    branch_two = dhidden_two.astype(LOW)
    mlp_dgate = ring.scatter_sum([dgate], order_a, 2 * rows)
    mlp_dup = ring.scatter_sum([dup], order_b, 2 * rows)
    ddown_left = ring.scatter_sum([ddown[:, :half]], order_a, units)
    ddown_right = ring.scatter_sum([ddown[:, half:]], order_b, units)
    mlp_ddown = jnp.concatenate([ddown_left, ddown_right], axis=1)

    def own_columns(values):
        return lax.dynamic_slice_in_dim(values, ring.half * half, half, 1)

    dcontext_two = dot_nt(branch_two, own_rows(out_two, half)).astype(LOW)
    dout_two = dot_tn(context_two, own_columns(branch_two)).astype(LOW)
    dquery, dkey, dvalue = attention_backward(
        info_two,
        cross_heads,
        memory_keys,
        memory_values,
        cross_context,
        dcontext_two,
        lse_two,
        False,
        patch_chunk,
    )
    part_two = dot_nt(dquery, query_two)
    cross_dgain = jnp.sum(part_two * plain_two, axis=0)
    part_low = part_two.astype(LOW)
    dnormed_two = part_low.astype(F32) + ring.swap(part_low).astype(F32)
    dhidden_one = dhidden_two + norm_back(plain_two, inverse_two, gain_two, dnormed_two)
    branch_one = dhidden_one.astype(LOW)
    dquery_two = dot_tn(normed_two, dquery).astype(LOW)
    dkey_two = dot_tn(patch_rows, dkey).astype(LOW)
    dvalue_two = dot_tn(patch_rows, dvalue).astype(LOW)
    cross_a = ring.scatter_sum([dout_two, dquery_two], order_a, 2 * rows)
    cross_b = ring.scatter_sum([dkey_two, dvalue_two], order_b, 2 * rows)

    def to_owner(part, count):
        part = part.reshape(ring.groups, 2, count, width)
        first, later = part[:, 0], part[:, 1]
        keep = jnp.where(ring.second, later, first)
        give = jnp.where(ring.second, first, later).astype(LOW)
        total = keep + ring.swap(give).astype(F32)
        for axis, bit in reversed(ring.group_bits):
            middle = total.shape[0] // 2
            total = total[:middle] + ring.send(total[middle:].astype(LOW), axis, bit).astype(F32)
        return total[0]

    memory_grad = to_owner(dot_nt(dkey, key_two) + dot_nt(dvalue, value_two), own_patches)

    dcontext_one = dot_nt(branch_one, own_rows(out_one, half)).astype(LOW)
    dout_one = dot_tn(context_one, own_columns(branch_one)).astype(LOW)
    dquery, dkey, dvalue = attention_backward(
        info_one,
        query_heads,
        key_heads,
        value_heads,
        context_heads,
        dcontext_one,
        lse_one,
        True,
        token_chunk,
    )
    dquery_one = dot_tn(mine_one, dquery).astype(LOW)
    dkey_one = dot_tn(normed_one, dkey).astype(LOW)
    dvalue_one = dot_tn(normed_one, dvalue).astype(LOW)
    part_one = dot_nt(dkey, key_one) + dot_nt(dvalue, value_one)
    part_mine = part_one[:both] + dot_nt(dquery, query_one)
    part_one = jnp.concatenate([part_mine, part_one[both:]], axis=0)
    self_dgain = jnp.sum(part_one * plain_one, axis=0)
    dgains = jnp.stack([self_dgain, cross_dgain, mlp_dgain], axis=1)
    dgains = jnp.pad(dgains, ((0, 0), (0, PAIR_LANES - 3))).astype(LOW)
    self_a = ring.scatter_sum([dquery_one, dout_one, dgains], order_a, 2 * rows)
    self_b = ring.scatter_sum([dkey_one, dvalue_one], order_b, 2 * rows)
    dnormed_one = to_owner(part_one, own)
    last = norm_back(
        own_rows(plain_one[:both], own), own_rows(inverse_one[:both], own), gain_one, dnormed_one
    )
    input_grad = own_rows(dhidden_one, own) + last

    def split(block, widths):
        cuts = [sum(widths[:i]) for i in range(len(widths) + 1)]
        return [block[:, cuts[i] : cuts[i + 1]] for i in range(len(widths))]

    def finished(block, widths):
        first, later = ring.unhalve(block)
        pieces = zip(split(first, widths), split(later, widths))
        return [jnp.concatenate(pair, axis=1) for pair in pieces]

    mlp_dgate = unit_whole(*ring.unhalve(mlp_dgate), units)
    mlp_dup = unit_whole(*ring.unhalve(mlp_dup), units)
    cross_dout, cross_dquery = finished(cross_a, [half] * 2)
    cross_dkey, cross_dvalue = finished(cross_b, [half] * 2)
    self_first, self_later = ring.unhalve(self_a)
    dgain_columns = self_first[:, 2 * half : 2 * half + 3] + self_later[:, 2 * half : 2 * half + 3]
    self_dquery = jnp.concatenate([self_first[:, :half], self_later[:, :half]], axis=1)
    self_dout = jnp.concatenate(
        [self_first[:, half : 2 * half], self_later[:, half : 2 * half]], axis=1
    )
    self_dkey, self_dvalue = finished(self_b, [half] * 2)

    return (
        output[None],
        input_grad[None],
        memory_grad[None],
        dgain_columns[:, 0],
        self_dquery,
        self_dkey,
        self_dvalue,
        self_dout,
        dgain_columns[:, 1],
        cross_dquery,
        cross_dkey,
        cross_dvalue,
        cross_dout,
        dgain_columns[:, 2],
        mlp_dgate,
        mlp_dup,
        mlp_ddown,
    )


def solution(mesh):
    rows = P(("dp", "head"), None)
    vector = P(("dp", "head"))
    grid = P("dp", "head", None)
    in_specs = (grid, grid, P("dp"), P("dp"))
    in_specs += (vector, rows, rows, rows, rows) * 2
    in_specs += (vector, rows, rows, rows, grid)
    out_specs = (grid, grid, grid)
    out_specs += (vector, rows, rows, rows, rows) * 2
    out_specs += (vector, rows, rows, rows)
    return jax.shard_map(
        on_device, mesh=mesh, in_specs=in_specs, out_specs=out_specs, check_vma=False
    )
```

```python
import functools
import math

import jax
import jax.numpy as jnp
from jax import lax
from jax.experimental import pallas as pl
from jax.experimental.pallas import tpu as pltpu
from jax.sharding import Mesh
from jax.sharding import PartitionSpec as P

HEAD_DIM = 64
PAIR_LANES = 128
NEG_FILL = -1e30
EPS = 1e-06
F32 = jnp.float32
LOW = jnp.bfloat16


NT = (((1,), (1,)), ((), ()))
TN = (((0,), (0,)), ((), ()))


def dot_nt(left, right):
    return lax.dot_general(left, right, NT, preferred_element_type=F32)


def dot_tn(left, right):
    return lax.dot_general(left, right, TN, preferred_element_type=F32)


def dot_nn(left, right):
    return jnp.dot(left, right, preferred_element_type=F32)


def query_limits(info, queries, causal):
    last = info[0] - 1
    if not causal:
        return jnp.full((1, queries), last, jnp.int32), last
    rows = info[1] + lax.broadcasted_iota(jnp.int32, (1, queries), 1)
    return jnp.minimum(rows, last), jnp.minimum(info[1] + queries - 1, last)


def head_lanes(head):
    lanes = lax.broadcasted_iota(jnp.int32, (1, PAIR_LANES), 1)
    return (lanes // HEAD_DIM) == head


def fold(values, op):
    rows, columns = values.shape
    return op(values.reshape(rows // 8, 8, columns), axis=0)


def forward_kernel(causal, chunk, info, q_ref, k_ref, v_ref, c_ref, lse_ref, s_ref, m_ref, l_ref, a_ref):
    queries = q_ref.shape[0]
    chunks = k_ref.shape[0] // chunk
    scaling = 1.0 / math.sqrt(HEAD_DIM)
    limit, latest = query_limits(info, queries, causal)
    q_all = q_ref[...] * jnp.asarray(scaling, q_ref.dtype)
    q_heads = [jnp.where(head_lanes(h), q_all, jnp.zeros_like(q_all)) for h in range(2)]
    m_ref[...] = jnp.full(m_ref.shape, NEG_FILL, F32)
    l_ref[...] = jnp.zeros(l_ref.shape, F32)
    a_ref[...] = jnp.zeros(a_ref.shape, F32)

    @pl.loop(0, chunks)
    def _(j):
        start = info[2 + j]

        @pl.when(start <= latest)
        def _():
            rows = pl.ds(pl.multiple_of(j * chunk, chunk), chunk)
            keys = k_ref[rows, :]
            place = start + lax.broadcasted_iota(jnp.int32, (chunk, queries), 0)
            allowed = place <= limit
            for h in range(2):
                scores = jnp.where(allowed, dot_nt(keys, q_heads[h]), NEG_FILL)
                s_ref[h, rows, :] = scores
                m_ref[h] = jnp.maximum(m_ref[h], fold(scores, jnp.max))

    highest = [jnp.max(m_ref[h], axis=0, keepdims=True) for h in range(2)]

    @pl.loop(0, chunks)
    def _(j):
        @pl.when(info[2 + j] <= latest)
        def _():
            rows = pl.ds(pl.multiple_of(j * chunk, chunk), chunk)
            values = v_ref[rows, :]
            for h in range(2):
                weight = jnp.exp(s_ref[h, rows, :] - highest[h])
                l_ref[h] = l_ref[h] + fold(weight, jnp.sum)
                a_ref[h] = a_ref[h] + dot_tn(values, weight.astype(LOW))

    parts = []
    for h in range(2):
        total = jnp.sum(l_ref[h], axis=0, keepdims=True)
        lse_ref[0, pl.ds(h, 1), :] = highest[h] + jnp.log(total)
        parts.append(a_ref[h, pl.ds(h * HEAD_DIM, HEAD_DIM), :] / total)
    c_ref[...] = jnp.concatenate(parts, axis=0).T.astype(c_ref.dtype)


def backward_kernel(causal, chunk, info, q_ref, k_ref, v_ref, c_ref, g_ref, lse_ref, dq_ref, dk_ref, dv_ref, a_ref):
    queries = q_ref.shape[0]
    chunks = k_ref.shape[0] // chunk
    scaling = 1.0 / math.sqrt(HEAD_DIM)
    limit, latest = query_limits(info, queries, causal)
    q_all = q_ref[...] * jnp.asarray(scaling, q_ref.dtype)
    g_all = g_ref[...]
    q_heads = [jnp.where(head_lanes(h), q_all, jnp.zeros_like(q_all)) for h in range(2)]
    g_heads = [jnp.where(head_lanes(h), g_all, jnp.zeros_like(g_all)) for h in range(2)]
    product = (c_ref[...].astype(F32) * g_all.astype(F32)).T
    centres = [
        jnp.sum(product[h * HEAD_DIM : (h + 1) * HEAD_DIM], axis=0, keepdims=True) for h in range(2)
    ]
    logs = [lse_ref[0, pl.ds(h, 1), :] for h in range(2)]
    a_ref[...] = jnp.zeros(a_ref.shape, F32)

    @pl.loop(0, chunks)
    def _(j):
        start = info[2 + j]
        rows = pl.ds(pl.multiple_of(j * chunk, chunk), chunk)

        @pl.when(start <= latest)
        def _():
            keys = k_ref[rows, :]
            values = v_ref[rows, :]
            place = start + lax.broadcasted_iota(jnp.int32, (chunk, queries), 0)
            allowed = place <= limit
            dk = jnp.zeros((chunk, PAIR_LANES), F32)
            dv = jnp.zeros((chunk, PAIR_LANES), F32)
            for h in range(2):
                scores = jnp.where(allowed, dot_nt(keys, q_heads[h]), NEG_FILL)
                prob = jnp.exp(scores - logs[h])
                dprob = dot_nt(values, g_heads[h])
                dv = dv + dot_nn(prob.astype(LOW), g_heads[h])
                dscore = (prob * (dprob - centres[h])).astype(LOW)
                dk = dk + dot_nn(dscore, q_heads[h])
                a_ref[h] = a_ref[h] + dot_tn(keys, dscore)
            dk_ref[rows, :] = dk.astype(dk_ref.dtype)
            dv_ref[rows, :] = dv.astype(dv_ref.dtype)

        @pl.when(start > latest)
        def _():
            dk_ref[rows, :] = jnp.zeros((chunk, PAIR_LANES), dk_ref.dtype)
            dv_ref[rows, :] = jnp.zeros((chunk, PAIR_LANES), dv_ref.dtype)

    parts = [a_ref[h, pl.ds(h * HEAD_DIM, HEAD_DIM), :] for h in range(2)]
    dq_ref[...] = (jnp.concatenate(parts, axis=0).T * scaling).astype(dq_ref.dtype)


def lane_spec(rows):
    return pl.BlockSpec((rows, PAIR_LANES), lambda i, info: (0, i))


def stat_spec(queries):
    return pl.BlockSpec((1, 2, queries), lambda i, info: (i, 0, 0))


def attention_forward(info, queries, keys, values, causal, chunk):
    rows, features = queries.shape
    key_rows = keys.shape[0]
    pairs = features // PAIR_LANES
    return pl.pallas_call(
        functools.partial(forward_kernel, causal, chunk),
        out_shape=(
            jax.ShapeDtypeStruct((rows, features), LOW),
            jax.ShapeDtypeStruct((pairs, 2, rows), F32),
        ),
        grid_spec=pltpu.PrefetchScalarGridSpec(
            num_scalar_prefetch=1,
            grid=(pairs,),
            in_specs=[lane_spec(rows), lane_spec(key_rows), lane_spec(key_rows)],
            out_specs=[lane_spec(rows), stat_spec(rows)],
            scratch_shapes=[
                pltpu.VMEM((2, key_rows, rows), F32),
                pltpu.VMEM((2, 8, rows), F32),
                pltpu.VMEM((2, 8, rows), F32),
                pltpu.VMEM((2, PAIR_LANES, rows), F32),
            ],
        ),
        compiler_params=pltpu.CompilerParams(vmem_limit_bytes=40 << 20),
        cost_estimate=pl.CostEstimate(
            flops=16 * rows * key_rows * features,
            transcendentals=rows * key_rows * features // HEAD_DIM,
            bytes_accessed=4 * (rows + key_rows) * features,
        ),
    )(info, queries, keys, values)


def attention_backward(info, queries, keys, values, context, grads, lse, causal, chunk):
    rows, features = queries.shape
    key_rows = keys.shape[0]
    pairs = features // PAIR_LANES
    return pl.pallas_call(
        functools.partial(backward_kernel, causal, chunk),
        out_shape=(
            jax.ShapeDtypeStruct((rows, features), LOW),
            jax.ShapeDtypeStruct((key_rows, features), LOW),
            jax.ShapeDtypeStruct((key_rows, features), LOW),
        ),
        grid_spec=pltpu.PrefetchScalarGridSpec(
            num_scalar_prefetch=1,
            grid=(pairs,),
            in_specs=[
                lane_spec(rows),
                lane_spec(key_rows),
                lane_spec(key_rows),
                lane_spec(rows),
                lane_spec(rows),
                stat_spec(rows),
            ],
            out_specs=[lane_spec(rows), lane_spec(key_rows), lane_spec(key_rows)],
            scratch_shapes=[pltpu.VMEM((2, PAIR_LANES, rows), F32)],
        ),
        compiler_params=pltpu.CompilerParams(vmem_limit_bytes=40 << 20),
        cost_estimate=pl.CostEstimate(
            flops=40 * rows * key_rows * features,
            transcendentals=rows * key_rows * features // HEAD_DIM,
            bytes_accessed=8 * (rows + key_rows) * features,
        ),
    )(info, queries, keys, values, context, grads, lse)


def whole_kernel(count, rows, cuts, index, first, later, *targets):
    half = count // 2
    for step in range(count):
        at = index[step]
        place = pl.ds(step * rows, rows)

        def put(source, block):
            for cut, target in zip(cuts, targets):
                target[place, :] = source[block, :, pl.ds(cut, target.shape[1])]

        @pl.when(at < half)
        def _():
            put(first, at)

        @pl.when(at >= half)
        def _():
            put(later, at - half)


def halves_kernel(count, rows, cuts, index, *refs):
    sources, targets = refs[: len(cuts)], refs[len(cuts) :]
    half = count // 2
    for step in range(count):
        at = pl.ds(pl.multiple_of(index[step] * rows, rows), rows)
        for cut, source in zip(cuts, sources):
            targets[step // half][step % half, :, pl.ds(cut, source.shape[1])] = source[at, :]


def cuts_of(widths):
    return [sum(widths[:i]) for i in range(len(widths))]


def vmem_specs(number):
    return [pl.BlockSpec(memory_space=pltpu.VMEM)] * number


def to_whole(first, later, index, widths):
    half, rows, columns = first.shape
    count = 2 * half
    cuts = cuts_of(widths)
    if rows % 16:
        blocks = jnp.concatenate([first, later], axis=0)
        whole = jnp.take(blocks, index, axis=0).reshape(count * rows, columns)
        return [whole[:, cut : cut + width] for cut, width in zip(cuts, widths)]
    return pl.pallas_call(
        functools.partial(whole_kernel, count, rows, cuts),
        out_shape=[jax.ShapeDtypeStruct((count * rows, width), first.dtype) for width in widths],
        in_specs=[pl.BlockSpec(memory_space=pltpu.SMEM)] + vmem_specs(2),
        out_specs=vmem_specs(len(widths)),
        cost_estimate=pl.CostEstimate(
            flops=0, transcendentals=0, bytes_accessed=4 * count * rows * columns
        ),
    )(index, first, later)


def to_halves(wholes, index, rows):
    widths = [whole.shape[1] for whole in wholes]
    columns = sum(widths)
    count = wholes[0].shape[0] // rows
    half = count // 2
    if rows % 16:
        joined = jnp.concatenate(wholes, axis=1).reshape(count, rows, columns)
        joined = jnp.take(joined, index, axis=0)
        return joined[:half], joined[half:]
    shape = jax.ShapeDtypeStruct((half, rows, columns), wholes[0].dtype)
    return pl.pallas_call(
        functools.partial(halves_kernel, count, rows, cuts_of(widths)),
        out_shape=[shape, shape],
        in_specs=[pl.BlockSpec(memory_space=pltpu.SMEM)] + vmem_specs(len(wholes)),
        out_specs=vmem_specs(2),
        cost_estimate=pl.CostEstimate(
            flops=0, transcendentals=0, bytes_accessed=4 * count * rows * columns
        ),
    )(index, *wholes)


def unit_tile(source, at, second):
    lanes = 2 * HEAD_DIM
    start = 2 * at * lanes + (HEAD_DIM if second else 0)
    return jnp.concatenate(
        [source[:, pl.ds(start, HEAD_DIM)], source[:, pl.ds(start + lanes, HEAD_DIM)]], axis=1
    )


def shards_kernel(kinds, place, *refs):
    sources, targets = refs[:-2], refs[-2:]

    def write(target, second):
        cut = 0
        for kind, source in zip(kinds, sources):
            columns = source.shape[1]
            if kind == "all":
                target[:, pl.ds(cut, columns)] = source[...]
                cut += columns
                continue
            if kind == "half":
                start = columns // 2 if second else 0
                target[:, pl.ds(cut, columns // 2)] = source[:, pl.ds(start, columns // 2)]
            else:
                for tile in range(columns // 256):
                    target[:, pl.ds(cut + 128 * tile, 128)] = unit_tile(source, tile, second)
            cut += columns // 2

    @pl.when(place[0] == 0)
    def _():
        write(targets[0], False)
        write(targets[1], True)

    @pl.when(place[0] != 0)
    def _():
        write(targets[0], True)
        write(targets[1], False)


def rows_kernel(widths, piece, place, mine, other, down, *targets):
    rows = mine.shape[0]

    def write(upper, lower):
        cut = 0
        for target, width in zip(targets[:-1], widths):
            target[0, pl.ds(0, rows), :] = upper[:, pl.ds(cut, width)]
            target[0, pl.ds(rows, rows), :] = lower[:, pl.ds(cut, width)]
            cut += width
        packed = targets[-1]
        columns = (mine.shape[1] - cut) // 2
        step = 8
        for start in range(0, 2 * rows, step):
            source = upper if start < rows else lower
            number, inner = start // piece, start % piece
            for matrix in range(2):
                place_at = (matrix * (2 * rows // piece) + number) * columns
                packed[pl.ds(inner, step), pl.ds(place_at, columns)] = source[
                    pl.ds(start % rows, step), pl.ds(cut + matrix * columns, columns)
                ]
        base = 2 * (2 * rows // piece) * columns
        width = down.shape[1]
        for number in range(down.shape[0] // piece):
            packed[:, pl.ds(base + number * width, width)] = down[pl.ds(number * piece, piece), :]

    @pl.when(place[0] == 0)
    def _():
        write(mine, other)

    @pl.when(place[0] != 0)
    def _():
        write(other, mine)


SMEM_SPEC = pl.BlockSpec(memory_space=pltpu.SMEM)


def cut_shards(place, shards, kinds):
    rows = shards[0].shape[0]
    columns = sum(w.shape[1] if k == "all" else w.shape[1] // 2 for w, k in zip(shards, kinds))
    shape = jax.ShapeDtypeStruct((rows, columns), LOW)
    return pl.pallas_call(
        functools.partial(shards_kernel, kinds),
        out_shape=[shape, shape],
        in_specs=[SMEM_SPEC] + vmem_specs(len(shards)),
        out_specs=vmem_specs(2),
    )(place, *shards)


def join_rows(place, mine, other, down, widths, piece):
    rows = 2 * mine.shape[0]
    rest = mine.shape[1] - sum(widths)
    packed = rest * (rows // piece) + down.shape[1] * (down.shape[0] // piece)
    return pl.pallas_call(
        functools.partial(rows_kernel, widths, piece),
        out_shape=[jax.ShapeDtypeStruct((1, rows, width), LOW) for width in widths]
        + [jax.ShapeDtypeStruct((piece, packed), LOW)],
        in_specs=[SMEM_SPEC] + vmem_specs(3),
        out_specs=vmem_specs(len(widths) + 1),
    )(place, mine, other, down)


def mlp_kernel(
    chunk, a_ref, g_ref, w_ref, part_ref, down_ref, grad_ref, gate_w, up_w, down_w, p_acc, d_acc, sems
):
    blocks, pieces, piece, units = gate_w.shape
    down_pieces, width = down_w.shape[1], down_w.shape[3]
    moves = []
    for number in range(pieces):
        moves.append((w_ref.at[:, :, pl.ds(number * units, units)], gate_w.at[:, number]))
    for number in range(pieces):
        moves.append((w_ref.at[:, :, pl.ds((pieces + number) * units, units)], up_w.at[:, number]))
    base = 2 * pieces * units
    for number in range(down_pieces):
        moves.append((w_ref.at[:, :, pl.ds(base + number * width, width)], down_w.at[:, number]))
    copies = [pltpu.make_async_copy(a, b, sems.at[i]) for i, (a, b) in enumerate(moves)]
    for copy in copies:
        copy.start()
    for copy in copies:
        copy.wait()

    a_in = a_ref[...]
    g_in = g_ref[...]
    per_block = down_pieces * piece
    step_blocks = chunk // per_block
    for start in range(0, units, chunk):
        columns = pl.ds(start, chunk)
        gate_part = gate_w[:, :, :, columns].reshape(blocks * pieces * piece, chunk)
        up_part = up_w[:, :, :, columns].reshape(blocks * pieces * piece, chunk)
        block_at = start // per_block
        down_part = down_w[pl.ds(block_at, step_blocks)].reshape(chunk, width)
        gate = dot_nn(a_in, gate_part)
        up = dot_nn(a_in, up_part)
        active, slope = gelu_parts(gate)
        mixed = (active * up).astype(LOW)
        grad = dot_nt(g_in, down_part)
        gate_low = (grad * up * slope).astype(LOW)
        up_low = (grad * active).astype(LOW)
        down_new = dot_nn(mixed, down_part)
        part_new = dot_nt(gate_low, gate_part) + dot_nt(up_low, up_part)
        if start == 0:
            d_acc[...] = down_new
            p_acc[...] = part_new
        else:
            d_acc[...] += down_new
            p_acc[...] += part_new
        dgate = dot_tn(a_in, gate_low).astype(LOW).reshape(blocks, pieces, piece, chunk)
        dup = dot_tn(a_in, up_low).astype(LOW).reshape(blocks, pieces, piece, chunk)
        for number in range(pieces):
            grad_ref[:, :, pl.ds(number * units + start, chunk)] = dgate[:, number]
            grad_ref[:, :, pl.ds((pieces + number) * units + start, chunk)] = dup[:, number]
        ddown = dot_tn(mixed, g_in).astype(LOW).reshape(step_blocks, down_pieces, piece, width)
        for number in range(down_pieces):
            grad_ref[pl.ds(block_at, step_blocks), :, pl.ds(base + number * width, width)] = ddown[
                :, number
            ]
    part_ref[...] = p_acc[...]
    down_ref[...] = d_acc[...]


def feed_forward(normed, grads, packed, pieces, down_pieces, units):
    rows, width = normed.shape
    blocks, piece, columns = packed.shape
    big = jax.ShapeDtypeStruct((rows, width), F32)
    return pl.pallas_call(
        functools.partial(mlp_kernel, 256),
        out_shape=[big, big, jax.ShapeDtypeStruct(packed.shape, LOW)],
        in_specs=vmem_specs(2) + [pl.BlockSpec(memory_space=pl.ANY)],
        out_specs=vmem_specs(3),
        scratch_shapes=[
            pltpu.VMEM((blocks, pieces, piece, units), LOW),
            pltpu.VMEM((blocks, pieces, piece, units), LOW),
            pltpu.VMEM((blocks, down_pieces, piece, width), LOW),
            pltpu.VMEM((rows, width), F32),
            pltpu.VMEM((rows, width), F32),
            pltpu.SemaphoreType.DMA((2 * pieces + down_pieces,)),
        ],
        compiler_params=pltpu.CompilerParams(vmem_limit_bytes=48 << 20),
        cost_estimate=pl.CostEstimate(
            flops=18 * rows * width * units,
            transcendentals=rows * units,
            bytes_accessed=4 * blocks * piece * columns + 12 * rows * width,
        ),
    )(normed, grads, packed)


def normalize(values):
    inverse = lax.rsqrt(jnp.mean(values * values, axis=-1, keepdims=True) + EPS)
    return values * inverse, inverse


def norm_back(normed, inverse, gain, grads):
    scaled = grads * gain
    return inverse * (scaled - normed * jnp.mean(scaled * normed, axis=-1, keepdims=True))


def gelu_parts(gate):
    factor = math.sqrt(2.0 / math.pi)
    inner = jnp.tanh(factor * (gate + 0.044715 * gate * gate * gate))
    value = 0.5 * gate * (1.0 + inner)
    slope = 0.5 * (1.0 + inner) + 0.5 * gate * (1.0 - inner * inner) * factor * (
        1.0 + 3.0 * 0.044715 * gate * gate
    )
    return value, slope


class Ring:
    def __init__(self):
        self.charts = lax.axis_size("dp")
        self.groups = lax.axis_size("hx")
        self.half = lax.axis_index("hc")
        self.second = self.half == 1
        self.group = lax.axis_index("hx")
        self.block = lax.axis_index("dp") * self.groups + self.group
        self.blocks = self.charts * self.groups
        chart_bits = [("dp", 1 << i) for i in range(self.charts.bit_length() - 1)]
        self.group_bits = [("hx", 1 << i) for i in range(self.groups.bit_length() - 1)]
        self.far = chart_bits[1:]
        near = chart_bits[:1]
        self.tails = (near + self.group_bits, self.group_bits + near)
        self.orders = tuple(self.far + tail for tail in self.tails)

    def send(self, values, axis, bit):
        size = self.charts if axis == "dp" else self.groups
        return lax.ppermute(values, axis, [(i, i ^ bit) for i in range(size)])

    def swap(self, values):
        return lax.ppermute(values, "hc", [(0, 1), (1, 0)])

    def in_order(self, mine, other):
        return jnp.where(self.second, other, mine), jnp.where(self.second, mine, other)

    def joined(self, mine, other, axis):
        return jnp.concatenate(self.in_order(mine, other), axis=axis)

    def masks(self, order):
        masks = [0]
        for axis, bit in order:
            step = bit * self.groups if axis == "dp" else bit
            masks = masks + [m ^ step for m in masks]
        return masks

    def arrivals(self, order):
        apart = self.block ^ jnp.arange(self.blocks, dtype=jnp.int32)
        index = jnp.zeros((self.blocks,), jnp.int32)
        for place, (axis, bit) in enumerate(order):
            step = bit * self.groups if axis == "dp" else bit
            index = index + jnp.where((apart & step) != 0, 1 << place, 0)
        return index

    def origins(self, order):
        return self.block ^ jnp.asarray(self.masks(order), jnp.int32)

    def gather(self, blocks, widths):
        for axis, bit in self.far:
            blocks = jnp.concatenate([blocks, self.send(blocks, axis, bit)], axis=0)
        cut = sum(widths[0])
        parts = [blocks[:, :, :cut], blocks[:, :, cut:]]
        got = [None, None]
        for place in range(len(self.tails[0])):
            for side, tail in enumerate(self.tails):
                if place:
                    parts[side] = jnp.concatenate([parts[side], got[side]], axis=0)
                got[side] = self.send(parts[side], *tail[place])
        whole = []
        for side, order in enumerate(self.orders):
            whole += to_whole(parts[side], got[side], self.arrivals(order), widths[side])
        return whole

    def scatter_sum(self, sides, rows):
        add = lambda keep, got: keep.astype(F32) + got.astype(F32)
        keeps, gives = [], []
        for wholes, order in zip(sides, self.orders):
            keep, give = to_halves(wholes, self.origins(order), rows)
            keeps.append(keep)
            gives.append(give)
        steps = len(self.tails[0])
        for place in reversed(range(steps)):
            for side, tail in enumerate(self.tails):
                got = self.send(gives[side], *tail[place])
                half = got.shape[0] // 2
                if place:
                    gives[side] = add(keeps[side][half:], got[half:]).astype(LOW)
                    keeps[side] = add(keeps[side][:half], got[:half]).astype(LOW)
                else:
                    gives[side] = add(keeps[side][half:], got[half:])
                    keeps[side] = add(keeps[side][:half], got[:half])
        keep = jnp.concatenate(keeps, axis=2)
        give = jnp.concatenate(gives, axis=2).astype(LOW)
        for place, (axis, bit) in enumerate(reversed(self.far)):
            got = self.send(give, axis, bit)
            half = keep.shape[0] // 2
            if half:
                give = add(keep[half:], got[half:]).astype(LOW)
                keep = add(keep[:half], got[:half])
            else:
                keep = add(keep, got)
        return keep[0]

    def pair_rows(self, mine, axis=0):
        return self.joined(mine, self.swap(mine), axis)

    def across(self, mine):
        rows = mine[None]
        for axis, bit in self.group_bits:
            rows = jnp.concatenate([rows, self.send(rows, axis, bit)], axis=0)
        return rows

    def halves(self, weights):
        first = jnp.concatenate([pair[0] for pair in weights], axis=1)
        later = jnp.concatenate([pair[1] for pair in weights], axis=1)
        mine = jnp.where(self.second, later, first)
        give = jnp.where(self.second, first, later)
        return self.joined(mine, self.swap(give), 0)

    def unhalve(self, pair_block):
        rows = pair_block.shape[0] // 2
        upper, lower = pair_block[:rows], pair_block[rows:]
        mine = jnp.where(self.second, lower, upper)
        give = jnp.where(self.second, upper, lower)
        return self.in_order(mine, self.swap(give))


def column_halves(weight):
    half = weight.shape[1] // 2
    return weight[:, :half], weight[:, half:]


def unit_halves(weight, units):
    rows, columns = weight.shape
    split = weight.reshape(rows, columns // (2 * units), 2, units)
    return split[:, :, 0].reshape(rows, -1), split[:, :, 1].reshape(rows, -1)


def unit_whole(first, later, units):
    rows, columns = first.shape
    pieces = [part.reshape(rows, columns // units, 1, units) for part in (first, later)]
    return jnp.concatenate(pieces, axis=2).reshape(rows, 2 * columns)


def on_device(
    tokens,
    memory,
    text_length,
    patch_count,
    self_gain,
    self_query,
    self_key,
    self_value,
    self_out,
    cross_gain,
    cross_query,
    cross_key,
    cross_value,
    cross_out,
    mlp_gain,
    mlp_gate,
    mlp_up,
    mlp_down,
    output_grad,
):
    ring = Ring()
    width = tokens.shape[-1]
    half = width // 2
    units = mlp_down.shape[0]
    hidden_half = units * ring.blocks
    rows = self_query.shape[0]
    own = tokens.shape[1]
    own_patches = memory.shape[1]
    both = 2 * own
    piece = 16
    packed = (2 * rows) % piece == 0 and units == HEAD_DIM and ring.blocks > 1
    pieces, down_pieces = 2 * rows // piece, units // piece
    pairs = ("dp", "hx")

    gain_columns = jnp.stack([self_gain, cross_gain, mlp_gain], axis=1)
    gain_columns = jnp.pad(gain_columns, ((0, 0), (0, PAIR_LANES - 3)))
    group_one = [self_query, gain_columns, self_key, self_value]
    group_two = [self_out, cross_query, cross_out, cross_key, cross_value]
    kinds_one = ["half", "all", "half", "half"]
    widths_one = ([half, PAIR_LANES], [half, half])
    widths_two = ([half] * 3, [half] * 2)
    total_one, total_two = 3 * half + PAIR_LANES, 5 * half
    if packed:
        place = ring.half.astype(jnp.int32)[None]
        shards = group_one + group_two + [mlp_gate, mlp_up]
        kinds = kinds_one + ["half"] * 5 + ["units"] * 2
        mine, give = cut_shards(place, shards, kinds)
        other = ring.swap(give)
        blocks_one, blocks_two, blocks_mlp = join_rows(
            place, mine, other, mlp_down, [total_one, total_two], piece
        )
        mlp_weights = lax.all_gather(blocks_mlp, pairs, axis=0, tiled=True)
        mlp_weights = mlp_weights.reshape(ring.blocks, piece, -1)
    else:
        both_halves = lambda w, k: (w, w) if k == "all" else column_halves(w)
        blocks_one = ring.halves([both_halves(w, k) for w, k in zip(group_one, kinds_one)])[None]
        blocks_two = ring.halves([column_halves(w) for w in group_two])[None]
        gate_up = ring.halves([unit_halves(mlp_gate, units), unit_halves(mlp_up, units)])
        gate_up = lax.all_gather(gate_up, pairs, axis=0, tiled=True)
        down_three = lax.all_gather(mlp_down, pairs, axis=0, tiled=True)
    token_rows = ring.pair_rows(ring.across(tokens[0]), 1).reshape(-1, width)
    query_one, gains, key_one, value_one = ring.gather(blocks_one, widths_one)
    patch_rows = ring.pair_rows(ring.across(memory[0]), 1).reshape(-1, width)
    out_one_half, query_two, out_two_half, key_two, value_two = ring.gather(
        blocks_two, widths_two
    )
    out_one = ring.pair_rows(out_one_half, 1)
    out_two = ring.pair_rows(out_two_half, 1)
    grad_low = ring.pair_rows(output_grad[0])

    gain_rows = gains[:, :3].astype(F32).T
    gain_one, gain_two, gain_three = gain_rows[0:1], gain_rows[1:2], gain_rows[2:3]

    token_chunk = math.gcd(256, both)
    patch_chunk = math.gcd(256, 2 * own_patches)

    def chunk_starts(rows_of_pair, chunk):
        groups = ring.group ^ jnp.arange(ring.groups, dtype=jnp.int32)
        inner = jnp.arange(rows_of_pair // chunk, dtype=jnp.int32) * chunk
        return (groups[:, None] * rows_of_pair + inner[None, :]).reshape(-1)

    first_query = (ring.group * both).astype(jnp.int32)[None]
    info_one = jnp.concatenate([text_length, first_query, chunk_starts(both, token_chunk)])
    info_two = jnp.concatenate(
        [patch_count, first_query, chunk_starts(2 * own_patches, patch_chunk)]
    )

    token_float = token_rows.astype(F32)
    plain_one, inverse_one = normalize(token_float)
    normed_one = (plain_one * gain_one).astype(LOW)
    mine_one = normed_one[:both]
    query_heads = dot_nn(mine_one, query_one).astype(LOW)
    key_heads = dot_nn(normed_one, key_one).astype(LOW)
    value_heads = dot_nn(normed_one, value_one).astype(LOW)
    context_heads, lse_one = attention_forward(
        info_one, query_heads, key_heads, value_heads, True, token_chunk
    )
    context_one = ring.pair_rows(context_heads, 1)
    hidden_one = token_float[:both] + dot_nn(context_one, out_one)
    plain_two, inverse_two = normalize(hidden_one)
    normed_two = (plain_two * gain_two).astype(LOW)
    cross_heads = dot_nn(normed_two, query_two).astype(LOW)
    memory_keys = dot_nn(patch_rows, key_two).astype(LOW)
    memory_values = dot_nn(patch_rows, value_two).astype(LOW)
    cross_context, lse_two = attention_forward(
        info_two, cross_heads, memory_keys, memory_values, False, patch_chunk
    )
    context_two = ring.pair_rows(cross_context, 1)
    hidden_two = hidden_one + dot_nn(context_two, out_two)
    plain_three, inverse_three = normalize(hidden_two)
    normed_three = (plain_three * gain_three).astype(LOW)
    def own_rows(values, count):
        return lax.dynamic_slice_in_dim(values, ring.half * count, count, 0)

    def other_rows(values, count):
        return lax.dynamic_slice_in_dim(values, (1 - ring.half) * count, count, 0)

    if packed:
        part_three, down_part, mlp_terms = feed_forward(
            normed_three, grad_low, mlp_weights, pieces, down_pieces, hidden_half
        )
        mlp_terms = mlp_terms.reshape(ring.blocks * piece, -1)
        mlp_sum = lax.psum_scatter(mlp_terms, pairs, scatter_dimension=0, tiled=True)
        mlp_sum = mlp_sum.astype(F32)
        take = lambda at, size: mlp_sum[:, at : at + size]
        gate_up = [
            jnp.concatenate(
                [take((m * pieces + j) * hidden_half, hidden_half) for j in range(pieces)], axis=0
            )
            for m in range(2)
        ]
        gate_up = jnp.concatenate(gate_up, axis=1)
        base = 2 * pieces * hidden_half
        mlp_ddown = jnp.concatenate(
            [take(base + j * width, width) for j in range(down_pieces)], axis=0
        )
    else:
        gate_three, up_three = gate_up[:, :hidden_half], gate_up[:, hidden_half:]
        active, slope = gelu_parts(dot_nn(normed_three, gate_three))
        up = dot_nn(normed_three, up_three)
        mixed = (active * up).astype(LOW)
        down_part = dot_nn(mixed, down_three)
        grad_mixed = dot_nt(grad_low, down_three)
        gate_low = (grad_mixed * up * slope).astype(LOW)
        up_low = (grad_mixed * active).astype(LOW)
        part_three = dot_nt(gate_low, gate_three) + dot_nt(up_low, up_three)
        terms = jnp.concatenate(
            [dot_tn(normed_three, gate_low), dot_tn(normed_three, up_low)], axis=1
        )
        gate_up = lax.psum_scatter(terms, pairs, scatter_dimension=0, tiled=True)
        ddown = dot_tn(mixed, grad_low)
        mlp_ddown = lax.psum_scatter(ddown, pairs, scatter_dimension=0, tiled=True)

    down_got = ring.swap(other_rows(down_part, own).astype(LOW))
    output = (
        own_rows(hidden_two, own) + own_rows(down_part, own) + down_got.astype(F32)
    ).astype(LOW)
    grad_float = grad_low.astype(F32)
    mlp_dgain = jnp.sum(part_three * plain_three, axis=0)
    part_low = part_three.astype(LOW)
    dnormed_three = part_low.astype(F32) + ring.swap(part_low).astype(F32)
    dhidden_two = grad_float + norm_back(plain_three, inverse_three, gain_three, dnormed_three)
    branch_two = dhidden_two.astype(LOW)
    def own_columns(values):
        return lax.dynamic_slice_in_dim(values, ring.half * half, half, 1)

    dcontext_two = dot_nt(branch_two, own_rows(out_two, half)).astype(LOW)
    dout_two = dot_tn(context_two, own_columns(branch_two)).astype(LOW)
    dquery, dkey, dvalue = attention_backward(
        info_two,
        cross_heads,
        memory_keys,
        memory_values,
        cross_context,
        dcontext_two,
        lse_two,
        False,
        patch_chunk,
    )
    part_two = dot_nt(dquery, query_two)
    cross_dgain = jnp.sum(part_two * plain_two, axis=0)
    part_low = part_two.astype(LOW)
    dnormed_two = part_low.astype(F32) + ring.swap(part_low).astype(F32)
    dhidden_one = dhidden_two + norm_back(plain_two, inverse_two, gain_two, dnormed_two)
    branch_one = dhidden_one.astype(LOW)
    dquery_two = dot_tn(normed_two, dquery).astype(LOW)
    dkey_two = dot_tn(patch_rows, dkey).astype(LOW)
    dvalue_two = dot_tn(patch_rows, dvalue).astype(LOW)
    cross_sum = ring.scatter_sum([[dout_two, dquery_two], [dkey_two, dvalue_two]], 2 * rows)

    def to_owner(part, count):
        part = part.reshape(ring.groups, 2, count, width)
        first, later = part[:, 0], part[:, 1]
        keep = jnp.where(ring.second, later, first)
        give = jnp.where(ring.second, first, later).astype(LOW)
        total = keep + ring.swap(give).astype(F32)
        for axis, bit in reversed(ring.group_bits):
            middle = total.shape[0] // 2
            total = total[:middle] + ring.send(total[middle:].astype(LOW), axis, bit).astype(F32)
        return total[0]

    memory_grad = to_owner(dot_nt(dkey, key_two) + dot_nt(dvalue, value_two), own_patches)

    dcontext_one = dot_nt(branch_one, own_rows(out_one, half)).astype(LOW)
    dout_one = dot_tn(context_one, own_columns(branch_one)).astype(LOW)
    dquery, dkey, dvalue = attention_backward(
        info_one,
        query_heads,
        key_heads,
        value_heads,
        context_heads,
        dcontext_one,
        lse_one,
        True,
        token_chunk,
    )
    dquery_one = dot_tn(mine_one, dquery).astype(LOW)
    dkey_one = dot_tn(normed_one, dkey).astype(LOW)
    dvalue_one = dot_tn(normed_one, dvalue).astype(LOW)
    part_one = dot_nt(dkey, key_one) + dot_nt(dvalue, value_one)
    part_mine = part_one[:both] + dot_nt(dquery, query_one)
    part_one = jnp.concatenate([part_mine, part_one[both:]], axis=0)
    self_dgain = jnp.sum(part_one * plain_one, axis=0)
    dgains = jnp.stack([self_dgain, cross_dgain, mlp_dgain], axis=1)
    dgains = jnp.pad(dgains, ((0, 0), (0, PAIR_LANES - 3))).astype(LOW)
    self_sum = ring.scatter_sum(
        [[dquery_one, dout_one, dgains], [dkey_one, dvalue_one]], 2 * rows
    )
    dnormed_one = to_owner(part_one, own)
    last = norm_back(
        own_rows(plain_one[:both], own), own_rows(inverse_one[:both], own), gain_one, dnormed_one
    )
    input_grad = own_rows(dhidden_one, own) + last

    def finished(block, count):
        first, later = ring.unhalve(block)
        return [
            jnp.concatenate([part[:, i * half : (i + 1) * half] for part in (first, later)], axis=1)
            for i in range(count)
        ]

    first, later = ring.unhalve(gate_up)
    mlp_dgate = unit_whole(first[:, :hidden_half], later[:, :hidden_half], units)
    mlp_dup = unit_whole(first[:, hidden_half:], later[:, hidden_half:], units)
    cross_dout, cross_dquery, cross_dkey, cross_dvalue = finished(cross_sum, 4)
    gain_at = 2 * half
    dgain_block = self_sum[:, gain_at : gain_at + PAIR_LANES]
    weights_sum = jnp.concatenate(
        [self_sum[:, :gain_at], self_sum[:, gain_at + PAIR_LANES :], dgain_block], axis=1
    )
    first, later = ring.unhalve(weights_sum)
    pick = lambda i: jnp.concatenate(
        [part[:, i * half : (i + 1) * half] for part in (first, later)], axis=1
    )
    self_dquery, self_dout, self_dkey, self_dvalue = (pick(i) for i in range(4))
    dgain_columns = first[:, 4 * half : 4 * half + 3] + later[:, 4 * half : 4 * half + 3]

    return (
        output[None],
        input_grad[None],
        memory_grad[None],
        dgain_columns[:, 0],
        self_dquery,
        self_dkey,
        self_dvalue,
        self_dout,
        dgain_columns[:, 1],
        cross_dquery,
        cross_dkey,
        cross_dvalue,
        cross_dout,
        dgain_columns[:, 2],
        mlp_dgate,
        mlp_dup,
        mlp_ddown,
    )


def solution(mesh):
    charts, heads = mesh.devices.shape
    inner = Mesh(mesh.devices.reshape(charts, heads // 2, 2), ("dp", "hx", "hc"))
    every = ("dp", "hx", "hc")
    rows = P(every, None)
    vector = P(every)
    grid = P("dp", ("hx", "hc"), None)
    in_specs = (grid, grid, P("dp"), P("dp"))
    in_specs += (vector, rows, rows, rows, rows) * 2
    in_specs += (vector, rows, rows, rows, grid)
    out_specs = (grid, grid, grid)
    out_specs += (vector, rows, rows, rows, rows) * 2
    out_specs += (vector, rows, rows, rows)
    return jax.shard_map(
        on_device, mesh=inner, in_specs=in_specs, out_specs=out_specs, check_vma=False
    )
```

```python
import functools
import math

import jax
import jax.numpy as jnp
from jax import lax
from jax.experimental import pallas as pl
from jax.experimental.pallas import tpu as pltpu
from jax.sharding import Mesh
from jax.sharding import PartitionSpec as P

HEAD_DIM = 64
PAIR_LANES = 128
NEG_FILL = -1e30
EPS = 1e-06
F32 = jnp.float32
LOW = jnp.bfloat16


NT = (((1,), (1,)), ((), ()))
TN = (((0,), (0,)), ((), ()))


def dot_nt(left, right):
    return lax.dot_general(left, right, NT, preferred_element_type=F32)


def dot_tn(left, right):
    return lax.dot_general(left, right, TN, preferred_element_type=F32)


def dot_nn(left, right):
    return jnp.dot(left, right, preferred_element_type=F32)


FIXED = 3


def query_limits(info, queries, causal):
    last = info[0] - 1
    if not causal:
        return jnp.full((1, queries), last, jnp.int32), last
    lanes = lax.broadcasted_iota(jnp.int32, (1, queries), 1)
    span = queries // 2
    swapped = jnp.where(lanes < span, lanes + info[2] * span, lanes - info[2] * span)
    return jnp.minimum(info[1] + swapped, last), jnp.minimum(info[1] + queries - 1, last)


def head_lanes(head):
    lanes = lax.broadcasted_iota(jnp.int32, (1, PAIR_LANES), 1)
    return (lanes // HEAD_DIM) == head


def fold(values, op):
    rows, columns = values.shape
    return op(values.reshape(rows // 8, 8, columns), axis=0)


def forward_kernel(causal, chunk, info, q_ref, k_ref, v_ref, c_ref, lse_ref, s_ref, m_ref, l_ref, a_ref):
    queries = q_ref.shape[0]
    chunks = k_ref.shape[0] // chunk
    scaling = 1.0 / math.sqrt(HEAD_DIM)
    limit, latest = query_limits(info, queries, causal)
    q_all = q_ref[...] * jnp.asarray(scaling, q_ref.dtype)
    q_heads = [jnp.where(head_lanes(h), q_all, jnp.zeros_like(q_all)) for h in range(2)]
    m_ref[...] = jnp.full(m_ref.shape, NEG_FILL, F32)
    l_ref[...] = jnp.zeros(l_ref.shape, F32)
    a_ref[...] = jnp.zeros(a_ref.shape, F32)

    @pl.loop(0, chunks)
    def _(j):
        start = info[FIXED + j]

        @pl.when(start <= latest)
        def _():
            rows = pl.ds(pl.multiple_of(j * chunk, chunk), chunk)
            keys = k_ref[rows, :]
            place = start + lax.broadcasted_iota(jnp.int32, (chunk, queries), 0)
            allowed = place <= limit
            for h in range(2):
                scores = jnp.where(allowed, dot_nt(keys, q_heads[h]), NEG_FILL)
                s_ref[h, rows, :] = scores
                m_ref[h] = jnp.maximum(m_ref[h], fold(scores, jnp.max))

    highest = [jnp.max(m_ref[h], axis=0, keepdims=True) for h in range(2)]

    @pl.loop(0, chunks)
    def _(j):
        @pl.when(info[FIXED + j] <= latest)
        def _():
            rows = pl.ds(pl.multiple_of(j * chunk, chunk), chunk)
            values = v_ref[rows, :]
            for h in range(2):
                weight = jnp.exp(s_ref[h, rows, :] - highest[h])
                l_ref[h] = l_ref[h] + fold(weight, jnp.sum)
                a_ref[h] = a_ref[h] + dot_tn(values, weight.astype(LOW))

    parts = []
    for h in range(2):
        total = jnp.sum(l_ref[h], axis=0, keepdims=True)
        lse_ref[0, pl.ds(h, 1), :] = highest[h] + jnp.log(total)
        parts.append(a_ref[h, pl.ds(h * HEAD_DIM, HEAD_DIM), :] / total)
    c_ref[...] = jnp.concatenate(parts, axis=0).T.astype(c_ref.dtype)


def backward_kernel(causal, chunk, info, q_ref, k_ref, v_ref, c_ref, g_ref, lse_ref, dq_ref, dk_ref, dv_ref, a_ref):
    queries = q_ref.shape[0]
    chunks = k_ref.shape[0] // chunk
    scaling = 1.0 / math.sqrt(HEAD_DIM)
    limit, latest = query_limits(info, queries, causal)
    q_all = q_ref[...] * jnp.asarray(scaling, q_ref.dtype)
    g_all = g_ref[...]
    q_heads = [jnp.where(head_lanes(h), q_all, jnp.zeros_like(q_all)) for h in range(2)]
    g_heads = [jnp.where(head_lanes(h), g_all, jnp.zeros_like(g_all)) for h in range(2)]
    product = (c_ref[...].astype(F32) * g_all.astype(F32)).T
    centres = [
        jnp.sum(product[h * HEAD_DIM : (h + 1) * HEAD_DIM], axis=0, keepdims=True) for h in range(2)
    ]
    logs = [lse_ref[0, pl.ds(h, 1), :] for h in range(2)]
    a_ref[...] = jnp.zeros(a_ref.shape, F32)

    @pl.loop(0, chunks)
    def _(j):
        start = info[FIXED + j]
        rows = pl.ds(pl.multiple_of(j * chunk, chunk), chunk)

        @pl.when(start <= latest)
        def _():
            keys = k_ref[rows, :]
            values = v_ref[rows, :]
            place = start + lax.broadcasted_iota(jnp.int32, (chunk, queries), 0)
            allowed = place <= limit
            dk = jnp.zeros((chunk, PAIR_LANES), F32)
            dv = jnp.zeros((chunk, PAIR_LANES), F32)
            for h in range(2):
                scores = jnp.where(allowed, dot_nt(keys, q_heads[h]), NEG_FILL)
                prob = jnp.exp(scores - logs[h])
                dprob = dot_nt(values, g_heads[h])
                dv = dv + dot_nn(prob.astype(LOW), g_heads[h])
                dscore = (prob * (dprob - centres[h])).astype(LOW)
                dk = dk + dot_nn(dscore, q_heads[h])
                a_ref[h] = a_ref[h] + dot_tn(keys, dscore)
            dk_ref[rows, :] = dk.astype(dk_ref.dtype)
            dv_ref[rows, :] = dv.astype(dv_ref.dtype)

        @pl.when(start > latest)
        def _():
            dk_ref[rows, :] = jnp.zeros((chunk, PAIR_LANES), dk_ref.dtype)
            dv_ref[rows, :] = jnp.zeros((chunk, PAIR_LANES), dv_ref.dtype)

    parts = [a_ref[h, pl.ds(h * HEAD_DIM, HEAD_DIM), :] for h in range(2)]
    dq_ref[...] = (jnp.concatenate(parts, axis=0).T * scaling).astype(dq_ref.dtype)


def lane_spec(rows):
    return pl.BlockSpec((rows, PAIR_LANES), lambda i, info: (0, i))


def stat_spec(queries):
    return pl.BlockSpec((1, 2, queries), lambda i, info: (i, 0, 0))


def attention_forward(info, queries, keys, values, causal, chunk):
    rows, features = queries.shape
    key_rows = keys.shape[0]
    pairs = features // PAIR_LANES
    return pl.pallas_call(
        functools.partial(forward_kernel, causal, chunk),
        out_shape=(
            jax.ShapeDtypeStruct((rows, features), LOW),
            jax.ShapeDtypeStruct((pairs, 2, rows), F32),
        ),
        grid_spec=pltpu.PrefetchScalarGridSpec(
            num_scalar_prefetch=1,
            grid=(pairs,),
            in_specs=[lane_spec(rows), lane_spec(key_rows), lane_spec(key_rows)],
            out_specs=[lane_spec(rows), stat_spec(rows)],
            scratch_shapes=[
                pltpu.VMEM((2, key_rows, rows), F32),
                pltpu.VMEM((2, 8, rows), F32),
                pltpu.VMEM((2, 8, rows), F32),
                pltpu.VMEM((2, PAIR_LANES, rows), F32),
            ],
        ),
        compiler_params=pltpu.CompilerParams(vmem_limit_bytes=VMEM_LIMIT),
        cost_estimate=pl.CostEstimate(flops=rows, transcendentals=0, bytes_accessed=0),
    )(info, queries, keys, values)


def attention_backward(info, queries, keys, values, context, grads, lse, causal, chunk):
    rows, features = queries.shape
    key_rows = keys.shape[0]
    pairs = features // PAIR_LANES
    return pl.pallas_call(
        functools.partial(backward_kernel, causal, chunk),
        out_shape=(
            jax.ShapeDtypeStruct((rows, features), LOW),
            jax.ShapeDtypeStruct((key_rows, features), LOW),
            jax.ShapeDtypeStruct((key_rows, features), LOW),
        ),
        grid_spec=pltpu.PrefetchScalarGridSpec(
            num_scalar_prefetch=1,
            grid=(pairs,),
            in_specs=[
                lane_spec(rows),
                lane_spec(key_rows),
                lane_spec(key_rows),
                lane_spec(rows),
                lane_spec(rows),
                stat_spec(rows),
            ],
            out_specs=[lane_spec(rows), lane_spec(key_rows), lane_spec(key_rows)],
            scratch_shapes=[pltpu.VMEM((2, PAIR_LANES, rows), F32)],
        ),
        compiler_params=pltpu.CompilerParams(vmem_limit_bytes=VMEM_LIMIT),
        cost_estimate=pl.CostEstimate(flops=rows, transcendentals=0, bytes_accessed=0),
    )(info, queries, keys, values, context, grads, lse)


SMEM_SPEC = pl.BlockSpec(memory_space=pltpu.SMEM)


def vmem_specs(number):
    return [pl.BlockSpec(memory_space=pltpu.VMEM)] * number


def cuts_of(widths):
    return [sum(widths[:i]) for i in range(len(widths))]


def place_blocks(index, first, later, targets):
    half, rows, _ = first.shape
    cuts = cuts_of([target.shape[1] for target in targets])
    for step in range(2 * half):
        at = index[step]
        place = pl.ds(step * rows, rows)

        def put(source, block):
            for cut, target in zip(cuts, targets):
                target[place, :] = source[block, :, pl.ds(cut, target.shape[1])]

        @pl.when(at < half)
        def _():
            put(first, at)

        @pl.when(at >= half)
        def _():
            put(later, at - half)


def send_order(index, whole, keep, give):
    half, rows, _ = keep.shape
    for step in range(2 * half):
        at = pl.ds(pl.multiple_of(index[step] * rows, rows), rows)
        target = keep if step < half else give
        target[step % half] = whole[at, :]


def whole_kernel(index, first, later, *targets):
    place_blocks(index, first, later, targets)


def to_whole(first, later, index, widths):
    half, rows, columns = first.shape
    count = 2 * half
    if rows % 16:
        blocks = jnp.concatenate([first, later], axis=0)
        whole = jnp.take(blocks, index, axis=0).reshape(count * rows, columns)
        return [whole[:, cut : cut + width] for cut, width in zip(cuts_of(widths), widths)]
    return run_kernel(
        whole_kernel,
        [low_shape(count * rows, width) for width in widths],
        count * rows * columns,
        [index],
        [first, later],
    )


def staged_kernel(body, late, sizes, *refs):
    parts, at = [], 0
    for size in sizes:
        parts.append(refs[at : at + size])
        at += size
    tables, arrays, streamed, outs, scratch, held_in, held_out, (in_sems, out_sems) = parts
    loads = [
        pltpu.make_async_copy(a, b, in_sems.at[i]) for i, (a, b) in enumerate(zip(arrays, held_in))
    ]
    for load in loads:
        load.start()

    def ready():
        for load in loads:
            load.wait()

    if late:
        body(ready, *tables, *held_in, *streamed, *held_out, *scratch)
    else:
        ready()
        body(*tables, *held_in, *streamed, *held_out, *scratch)
    stores = [
        pltpu.make_async_copy(a, b, out_sems.at[i]) for i, (a, b) in enumerate(zip(held_out, outs))
    ]
    for store in stores:
        store.start()
    for store in stores:
        store.wait()


HBM_SPEC = pl.BlockSpec(memory_space=pltpu.HBM)


def run_kernel(body, out_shape, cost, tables, arrays, scratch=(), streamed=(), late=False):
    sizes = (len(tables), len(arrays), len(streamed), len(out_shape), len(scratch))
    sizes += (len(arrays), len(out_shape), 2)
    held = [pltpu.VMEM(x.shape, x.dtype) for x in [*arrays, *out_shape]]
    sems = [pltpu.SemaphoreType.DMA((len(arrays),)), pltpu.SemaphoreType.DMA((len(out_shape),))]
    return pl.pallas_call(
        functools.partial(staged_kernel, body, late, sizes),
        out_shape=out_shape,
        in_specs=[SMEM_SPEC] * len(tables) + [HBM_SPEC] * (len(arrays) + len(streamed)),
        out_specs=[HBM_SPEC] * len(out_shape),
        scratch_shapes=list(scratch) + held + sems,
        compiler_params=pltpu.CompilerParams(vmem_limit_bytes=VMEM_LIMIT),
        cost_estimate=pl.CostEstimate(flops=cost // 1000, transcendentals=0, bytes_accessed=0),
    )(*tables, *arrays, *streamed)


VMEM_LIMIT = 56 << 20


def low_shape(*shape):
    return jax.ShapeDtypeStruct(shape, LOW)


def full_shape(*shape):
    return jax.ShapeDtypeStruct(shape, F32)


def unit_tile(source, at, second):
    lanes = 2 * HEAD_DIM
    start = 2 * at * lanes + (HEAD_DIM if second else 0)
    return jnp.concatenate(
        [source[:, pl.ds(start, HEAD_DIM)], source[:, pl.ds(start + lanes, HEAD_DIM)]], axis=1
    )


def shards_kernel(kinds, place, *refs):
    sources, targets = refs[:-2], refs[-2:]

    def write(target, second):
        cut = 0
        for kind, source in zip(kinds, sources):
            columns = source.shape[1]
            if kind == "all":
                target[:, pl.ds(cut, columns)] = source[...]
                cut += columns
                continue
            if kind == "half":
                start = columns // 2 if second else 0
                target[:, pl.ds(cut, columns // 2)] = source[:, pl.ds(start, columns // 2)]
            else:
                for tile in range(columns // 256):
                    target[:, pl.ds(cut + 128 * tile, 128)] = unit_tile(source, tile, second)
            cut += columns // 2

    @pl.when(place[0] == 0)
    def _():
        write(targets[0], False)
        write(targets[1], True)

    @pl.when(place[0] != 0)
    def _():
        write(targets[0], True)
        write(targets[1], False)


def rows_kernel(widths, piece, place, mine, other, down, *targets):
    *widths, matrices, extra = widths
    rows = mine.shape[0]

    def write(upper, lower):
        cut = 0
        for target, width in zip(targets[:-1], widths):
            target[0, pl.ds(0, rows), :] = upper[:, pl.ds(cut, width)]
            target[0, pl.ds(rows, rows), :] = lower[:, pl.ds(cut, width)]
            cut += width
        packed = targets[-1]
        columns = (mine.shape[1] - cut - extra) // matrices
        step = 8
        base = matrices * (2 * rows // piece) * columns
        last = base + down.shape[1] * (down.shape[0] // piece)
        for start in range(0, 2 * rows, step):
            source = upper if start < rows else lower
            number, inner = start // piece, start % piece
            for matrix in range(matrices):
                place_at = (matrix * (2 * rows // piece) + number) * columns
                packed[pl.ds(inner, step), pl.ds(place_at, columns)] = source[
                    pl.ds(start % rows, step), pl.ds(cut + matrix * columns, columns)
                ]
            packed[pl.ds(inner, step), pl.ds(last + number * extra, extra)] = source[
                pl.ds(start % rows, step), pl.ds(cut + matrices * columns, extra)
            ]
        width = down.shape[1]
        for number in range(down.shape[0] // piece):
            packed[:, pl.ds(base + number * width, width)] = down[pl.ds(number * piece, piece), :]

    @pl.when(place[0] == 0)
    def _():
        write(mine, other)

    @pl.when(place[0] != 0)
    def _():
        write(other, mine)


def cut_shards(place, shards, kinds):
    rows = shards[0].shape[0]
    columns = sum(w.shape[1] if k == "all" else w.shape[1] // 2 for w, k in zip(shards, kinds))
    return run_kernel(
        functools.partial(shards_kernel, kinds), [low_shape(rows, columns)] * 2, rows * columns, [place], shards
    )


def join_rows(place, mine, other, down, widths, extra, piece):
    rows = 2 * mine.shape[0]
    rest = mine.shape[1] - sum(widths)
    packed = rest * (rows // piece) + down.shape[1] * (down.shape[0] // piece)
    return run_kernel(
        functools.partial(rows_kernel, [*widths, 2, extra], piece),
        [low_shape(1, rows, width) for width in widths] + [low_shape(piece, packed)],
        rows * rest,
        [place],
        [mine, other, down],
    )


def pieces_kernel(cut, source, target, held, sem):
    blocks, pieces, piece, columns = held.shape
    copies = [
        pltpu.make_async_copy(
            source.at[:, :, pl.ds(cut + i * columns, columns)], held.at[:, i], sem.at[i]
        )
        for i in range(pieces)
    ]
    for copy in copies:
        copy.start()
    for copy in copies:
        copy.wait()
    target[...] = held[...].reshape(target.shape)


def from_pieces(packed, cut, pieces, columns):
    blocks, piece, _ = packed.shape
    return pl.pallas_call(
        functools.partial(pieces_kernel, cut),
        out_shape=low_shape(blocks * pieces * piece, columns),
        in_specs=[HBM_SPEC],
        out_specs=pl.BlockSpec(memory_space=pltpu.VMEM),
        scratch_shapes=[
            pltpu.VMEM((blocks, pieces, piece, columns), LOW),
            pltpu.SemaphoreType.DMA((pieces,)),
        ],
        cost_estimate=pl.CostEstimate(flops=1000, transcendentals=0, bytes_accessed=0),
    )(packed)


def normalize(values):
    inverse = lax.rsqrt(jnp.mean(values * values, axis=-1, keepdims=True) + EPS)
    return values * inverse, inverse


def norm_back(normed, inverse, gain, grads):
    scaled = grads * gain
    return inverse * (scaled - normed * jnp.mean(scaled * normed, axis=-1, keepdims=True))


def gelu_parts(gate):
    factor = math.sqrt(2.0 / math.pi)
    inner = jnp.tanh(factor * (gate + 0.044715 * gate * gate * gate))
    value = 0.5 * gate * (1.0 + inner)
    slope = 0.5 * (1.0 + inner) + 0.5 * gate * (1.0 - inner * inner) * factor * (
        1.0 + 3.0 * 0.044715 * gate * gate
    )
    return value, slope


def head_slices(place, half):
    mine = pl.ds(pl.multiple_of(place[0] * half, half), half)
    other = pl.ds(pl.multiple_of((1 - place[0]) * half, half), half)
    return mine, other


def project_heads(gain_cols, token_m, token_g, weights, rows_ref, normed_ref, heads):
    gain_rows = gain_cols.astype(F32).T[0:8]
    rows_ref[...] = gain_rows
    groups, own, _ = token_m.shape
    for group in range(groups):
        for side, source in enumerate((token_m, token_g)):
            plain, _ = normalize(source[group].astype(F32))
            at = pl.ds((2 * group + side) * own, own)
            normed_ref[at, :] = (plain * gain_rows[0:1]).astype(LOW)
    for number, (weight, target) in enumerate(zip(weights, heads)):
        target[...] = dot_nn(normed_ref[pl.ds(0, target.shape[0]), :], weight[...]).astype(LOW)


def query_kernel(packed, *refs):
    if packed:
        index_a, index_b, first_a, later_a, first_b, later_b, token_m, token_g = refs[:8]
        rows_ref, normed_ref, q_ref, k_ref, v_ref, wq, gain_cols, wk, wv = refs[8:]
        place_blocks(index_a, first_a, later_a, [wq, gain_cols])
        place_blocks(index_b, first_b, later_b, [wk, wv])
    else:
        wq, gain_cols, wk, wv, token_m, token_g = refs[:6]
        rows_ref, normed_ref, q_ref, k_ref, v_ref = refs[6:]
    heads = (q_ref, k_ref, v_ref)
    project_heads(gain_cols[...], token_m, token_g, (wq, wk, wv), rows_ref, normed_ref, heads)


def add_context(place, target, base, c_m, c_g, w_m, w_g):
    rows, half = c_m.shape
    own = rows // 2
    mine, other = head_slices(place, half)
    for side in range(2):
        at = pl.ds(side * own, own)
        left = c_m[at, :]
        right = c_g[pl.ds((1 - side) * own, own), :]
        for weight, columns in ((w_m, mine), (w_g, other)):
            value = dot_nn(left, weight[mine, :]) + dot_nn(right, weight[other, :])
            target[at, columns] = base(side, columns) + value


def cross_query_kernel(place, token_m, token_g, c_m, c_g, w_m, w_g, rows_ref, wq, h_ref, normed_ref, q_ref):
    tokens = (token_m, token_g)
    base = lambda side, columns: tokens[side][:, columns].astype(F32)
    add_context(place, h_ref, base, c_m, c_g, w_m, w_g)
    plain, _ = normalize(h_ref[...])
    normed_ref[...] = (plain * rows_ref[1:2, :]).astype(LOW)
    q_ref[...] = dot_nn(normed_ref[...], wq[...]).astype(LOW)


def memory_kernel(packed, *refs):
    if packed:
        index, first, later, patch_m, patch_g, k_ref, v_ref, wk, wv = refs
        place_blocks(index, first, later, [wk, wv])
    else:
        wk, wv, patch_m, patch_g, k_ref, v_ref = refs
    count = patch_m.shape[0]
    step = math.gcd(count, 1024)
    for side, source in enumerate((patch_m, patch_g)):
        for row in range(0, count, step):
            part = source[pl.ds(row, step), :]
            place = pl.ds(side * count + row, step)
            k_ref[place, :] = dot_nn(part, wk[...]).astype(LOW)
            v_ref[place, :] = dot_nn(part, wv[...]).astype(LOW)


def lane_column(column, lane):
    lanes = lax.broadcasted_iota(jnp.int32, (1, PAIR_LANES), 1)
    return jnp.where(lanes == lane, column, 0.0)


def mlp_kernel(
    chunk,
    ready,
    place,
    h_in,
    c_m,
    c_g,
    out_m,
    out_g,
    rows_ref,
    cols_ref,
    g_m,
    g_g,
    w_ref,
    h_ref,
    part_ref,
    keep_ref,
    give_ref,
    gain_ref,
    grad_ref,
    gate_w,
    up_w,
    down_w,
    a_ref,
    t_ref,
    g_ref,
    p_acc,
    d_acc,
    r_acc,
    sems,
):
    blocks, pieces, piece, units = gate_w.shape
    down_pieces, width = down_w.shape[1], down_w.shape[3]
    total = blocks * pieces * piece
    own = g_m.shape[0]
    moves = []
    for number in range(pieces):
        moves.append((w_ref.at[:, :, pl.ds(number * units, units)], gate_w.at[:, number]))
    for number in range(pieces):
        moves.append((w_ref.at[:, :, pl.ds((pieces + number) * units, units)], up_w.at[:, number]))
    base = 2 * pieces * units
    for number in range(down_pieces):
        moves.append((w_ref.at[:, :, pl.ds(base + number * width, width)], down_w.at[:, number]))
    copies = [pltpu.make_async_copy(a, b, sems.at[i]) for i, (a, b) in enumerate(moves)]
    for copy in copies:
        copy.start()
    ready()
    add_context(
        place, h_ref, lambda side, columns: h_in[pl.ds(side * own, own), columns], c_m, c_g, out_m, out_g
    )
    plain, _ = normalize(h_ref[...])
    a_ref[...] = (plain * rows_ref[2:3, :]).astype(LOW)
    t_ref[...] = a_ref[...].T
    g_ref[pl.ds(0, own), :] = g_m[...]
    g_ref[pl.ds(own, own), :] = g_g[...]
    p_acc[...] = jnp.zeros(p_acc.shape, F32)
    d_acc[...] = jnp.zeros(d_acc.shape, F32)
    r_acc[...] = jnp.zeros(r_acc.shape, F32)
    for copy in copies:
        copy.wait()

    per_block = down_pieces * piece
    step_blocks = chunk // per_block

    @pl.loop(0, units // chunk)
    def _(step):
        start = pl.multiple_of(step * chunk, chunk)
        a_in = a_ref[...]
        g_in = g_ref[...]
        columns = pl.ds(start, chunk)
        gate_part = gate_w[:, :, :, columns].reshape(total, chunk)
        up_part = up_w[:, :, :, columns].reshape(total, chunk)
        down_at = pl.ds(step * step_blocks, step_blocks)
        down_part = down_w[down_at].reshape(chunk, width)
        gate = dot_nn(a_in, gate_part)
        up = dot_nn(a_in, up_part)
        active, slope = gelu_parts(gate)
        mixed = (active * up).astype(LOW)
        grad = dot_nt(g_in, down_part)
        gate_low = (grad * up * slope).astype(LOW)
        up_low = (grad * active).astype(LOW)
        d_acc[...] += dot_nn(mixed, down_part)
        p_acc[...] += dot_nt(gate_low, gate_part) + dot_nt(up_low, up_part)
        dgate = dot_nn(t_ref[...], gate_low)
        dup = dot_nn(t_ref[...], up_low)
        gain_terms = dgate * gate_part.astype(F32) + dup * up_part.astype(F32)
        for lane in range(0, chunk, PAIR_LANES):
            r_acc[...] += gain_terms[:, lane : lane + PAIR_LANES]
        dgate = dgate.astype(LOW).reshape(blocks, pieces, piece, chunk)
        dup = dup.astype(LOW).reshape(blocks, pieces, piece, chunk)
        for number in range(pieces):
            gate_at = pl.multiple_of(number * units + start, chunk)
            up_at = pl.multiple_of((pieces + number) * units + start, chunk)
            grad_ref[:, :, pl.ds(gate_at, chunk)] = dgate[:, number]
            grad_ref[:, :, pl.ds(up_at, chunk)] = dup[:, number]
        ddown = dot_tn(mixed, g_in).astype(LOW).reshape(step_blocks, down_pieces, piece, width)
        for number in range(down_pieces):
            grad_ref[down_at, :, pl.ds(base + number * width, width)] = ddown[:, number]

    part_ref[...] = p_acc[...].astype(LOW)
    keep_ref[...] = d_acc[pl.ds(0, own), :]
    give_ref[...] = d_acc[pl.ds(own, own), :].astype(LOW)
    summed = jnp.sum(r_acc[...], axis=1, keepdims=True)
    gain_ref[...] = lane_column(summed / cols_ref[:, 2:3].astype(F32), 2)


def branch_kernel(gain_at, place, *refs):
    h_ref, rows_ref, part_m, part_g, w_m, w_g = refs[:6]
    base, (d_ref, low_ref, c_ref) = refs[6:-3], refs[-3:]
    rows = h_ref.shape[0]
    own = rows // 2
    half = w_m.shape[1]
    mine, other = head_slices(place, half)
    for side in range(2):
        at = pl.ds(side * own, own)
        plain, inverse = normalize(h_ref[at, :])
        got = part_g[pl.ds((1 - side) * own, own), :]
        grads = part_m[at, :].astype(F32) + got.astype(F32)
        value = norm_back(plain, inverse, rows_ref[gain_at : gain_at + 1, :], grads)
        before = base[side][...].astype(F32) if len(base) == 2 else base[0][at, :]
        d_ref[at, :] = before + value
    low_ref[...] = d_ref[...].astype(LOW)
    value = dot_nt(low_ref[:, mine], w_m[mine, :]) + dot_nt(low_ref[:, other], w_g[mine, :])
    c_ref[...] = value.astype(LOW)


def dot_rows(left, right):
    columns = left.shape[1]
    step = math.gcd(columns, 256)
    return [(i, dot_tn(left[:, i : i + step], right)) for i in range(0, columns, step)]


def out_grad(place, whole, cut, c_m, c_g, branch):
    rows, half = c_m.shape
    own = rows // 2
    mine, other = head_slices(place, half)
    grads = branch[:, mine]
    columns = pl.ds(cut, half)
    whole[mine, columns] = dot_tn(c_m[...], grads).astype(LOW)
    value = dot_tn(c_g[pl.ds(own, own), :], grads[:own]) + dot_tn(c_g[pl.ds(0, own), :], grads[own:])
    whole[other, columns] = value.astype(LOW)


def weight_grads(targets, lefts, rights, gain_acc=None):
    features = lefts[0].shape[1]
    step = math.gcd(features, 256)
    for row in range(0, features, step):
        turned = [left[:, row : row + step].T for left in lefts]
        at = pl.ds(row, step)
        for (whole, cut, weight), terms in zip(targets, rights):
            width = terms[0].shape[1]
            value = sum(dot_nn(left, right[...]) for left, right in zip(turned, terms))
            whole[at, pl.ds(cut, width)] = value.astype(LOW)
            if weight is not None:
                products = value * weight[at, :].astype(F32)
                gain_acc[at, :] += sum(
                    products[:, lane : lane + PAIR_LANES] for lane in range(0, width, PAIR_LANES)
                )


def finish_blocks(packed, refs, whole_a, whole_b):
    if packed:
        index_a, index_b, keep_a, give_a, keep_b, give_b = refs
        send_order(index_a, whole_a, keep_a, give_a)
        send_order(index_b, whole_b, keep_b, give_b)


def cross_grads_kernel(packed, place, *refs):
    index, refs = (refs[:2], refs[2:]) if packed else ((), refs)
    c_m, c_g, branch, normed, dq, patch_m, patch_g, dk, dv, wq, cols_ref = refs[:11]
    gain_ref, *outs, whole_a, whole_b, gain_acc = refs[11:]
    half = dq.shape[1]
    count = patch_m.shape[0]
    gain_acc[...] = jnp.zeros(gain_acc.shape, F32)
    out_grad(place, whole_a, 0, c_m, c_g, branch)
    weight_grads([(whole_a, half, wq)], [normed], [[dq]], gain_acc)
    halves = [[g.at[pl.ds(i * count, count), :] for i in range(2)] for g in (dk, dv)]
    weight_grads(
        [(whole_b, 0, None), (whole_b, half, None)], [patch_m, patch_g], halves
    )
    summed = jnp.sum(gain_acc[...], axis=1, keepdims=True)
    gain_ref[...] = lane_column(summed / cols_ref[:, 1:2].astype(F32), 1)
    finish_blocks(packed, (*index, *outs), whole_a, whole_b)


def self_grads_kernel(packed, place, *refs):
    index, refs = (refs[:2], refs[2:]) if packed else ((), refs)
    c_m, c_g, branch, normed, dq, dk, dv, wq, wk, wv, cols_ref, gain_two, gain_three = refs[:13]
    *outs, whole_a, whole_b, gain_acc = refs[13:]
    rows, half = dq.shape
    gain_acc[...] = jnp.zeros(gain_acc.shape, F32)
    weight_grads([(whole_a, 0, wq)], [normed.at[pl.ds(0, rows), :]], [[dq]], gain_acc)
    out_grad(place, whole_a, half, c_m, c_g, branch)
    weight_grads(
        [(whole_b, 0, wk), (whole_b, half, wv)], [normed], [[dk], [dv]], gain_acc
    )
    summed = jnp.sum(gain_acc[...], axis=1, keepdims=True)
    gains = lane_column(summed / cols_ref[:, 0:1].astype(F32), 0) + gain_two[...] + gain_three[...]
    whole_a[:, pl.ds(2 * half, PAIR_LANES)] = gains.astype(LOW)
    finish_blocks(packed, (*index, *outs), whole_a, whole_b)


def columns_kernel(place, keep, got, *targets):
    rows = got.shape[0]

    def write(start, first, later):
        for number, target in enumerate(targets):
            half = target.shape[1] // 2
            columns = pl.ds(number * half, half)
            target[:, pl.ds(0, half)] = first(start, columns)
            target[:, pl.ds(half, half)] = later(start, columns)

    from_keep = lambda start, columns: keep[pl.ds(start, rows), columns]
    from_got = lambda start, columns: got[:, columns]

    @pl.when(place[0] == 0)
    def _():
        write(0, from_keep, from_got)

    @pl.when(place[0] != 0)
    def _():
        write(rows, from_got, from_keep)


def after(values, *others):
    return lax.optimization_barrier((values, *others))[0]


def together(*values):
    return lax.optimization_barrier(values)


class Ring:
    def __init__(self):
        self.charts = lax.axis_size("dp")
        self.groups = lax.axis_size("hx")
        self.half = lax.axis_index("hc").astype(jnp.int32)
        self.second = self.half == 1
        self.place = self.half[None]
        self.group = lax.axis_index("hx").astype(jnp.int32)
        self.block = lax.axis_index("dp").astype(jnp.int32) * self.groups + self.group
        self.blocks = self.charts * self.groups
        chart_bits = [("dp", 1 << i) for i in range(self.charts.bit_length() - 1)]
        self.group_bits = [("hx", 1 << i) for i in range(self.groups.bit_length() - 1)]
        self.far = chart_bits[:0:-1]
        near = chart_bits[:1]
        self.tails = (near + self.group_bits, self.group_bits + near)
        self.orders = tuple(self.far + tail for tail in self.tails)

    def send(self, values, axis, bit):
        size = self.charts if axis == "dp" else self.groups
        return lax.ppermute(values, axis, [(i, i ^ bit) for i in range(size)])

    def swap(self, values):
        return lax.ppermute(values, "hc", [(0, 1), (1, 0)])

    def in_order(self, mine, other):
        return jnp.where(self.second, other, mine), jnp.where(self.second, mine, other)

    def steps(self, order):
        return [bit * self.groups if axis == "dp" else bit for axis, bit in order]

    def arrivals(self):
        apart = self.block ^ jnp.arange(self.blocks, dtype=jnp.int32)
        indices = []
        for order in self.orders:
            index = jnp.zeros((self.blocks,), jnp.int32)
            for place, step in enumerate(self.steps(order)):
                index = index + jnp.where((apart & step) != 0, 1 << place, 0)
            indices.append(index)
        return indices

    def origins(self):
        indices = []
        for order in self.orders:
            masks = [0]
            for step in self.steps(order):
                masks = masks + [m ^ step for m in masks]
            indices.append(self.block ^ jnp.asarray(masks, jnp.int32))
        return indices

    def far_step(self, blocks, step):
        return jnp.concatenate([blocks, self.send(blocks, *self.far[step])], axis=0)

    def near_step(self, parts, step):
        return [self.send(part, *tail[step]) for part, tail in zip(parts, self.tails)]

    def near_sends(self, gives, place):
        return [self.send(give, *tail[place]) for give, tail in zip(gives, self.tails)]

    def near_sums(self, keeps, gots):
        add = lambda keep, got: keep.astype(F32) + got.astype(F32)
        for place in reversed(range(len(self.tails[0]))):
            halves = [got.shape[0] // 2 for got in gots]
            kind = LOW if place else F32
            gives = [add(k[h:], g[h:]).astype(kind) for k, g, h in zip(keeps, gots, halves)]
            keeps = [add(k[:h], g[:h]).astype(kind) for k, g, h in zip(keeps, gots, halves)]
            if place:
                gots = self.near_sends(gives, place - 1)
        return jnp.concatenate(keeps, axis=2), jnp.concatenate(gives, axis=2).astype(LOW)

    def far_sum(self, keep, give, step):
        got = self.send(give, *self.far[len(self.far) - 1 - step])
        half = keep.shape[0] // 2
        if not half:
            return keep + got.astype(F32), None
        later = (keep[half:] + got[half:].astype(F32)).astype(LOW)
        return keep[:half] + got[:half].astype(F32), later

    def halve_wholes(self, wholes, rows):
        keeps, gives = [], []
        for whole, index in zip(wholes, self.origins()):
            blocks = jnp.take(whole.reshape(self.blocks, rows, -1), index, axis=0)
            keeps.append(blocks[: self.blocks // 2])
            gives.append(blocks[self.blocks // 2 :])
        return keeps, gives

    def across(self, mine):
        rows = mine[None]
        for axis, bit in self.group_bits:
            rows = jnp.concatenate([rows, self.send(rows, axis, bit)], axis=0)
        return rows

    def halves(self, first, later):
        mine = jnp.where(self.second, later, first)
        give = jnp.where(self.second, first, later)
        return jnp.concatenate(self.in_order(mine, self.swap(give)), axis=0)

    def pair_sum(self, keep, give):
        return keep + self.swap(give.astype(LOW)).astype(F32)

    def group_terms(self, total):
        for axis, bit in reversed(self.group_bits):
            middle = total.shape[0] // 2
            total = total[:middle] + self.send(total[middle:].astype(LOW), axis, bit).astype(F32)
        return total[0]

    def finished(self, keep, count):
        rows = keep.shape[0] // 2
        give = lax.dynamic_slice_in_dim(keep, (1 - self.half) * rows, rows, 0)
        got = self.swap(give)
        width = keep.shape[1] // count * 2
        return run_kernel(
            columns_kernel, [full_shape(rows, width)] * count, rows * width, [self.place], [keep, got]
        )


def column_halves(weights):
    half = weights[0].shape[1] // 2
    return [jnp.concatenate([w[:, i * half : (i + 1) * half] for w in weights], axis=1) for i in range(2)]


def unit_halves(weight, units):
    rows, columns = weight.shape
    split = weight.reshape(rows, columns // (2 * units), 2, units)
    return split[:, :, 0].reshape(rows, -1), split[:, :, 1].reshape(rows, -1)


def unit_whole(first, later, units):
    rows, columns = first.shape
    pieces = [part.reshape(rows, columns // units, 1, units) for part in (first, later)]
    return jnp.concatenate(pieces, axis=2).reshape(rows, 2 * columns)


def on_device(
    tokens,
    memory,
    text_length,
    patch_count,
    self_gain,
    self_query,
    self_key,
    self_value,
    self_out,
    cross_gain,
    cross_query,
    cross_key,
    cross_value,
    cross_out,
    mlp_gain,
    mlp_gate,
    mlp_up,
    mlp_down,
    output_grad,
):
    ring = Ring()
    place = ring.place
    width = tokens.shape[-1]
    half = width // 2
    units = mlp_down.shape[0]
    hidden_half = units * ring.blocks
    rows = self_query.shape[0]
    own = tokens.shape[1]
    own_patches = memory.shape[1]
    both = 2 * own
    keys = both * ring.groups
    patches = 2 * own_patches * ring.groups
    piece = 16
    packed = (2 * rows) % piece == 0 and units == HEAD_DIM and ring.blocks > 1
    pieces, down_pieces = 2 * rows // piece, units // piece
    pairs = ("dp", "hx")
    index_in = tuple(ring.arrivals()) if packed else ()
    index_out = tuple(ring.origins()) if packed else ()
    index_specs = [SMEM_SPEC] * len(index_in)
    block_rows = 2 * rows

    gain_columns = jnp.stack([self_gain, cross_gain, mlp_gain], axis=1)
    gain_columns = jnp.pad(gain_columns, ((0, 0), (0, PAIR_LANES - 3)))
    cut_one, cut_two = half + PAIR_LANES, 2 * half
    packed_columns = (2 * hidden_half) * pieces + width * down_pieces
    widths_one = ([half, PAIR_LANES], [half, half])
    widths_two = ([half] * 2, [half] * 2)

    def columns_of(weight, which):
        return lax.dynamic_slice_in_dim(weight, which * half, half, 1)

    def first_weights(which):
        parts = [columns_of(w, which) for w in (self_query, self_key, self_value)]
        return jnp.concatenate([parts[0], gain_columns, parts[1], parts[2]], axis=1)

    got_one = ring.swap(first_weights(1 - ring.half))
    blocks_one = jnp.concatenate(ring.in_order(first_weights(ring.half), got_one), axis=0)[None]
    group_two = [self_out, cross_query, cross_key, cross_value]
    far_one = ring.far_step(blocks_one, 0)
    token_m = ring.across(tokens[0])
    if packed:
        kinds = ["half"] * 4 + ["units"] * 2 + ["half"]
        mine, give = cut_shards(place, group_two + [mlp_gate, mlp_up, cross_out], kinds)
        other = ring.swap(give)
        blocks_two, blocks_mlp = join_rows(place, mine, other, mlp_down, [4 * half], half, piece)
    else:
        blocks_two = ring.halves(*column_halves(group_two))[None]
        gate_halves, up_halves = unit_halves(mlp_gate, units), unit_halves(mlp_up, units)
        rest = [
            jnp.concatenate([gate_halves[i], up_halves[i], column_halves([cross_out])[i]], axis=1)
            for i in range(2)
        ]
        gate_up = lax.all_gather(ring.halves(*rest), pairs, axis=0, tiled=True)
        down_three = lax.all_gather(mlp_down, pairs, axis=0, tiled=True)
        out_two = gate_up[:, 2 * hidden_half :]
    far_one, token_m, blocks_two, memory = together(far_one, token_m, blocks_two, memory)
    middle = own_patches // 2
    patch_a = ring.across(memory[0, :middle])
    far_two = ring.far_step(blocks_two, 0)
    for step in range(1, len(ring.far)):
        far_one = ring.far_step(far_one, step)
    far_one, far_two = together(far_one, far_two)
    if packed:
        mlp_weights = lax.all_gather(after(blocks_mlp, far_one), pairs, axis=0, tiled=True)
        mlp_weights = mlp_weights.reshape(ring.blocks, piece, -1)
    parts_one = [far_one[:, :, :cut_one], far_one[:, :, cut_one:]]
    near_one = ring.near_step(parts_one, 0)
    token_g = ring.swap(after(token_m, far_one))
    for step in range(1, len(ring.far)):
        far_two = ring.far_step(far_two, step)
    near_one, far_two, token_g, patch_a, memory = together(
        near_one, far_two, token_g, patch_a, memory
    )
    parts_two = [far_two[:, :, :cut_two], far_two[:, :, cut_two:]]
    near_two = ring.near_step(parts_two, 0)
    for step in range(1, len(ring.tails[0])):
        parts_one = [jnp.concatenate(pair, axis=0) for pair in zip(parts_one, near_one)]
        near_one = ring.near_step(parts_one, step)
    near_one, near_two, memory = together(near_one, near_two, memory)
    for step in range(1, len(ring.tails[0])):
        parts_two = [jnp.concatenate(pair, axis=0) for pair in zip(parts_two, near_two)]
        near_two = ring.near_step(parts_two, step)
    patch_b = ring.across(memory[0, middle:])
    near_one = (parts_one[0], near_one[0], parts_one[1], near_one[1])
    arrivals = ring.arrivals()

    token_chunk = math.gcd(256, own)
    patch_chunk = math.gcd(256, own_patches)

    def chunk_starts(span, chunk, side_first):
        groups = ring.group ^ jnp.arange(ring.groups, dtype=jnp.int32)
        sides = ring.half ^ jnp.arange(2, dtype=jnp.int32)
        inner = jnp.arange(span // chunk, dtype=jnp.int32) * chunk
        if side_first:
            starts = groups[None, :, None] * 2 * span + sides[:, None, None] * span
        else:
            starts = groups[:, None, None] * 2 * span + sides[None, :, None] * span
        return (starts + inner).reshape(-1)

    fixed = jnp.stack([ring.group * both, ring.half])
    info_one = jnp.concatenate([text_length, fixed, chunk_starts(own, token_chunk, False)])
    info_two = jnp.concatenate([patch_count, fixed, chunk_starts(own_patches, patch_chunk, True)])

    head_shapes = [low_shape(both, half), low_shape(keys, half), low_shape(keys, half)]
    query_outs = [full_shape(8, width), low_shape(keys, width), *head_shapes]
    projections = [low_shape(width, w) for w in widths_one[0] + widths_one[1]]
    cost = keys * width * half
    if packed:
        outs = run_kernel(
            functools.partial(query_kernel, True),
            query_outs + projections,
            cost,
            index_in,
            [*near_one, token_m, token_g],
        )
        gain_rows, normed_one, query_heads, key_heads, value_heads = outs[:5]
        query_one, gain_cols, key_one, value_one = outs[5:]
    else:
        query_one, gain_cols = to_whole(near_one[0], near_one[1], arrivals[0], widths_one[0])
        key_one, value_one = to_whole(near_one[2], near_one[3], arrivals[1], widths_one[1])
        gain_rows, normed_one, query_heads, key_heads, value_heads = run_kernel(
            functools.partial(query_kernel, False),
            query_outs,
            cost,
            [],
            [query_one, gain_cols, key_one, value_one, token_m, token_g],
        )
    near_one = None
    grad_g = ring.swap(after(output_grad[0], query_heads))
    context_one, lse_one = attention_forward(
        info_one, query_heads, key_heads, value_heads, True, token_chunk
    )
    context_one, near_two, patch_b, grad_g = together(context_one, near_two, patch_b, grad_g)
    near_two = (parts_two[0], near_two[0], parts_two[1], near_two[1])
    context_one_g = ring.swap(context_one)
    patch_m = jnp.concatenate([patch_a, patch_b], axis=1)
    patch_g = ring.swap(patch_m)
    out_one, query_two = to_whole(near_two[0], near_two[1], arrivals[0], widths_two[0])
    out_one_g = ring.swap(out_one)
    hidden_one, normed_two, cross_heads = run_kernel(
        cross_query_kernel,
        [full_shape(both, width), low_shape(both, width), low_shape(both, half)],
        both * width * half,
        [place],
        [token_m[0], token_g[0], context_one, context_one_g, out_one, out_one_g, gain_rows, query_two],
    )

    patch_all = [part.reshape(-1, width) for part in (patch_m, patch_g)]
    memory_heads = [low_shape(patches, half)] * 2
    if packed:
        memory_keys, memory_values, key_two, value_two = run_kernel(
            functools.partial(memory_kernel, True),
            memory_heads + [low_shape(width, half)] * 2,
            patches * width * half,
            index_in[1:],
            [*near_two[2:], *patch_all],
        )
    else:
        key_two, value_two = to_whole(near_two[2], near_two[3], arrivals[1], widths_two[1])
        memory_keys, memory_values = run_kernel(
            functools.partial(memory_kernel, False),
            memory_heads,
            patches * width * half,
            [],
            [key_two, value_two, *patch_all],
        )
    context_two, lse_two = attention_forward(
        info_two, cross_heads, memory_keys, memory_values, False, patch_chunk
    )
    context_two_g = ring.swap(context_two)
    if packed:
        out_two = from_pieces(mlp_weights, packed_columns, pieces, half)
    out_two_g = ring.swap(out_two)

    if packed:
        hidden_two, part_low, down_keep, down_give, gain_three, mlp_terms = run_kernel(
            functools.partial(mlp_kernel, 256),
            [
                full_shape(both, width),
                low_shape(both, width),
                full_shape(own, width),
                low_shape(own, width),
                full_shape(width, PAIR_LANES),
                low_shape(ring.blocks, piece, packed_columns),
            ],
            2 * both * width * hidden_half,
            [place],
            [
                hidden_one,
                context_two,
                context_two_g,
                out_two,
                out_two_g,
                gain_rows,
                gain_cols,
                output_grad[0],
                grad_g,
            ],
            [
                pltpu.VMEM((ring.blocks, pieces, piece, hidden_half), LOW),
                pltpu.VMEM((ring.blocks, pieces, piece, hidden_half), LOW),
                pltpu.VMEM((ring.blocks, down_pieces, piece, width), LOW),
                pltpu.VMEM((both, width), LOW),
                pltpu.VMEM((width, both), LOW),
                pltpu.VMEM((both, width), LOW),
                pltpu.VMEM((both, width), F32),
                pltpu.VMEM((both, width), F32),
                pltpu.VMEM((width, PAIR_LANES), F32),
                pltpu.SemaphoreType.DMA((2 * pieces + down_pieces,)),
            ],
            [mlp_weights],
            late=True,
        )
        mlp_terms = mlp_terms.reshape(ring.blocks * piece, -1)
        mlp_sum = lax.psum_scatter(mlp_terms, pairs, scatter_dimension=0, tiled=True)
    else:
        joined = jnp.concatenate(ring.in_order(out_two, out_two_g), axis=1)
        swapped = jnp.concatenate([context_two_g[own:], context_two_g[:own]], axis=0)
        context = jnp.concatenate(ring.in_order(context_two, swapped), axis=1)
        hidden_two = hidden_one + dot_nn(context, joined)
        normed_three = (normalize(hidden_two)[0] * gain_rows[2:3]).astype(LOW)
        grad_low = jnp.concatenate([output_grad[0], grad_g], axis=0)
        gate_up = gate_up[:, : 2 * hidden_half]
        gate_three, up_three = gate_up[:, :hidden_half], gate_up[:, hidden_half:]
        active, slope = gelu_parts(dot_nn(normed_three, gate_three))
        up = dot_nn(normed_three, up_three)
        mixed = (active * up).astype(LOW)
        down_part = dot_nn(mixed, down_three)
        down_keep, down_give = down_part[:own], down_part[own:].astype(LOW)
        grad_mixed = dot_nt(grad_low, down_three)
        gate_low = (grad_mixed * up * slope).astype(LOW)
        up_low = (grad_mixed * active).astype(LOW)
        part_low = (dot_nt(gate_low, gate_three) + dot_nt(up_low, up_three)).astype(LOW)
        terms = jnp.concatenate(
            [dot_tn(normed_three, gate_low), dot_tn(normed_three, up_low)], axis=1
        )
        column = jnp.sum(terms * gate_up.astype(F32), axis=1, keepdims=True)
        gain_three = lane_column(column / gain_cols[:, 2:3].astype(F32), 2)
        gate_up = lax.psum_scatter(terms, pairs, scatter_dimension=0, tiled=True)
        mlp_ddown = lax.psum_scatter(
            dot_tn(mixed, grad_low), pairs, scatter_dimension=0, tiled=True
        )

    part_g = ring.swap(part_low)
    down_got = ring.swap(down_give)
    output = (hidden_two[:own] + down_keep + down_got.astype(F32)).astype(LOW)

    def branch(gain_at, hidden, mine, got, weight_m, weight_g, base):
        return run_kernel(
            functools.partial(branch_kernel, gain_at),
            [full_shape(both, width), low_shape(both, width), low_shape(both, half)],
            both * width * half,
            [place],
            [hidden, gain_rows, mine, got, weight_m, weight_g, *base],
        )

    dhidden_two, branch_two, dcontext_two = branch(
        2, hidden_two, part_low, part_g, out_two, out_two_g, [output_grad[0], grad_g]
    )
    dquery, dkey, dvalue = attention_backward(
        info_two,
        cross_heads,
        memory_keys,
        memory_values,
        context_two,
        dcontext_two,
        lse_two,
        False,
        patch_chunk,
    )
    part_low = dot_nt(dquery, query_two).astype(LOW)
    part_g = ring.swap(part_low)

    count = ring.blocks // 2

    def grads(body, inputs, columns, gain_outs, cost):
        scratch = [pltpu.VMEM((width, c), LOW) for c in columns]
        acc = pltpu.VMEM((width, PAIR_LANES), F32)
        if packed:
            shapes = [low_shape(count, block_rows, c) for c in columns for _ in range(2)]
            outs = run_kernel(
                functools.partial(body, True),
                gain_outs + shapes,
                cost,
                [place, *index_out],
                inputs,
                scratch + [acc],
            )
            blocks = outs[len(gain_outs) :]
            return outs[: len(gain_outs)], blocks[0::2], blocks[1::2]
        wholes = [low_shape(width, c) for c in columns]
        outs = run_kernel(
            functools.partial(body, False), gain_outs + wholes, cost, [place], inputs, [acc]
        )
        return outs[: len(gain_outs)], *ring.halve_wholes(outs[len(gain_outs) :], block_rows)

    (gain_two,), cross_keep, cross_give = grads(
        cross_grads_kernel,
        [
            context_two,
            context_two_g,
            branch_two,
            normed_two,
            dquery,
            *patch_all,
            dkey,
            dvalue,
            query_two,
            gain_cols,
        ],
        (2 * half, 2 * half),
        [full_shape(width, PAIR_LANES)],
        (both + patches) * width * half,
    )
    memory_part = dot_nt(dkey, key_two) + dot_nt(dvalue, value_two)
    memory_part = memory_part.reshape(2, ring.groups, own_patches, width)
    memory_total = ring.pair_sum(memory_part[0], memory_part[1])
    memory_sent = ring.group_terms(memory_total)
    cross_got = ring.near_sends(cross_give, len(ring.tails[0]) - 1)

    dhidden_one, branch_one, dcontext_one = branch(
        1, hidden_one, part_low, part_g, out_one, out_one_g, [dhidden_two]
    )
    dquery_one, dkey_one, dvalue_one = attention_backward(
        info_one,
        query_heads,
        key_heads,
        value_heads,
        context_one,
        dcontext_one,
        lse_one,
        True,
        token_chunk,
    )
    dquery_one, dkey_one, dvalue_one, memory_sent, cross_got = together(
        dquery_one, dkey_one, dvalue_one, memory_sent, cross_got
    )
    memory_grad = memory_sent
    cross_left, cross_give = ring.near_sums(cross_keep, cross_got)
    _, self_keep, self_give = grads(
        self_grads_kernel,
        [
            context_one,
            context_one_g,
            branch_one,
            normed_one,
            dquery_one,
            dkey_one,
            dvalue_one,
            query_one,
            key_one,
            value_one,
            gain_cols,
            gain_two,
            gain_three,
        ],
        (2 * half + PAIR_LANES, 2 * half),
        [],
        (both + keys) * width * half,
    )
    self_got = ring.near_sends(self_give, len(ring.tails[0]) - 1)
    for step in range(len(ring.far)):
        cross_left, cross_give = ring.far_sum(cross_left, cross_give, step)
    cross_sum = cross_left[0]
    self_left, self_give = ring.near_sums(self_keep, self_got)
    if packed:
        self_give, mlp_sum = together(self_give, mlp_sum)
        mlp_sum = mlp_sum.astype(F32)
        take = lambda at, size: mlp_sum[:, at : at + size]
        gate_up = jnp.concatenate(
            [
                jnp.concatenate([take((m * pieces + j) * hidden_half, hidden_half) for m in range(2)], axis=1)
                for j in range(pieces)
            ],
            axis=0,
        )
        base = 2 * pieces * hidden_half
        mlp_ddown = jnp.concatenate(
            [take(base + j * width, width) for j in range(down_pieces)], axis=0
        )
    late = self_give
    for step in range(len(ring.far)):
        self_left, self_give = ring.far_sum(self_left, self_give, step)

    part_one = dot_nt(dkey_one, key_one) + dot_nt(dvalue_one, value_one)
    part_mine = part_one[:both] + dot_nt(dquery_one, query_one)
    part_one = jnp.concatenate([part_mine, part_one[both:]], axis=0)
    part_one = part_one.reshape(ring.groups, 2, own, width)
    dnormed_one = ring.group_terms(after(ring.pair_sum(part_one[:, 0], part_one[:, 1]), late))
    plain, inverse = normalize(tokens[0].astype(F32))
    input_grad = dhidden_one[:own] + norm_back(plain, inverse, gain_rows[0:1], dnormed_one)

    (gate_up,) = ring.finished(gate_up, 1)
    gate_columns = [gate_up[:, i * hidden_half : (i + 1) * hidden_half] for i in range(4)]
    mlp_dgate = unit_whole(gate_columns[0], gate_columns[2], units)
    mlp_dup = unit_whole(gate_columns[1], gate_columns[3], units)
    cross_dout, cross_dquery, cross_dkey, cross_dvalue = ring.finished(cross_sum, 4)
    self_left, mlp_dgate, mlp_dup, mlp_ddown = together(self_left, mlp_dgate, mlp_dup, mlp_ddown)
    self_sum = self_left[0]
    gain_at = 2 * half
    gain_block = self_sum[:, gain_at : gain_at + PAIR_LANES]
    gain_block = jnp.pad(gain_block, ((0, 0), (0, half - PAIR_LANES)))
    self_sum = jnp.concatenate(
        [self_sum[:, :gain_at], self_sum[:, gain_at + PAIR_LANES :], gain_block], axis=1
    )
    self_dquery, self_dout, self_dkey, self_dvalue, gain_terms = ring.finished(self_sum, 5)
    dgains = gain_terms[:, :3] + gain_terms[:, half : half + 3]

    return (
        output[None],
        input_grad[None],
        memory_grad[None],
        dgains[:, 0],
        self_dquery,
        self_dkey,
        self_dvalue,
        self_dout,
        dgains[:, 1],
        cross_dquery,
        cross_dkey,
        cross_dvalue,
        cross_dout,
        dgains[:, 2],
        mlp_dgate,
        mlp_dup,
        mlp_ddown,
    )


def solution(mesh):
    charts, heads = mesh.devices.shape
    inner = Mesh(mesh.devices.reshape(charts, heads // 2, 2), ("dp", "hx", "hc"))
    every = ("dp", "hx", "hc")
    rows = P(every, None)
    vector = P(every)
    grid = P("dp", ("hx", "hc"), None)
    in_specs = (grid, grid, P("dp"), P("dp"))
    in_specs += (vector, rows, rows, rows, rows) * 2
    in_specs += (vector, rows, rows, rows, grid)
    out_specs = (grid, grid, grid)
    out_specs += (vector, rows, rows, rows, rows) * 2
    out_specs += (vector, rows, rows, rows)
    return jax.shard_map(
        on_device, mesh=inner, in_specs=in_specs, out_specs=out_specs, check_vma=False
    )
```

```python
import functools
import math

import jax
import jax.numpy as jnp
from jax import lax
from jax.experimental import pallas as pl
from jax.experimental.pallas import tpu as pltpu
from jax.sharding import Mesh
from jax.sharding import PartitionSpec as P

HEAD_DIM = 64
PAIR_LANES = 128
NEG_FILL = -1e30
EPS = 1e-06
F32 = jnp.float32
LOW = jnp.bfloat16


NT = (((1,), (1,)), ((), ()))
TN = (((0,), (0,)), ((), ()))


def dot_nt(left, right):
    return lax.dot_general(left, right, NT, preferred_element_type=F32)


def dot_tn(left, right):
    return lax.dot_general(left, right, TN, preferred_element_type=F32)


def dot_nn(left, right):
    return jnp.dot(left, right, preferred_element_type=F32)


FIXED = 3
SPANS = 4


def query_limits(info, queries, causal):
    last = info[0] - 1
    if not causal:
        return jnp.full((1, queries), last, jnp.int32), last
    lanes = lax.broadcasted_iota(jnp.int32, (1, queries), 1)
    span = queries // 2
    swapped = jnp.where(lanes < span, lanes + info[2] * span, lanes - info[2] * span)
    return jnp.minimum(info[1] + swapped, last), jnp.minimum(info[1] + queries - 1, last)


def key_places(info, chunk, span, queries, j):
    parts = chunk // span
    starts = [info[FIXED + j * parts + i] for i in range(parts)]
    inner = lax.broadcasted_iota(jnp.int32, (span, queries), 0)
    first = functools.reduce(jnp.minimum, starts)
    return jnp.concatenate([start + inner for start in starts], axis=0), first


def first_place(info, chunk, span, j):
    parts = chunk // span
    return functools.reduce(jnp.minimum, [info[FIXED + j * parts + i] for i in range(parts)])


def head_lanes(head):
    lanes = lax.broadcasted_iota(jnp.int32, (1, PAIR_LANES), 1)
    return (lanes // HEAD_DIM) == head


def fold(values, op):
    rows, columns = values.shape
    return op(values.reshape(rows // 8, 8, columns), axis=0)


def forward_kernel(causal, chunk, span, info, q_ref, k_ref, v_ref, c_ref, lse_ref, s_ref, m_ref, l_ref, a_ref):
    queries = q_ref.shape[0]
    chunks = k_ref.shape[0] // chunk
    scaling = 1.0 / math.sqrt(HEAD_DIM)
    limit, latest = query_limits(info, queries, causal)
    q_all = q_ref[...] * jnp.asarray(scaling, q_ref.dtype)
    q_heads = [jnp.where(head_lanes(h), q_all, jnp.zeros_like(q_all)) for h in range(2)]
    m_ref[...] = jnp.full(m_ref.shape, NEG_FILL, F32)
    l_ref[...] = jnp.zeros(l_ref.shape, F32)
    a_ref[...] = jnp.zeros(a_ref.shape, F32)

    @pl.loop(0, chunks)
    def _(j):
        @pl.when(first_place(info, chunk, span, j) <= latest)
        def _():
            rows = pl.ds(pl.multiple_of(j * chunk, chunk), chunk)
            keys = k_ref[rows, :]
            place, _ = key_places(info, chunk, span, queries, j)
            allowed = place <= limit
            for h in range(2):
                scores = jnp.where(allowed, dot_nt(keys, q_heads[h]), NEG_FILL)
                s_ref[h, rows, :] = scores
                m_ref[h] = jnp.maximum(m_ref[h], fold(scores, jnp.max))

    highest = [jnp.max(m_ref[h], axis=0, keepdims=True) for h in range(2)]

    @pl.loop(0, chunks)
    def _(j):
        @pl.when(first_place(info, chunk, span, j) <= latest)
        def _():
            rows = pl.ds(pl.multiple_of(j * chunk, chunk), chunk)
            values = v_ref[rows, :]
            for h in range(2):
                weight = jnp.exp(s_ref[h, rows, :] - highest[h])
                l_ref[h] = l_ref[h] + fold(weight, jnp.sum)
                a_ref[h] = a_ref[h] + dot_tn(values, weight.astype(LOW))

    parts = []
    for h in range(2):
        total = jnp.sum(l_ref[h], axis=0, keepdims=True)
        lse_ref[0, pl.ds(h, 1), :] = highest[h] + jnp.log(total)
        parts.append(a_ref[h, pl.ds(h * HEAD_DIM, HEAD_DIM), :] / total)
    c_ref[...] = jnp.concatenate(parts, axis=0).T.astype(c_ref.dtype)


def backward_kernel(causal, chunk, span, info, q_ref, k_ref, v_ref, c_ref, g_ref, lse_ref, dq_ref, dk_ref, dv_ref, a_ref):
    queries = q_ref.shape[0]
    chunks = k_ref.shape[0] // chunk
    scaling = 1.0 / math.sqrt(HEAD_DIM)
    limit, latest = query_limits(info, queries, causal)
    q_all = q_ref[...] * jnp.asarray(scaling, q_ref.dtype)
    g_all = g_ref[...]
    q_heads = [jnp.where(head_lanes(h), q_all, jnp.zeros_like(q_all)) for h in range(2)]
    g_heads = [jnp.where(head_lanes(h), g_all, jnp.zeros_like(g_all)) for h in range(2)]
    product = (c_ref[...].astype(F32) * g_all.astype(F32)).T
    centres = [
        jnp.sum(product[h * HEAD_DIM : (h + 1) * HEAD_DIM], axis=0, keepdims=True) for h in range(2)
    ]
    logs = [lse_ref[0, pl.ds(h, 1), :] for h in range(2)]
    a_ref[...] = jnp.zeros(a_ref.shape, F32)

    @pl.loop(0, chunks)
    def _(j):
        start = first_place(info, chunk, span, j)
        rows = pl.ds(pl.multiple_of(j * chunk, chunk), chunk)

        @pl.when(start <= latest)
        def _():
            keys = k_ref[rows, :]
            values = v_ref[rows, :]
            place, _ = key_places(info, chunk, span, queries, j)
            allowed = place <= limit
            dk = jnp.zeros((chunk, PAIR_LANES), F32)
            dv = jnp.zeros((chunk, PAIR_LANES), F32)
            for h in range(2):
                scores = jnp.where(allowed, dot_nt(keys, q_heads[h]), NEG_FILL)
                prob = jnp.exp(scores - logs[h])
                dprob = dot_nt(values, g_heads[h])
                dv = dv + dot_nn(prob.astype(LOW), g_heads[h])
                dscore = (prob * (dprob - centres[h])).astype(LOW)
                dk = dk + dot_nn(dscore, q_heads[h])
                a_ref[h] = a_ref[h] + dot_tn(keys, dscore)
            dk_ref[rows, :] = dk.astype(dk_ref.dtype)
            dv_ref[rows, :] = dv.astype(dv_ref.dtype)

        @pl.when(start > latest)
        def _():
            dk_ref[rows, :] = jnp.zeros((chunk, PAIR_LANES), dk_ref.dtype)
            dv_ref[rows, :] = jnp.zeros((chunk, PAIR_LANES), dv_ref.dtype)

    parts = [a_ref[h, pl.ds(h * HEAD_DIM, HEAD_DIM), :] for h in range(2)]
    dq_ref[...] = (jnp.concatenate(parts, axis=0).T * scaling).astype(dq_ref.dtype)


def lane_spec(rows):
    return pl.BlockSpec((rows, PAIR_LANES), lambda i, info: (0, i))


def stat_spec(queries):
    return pl.BlockSpec((1, 2, queries), lambda i, info: (i, 0, 0))


def attention_forward(info, queries, keys, values, causal, span):
    chunk = math.gcd(SPANS * span, keys.shape[0])
    rows, features = queries.shape
    key_rows = keys.shape[0]
    pairs = features // PAIR_LANES
    return pl.pallas_call(
        functools.partial(forward_kernel, causal, chunk, span),
        out_shape=(
            jax.ShapeDtypeStruct((rows, features), LOW),
            jax.ShapeDtypeStruct((pairs, 2, rows), F32),
        ),
        grid_spec=pltpu.PrefetchScalarGridSpec(
            num_scalar_prefetch=1,
            grid=(pairs,),
            in_specs=[lane_spec(rows), lane_spec(key_rows), lane_spec(key_rows)],
            out_specs=[lane_spec(rows), stat_spec(rows)],
            scratch_shapes=[
                pltpu.VMEM((2, key_rows, rows), F32),
                pltpu.VMEM((2, 8, rows), F32),
                pltpu.VMEM((2, 8, rows), F32),
                pltpu.VMEM((2, PAIR_LANES, rows), F32),
            ],
        ),
        compiler_params=pltpu.CompilerParams(vmem_limit_bytes=VMEM_LIMIT),
        cost_estimate=pl.CostEstimate(flops=rows, transcendentals=0, bytes_accessed=0),
    )(info, queries, keys, values)


def attention_backward(info, queries, keys, values, context, grads, lse, causal, span):
    chunk = math.gcd(SPANS * span, keys.shape[0])
    rows, features = queries.shape
    key_rows = keys.shape[0]
    pairs = features // PAIR_LANES
    return pl.pallas_call(
        functools.partial(backward_kernel, causal, chunk, span),
        out_shape=(
            jax.ShapeDtypeStruct((rows, features), LOW),
            jax.ShapeDtypeStruct((key_rows, features), LOW),
            jax.ShapeDtypeStruct((key_rows, features), LOW),
        ),
        grid_spec=pltpu.PrefetchScalarGridSpec(
            num_scalar_prefetch=1,
            grid=(pairs,),
            in_specs=[
                lane_spec(rows),
                lane_spec(key_rows),
                lane_spec(key_rows),
                lane_spec(rows),
                lane_spec(rows),
                stat_spec(rows),
            ],
            out_specs=[lane_spec(rows), lane_spec(key_rows), lane_spec(key_rows)],
            scratch_shapes=[pltpu.VMEM((2, PAIR_LANES, rows), F32)],
        ),
        compiler_params=pltpu.CompilerParams(vmem_limit_bytes=VMEM_LIMIT),
        cost_estimate=pl.CostEstimate(flops=rows, transcendentals=0, bytes_accessed=0),
    )(info, queries, keys, values, context, grads, lse)


SMEM_SPEC = pl.BlockSpec(memory_space=pltpu.SMEM)


def vmem_specs(number):
    return [pl.BlockSpec(memory_space=pltpu.VMEM)] * number


def cuts_of(widths):
    return [sum(widths[:i]) for i in range(len(widths))]


def place_blocks(index, first, later, targets):
    half, rows, _ = first.shape
    cuts = cuts_of([target.shape[1] for target in targets])

    @pl.loop(0, 2 * half)
    def _(step):
        at = index[step]
        place = pl.ds(pl.multiple_of(step * rows, rows), rows)

        def put(source, block):
            for cut, target in zip(cuts, targets):
                target[place, :] = source[block, :, pl.ds(cut, target.shape[1])]

        @pl.when(at < half)
        def _():
            put(first, at)

        @pl.when(at >= half)
        def _():
            put(later, at - half)


def send_order(index, whole, keep, give):
    half, rows, _ = keep.shape

    @pl.loop(0, half)
    def _(step):
        for side, target in enumerate((keep, give)):
            at = pl.ds(pl.multiple_of(index[step + side * half] * rows, rows), rows)
            target[step] = whole[at, :]


def whole_kernel(index, first, later, *targets):
    place_blocks(index, first, later, targets)


def to_whole(first, later, index, widths):
    half, rows, columns = first.shape
    count = 2 * half
    if rows % 16:
        blocks = jnp.concatenate([first, later], axis=0)
        whole = jnp.take(blocks, index, axis=0).reshape(count * rows, columns)
        return [whole[:, cut : cut + width] for cut, width in zip(cuts_of(widths), widths)]
    return run_kernel(
        whole_kernel,
        [low_shape(count * rows, width) for width in widths],
        count * rows * columns,
        [index],
        [first, later],
    )


def staged_kernel(body, late, sizes, *refs):
    parts, at = [], 0
    for size in sizes:
        parts.append(refs[at : at + size])
        at += size
    tables, arrays, streamed, outs, scratch, held_in, held_out, (in_sems, out_sems) = parts
    loads = [
        pltpu.make_async_copy(a, b, in_sems.at[i]) for i, (a, b) in enumerate(zip(arrays, held_in))
    ]
    for load in loads:
        load.start()

    def ready():
        for load in loads:
            load.wait()

    if late:
        body(ready, *tables, *held_in, *streamed, *held_out, *scratch)
    else:
        ready()
        body(*tables, *held_in, *streamed, *held_out, *scratch)
    stores = [
        pltpu.make_async_copy(a, b, out_sems.at[i]) for i, (a, b) in enumerate(zip(held_out, outs))
    ]
    for store in stores:
        store.start()
    for store in stores:
        store.wait()


HBM_SPEC = pl.BlockSpec(memory_space=pltpu.HBM)


def run_kernel(body, out_shape, cost, tables, arrays, scratch=(), streamed=(), late=False):
    sizes = (len(tables), len(arrays), len(streamed), len(out_shape), len(scratch))
    sizes += (len(arrays), len(out_shape), 2)
    held = [pltpu.VMEM(x.shape, x.dtype) for x in [*arrays, *out_shape]]
    sems = [pltpu.SemaphoreType.DMA((len(arrays),)), pltpu.SemaphoreType.DMA((len(out_shape),))]
    return pl.pallas_call(
        functools.partial(staged_kernel, body, late, sizes),
        out_shape=out_shape,
        in_specs=[SMEM_SPEC] * len(tables) + [HBM_SPEC] * (len(arrays) + len(streamed)),
        out_specs=[HBM_SPEC] * len(out_shape),
        scratch_shapes=list(scratch) + held + sems,
        compiler_params=pltpu.CompilerParams(vmem_limit_bytes=VMEM_LIMIT),
        cost_estimate=pl.CostEstimate(flops=cost // 1000, transcendentals=0, bytes_accessed=0),
    )(*tables, *arrays, *streamed)


VMEM_LIMIT = 56 << 20


def low_shape(*shape):
    return jax.ShapeDtypeStruct(shape, LOW)


def full_shape(*shape):
    return jax.ShapeDtypeStruct(shape, F32)


def unit_tile(source, at, second):
    lanes = 2 * HEAD_DIM
    start = 2 * at * lanes + (HEAD_DIM if second else 0)
    return jnp.concatenate(
        [source[:, pl.ds(start, HEAD_DIM)], source[:, pl.ds(start + lanes, HEAD_DIM)]], axis=1
    )


def shards_kernel(kinds, place, *refs):
    sources, targets = refs[:-2], refs[-2:]

    def write(target, second):
        cut = 0
        for kind, source in zip(kinds, sources):
            columns = source.shape[1]
            if kind == "all":
                target[:, pl.ds(cut, columns)] = source[...]
                cut += columns
                continue
            if kind == "half":
                start = columns // 2 if second else 0
                target[:, pl.ds(cut, columns // 2)] = source[:, pl.ds(start, columns // 2)]
            else:
                for tile in range(columns // 256):
                    target[:, pl.ds(cut + 128 * tile, 128)] = unit_tile(source, tile, second)
            cut += columns // 2

    @pl.when(place[0] == 0)
    def _():
        write(targets[0], False)
        write(targets[1], True)

    @pl.when(place[0] != 0)
    def _():
        write(targets[0], True)
        write(targets[1], False)


def rows_kernel(widths, piece, place, mine, other, down, *targets):
    *widths, matrices, extra = widths
    rows = mine.shape[0]

    def write(upper, lower):
        cut = 0
        for target, width in zip(targets[:-1], widths):
            target[0, pl.ds(0, rows), :] = upper[:, pl.ds(cut, width)]
            target[0, pl.ds(rows, rows), :] = lower[:, pl.ds(cut, width)]
            cut += width
        packed = targets[-1]
        columns = (mine.shape[1] - cut - extra) // matrices
        step = 8
        base = matrices * (2 * rows // piece) * columns
        last = base + down.shape[1] * (down.shape[0] // piece)
        for start in range(0, 2 * rows, step):
            source = upper if start < rows else lower
            number, inner = start // piece, start % piece
            for matrix in range(matrices):
                place_at = (matrix * (2 * rows // piece) + number) * columns
                packed[pl.ds(inner, step), pl.ds(place_at, columns)] = source[
                    pl.ds(start % rows, step), pl.ds(cut + matrix * columns, columns)
                ]
            packed[pl.ds(inner, step), pl.ds(last + number * extra, extra)] = source[
                pl.ds(start % rows, step), pl.ds(cut + matrices * columns, extra)
            ]
        width = down.shape[1]
        for number in range(down.shape[0] // piece):
            packed[:, pl.ds(base + number * width, width)] = down[pl.ds(number * piece, piece), :]

    @pl.when(place[0] == 0)
    def _():
        write(mine, other)

    @pl.when(place[0] != 0)
    def _():
        write(other, mine)


def cut_shards(place, shards, kinds):
    rows = shards[0].shape[0]
    columns = sum(w.shape[1] if k == "all" else w.shape[1] // 2 for w, k in zip(shards, kinds))
    return run_kernel(
        functools.partial(shards_kernel, kinds), [low_shape(rows, columns)] * 2, rows * columns, [place], shards
    )


def join_rows(place, mine, other, down, widths, extra, piece):
    rows = 2 * mine.shape[0]
    rest = mine.shape[1] - sum(widths)
    packed = rest * (rows // piece) + down.shape[1] * (down.shape[0] // piece)
    return run_kernel(
        functools.partial(rows_kernel, [*widths, 2, extra], piece),
        [low_shape(1, rows, width) for width in widths] + [low_shape(piece, packed)],
        rows * rest,
        [place],
        [mine, other, down],
    )


def pieces_kernel(cut, source, target, held, sem):
    blocks, pieces, piece, columns = held.shape
    copies = [
        pltpu.make_async_copy(
            source.at[:, :, pl.ds(cut + i * columns, columns)], held.at[:, i], sem.at[i]
        )
        for i in range(pieces)
    ]
    for copy in copies:
        copy.start()
    for copy in copies:
        copy.wait()
    target[...] = held[...].reshape(target.shape)


def from_pieces(packed, cut, pieces, columns):
    blocks, piece, _ = packed.shape
    return pl.pallas_call(
        functools.partial(pieces_kernel, cut),
        out_shape=low_shape(blocks * pieces * piece, columns),
        in_specs=[HBM_SPEC],
        out_specs=pl.BlockSpec(memory_space=pltpu.VMEM),
        scratch_shapes=[
            pltpu.VMEM((blocks, pieces, piece, columns), LOW),
            pltpu.SemaphoreType.DMA((pieces,)),
        ],
        cost_estimate=pl.CostEstimate(flops=1000, transcendentals=0, bytes_accessed=0),
    )(packed)


def normalize(values):
    inverse = lax.rsqrt(jnp.mean(values * values, axis=-1, keepdims=True) + EPS)
    return values * inverse, inverse


def norm_back(normed, inverse, gain, grads):
    scaled = grads * gain
    return inverse * (scaled - normed * jnp.mean(scaled * normed, axis=-1, keepdims=True))


def gelu_parts(gate):
    factor = math.sqrt(2.0 / math.pi)
    inner = jnp.tanh(factor * (gate + 0.044715 * gate * gate * gate))
    value = 0.5 * gate * (1.0 + inner)
    slope = 0.5 * (1.0 + inner) + 0.5 * gate * (1.0 - inner * inner) * factor * (
        1.0 + 3.0 * 0.044715 * gate * gate
    )
    return value, slope


def head_slices(place, half):
    mine = pl.ds(pl.multiple_of(place[0] * half, half), half)
    other = pl.ds(pl.multiple_of((1 - place[0]) * half, half), half)
    return mine, other


def project_heads(gain_cols, token_m, token_g, weights, rows_ref, normed_ref, heads):
    gain_rows = gain_cols.astype(F32).T[0:8]
    rows_ref[...] = gain_rows
    groups, own, _ = token_m.shape
    for group in range(groups):
        for side, source in enumerate((token_m, token_g)):
            plain, _ = normalize(source[group].astype(F32))
            at = pl.ds((2 * group + side) * own, own)
            normed_ref[at, :] = (plain * gain_rows[0:1]).astype(LOW)
    for number, (weight, target) in enumerate(zip(weights, heads)):
        target[...] = dot_nn(normed_ref[pl.ds(0, target.shape[0]), :], weight[...]).astype(LOW)


def query_kernel(packed, *refs):
    if packed:
        index_a, index_b, first_a, later_a, first_b, later_b, token_m, token_g = refs[:8]
        rows_ref, normed_ref, q_ref, k_ref, v_ref, wq, gain_cols, wk, wv = refs[8:]
        place_blocks(index_a, first_a, later_a, [wq, gain_cols])
        place_blocks(index_b, first_b, later_b, [wk, wv])
    else:
        wq, gain_cols, wk, wv, token_m, token_g = refs[:6]
        rows_ref, normed_ref, q_ref, k_ref, v_ref = refs[6:]
    heads = (q_ref, k_ref, v_ref)
    project_heads(gain_cols[...], token_m, token_g, (wq, wk, wv), rows_ref, normed_ref, heads)


def add_context(place, target, base, c_m, c_g, w_m, w_g):
    rows, half = c_m.shape
    own = rows // 2
    mine, other = head_slices(place, half)
    for side in range(2):
        at = pl.ds(side * own, own)
        left = c_m[at, :]
        right = c_g[pl.ds((1 - side) * own, own), :]
        for weight, columns in ((w_m, mine), (w_g, other)):
            value = dot_nn(left, weight[mine, :]) + dot_nn(right, weight[other, :])
            target[at, columns] = base(side, columns) + value


def cross_query_kernel(place, token_m, token_g, c_m, c_g, w_m, w_g, rows_ref, wq, h_ref, normed_ref, q_ref):
    tokens = (token_m, token_g)
    base = lambda side, columns: tokens[side][:, columns].astype(F32)
    add_context(place, h_ref, base, c_m, c_g, w_m, w_g)
    plain, _ = normalize(h_ref[...])
    normed_ref[...] = (plain * rows_ref[1:2, :]).astype(LOW)
    q_ref[...] = dot_nn(normed_ref[...], wq[...]).astype(LOW)


def memory_kernel(packed, *refs):
    if packed:
        index, first, later, patch_m, patch_g, k_ref, v_ref, wk, wv = refs
        place_blocks(index, first, later, [wk, wv])
    else:
        wk, wv, patch_m, patch_g, k_ref, v_ref = refs
    count = patch_m.shape[0]
    step = math.gcd(count, 512)
    for side, source in enumerate((patch_m, patch_g)):

        @pl.loop(0, count // step)
        def _(number):
            part = source[pl.ds(pl.multiple_of(number * step, step), step), :]
            place = pl.ds(pl.multiple_of(side * count + number * step, step), step)
            k_ref[place, :] = dot_nn(part, wk[...]).astype(LOW)
            v_ref[place, :] = dot_nn(part, wv[...]).astype(LOW)


def lane_column(column, lane):
    lanes = lax.broadcasted_iota(jnp.int32, (1, PAIR_LANES), 1)
    return jnp.where(lanes == lane, column, 0.0)


def mlp_kernel(
    chunk,
    ready,
    place,
    h_in,
    c_m,
    c_g,
    out_m,
    out_g,
    rows_ref,
    cols_ref,
    g_m,
    g_g,
    w_ref,
    h_ref,
    part_ref,
    keep_ref,
    give_ref,
    gain_ref,
    grad_ref,
    gate_w,
    up_w,
    down_w,
    a_ref,
    t_ref,
    g_ref,
    p_acc,
    d_acc,
    r_acc,
    sems,
):
    blocks, pieces, piece, units = gate_w.shape
    down_pieces, width = down_w.shape[1], down_w.shape[3]
    total = blocks * pieces * piece
    own = g_m.shape[0]
    moves = []
    for number in range(pieces):
        moves.append((w_ref.at[:, :, pl.ds(number * units, units)], gate_w.at[:, number]))
    for number in range(pieces):
        moves.append((w_ref.at[:, :, pl.ds((pieces + number) * units, units)], up_w.at[:, number]))
    base = 2 * pieces * units
    for number in range(down_pieces):
        moves.append((w_ref.at[:, :, pl.ds(base + number * width, width)], down_w.at[:, number]))
    copies = [pltpu.make_async_copy(a, b, sems.at[i]) for i, (a, b) in enumerate(moves)]
    for copy in copies:
        copy.start()
    ready()
    add_context(
        place, h_ref, lambda side, columns: h_in[pl.ds(side * own, own), columns], c_m, c_g, out_m, out_g
    )
    plain, _ = normalize(h_ref[...])
    a_ref[...] = (plain * rows_ref[2:3, :]).astype(LOW)
    t_ref[...] = a_ref[...].T
    g_ref[pl.ds(0, own), :] = g_m[...]
    g_ref[pl.ds(own, own), :] = g_g[...]
    p_acc[...] = jnp.zeros(p_acc.shape, F32)
    d_acc[...] = jnp.zeros(d_acc.shape, F32)
    r_acc[...] = jnp.zeros(r_acc.shape, F32)
    for copy in copies:
        copy.wait()

    per_block = down_pieces * piece
    step_blocks = chunk // per_block

    @pl.loop(0, units // chunk)
    def _(step):
        start = pl.multiple_of(step * chunk, chunk)
        a_in = a_ref[...]
        g_in = g_ref[...]
        columns = pl.ds(start, chunk)
        gate_part = gate_w[:, :, :, columns].reshape(total, chunk)
        up_part = up_w[:, :, :, columns].reshape(total, chunk)
        down_at = pl.ds(step * step_blocks, step_blocks)
        down_part = down_w[down_at].reshape(chunk, width)
        gate = dot_nn(a_in, gate_part)
        up = dot_nn(a_in, up_part)
        active, slope = gelu_parts(gate)
        mixed = (active * up).astype(LOW)
        grad = dot_nt(g_in, down_part)
        gate_low = (grad * up * slope).astype(LOW)
        up_low = (grad * active).astype(LOW)
        d_acc[...] += dot_nn(mixed, down_part)
        p_acc[...] += dot_nt(gate_low, gate_part) + dot_nt(up_low, up_part)
        dgate = dot_nn(t_ref[...], gate_low)
        dup = dot_nn(t_ref[...], up_low)
        gain_terms = dgate * gate_part.astype(F32) + dup * up_part.astype(F32)
        for lane in range(0, chunk, PAIR_LANES):
            r_acc[...] += gain_terms[:, lane : lane + PAIR_LANES]
        dgate = dgate.astype(LOW).reshape(blocks, pieces, piece, chunk)
        dup = dup.astype(LOW).reshape(blocks, pieces, piece, chunk)
        for number in range(pieces):
            gate_at = pl.multiple_of(number * units + start, chunk)
            up_at = pl.multiple_of((pieces + number) * units + start, chunk)
            grad_ref[:, :, pl.ds(gate_at, chunk)] = dgate[:, number]
            grad_ref[:, :, pl.ds(up_at, chunk)] = dup[:, number]
        ddown = dot_tn(mixed, g_in).astype(LOW).reshape(step_blocks, down_pieces, piece, width)
        for number in range(down_pieces):
            grad_ref[down_at, :, pl.ds(base + number * width, width)] = ddown[:, number]

    part_ref[...] = p_acc[...].astype(LOW)
    keep_ref[...] = d_acc[pl.ds(0, own), :]
    give_ref[...] = d_acc[pl.ds(own, own), :].astype(LOW)
    summed = jnp.sum(r_acc[...], axis=1, keepdims=True)
    gain_ref[...] = lane_column(summed / cols_ref[:, 2:3].astype(F32), 2)


def branch_kernel(gain_at, place, *refs):
    h_ref, rows_ref, part_m, part_g, w_m, w_g = refs[:6]
    base, (d_ref, low_ref, c_ref) = refs[6:-3], refs[-3:]
    rows = h_ref.shape[0]
    own = rows // 2
    half = w_m.shape[1]
    mine, other = head_slices(place, half)
    for side in range(2):
        at = pl.ds(side * own, own)
        plain, inverse = normalize(h_ref[at, :])
        got = part_g[pl.ds((1 - side) * own, own), :]
        grads = part_m[at, :].astype(F32) + got.astype(F32)
        value = norm_back(plain, inverse, rows_ref[gain_at : gain_at + 1, :], grads)
        before = base[side][...].astype(F32) if len(base) == 2 else base[0][at, :]
        d_ref[at, :] = before + value
    low_ref[...] = d_ref[...].astype(LOW)
    value = dot_nt(low_ref[:, mine], w_m[mine, :]) + dot_nt(low_ref[:, other], w_g[mine, :])
    c_ref[...] = value.astype(LOW)


def dot_rows(left, right):
    columns = left.shape[1]
    step = math.gcd(columns, 256)
    return [(i, dot_tn(left[:, i : i + step], right)) for i in range(0, columns, step)]


def out_grad(place, whole, cut, c_m, c_g, branch):
    rows, half = c_m.shape
    own = rows // 2
    mine, other = head_slices(place, half)
    grads = branch[:, mine]
    columns = pl.ds(cut, half)
    whole[mine, columns] = dot_tn(c_m[...], grads).astype(LOW)
    value = dot_tn(c_g[pl.ds(own, own), :], grads[:own]) + dot_tn(c_g[pl.ds(0, own), :], grads[own:])
    whole[other, columns] = value.astype(LOW)


def weight_grads(targets, lefts, rights, gain_acc=None):
    features = lefts[0].shape[1]
    step = math.gcd(features, 256)

    for number in range(features // step):
        at = pl.ds(number * step, step)
        turned = [left[:, at].T for left in lefts]
        for (whole, cut, weight), terms in zip(targets, rights):
            width = terms[0].shape[1]
            value = sum(dot_nn(left, right[...]) for left, right in zip(turned, terms))
            whole[at, pl.ds(cut, width)] = value.astype(LOW)
            if weight is not None:
                products = value * weight[at, :].astype(F32)
                gain_acc[at, :] += sum(
                    products[:, lane : lane + PAIR_LANES] for lane in range(0, width, PAIR_LANES)
                )


def finish_blocks(packed, refs, whole_a, whole_b):
    if packed:
        index_a, index_b, keep_a, give_a, keep_b, give_b = refs
        send_order(index_a, whole_a, keep_a, give_a)
        send_order(index_b, whole_b, keep_b, give_b)


def cross_grads_kernel(packed, place, *refs):
    index, refs = (refs[:2], refs[2:]) if packed else ((), refs)
    c_m, c_g, branch, normed, dq, patch_m, patch_g, dk, dv, wq, cols_ref = refs[:11]
    gain_ref, *outs, whole_a, whole_b, gain_acc = refs[11:]
    half = dq.shape[1]
    count = patch_m.shape[0]
    gain_acc[...] = jnp.zeros(gain_acc.shape, F32)
    out_grad(place, whole_a, 0, c_m, c_g, branch)
    weight_grads([(whole_a, half, wq)], [normed], [[dq]], gain_acc)
    halves = [[g.at[pl.ds(i * count, count), :] for i in range(2)] for g in (dk, dv)]
    weight_grads(
        [(whole_b, 0, None), (whole_b, half, None)], [patch_m, patch_g], halves
    )
    summed = jnp.sum(gain_acc[...], axis=1, keepdims=True)
    gain_ref[...] = lane_column(summed / cols_ref[:, 1:2].astype(F32), 1)
    finish_blocks(packed, (*index, *outs), whole_a, whole_b)


def self_grads_kernel(packed, place, *refs):
    index, refs = (refs[:2], refs[2:]) if packed else ((), refs)
    c_m, c_g, branch, normed, dq, dk, dv, wq, wk, wv, cols_ref, gain_two, gain_three = refs[:13]
    *outs, whole_a, whole_b, gain_acc = refs[13:]
    rows, half = dq.shape
    gain_acc[...] = jnp.zeros(gain_acc.shape, F32)
    weight_grads([(whole_a, 0, wq)], [normed.at[pl.ds(0, rows), :]], [[dq]], gain_acc)
    out_grad(place, whole_a, half, c_m, c_g, branch)
    weight_grads(
        [(whole_b, 0, wk), (whole_b, half, wv)], [normed], [[dk], [dv]], gain_acc
    )
    summed = jnp.sum(gain_acc[...], axis=1, keepdims=True)
    gains = lane_column(summed / cols_ref[:, 0:1].astype(F32), 0) + gain_two[...] + gain_three[...]
    whole_a[:, pl.ds(2 * half, PAIR_LANES)] = gains.astype(LOW)
    finish_blocks(packed, (*index, *outs), whole_a, whole_b)


def back_kernel(grads, weight, out):
    out[...] = dot_nt(grads[...], weight[...]).astype(LOW)


def rows_back_kernel(spans, with_query, *refs):
    dk, dv, wk, wv = refs[:4]
    queries = refs[4:6] if with_query else None
    keep, give = refs[-2:]
    rows = dk.shape[0] // len(spans)
    for number, (mine, place) in enumerate(spans):
        at = pl.ds(number * rows, rows)
        value = dot_nt(dk[at, :], wk[...]) + dot_nt(dv[at, :], wv[...])
        if queries and number < 2:
            value = value + dot_nt(queries[0][at, :], queries[1][...])
        if mine:
            keep[place] = value
        else:
            give[place] = value.astype(LOW)


def columns_kernel(place, keep, got, *targets):
    rows = got.shape[0]

    def write(start, first, later):
        for number, target in enumerate(targets):
            half = target.shape[1] // 2
            columns = pl.ds(number * half, half)
            target[:, pl.ds(0, half)] = first(start, columns)
            target[:, pl.ds(half, half)] = later(start, columns)

    from_keep = lambda start, columns: keep[pl.ds(start, rows), columns]
    from_got = lambda start, columns: got[:, columns]

    @pl.when(place[0] == 0)
    def _():
        write(0, from_keep, from_got)

    @pl.when(place[0] != 0)
    def _():
        write(rows, from_got, from_keep)


def after(values, *others):
    return lax.optimization_barrier((values, *others))[0]


def together(*values):
    return lax.optimization_barrier(values)


class Ring:
    def __init__(self):
        self.charts = lax.axis_size("dp")
        self.groups = lax.axis_size("hx")
        self.half = lax.axis_index("hc").astype(jnp.int32)
        self.second = self.half == 1
        self.place = self.half[None]
        self.group = lax.axis_index("hx").astype(jnp.int32)
        self.block = lax.axis_index("dp").astype(jnp.int32) * self.groups + self.group
        self.blocks = self.charts * self.groups
        chart_bits = [("dp", 1 << i) for i in range(self.charts.bit_length() - 1)]
        self.group_bits = [("hx", 1 << i) for i in range(self.groups.bit_length() - 1)]
        self.far = chart_bits[:0:-1]
        near = chart_bits[:1]
        self.tails = (near + self.group_bits, self.group_bits + near)
        self.orders = tuple(self.far + tail for tail in self.tails)

    def send(self, values, axis, bit):
        size = self.charts if axis == "dp" else self.groups
        return lax.ppermute(values, axis, [(i, i ^ bit) for i in range(size)])

    def swap(self, values):
        return lax.ppermute(values, "hc", [(0, 1), (1, 0)])

    def in_order(self, mine, other):
        return jnp.where(self.second, other, mine), jnp.where(self.second, mine, other)

    def steps(self, order):
        return [bit * self.groups if axis == "dp" else bit for axis, bit in order]

    def arrivals(self):
        apart = self.block ^ jnp.arange(self.blocks, dtype=jnp.int32)
        indices = []
        for order in self.orders:
            index = jnp.zeros((self.blocks,), jnp.int32)
            for place, step in enumerate(self.steps(order)):
                index = index + jnp.where((apart & step) != 0, 1 << place, 0)
            indices.append(index)
        return indices

    def origins(self):
        indices = []
        for order in self.orders:
            masks = [0]
            for step in self.steps(order):
                masks = masks + [m ^ step for m in masks]
            indices.append(self.block ^ jnp.asarray(masks, jnp.int32))
        return indices

    def far_step(self, blocks, step):
        return jnp.concatenate([blocks, self.send(blocks, *self.far[step])], axis=0)

    def near_step(self, parts, step):
        return [self.send(part, *tail[step]) for part, tail in zip(parts, self.tails)]

    def near_sends(self, gives, place):
        return [self.send(give, *tail[place]) for give, tail in zip(gives, self.tails)]

    def near_sums(self, keeps, gots):
        add = lambda keep, got: keep.astype(F32) + got.astype(F32)
        for place in reversed(range(len(self.tails[0]))):
            halves = [got.shape[0] // 2 for got in gots]
            kind = LOW if place else F32
            gives = [add(k[h:], g[h:]).astype(kind) for k, g, h in zip(keeps, gots, halves)]
            keeps = [add(k[:h], g[:h]).astype(kind) for k, g, h in zip(keeps, gots, halves)]
            if place:
                gots = self.near_sends(gives, place - 1)
        return jnp.concatenate(keeps, axis=2), jnp.concatenate(gives, axis=2).astype(LOW)

    def far_sum(self, keep, give, step):
        got = self.send(give, *self.far[len(self.far) - 1 - step])
        half = keep.shape[0] // 2
        if not half:
            return keep + got.astype(F32), None
        later = (keep[half:] + got[half:].astype(F32)).astype(LOW)
        return keep[:half] + got[:half].astype(F32), later

    def halve_wholes(self, wholes, rows):
        keeps, gives = [], []
        for whole, index in zip(wholes, self.origins()):
            blocks = jnp.take(whole.reshape(self.blocks, rows, -1), index, axis=0)
            keeps.append(blocks[: self.blocks // 2])
            gives.append(blocks[self.blocks // 2 :])
        return keeps, gives

    def across(self, mine):
        rows = mine[None]
        for axis, bit in self.group_bits:
            rows = jnp.concatenate([rows, self.send(rows, axis, bit)], axis=0)
        return rows

    def halves(self, first, later):
        mine = jnp.where(self.second, later, first)
        give = jnp.where(self.second, first, later)
        return jnp.concatenate(self.in_order(mine, self.swap(give)), axis=0)

    def pair_sum(self, keep, give):
        return keep + self.swap(give.astype(LOW)).astype(F32)

    def group_terms(self, total):
        for axis, bit in reversed(self.group_bits):
            middle = total.shape[0] // 2
            total = total[:middle] + self.send(total[middle:].astype(LOW), axis, bit).astype(F32)
        return total[0]

    def finished(self, keep, count):
        rows = keep.shape[0] // 2
        give = lax.dynamic_slice_in_dim(keep, (1 - self.half) * rows, rows, 0)
        got = self.swap(give)
        width = keep.shape[1] // count * 2
        return run_kernel(
            columns_kernel, [full_shape(rows, width)] * count, rows * width, [self.place], [keep, got]
        )


def column_halves(weights):
    half = weights[0].shape[1] // 2
    return [jnp.concatenate([w[:, i * half : (i + 1) * half] for w in weights], axis=1) for i in range(2)]


def unit_halves(weight, units):
    rows, columns = weight.shape
    split = weight.reshape(rows, columns // (2 * units), 2, units)
    return split[:, :, 0].reshape(rows, -1), split[:, :, 1].reshape(rows, -1)


def unit_whole(first, later, units):
    rows, columns = first.shape
    pieces = [part.reshape(rows, columns // units, 1, units) for part in (first, later)]
    return jnp.concatenate(pieces, axis=2).reshape(rows, 2 * columns)


def on_device(
    tokens,
    memory,
    text_length,
    patch_count,
    self_gain,
    self_query,
    self_key,
    self_value,
    self_out,
    cross_gain,
    cross_query,
    cross_key,
    cross_value,
    cross_out,
    mlp_gain,
    mlp_gate,
    mlp_up,
    mlp_down,
    output_grad,
):
    ring = Ring()
    place = ring.place
    width = tokens.shape[-1]
    half = width // 2
    units = mlp_down.shape[0]
    hidden_half = units * ring.blocks
    rows = self_query.shape[0]
    own = tokens.shape[1]
    own_patches = memory.shape[1]
    both = 2 * own
    keys = both * ring.groups
    patches = 2 * own_patches * ring.groups
    piece = 16
    packed = (2 * rows) % piece == 0 and units == HEAD_DIM and ring.blocks > 1
    pieces, down_pieces = 2 * rows // piece, units // piece
    pairs = ("dp", "hx")
    index_in = tuple(ring.arrivals()) if packed else ()
    index_out = tuple(ring.origins()) if packed else ()
    index_specs = [SMEM_SPEC] * len(index_in)
    block_rows = 2 * rows

    gain_columns = jnp.stack([self_gain, cross_gain, mlp_gain], axis=1)
    gain_columns = jnp.pad(gain_columns, ((0, 0), (0, PAIR_LANES - 3)))
    chains = ([self_query, gain_columns, self_out, cross_query], [self_key, self_value, cross_key, cross_value])
    splits = (half + PAIR_LANES, 2 * half)
    cut_all = 3 * half + PAIR_LANES
    packed_columns = (2 * hidden_half) * pieces + width * down_pieces
    widths_one = ([half, PAIR_LANES], [half, half])
    widths_two = ([half] * 2, [half] * 2)

    if packed:
        kinds = ["all" if w is gain_columns else "half" for w in chains[0] + chains[1]]
        mine, give = cut_shards(place, chains[0] + chains[1], kinds)
        blocks = jnp.concatenate(ring.in_order(mine, ring.swap(give)), axis=0)[None]
    else:
        sides = [
            jnp.concatenate(
                [w if w is gain_columns else column_halves([w])[i] for w in chains[0] + chains[1]],
                axis=1,
            )
            for i in range(2)
        ]
        blocks = ring.halves(*sides)[None]
    middle = own_patches // 2
    blocks = ring.far_step(blocks, 0)
    token_m = ring.across(tokens[0])
    patch_a = ring.across(memory[0, :middle])
    if packed:
        mine, give = cut_shards(place, [mlp_gate, mlp_up, cross_out], ["units"] * 2 + ["half"])
        blocks_mlp = join_rows(place, mine, ring.swap(give), mlp_down, [], half, piece)[0]
    else:
        gate_halves, up_halves = unit_halves(mlp_gate, units), unit_halves(mlp_up, units)
        rest = [
            jnp.concatenate([gate_halves[i], up_halves[i], column_halves([cross_out])[i]], axis=1)
            for i in range(2)
        ]
        gate_up = lax.all_gather(ring.halves(*rest), pairs, axis=0, tiled=True)
        down_three = lax.all_gather(mlp_down, pairs, axis=0, tiled=True)
        out_two = gate_up[:, 2 * hidden_half :]
    blocks, token_m, memory = together(blocks, token_m, memory)
    if packed:
        mlp_weights = lax.all_gather(after(blocks_mlp, blocks), pairs, axis=0, tiled=True)
        mlp_weights = mlp_weights.reshape(ring.blocks, piece, -1)
    patch_b = ring.across(memory[0, middle:])
    for step in range(1, len(ring.far)):
        blocks = ring.far_step(blocks, step)
    blocks, patch_a, token_m = together(blocks, patch_a, token_m)
    parts = [blocks[:, :, :cut_all], blocks[:, :, cut_all:]]
    token_g = ring.swap(token_m)
    last = len(ring.tails[0]) - 1
    for step in range(last):
        got = ring.near_step(parts, step)
        parts = [jnp.concatenate(pair, axis=0) for pair in zip(parts, got)]
    parts, token_g, patch_b = together(parts, token_g, patch_b)
    parts_one = [part[:, :, :split] for part, split in zip(parts, splits)]
    parts_two = [part[:, :, split:] for part, split in zip(parts, splits)]
    near_one = ring.near_step(parts_one, last)
    patch_m = jnp.concatenate([patch_a, patch_b], axis=1)
    patch_g = ring.swap(patch_m)
    near_one, parts_two, patch_g = together(near_one, parts_two, patch_g)
    near_two = ring.near_step(parts_two, last)
    near_one = (parts_one[0], near_one[0], parts_one[1], near_one[1])
    arrivals = ring.arrivals()

    token_chunk = math.gcd(256, own)
    patch_chunk = math.gcd(256, own_patches)

    def chunk_starts(span, chunk, side_first):
        groups = ring.group ^ jnp.arange(ring.groups, dtype=jnp.int32)
        sides = ring.half ^ jnp.arange(2, dtype=jnp.int32)
        inner = jnp.arange(span // chunk, dtype=jnp.int32) * chunk
        if side_first:
            starts = groups[None, :, None] * 2 * span + sides[:, None, None] * span
        else:
            starts = groups[:, None, None] * 2 * span + sides[None, :, None] * span
        return (starts + inner).reshape(-1)

    fixed = jnp.stack([ring.group * both, ring.half])
    info_one = jnp.concatenate([text_length, fixed, chunk_starts(own, token_chunk, False)])
    info_two = jnp.concatenate([patch_count, fixed, chunk_starts(own_patches, patch_chunk, True)])

    head_shapes = [low_shape(both, half), low_shape(keys, half), low_shape(keys, half)]
    query_outs = [full_shape(8, width), low_shape(keys, width), *head_shapes]
    projections = [low_shape(width, w) for w in widths_one[0] + widths_one[1]]
    cost = keys * width * half
    if packed:
        outs = run_kernel(
            functools.partial(query_kernel, True),
            query_outs + projections,
            cost,
            index_in,
            [*near_one, token_m, token_g],
        )
        gain_rows, normed_one, query_heads, key_heads, value_heads = outs[:5]
        query_one, gain_cols, key_one, value_one = outs[5:]
    else:
        query_one, gain_cols = to_whole(near_one[0], near_one[1], arrivals[0], widths_one[0])
        key_one, value_one = to_whole(near_one[2], near_one[3], arrivals[1], widths_one[1])
        gain_rows, normed_one, query_heads, key_heads, value_heads = run_kernel(
            functools.partial(query_kernel, False),
            query_outs,
            cost,
            [],
            [query_one, gain_cols, key_one, value_one, token_m, token_g],
        )
    near_one = None
    grad_g = ring.swap(after(output_grad[0], query_heads))
    context_one, lse_one = attention_forward(
        info_one, query_heads, key_heads, value_heads, True, token_chunk
    )
    context_one, near_b, grad_g = together(context_one, near_two[1], grad_g)
    context_one_g = ring.swap(context_one)
    patch_all = [part.reshape(-1, width) for part in (patch_m, patch_g)]
    memory_heads = [low_shape(patches, half)] * 2
    if packed:
        memory_keys, memory_values, key_two, value_two = run_kernel(
            functools.partial(memory_kernel, True),
            memory_heads + [low_shape(width, half)] * 2,
            patches * width * half,
            index_in[1:],
            [parts_two[1], near_b, *patch_all],
        )
    else:
        key_two, value_two = to_whole(parts_two[1], near_b, arrivals[1], widths_two[1])
        memory_keys, memory_values = run_kernel(
            functools.partial(memory_kernel, False),
            memory_heads,
            patches * width * half,
            [],
            [key_two, value_two, *patch_all],
        )
    near_a, memory_keys = together(near_two[0], memory_keys)
    out_one, query_two = to_whole(parts_two[0], near_a, arrivals[0], widths_two[0])
    out_one_g = ring.swap(out_one)
    hidden_one, normed_two, cross_heads = run_kernel(
        cross_query_kernel,
        [full_shape(both, width), low_shape(both, width), low_shape(both, half)],
        both * width * half,
        [place],
        [token_m[0], token_g[0], context_one, context_one_g, out_one, out_one_g, gain_rows, query_two],
    )
    context_two, lse_two = attention_forward(
        info_two, cross_heads, memory_keys, memory_values, False, patch_chunk
    )
    context_two_g = ring.swap(context_two)
    if packed:
        out_two = from_pieces(after(mlp_weights, context_two), packed_columns, pieces, half)
    out_two_g = ring.swap(out_two)

    if packed:
        hidden_two, part_low, down_keep, down_give, gain_three, mlp_terms = run_kernel(
            functools.partial(mlp_kernel, 512),
            [
                full_shape(both, width),
                low_shape(both, width),
                full_shape(own, width),
                low_shape(own, width),
                full_shape(width, PAIR_LANES),
                low_shape(ring.blocks, piece, packed_columns),
            ],
            2 * both * width * hidden_half,
            [place],
            [
                hidden_one,
                context_two,
                context_two_g,
                out_two,
                out_two_g,
                gain_rows,
                gain_cols,
                output_grad[0],
                grad_g,
            ],
            [
                pltpu.VMEM((ring.blocks, pieces, piece, hidden_half), LOW),
                pltpu.VMEM((ring.blocks, pieces, piece, hidden_half), LOW),
                pltpu.VMEM((ring.blocks, down_pieces, piece, width), LOW),
                pltpu.VMEM((both, width), LOW),
                pltpu.VMEM((width, both), LOW),
                pltpu.VMEM((both, width), LOW),
                pltpu.VMEM((both, width), F32),
                pltpu.VMEM((both, width), F32),
                pltpu.VMEM((width, PAIR_LANES), F32),
                pltpu.SemaphoreType.DMA((2 * pieces + down_pieces,)),
            ],
            [mlp_weights],
            late=True,
        )
        mlp_terms = mlp_terms.reshape(ring.blocks * piece, -1)
        mlp_sum = lax.psum_scatter(mlp_terms, pairs, scatter_dimension=0, tiled=True)
    else:
        joined = jnp.concatenate(ring.in_order(out_two, out_two_g), axis=1)
        swapped = jnp.concatenate([context_two_g[own:], context_two_g[:own]], axis=0)
        context = jnp.concatenate(ring.in_order(context_two, swapped), axis=1)
        hidden_two = hidden_one + dot_nn(context, joined)
        normed_three = (normalize(hidden_two)[0] * gain_rows[2:3]).astype(LOW)
        grad_low = jnp.concatenate([output_grad[0], grad_g], axis=0)
        gate_up = gate_up[:, : 2 * hidden_half]
        gate_three, up_three = gate_up[:, :hidden_half], gate_up[:, hidden_half:]
        active, slope = gelu_parts(dot_nn(normed_three, gate_three))
        up = dot_nn(normed_three, up_three)
        mixed = (active * up).astype(LOW)
        down_part = dot_nn(mixed, down_three)
        down_keep, down_give = down_part[:own], down_part[own:].astype(LOW)
        grad_mixed = dot_nt(grad_low, down_three)
        gate_low = (grad_mixed * up * slope).astype(LOW)
        up_low = (grad_mixed * active).astype(LOW)
        part_low = (dot_nt(gate_low, gate_three) + dot_nt(up_low, up_three)).astype(LOW)
        terms = jnp.concatenate(
            [dot_tn(normed_three, gate_low), dot_tn(normed_three, up_low)], axis=1
        )
        column = jnp.sum(terms * gate_up.astype(F32), axis=1, keepdims=True)
        gain_three = lane_column(column / gain_cols[:, 2:3].astype(F32), 2)
        gate_up = lax.psum_scatter(terms, pairs, scatter_dimension=0, tiled=True)
        mlp_ddown = lax.psum_scatter(
            dot_tn(mixed, grad_low), pairs, scatter_dimension=0, tiled=True
        )

    part_g = ring.swap(part_low)
    down_got = ring.swap(down_give)
    output = (hidden_two[:own] + down_keep + down_got.astype(F32)).astype(LOW)

    def branch(gain_at, hidden, mine, got, weight_m, weight_g, base):
        return run_kernel(
            functools.partial(branch_kernel, gain_at),
            [full_shape(both, width), low_shape(both, width), low_shape(both, half)],
            both * width * half,
            [place],
            [hidden, gain_rows, mine, got, weight_m, weight_g, *base],
        )

    dhidden_two, branch_two, dcontext_two = branch(
        2, hidden_two, part_low, part_g, out_two, out_two_g, [output_grad[0], grad_g]
    )
    dquery, dkey, dvalue = attention_backward(
        info_two,
        cross_heads,
        memory_keys,
        memory_values,
        context_two,
        dcontext_two,
        lse_two,
        False,
        patch_chunk,
    )
    (part_low,) = run_kernel(
        back_kernel, [low_shape(both, width)], both * width, [], [dquery, query_two]
    )
    part_g = ring.swap(part_low)

    count = ring.blocks // 2

    def grads(body, inputs, columns, gain_outs, cost):
        scratch = [pltpu.VMEM((width, c), LOW) for c in columns]
        acc = pltpu.VMEM((width, PAIR_LANES), F32)
        if packed:
            shapes = [low_shape(count, block_rows, c) for c in columns for _ in range(2)]
            outs = run_kernel(
                functools.partial(body, True),
                gain_outs + shapes,
                cost,
                [place, *index_out],
                inputs,
                scratch + [acc],
            )
            blocks = outs[len(gain_outs) :]
            return outs[: len(gain_outs)], blocks[0::2], blocks[1::2]
        wholes = [low_shape(width, c) for c in columns]
        outs = run_kernel(
            functools.partial(body, False), gain_outs + wholes, cost, [place], inputs, [acc]
        )
        return outs[: len(gain_outs)], *ring.halve_wholes(outs[len(gain_outs) :], block_rows)

    (gain_two,), cross_keep, cross_give = grads(
        cross_grads_kernel,
        [
            context_two,
            context_two_g,
            branch_two,
            normed_two,
            dquery,
            *patch_all,
            dkey,
            dvalue,
            query_two,
            gain_cols,
        ],
        (2 * half, 2 * half),
        [full_shape(width, PAIR_LANES)],
        (both + patches) * width * half,
    )
    patch_spans = [(side == 0, g) for side in range(2) for g in range(ring.groups)]
    patch_shape = (ring.groups, own_patches, width)
    memory_keep, memory_give = run_kernel(
        functools.partial(rows_back_kernel, patch_spans, False),
        [full_shape(*patch_shape), low_shape(*patch_shape)],
        patches * width,
        [],
        [dkey, dvalue, key_two, value_two],
    )
    memory_total = ring.pair_sum(memory_keep, memory_give)
    memory_sent = ring.group_terms(memory_total)
    cross_got = ring.near_sends(cross_give, len(ring.tails[0]) - 1)

    dhidden_one, branch_one, dcontext_one = branch(
        1, hidden_one, part_low, part_g, out_one, out_one_g, [dhidden_two]
    )
    dquery_one, dkey_one, dvalue_one = attention_backward(
        info_one,
        query_heads,
        key_heads,
        value_heads,
        context_one,
        dcontext_one,
        lse_one,
        True,
        token_chunk,
    )
    dquery_one, dkey_one, dvalue_one, memory_sent, cross_got = together(
        dquery_one, dkey_one, dvalue_one, memory_sent, cross_got
    )
    memory_grad = memory_sent
    cross_left, cross_give = ring.near_sums(cross_keep, cross_got)
    _, self_keep, self_give = grads(
        self_grads_kernel,
        [
            context_one,
            context_one_g,
            branch_one,
            normed_one,
            dquery_one,
            dkey_one,
            dvalue_one,
            query_one,
            key_one,
            value_one,
            gain_cols,
            gain_two,
            gain_three,
        ],
        (2 * half + PAIR_LANES, 2 * half),
        [],
        (both + keys) * width * half,
    )
    self_got = ring.near_sends(self_give, len(ring.tails[0]) - 1)
    for step in range(len(ring.far)):
        cross_left, cross_give = ring.far_sum(cross_left, cross_give, step)
    cross_sum = cross_left[0]
    self_left, self_give = ring.near_sums(self_keep, self_got)
    late = self_give
    for step in range(len(ring.far)):
        if packed and step == len(ring.far) - 1:
            self_give, mlp_sum = together(self_give, mlp_sum)
        self_left, self_give = ring.far_sum(self_left, self_give, step)
    if packed:
        mlp_sum = mlp_sum.astype(F32)
        take = lambda at, size: mlp_sum[:, at : at + size]
        gate_up = jnp.concatenate(
            [
                jnp.concatenate([take((m * pieces + j) * hidden_half, hidden_half) for m in range(2)], axis=1)
                for j in range(pieces)
            ],
            axis=0,
        )
        base = 2 * pieces * hidden_half
        mlp_ddown = jnp.concatenate(
            [take(base + j * width, width) for j in range(down_pieces)], axis=0
        )

    dquery_one, dkey_one, dvalue_one = after((dquery_one, dkey_one, dvalue_one), self_keep[0])
    token_spans = [(side == 0, g) for g in range(ring.groups) for side in range(2)]
    token_shape = (ring.groups, own, width)
    part_keep, part_give = run_kernel(
        functools.partial(rows_back_kernel, token_spans, True),
        [full_shape(*token_shape), low_shape(*token_shape)],
        keys * width,
        [],
        [dkey_one, dvalue_one, key_one, value_one, dquery_one, query_one],
    )
    dnormed_one = ring.group_terms(after(ring.pair_sum(part_keep, part_give), late))
    plain, inverse = normalize(tokens[0].astype(F32))
    input_grad = dhidden_one[:own] + norm_back(plain, inverse, gain_rows[0:1], dnormed_one)

    (gate_up,) = ring.finished(gate_up, 1)
    gate_columns = [gate_up[:, i * hidden_half : (i + 1) * hidden_half] for i in range(4)]
    mlp_dgate = unit_whole(gate_columns[0], gate_columns[2], units)
    mlp_dup = unit_whole(gate_columns[1], gate_columns[3], units)
    cross_dout, cross_dquery, cross_dkey, cross_dvalue = ring.finished(cross_sum, 4)
    self_left, mlp_dgate, mlp_dup, mlp_ddown = together(self_left, mlp_dgate, mlp_dup, mlp_ddown)
    self_sum = self_left[0]
    gain_at = 2 * half
    gain_block = self_sum[:, gain_at : gain_at + PAIR_LANES]
    gain_block = jnp.pad(gain_block, ((0, 0), (0, half - PAIR_LANES)))
    self_sum = jnp.concatenate(
        [self_sum[:, :gain_at], self_sum[:, gain_at + PAIR_LANES :], gain_block], axis=1
    )
    self_dquery, self_dout, self_dkey, self_dvalue, gain_terms = ring.finished(self_sum, 5)
    dgains = gain_terms[:, :3] + gain_terms[:, half : half + 3]

    return (
        output[None],
        input_grad[None],
        memory_grad[None],
        dgains[:, 0],
        self_dquery,
        self_dkey,
        self_dvalue,
        self_dout,
        dgains[:, 1],
        cross_dquery,
        cross_dkey,
        cross_dvalue,
        cross_dout,
        dgains[:, 2],
        mlp_dgate,
        mlp_dup,
        mlp_ddown,
    )


def solution(mesh):
    charts, heads = mesh.devices.shape
    inner = Mesh(mesh.devices.reshape(charts, heads // 2, 2), ("dp", "hx", "hc"))
    every = ("dp", "hx", "hc")
    rows = P(every, None)
    vector = P(every)
    grid = P("dp", ("hx", "hc"), None)
    in_specs = (grid, grid, P("dp"), P("dp"))
    in_specs += (vector, rows, rows, rows, rows) * 2
    in_specs += (vector, rows, rows, rows, grid)
    out_specs = (grid, grid, grid)
    out_specs += (vector, rows, rows, rows, rows) * 2
    out_specs += (vector, rows, rows, rows)
    return jax.shard_map(
        on_device, mesh=inner, in_specs=in_specs, out_specs=out_specs, check_vma=False
    )
```

```python
import functools
import math

import jax
import jax.numpy as jnp
from jax import lax
from jax.experimental import pallas as pl
from jax.experimental.pallas import tpu as pltpu
from jax.sharding import Mesh
from jax.sharding import PartitionSpec as P

HEAD_DIM = 64
PAIR_LANES = 128
NEG_FILL = -1e30
EPS = 1e-06
F32 = jnp.float32
LOW = jnp.bfloat16


NT = (((1,), (1,)), ((), ()))
TN = (((0,), (0,)), ((), ()))


def dot_nt(left, right):
    return lax.dot_general(left, right, NT, preferred_element_type=F32)


def dot_tn(left, right):
    return lax.dot_general(left, right, TN, preferred_element_type=F32)


def dot_nn(left, right):
    return jnp.dot(left, right, preferred_element_type=F32)


FIXED = 3
SPANS = 4


def query_limits(info, queries, causal):
    last = info[0] - 1
    if not causal:
        return jnp.full((1, queries), last, jnp.int32), last
    lanes = lax.broadcasted_iota(jnp.int32, (1, queries), 1)
    span = queries // 2
    swapped = jnp.where(lanes < span, lanes + info[2] * span, lanes - info[2] * span)
    return jnp.minimum(info[1] + swapped, last), jnp.minimum(info[1] + queries - 1, last)


def key_places(info, chunk, span, queries, j):
    parts = chunk // span
    starts = [info[FIXED + j * parts + i] for i in range(parts)]
    inner = lax.broadcasted_iota(jnp.int32, (span, queries), 0)
    first = functools.reduce(jnp.minimum, starts)
    return jnp.concatenate([start + inner for start in starts], axis=0), first


def first_place(info, chunk, span, j):
    parts = chunk // span
    return functools.reduce(jnp.minimum, [info[FIXED + j * parts + i] for i in range(parts)])


def head_lanes(head):
    lanes = lax.broadcasted_iota(jnp.int32, (1, PAIR_LANES), 1)
    return (lanes // HEAD_DIM) == head


def fold(values, op):
    rows, columns = values.shape
    return op(values.reshape(rows // 8, 8, columns), axis=0)


def forward_kernel(causal, chunk, span, info, q_ref, k_ref, v_ref, c_ref, lse_ref, s_ref, m_ref, l_ref, a_ref):
    queries = q_ref.shape[0]
    chunks = k_ref.shape[0] // chunk
    scaling = 1.0 / math.sqrt(HEAD_DIM)
    limit, latest = query_limits(info, queries, causal)
    q_all = q_ref[...] * jnp.asarray(scaling, q_ref.dtype)
    q_heads = [jnp.where(head_lanes(h), q_all, jnp.zeros_like(q_all)) for h in range(2)]
    m_ref[...] = jnp.full(m_ref.shape, NEG_FILL, F32)
    l_ref[...] = jnp.zeros(l_ref.shape, F32)
    a_ref[...] = jnp.zeros(a_ref.shape, F32)

    @pl.loop(0, chunks)
    def _(j):
        @pl.when(first_place(info, chunk, span, j) <= latest)
        def _():
            rows = pl.ds(pl.multiple_of(j * chunk, chunk), chunk)
            keys = k_ref[rows, :]
            place, _ = key_places(info, chunk, span, queries, j)
            allowed = place <= limit
            for h in range(2):
                scores = jnp.where(allowed, dot_nt(keys, q_heads[h]), NEG_FILL)
                s_ref[h, rows, :] = scores
                m_ref[h] = jnp.maximum(m_ref[h], fold(scores, jnp.max))

    highest = [jnp.max(m_ref[h], axis=0, keepdims=True) for h in range(2)]

    @pl.loop(0, chunks)
    def _(j):
        @pl.when(first_place(info, chunk, span, j) <= latest)
        def _():
            rows = pl.ds(pl.multiple_of(j * chunk, chunk), chunk)
            values = v_ref[rows, :]
            for h in range(2):
                weight = jnp.exp(s_ref[h, rows, :] - highest[h])
                l_ref[h] = l_ref[h] + fold(weight, jnp.sum)
                a_ref[h] = a_ref[h] + dot_tn(values, weight.astype(LOW))

    parts = []
    for h in range(2):
        total = jnp.sum(l_ref[h], axis=0, keepdims=True)
        lse_ref[0, pl.ds(h, 1), :] = highest[h] + jnp.log(total)
        parts.append(a_ref[h, pl.ds(h * HEAD_DIM, HEAD_DIM), :] / total)
    c_ref[...] = jnp.concatenate(parts, axis=0).T.astype(c_ref.dtype)


def backward_kernel(causal, chunk, span, info, q_ref, k_ref, v_ref, c_ref, g_ref, lse_ref, dq_ref, dk_ref, dv_ref, a_ref):
    queries = q_ref.shape[0]
    chunks = k_ref.shape[0] // chunk
    scaling = 1.0 / math.sqrt(HEAD_DIM)
    limit, latest = query_limits(info, queries, causal)
    q_all = q_ref[...] * jnp.asarray(scaling, q_ref.dtype)
    g_all = g_ref[...]
    q_heads = [jnp.where(head_lanes(h), q_all, jnp.zeros_like(q_all)) for h in range(2)]
    g_heads = [jnp.where(head_lanes(h), g_all, jnp.zeros_like(g_all)) for h in range(2)]
    product = (c_ref[...].astype(F32) * g_all.astype(F32)).T
    centres = [
        jnp.sum(product[h * HEAD_DIM : (h + 1) * HEAD_DIM], axis=0, keepdims=True) for h in range(2)
    ]
    logs = [lse_ref[0, pl.ds(h, 1), :] for h in range(2)]
    a_ref[...] = jnp.zeros(a_ref.shape, F32)

    @pl.loop(0, chunks)
    def _(j):
        start = first_place(info, chunk, span, j)
        rows = pl.ds(pl.multiple_of(j * chunk, chunk), chunk)

        @pl.when(start <= latest)
        def _():
            keys = k_ref[rows, :]
            values = v_ref[rows, :]
            place, _ = key_places(info, chunk, span, queries, j)
            allowed = place <= limit
            dk = jnp.zeros((chunk, PAIR_LANES), F32)
            dv = jnp.zeros((chunk, PAIR_LANES), F32)
            for h in range(2):
                scores = jnp.where(allowed, dot_nt(keys, q_heads[h]), NEG_FILL)
                prob = jnp.exp(scores - logs[h])
                dprob = dot_nt(values, g_heads[h])
                dv = dv + dot_nn(prob.astype(LOW), g_heads[h])
                dscore = (prob * (dprob - centres[h])).astype(LOW)
                dk = dk + dot_nn(dscore, q_heads[h])
                a_ref[h] = a_ref[h] + dot_tn(keys, dscore)
            dk_ref[rows, :] = dk.astype(dk_ref.dtype)
            dv_ref[rows, :] = dv.astype(dv_ref.dtype)

        @pl.when(start > latest)
        def _():
            dk_ref[rows, :] = jnp.zeros((chunk, PAIR_LANES), dk_ref.dtype)
            dv_ref[rows, :] = jnp.zeros((chunk, PAIR_LANES), dv_ref.dtype)

    parts = [a_ref[h, pl.ds(h * HEAD_DIM, HEAD_DIM), :] for h in range(2)]
    dq_ref[...] = (jnp.concatenate(parts, axis=0).T * scaling).astype(dq_ref.dtype)


def lane_spec(rows):
    return pl.BlockSpec((rows, PAIR_LANES), lambda i, info: (0, i))


def stat_spec(queries):
    return pl.BlockSpec((1, 2, queries), lambda i, info: (i, 0, 0))


def attention_forward(info, queries, keys, values, causal, span):
    chunk = math.gcd(SPANS * span, keys.shape[0])
    rows, features = queries.shape
    key_rows = keys.shape[0]
    pairs = features // PAIR_LANES
    return pl.pallas_call(
        functools.partial(forward_kernel, causal, chunk, span),
        out_shape=(
            jax.ShapeDtypeStruct((rows, features), LOW),
            jax.ShapeDtypeStruct((pairs, 2, rows), F32),
        ),
        grid_spec=pltpu.PrefetchScalarGridSpec(
            num_scalar_prefetch=1,
            grid=(pairs,),
            in_specs=[lane_spec(rows), lane_spec(key_rows), lane_spec(key_rows)],
            out_specs=[lane_spec(rows), stat_spec(rows)],
            scratch_shapes=[
                pltpu.VMEM((2, key_rows, rows), F32),
                pltpu.VMEM((2, 8, rows), F32),
                pltpu.VMEM((2, 8, rows), F32),
                pltpu.VMEM((2, PAIR_LANES, rows), F32),
            ],
        ),
        compiler_params=pltpu.CompilerParams(vmem_limit_bytes=VMEM_LIMIT),
        cost_estimate=pl.CostEstimate(flops=rows, transcendentals=0, bytes_accessed=0),
    )(info, queries, keys, values)


def attention_backward(info, queries, keys, values, context, grads, lse, causal, span):
    chunk = math.gcd(SPANS * span, keys.shape[0])
    rows, features = queries.shape
    key_rows = keys.shape[0]
    pairs = features // PAIR_LANES
    return pl.pallas_call(
        functools.partial(backward_kernel, causal, chunk, span),
        out_shape=(
            jax.ShapeDtypeStruct((rows, features), LOW),
            jax.ShapeDtypeStruct((key_rows, features), LOW),
            jax.ShapeDtypeStruct((key_rows, features), LOW),
        ),
        grid_spec=pltpu.PrefetchScalarGridSpec(
            num_scalar_prefetch=1,
            grid=(pairs,),
            in_specs=[
                lane_spec(rows),
                lane_spec(key_rows),
                lane_spec(key_rows),
                lane_spec(rows),
                lane_spec(rows),
                stat_spec(rows),
            ],
            out_specs=[lane_spec(rows), lane_spec(key_rows), lane_spec(key_rows)],
            scratch_shapes=[pltpu.VMEM((2, PAIR_LANES, rows), F32)],
        ),
        compiler_params=pltpu.CompilerParams(vmem_limit_bytes=VMEM_LIMIT),
        cost_estimate=pl.CostEstimate(flops=rows, transcendentals=0, bytes_accessed=0),
    )(info, queries, keys, values, context, grads, lse)


SMEM_SPEC = pl.BlockSpec(memory_space=pltpu.SMEM)


def vmem_specs(number):
    return [pl.BlockSpec(memory_space=pltpu.VMEM)] * number


def cuts_of(widths):
    return [sum(widths[:i]) for i in range(len(widths))]


def place_blocks(index, first, later, targets):
    half, rows, _ = first.shape
    cuts = cuts_of([target.shape[1] for target in targets])

    @pl.loop(0, 2 * half)
    def _(step):
        at = index[step]
        place = pl.ds(pl.multiple_of(step * rows, rows), rows)

        def put(source, block):
            for cut, target in zip(cuts, targets):
                target[place, :] = source[block, :, pl.ds(cut, target.shape[1])]

        @pl.when(at < half)
        def _():
            put(first, at)

        @pl.when(at >= half)
        def _():
            put(later, at - half)


def send_order(index, whole, keep, give):
    half, rows, _ = keep.shape

    @pl.loop(0, half)
    def _(step):
        for side, target in enumerate((keep, give)):
            at = pl.ds(pl.multiple_of(index[step + side * half] * rows, rows), rows)
            target[step] = whole[at, :]


def whole_kernel(index, first, later, *targets):
    place_blocks(index, first, later, targets)


def to_whole(first, later, index, widths):
    half, rows, columns = first.shape
    count = 2 * half
    if rows % 16:
        blocks = jnp.concatenate([first, later], axis=0)
        whole = jnp.take(blocks, index, axis=0).reshape(count * rows, columns)
        return [whole[:, cut : cut + width] for cut, width in zip(cuts_of(widths), widths)]
    return run_kernel(
        whole_kernel,
        [low_shape(count * rows, width) for width in widths],
        count * rows * columns,
        [index],
        [first, later],
    )


class Stage:
    def __init__(self, loads, stores):
        self.loads, self.stores = loads, stores
        self.waited, self.sent = set(), set()

    def need(self, *numbers):
        for i in numbers or range(len(self.loads)):
            if i not in self.waited:
                self.waited.add(i)
                self.loads[i].wait()

    def done(self, *numbers):
        for i in numbers or range(len(self.stores)):
            if i not in self.sent:
                self.sent.add(i)
                self.stores[i].start()


def staged_kernel(body, late, sizes, *refs):
    parts, at = [], 0
    for size in sizes:
        parts.append(refs[at : at + size])
        at += size
    tables, arrays, streamed, outs, scratch, held_in, held_out, (in_sems, out_sems) = parts
    stage = Stage(
        [pltpu.make_async_copy(a, b, in_sems.at[i]) for i, (a, b) in enumerate(zip(arrays, held_in))],
        [pltpu.make_async_copy(a, b, out_sems.at[i]) for i, (a, b) in enumerate(zip(held_out, outs))],
    )
    for load in stage.loads:
        load.start()
    if late:
        body(stage, *tables, *held_in, *streamed, *held_out, *scratch)
    else:
        stage.need()
        body(*tables, *held_in, *streamed, *held_out, *scratch)
    stage.need()
    stage.done()
    for store in stage.stores:
        store.wait()


HBM_SPEC = pl.BlockSpec(memory_space=pltpu.HBM)


def run_kernel(body, out_shape, cost, tables, arrays, scratch=(), streamed=(), late=False):
    sizes = (len(tables), len(arrays), len(streamed), len(out_shape), len(scratch))
    sizes += (len(arrays), len(out_shape), 2)
    held = [pltpu.VMEM(x.shape, x.dtype) for x in [*arrays, *out_shape]]
    sems = [pltpu.SemaphoreType.DMA((len(arrays),)), pltpu.SemaphoreType.DMA((len(out_shape),))]
    return pl.pallas_call(
        functools.partial(staged_kernel, body, late, sizes),
        out_shape=out_shape,
        in_specs=[SMEM_SPEC] * len(tables) + [HBM_SPEC] * (len(arrays) + len(streamed)),
        out_specs=[HBM_SPEC] * len(out_shape),
        scratch_shapes=list(scratch) + held + sems,
        compiler_params=pltpu.CompilerParams(vmem_limit_bytes=VMEM_LIMIT),
        cost_estimate=pl.CostEstimate(flops=cost // 1000, transcendentals=0, bytes_accessed=0),
    )(*tables, *arrays, *streamed)


VMEM_LIMIT = 56 << 20


def low_shape(*shape):
    return jax.ShapeDtypeStruct(shape, LOW)


def full_shape(*shape):
    return jax.ShapeDtypeStruct(shape, F32)


def unit_tile(source, at, second):
    lanes = 2 * HEAD_DIM
    start = 2 * at * lanes + (HEAD_DIM if second else 0)
    return jnp.concatenate(
        [source[:, pl.ds(start, HEAD_DIM)], source[:, pl.ds(start + lanes, HEAD_DIM)]], axis=1
    )


def shards_kernel(kinds, place, *refs):
    sources, targets = refs[:-2], refs[-2:]

    def write(target, second):
        cut = 0
        for kind, source in zip(kinds, sources):
            columns = source.shape[1]
            if kind == "all":
                target[:, pl.ds(cut, columns)] = source[...]
                cut += columns
                continue
            if kind == "half":
                start = columns // 2 if second else 0
                target[:, pl.ds(cut, columns // 2)] = source[:, pl.ds(start, columns // 2)]
            else:
                for tile in range(columns // 256):
                    target[:, pl.ds(cut + 128 * tile, 128)] = unit_tile(source, tile, second)
            cut += columns // 2

    @pl.when(place[0] == 0)
    def _():
        write(targets[0], False)
        write(targets[1], True)

    @pl.when(place[0] != 0)
    def _():
        write(targets[0], True)
        write(targets[1], False)


def rows_kernel(widths, piece, place, mine, other, down, *targets):
    *widths, matrices, extra = widths
    rows = mine.shape[0]

    def write(upper, lower):
        cut = 0
        for target, width in zip(targets[:-1], widths):
            target[0, pl.ds(0, rows), :] = upper[:, pl.ds(cut, width)]
            target[0, pl.ds(rows, rows), :] = lower[:, pl.ds(cut, width)]
            cut += width
        packed = targets[-1]
        columns = (mine.shape[1] - cut - extra) // matrices
        step = 8
        base = matrices * (2 * rows // piece) * columns
        last = base + down.shape[1] * (down.shape[0] // piece)
        for start in range(0, 2 * rows, step):
            source = upper if start < rows else lower
            number, inner = start // piece, start % piece
            for matrix in range(matrices):
                place_at = (matrix * (2 * rows // piece) + number) * columns
                packed[pl.ds(inner, step), pl.ds(place_at, columns)] = source[
                    pl.ds(start % rows, step), pl.ds(cut + matrix * columns, columns)
                ]
            packed[pl.ds(inner, step), pl.ds(last + number * extra, extra)] = source[
                pl.ds(start % rows, step), pl.ds(cut + matrices * columns, extra)
            ]
        width = down.shape[1]
        for number in range(down.shape[0] // piece):
            packed[:, pl.ds(base + number * width, width)] = down[pl.ds(number * piece, piece), :]

    @pl.when(place[0] == 0)
    def _():
        write(mine, other)

    @pl.when(place[0] != 0)
    def _():
        write(other, mine)


def cut_shards(place, shards, kinds):
    rows = shards[0].shape[0]
    columns = sum(w.shape[1] if k == "all" else w.shape[1] // 2 for w, k in zip(shards, kinds))
    return run_kernel(
        functools.partial(shards_kernel, kinds), [low_shape(rows, columns)] * 2, rows * columns, [place], shards
    )


def join_rows(place, mine, other, down, widths, extra, piece):
    rows = 2 * mine.shape[0]
    rest = mine.shape[1] - sum(widths)
    packed = rest * (rows // piece) + down.shape[1] * (down.shape[0] // piece)
    return run_kernel(
        functools.partial(rows_kernel, [*widths, 2, extra], piece),
        [low_shape(1, rows, width) for width in widths] + [low_shape(piece, packed)],
        rows * rest,
        [place],
        [mine, other, down],
    )


def pieces_kernel(cut, source, target, held, sem):
    blocks, pieces, piece, columns = held.shape
    copies = [
        pltpu.make_async_copy(
            source.at[:, :, pl.ds(cut + i * columns, columns)], held.at[:, i], sem.at[i]
        )
        for i in range(pieces)
    ]
    for copy in copies:
        copy.start()
    for copy in copies:
        copy.wait()
    target[...] = held[...].reshape(target.shape)


def from_pieces(packed, cut, pieces, columns):
    blocks, piece, _ = packed.shape
    return pl.pallas_call(
        functools.partial(pieces_kernel, cut),
        out_shape=low_shape(blocks * pieces * piece, columns),
        in_specs=[HBM_SPEC],
        out_specs=pl.BlockSpec(memory_space=pltpu.VMEM),
        scratch_shapes=[
            pltpu.VMEM((blocks, pieces, piece, columns), LOW),
            pltpu.SemaphoreType.DMA((pieces,)),
        ],
        cost_estimate=pl.CostEstimate(flops=1000, transcendentals=0, bytes_accessed=0),
    )(packed)


def normalize(values):
    inverse = lax.rsqrt(jnp.mean(values * values, axis=-1, keepdims=True) + EPS)
    return values * inverse, inverse


def norm_back(normed, inverse, gain, grads):
    scaled = grads * gain
    return inverse * (scaled - normed * jnp.mean(scaled * normed, axis=-1, keepdims=True))


def gelu_parts(gate):
    factor = math.sqrt(2.0 / math.pi)
    inner = jnp.tanh(factor * (gate + 0.044715 * gate * gate * gate))
    value = 0.5 * gate * (1.0 + inner)
    slope = 0.5 * (1.0 + inner) + 0.5 * gate * (1.0 - inner * inner) * factor * (
        1.0 + 3.0 * 0.044715 * gate * gate
    )
    return value, slope


def head_slices(place, half):
    mine = pl.ds(pl.multiple_of(place[0] * half, half), half)
    other = pl.ds(pl.multiple_of((1 - place[0]) * half, half), half)
    return mine, other


def query_kernel(packed, stage, *refs):
    if packed:
        index_a, index_b, first_a, later_a, first_b, later_b, token_m, token_g = refs[:8]
        rows_ref, normed_ref, q_ref, k_ref, v_ref, wq, gain_cols, wkv = refs[8:]
        stage.need(0, 1)
        place_blocks(index_a, first_a, later_a, [wq, gain_cols])
        stage.done(5, 6)
        stage.need(2, 3)
        place_blocks(index_b, first_b, later_b, [wkv])
        stage.done(7)
    else:
        wq, gain_cols, wkv, token_m, token_g = refs[:5]
        rows_ref, normed_ref, q_ref, k_ref, v_ref = refs[5:]
    stage.need()
    gain_rows = gain_cols[...].astype(F32).T[0:8]
    rows_ref[...] = gain_rows
    groups, own, _ = token_m.shape
    half = q_ref.shape[1]
    for group in range(groups):
        for side, source in enumerate((token_m, token_g)):
            plain, _ = normalize(source[group].astype(F32))
            at = pl.ds((2 * group + side) * own, own)
            normed_ref[at, :] = (plain * gain_rows[0:1]).astype(LOW)
    stage.done(0, 1)
    q_ref[...] = dot_nn(normed_ref[pl.ds(0, 2 * own), :], wq[...]).astype(LOW)
    stage.done(2)
    value = dot_nn(normed_ref[...], wkv[...]).astype(LOW)
    k_ref[...] = value[:, :half]
    v_ref[...] = value[:, half:]


def add_context(place, target, base, c_m, c_g, w_m, w_g):
    rows, half = c_m.shape
    own = rows // 2
    mine, other = head_slices(place, half)
    for side in range(2):
        at = pl.ds(side * own, own)
        left = c_m[at, :]
        right = c_g[pl.ds((1 - side) * own, own), :]
        for weight, columns in ((w_m, mine), (w_g, other)):
            value = dot_nn(left, weight[mine, :]) + dot_nn(right, weight[other, :])
            target[at, columns] = base(side, columns) + value


def cross_query_kernel(stage, place, token_m, token_g, c_m, c_g, w_m, w_g, rows_ref, wq, h_ref, normed_ref, q_ref):
    tokens = (token_m, token_g)
    base = lambda side, columns: tokens[side][:, columns].astype(F32)
    stage.need(*range(7))
    add_context(place, h_ref, base, c_m, c_g, w_m, w_g)
    stage.done(0)
    plain, _ = normalize(h_ref[...])
    normed_ref[...] = (plain * rows_ref[1:2, :]).astype(LOW)
    stage.done(1)
    stage.need()
    q_ref[...] = dot_nn(normed_ref[...], wq[...]).astype(LOW)


def memory_kernel(packed, stage, *refs):
    if packed:
        index, first, later, patch_m, patch_g, k_ref, v_ref, wkv = refs
        stage.need(0, 1)
        place_blocks(index, first, later, [wkv])
        stage.done(2)
    else:
        wkv, patch_m, patch_g, k_ref, v_ref = refs
    stage.need()
    count = patch_m.shape[0]
    half = k_ref.shape[1]
    for side, source in enumerate((patch_m, patch_g)):
        value = dot_nn(source[...], wkv[...]).astype(LOW)
        k_ref[pl.ds(side * count, count), :] = value[:, :half]
        v_ref[pl.ds(side * count, count), :] = value[:, half:]


def lane_column(column, lane):
    lanes = lax.broadcasted_iota(jnp.int32, (1, PAIR_LANES), 1)
    return jnp.where(lanes == lane, column, 0.0)


def mlp_kernel(
    chunk,
    stage,
    place,
    h_in,
    c_m,
    c_g,
    out_m,
    out_g,
    rows_ref,
    cols_ref,
    g_m,
    g_g,
    w_ref,
    h_ref,
    part_ref,
    keep_ref,
    give_ref,
    gain_ref,
    grad_ref,
    gate_w,
    up_w,
    down_w,
    a_ref,
    t_ref,
    g_ref,
    p_acc,
    d_acc,
    r_acc,
    sems,
):
    blocks, pieces, piece, units = gate_w.shape
    down_pieces, width = down_w.shape[1], down_w.shape[3]
    total = blocks * pieces * piece
    own = g_m.shape[0]
    moves = []
    for number in range(pieces):
        moves.append((w_ref.at[:, :, pl.ds(number * units, units)], gate_w.at[:, number]))
    for number in range(pieces):
        moves.append((w_ref.at[:, :, pl.ds((pieces + number) * units, units)], up_w.at[:, number]))
    base = 2 * pieces * units
    for number in range(down_pieces):
        moves.append((w_ref.at[:, :, pl.ds(base + number * width, width)], down_w.at[:, number]))
    copies = [pltpu.make_async_copy(a, b, sems.at[i]) for i, (a, b) in enumerate(moves)]
    for copy in copies:
        copy.start()
    stage.need(*range(6))
    add_context(
        place, h_ref, lambda side, columns: h_in[pl.ds(side * own, own), columns], c_m, c_g, out_m, out_g
    )
    stage.done(0)
    plain, _ = normalize(h_ref[...])
    a_ref[...] = (plain * rows_ref[2:3, :]).astype(LOW)
    t_ref[...] = a_ref[...].T
    stage.need()
    g_ref[pl.ds(0, own), :] = g_m[...]
    g_ref[pl.ds(own, own), :] = g_g[...]
    p_acc[...] = jnp.zeros(p_acc.shape, F32)
    d_acc[...] = jnp.zeros(d_acc.shape, F32)
    r_acc[...] = jnp.zeros(r_acc.shape, F32)
    for copy in copies:
        copy.wait()

    per_block = down_pieces * piece
    step_blocks = chunk // per_block

    @pl.loop(0, units // chunk)
    def _(step):
        start = pl.multiple_of(step * chunk, chunk)
        a_in = a_ref[...]
        g_in = g_ref[...]
        columns = pl.ds(start, chunk)
        gate_part = gate_w[:, :, :, columns].reshape(total, chunk)
        up_part = up_w[:, :, :, columns].reshape(total, chunk)
        down_at = pl.ds(step * step_blocks, step_blocks)
        down_part = down_w[down_at].reshape(chunk, width)
        gate = dot_nn(a_in, gate_part)
        up = dot_nn(a_in, up_part)
        active, slope = gelu_parts(gate)
        mixed = (active * up).astype(LOW)
        grad = dot_nt(g_in, down_part)
        gate_low = (grad * up * slope).astype(LOW)
        up_low = (grad * active).astype(LOW)
        d_acc[...] += dot_nn(mixed, down_part)
        p_acc[...] += dot_nt(gate_low, gate_part) + dot_nt(up_low, up_part)
        dgate = dot_nn(t_ref[...], gate_low)
        dup = dot_nn(t_ref[...], up_low)
        gain_terms = dgate * gate_part.astype(F32) + dup * up_part.astype(F32)
        for lane in range(0, chunk, PAIR_LANES):
            r_acc[...] += gain_terms[:, lane : lane + PAIR_LANES]
        dgate = dgate.astype(LOW).reshape(blocks, pieces, piece, chunk)
        dup = dup.astype(LOW).reshape(blocks, pieces, piece, chunk)
        for number in range(pieces):
            gate_at = pl.multiple_of(number * units + start, chunk)
            up_at = pl.multiple_of((pieces + number) * units + start, chunk)
            grad_ref[:, :, pl.ds(gate_at, chunk)] = dgate[:, number]
            grad_ref[:, :, pl.ds(up_at, chunk)] = dup[:, number]
        ddown = dot_tn(mixed, g_in).astype(LOW).reshape(step_blocks, down_pieces, piece, width)
        for number in range(down_pieces):
            grad_ref[down_at, :, pl.ds(base + number * width, width)] = ddown[:, number]

    stage.done(5)
    part_ref[...] = p_acc[...].astype(LOW)
    stage.done(1)
    keep_ref[...] = d_acc[pl.ds(0, own), :]
    give_ref[...] = d_acc[pl.ds(own, own), :].astype(LOW)
    summed = jnp.sum(r_acc[...], axis=1, keepdims=True)
    gain_ref[...] = lane_column(summed / cols_ref[:, 2:3].astype(F32), 2)


def branch_kernel(gain_at, stage, place, *refs):
    h_ref, rows_ref, part_m, part_g, w_m, w_g = refs[:6]
    base, (d_ref, low_ref, c_ref) = refs[6:-3], refs[-3:]
    rows = h_ref.shape[0]
    own = rows // 2
    half = w_m.shape[1]
    mine, other = head_slices(place, half)
    stage.need(0, 1, 2, 3, *range(6, 6 + len(base)))
    for side in range(2):
        at = pl.ds(side * own, own)
        plain, inverse = normalize(h_ref[at, :])
        got = part_g[pl.ds((1 - side) * own, own), :]
        grads = part_m[at, :].astype(F32) + got.astype(F32)
        value = norm_back(plain, inverse, rows_ref[gain_at : gain_at + 1, :], grads)
        before = base[side][...].astype(F32) if len(base) == 2 else base[0][at, :]
        d_ref[at, :] = before + value
    stage.done(0)
    low_ref[...] = d_ref[...].astype(LOW)
    stage.done(1)
    stage.need()
    value = dot_nt(low_ref[:, mine], w_m[mine, :]) + dot_nt(low_ref[:, other], w_g[mine, :])
    c_ref[...] = value.astype(LOW)


def dot_rows(left, right):
    columns = left.shape[1]
    step = math.gcd(columns, 256)
    return [(i, dot_tn(left[:, i : i + step], right)) for i in range(0, columns, step)]


def out_grad(place, whole, cut, c_m, c_g, branch):
    rows, half = c_m.shape
    own = rows // 2
    mine, other = head_slices(place, half)
    grads = branch[:, mine]
    columns = pl.ds(cut, half)
    whole[mine, columns] = dot_tn(c_m[...], grads).astype(LOW)
    value = dot_tn(c_g[pl.ds(own, own), :], grads[:own]) + dot_tn(c_g[pl.ds(0, own), :], grads[own:])
    whole[other, columns] = value.astype(LOW)


def weight_grads(targets, lefts, rights, gain_acc=None):
    features = lefts[0].shape[1]
    step = math.gcd(features, 256)

    for number in range(features // step):
        at = pl.ds(number * step, step)
        turned = [left[:, at].T for left in lefts]
        for (whole, cut, weight), terms in zip(targets, rights):
            width = terms[0].shape[1]
            value = sum(dot_nn(left, right[...]) for left, right in zip(turned, terms))
            whole[at, pl.ds(cut, width)] = value.astype(LOW)
            if weight is not None:
                products = value * weight[at, :].astype(F32)
                gain_acc[at, :] += sum(
                    products[:, lane : lane + PAIR_LANES] for lane in range(0, width, PAIR_LANES)
                )


def cross_grads_kernel(packed, stage, place, *refs):
    index, refs = (refs[:2], refs[2:]) if packed else ((), refs)
    c_m, c_g, branch, normed, dq, patch_m, patch_g, dk, dv, wq, cols_ref = refs[:11]
    one_m, one_g, branch_one = refs[11:14]
    gain_ref, *outs, whole_a, whole_b, gain_acc = refs[14:]
    half = dq.shape[1]
    stage.need(0, 1, 2, 3, 4, 9, 10, 11, 12, 13)
    out_grad(place, whole_a, 2 * half, one_m, one_g, branch_one)
    count = patch_m.shape[0]
    gain_acc[...] = jnp.zeros(gain_acc.shape, F32)
    out_grad(place, whole_a, 0, c_m, c_g, branch)
    weight_grads([(whole_a, half, wq)], [normed], [[dq]], gain_acc)
    if packed:
        send_order(index[0], whole_a, outs[0], outs[1])
        stage.done(1, 2)
    summed = jnp.sum(gain_acc[...], axis=1, keepdims=True)
    gain_ref[...] = lane_column(summed / cols_ref[:, 1:2].astype(F32), 1)
    stage.need()
    halves = [[g.at[pl.ds(i * count, count), :] for i in range(2)] for g in (dk, dv)]
    weight_grads(
        [(whole_b, 0, None), (whole_b, half, None)], [patch_m, patch_g], halves
    )
    if packed:
        send_order(index[1], whole_b, outs[2], outs[3])


def self_grads_kernel(packed, stage, place, *refs):
    index, refs = (refs[:2], refs[2:]) if packed else ((), refs)
    normed, dq, dk, dv, wq, wkv, cols_ref, gain_two, gain_three = refs[:9]
    *outs, whole_a, whole_b, gain_acc = refs[9:]
    rows, half = dq.shape
    gain_acc[...] = jnp.zeros(gain_acc.shape, F32)
    stage.need(0, 3, 5)
    weight_grads([(whole_b, 0, wkv.at[:, pl.ds(half, half)])], [normed], [[dv]], gain_acc)
    stage.need(2)
    weight_grads([(whole_b, half, wkv.at[:, pl.ds(0, half)])], [normed], [[dk]], gain_acc)
    if packed:
        send_order(index[1], whole_b, outs[2], outs[3])
        stage.done(2, 3)
    stage.need()
    weight_grads([(whole_a, 0, wq)], [normed.at[pl.ds(0, rows), :]], [[dq]], gain_acc)
    summed = jnp.sum(gain_acc[...], axis=1, keepdims=True)
    gains = lane_column(summed / cols_ref[:, 0:1].astype(F32), 0) + gain_two[...] + gain_three[...]
    whole_a[:, pl.ds(half, PAIR_LANES)] = gains.astype(LOW)
    if packed:
        send_order(index[0], whole_a, outs[0], outs[1])


def back_kernel(grads, weight, out):
    out[...] = dot_nt(grads[...], weight[...]).astype(LOW)


def rows_back_kernel(spans, with_query, *refs):
    dk, dv, wkv = refs[:3]
    queries = refs[3:5] if with_query else None
    half = dk.shape[1]
    wk, wv = wkv.at[:, pl.ds(0, half)], wkv.at[:, pl.ds(half, half)]
    keep, give = refs[-2:]
    rows = dk.shape[0] // len(spans)
    for number, (mine, place) in enumerate(spans):
        at = pl.ds(number * rows, rows)
        value = dot_nt(dk[at, :], wk[...]) + dot_nt(dv[at, :], wv[...])
        if queries and number < 2:
            value = value + dot_nt(queries[0][at, :], queries[1][...])
        if mine:
            keep[place] = value
        else:
            give[place] = value.astype(LOW)


def feed_forward_grads_kernel(pieces, units, place, sums, got, gate_ref, up_ref, down_ref):
    piece = sums.shape[0]
    rows = got.shape[0]
    hidden = got.shape[1] // 2
    step = 8

    def write(second):
        for row in range(0, rows, step):
            at = row + (rows if second else 0)
            number, inner = at // piece, at % piece
            for matrix, target in enumerate((gate_ref, up_ref)):
                start = (matrix * pieces + number) * hidden
                mine = sums[pl.ds(inner, step), pl.ds(start, hidden)].astype(F32)
                other = got[pl.ds(row, step), pl.ds(matrix * hidden, hidden)].astype(F32)
                pair = (other, mine) if second else (mine, other)
                for unit in range(0, hidden, units):
                    tile = jnp.concatenate([part[:, unit : unit + units] for part in pair], axis=1)
                    target[pl.ds(row, step), pl.ds(2 * unit, 2 * units)] = tile

    @pl.when(place[0] == 0)
    def _():
        write(False)

    @pl.when(place[0] != 0)
    def _():
        write(True)

    base = 2 * pieces * hidden
    width = down_ref.shape[1]
    for number in range(down_ref.shape[0] // piece):
        down_ref[pl.ds(number * piece, piece), :] = sums[:, pl.ds(base + number * width, width)].astype(F32)


def columns_kernel(place, keep, got, *targets):
    rows = got.shape[0]

    def write(start, first, later):
        for number, target in enumerate(targets):
            half = target.shape[1] // 2
            columns = pl.ds(number * half, half)
            target[:, pl.ds(0, half)] = first(start, columns)
            target[:, pl.ds(half, half)] = later(start, columns)

    from_keep = lambda start, columns: keep[pl.ds(start, rows), columns]
    from_got = lambda start, columns: got[:, columns]

    @pl.when(place[0] == 0)
    def _():
        write(0, from_keep, from_got)

    @pl.when(place[0] != 0)
    def _():
        write(rows, from_got, from_keep)


def after(values, *others):
    return lax.optimization_barrier((values, *others))[0]


def together(*values):
    return lax.optimization_barrier(values)


class Ring:
    def __init__(self):
        self.charts = lax.axis_size("dp")
        self.groups = lax.axis_size("hx")
        self.half = lax.axis_index("hc").astype(jnp.int32)
        self.second = self.half == 1
        self.place = self.half[None]
        self.group = lax.axis_index("hx").astype(jnp.int32)
        self.block = lax.axis_index("dp").astype(jnp.int32) * self.groups + self.group
        self.blocks = self.charts * self.groups
        chart_bits = [("dp", 1 << i) for i in range(self.charts.bit_length() - 1)]
        self.group_bits = [("hx", 1 << i) for i in range(self.groups.bit_length() - 1)]
        self.far = chart_bits[:0:-1]
        near = chart_bits[:1]
        self.tails = (near + self.group_bits, self.group_bits + near)
        self.orders = tuple(self.far + tail for tail in self.tails)

    def send(self, values, axis, bit):
        size = self.charts if axis == "dp" else self.groups
        return lax.ppermute(values, axis, [(i, i ^ bit) for i in range(size)])

    def swap(self, values):
        return lax.ppermute(values, "hc", [(0, 1), (1, 0)])

    def in_order(self, mine, other):
        return jnp.where(self.second, other, mine), jnp.where(self.second, mine, other)

    def steps(self, order):
        return [bit * self.groups if axis == "dp" else bit for axis, bit in order]

    def arrivals(self):
        apart = self.block ^ jnp.arange(self.blocks, dtype=jnp.int32)
        indices = []
        for order in self.orders:
            index = jnp.zeros((self.blocks,), jnp.int32)
            for place, step in enumerate(self.steps(order)):
                index = index + jnp.where((apart & step) != 0, 1 << place, 0)
            indices.append(index)
        return indices

    def origins(self):
        indices = []
        for order in self.orders:
            masks = [0]
            for step in self.steps(order):
                masks = masks + [m ^ step for m in masks]
            indices.append(self.block ^ jnp.asarray(masks, jnp.int32))
        return indices

    def far_masks(self):
        masks = [0]
        for _, bit in self.far:
            masks = masks + [m | bit for m in masks]
        return masks

    def far_step(self, blocks, step):
        return jnp.concatenate([blocks, self.send(blocks, *self.far[step])], axis=0)

    def near_step(self, parts, step):
        return [self.send(part, *tail[step]) for part, tail in zip(parts, self.tails)]

    def near_sends(self, gives, place):
        return [self.send(give, *tail[place]) for give, tail in zip(gives, self.tails)]

    def near_sums(self, keeps, gots, place):
        halves = [got.shape[0] // 2 for got in gots]
        add = lambda k, g: (k.astype(F32) + g.astype(F32)).astype(LOW)
        gives = [add(k[h:], g[h:]) for k, g, h in zip(keeps, gots, halves)]
        keeps = [add(k[:h], g[:h]) for k, g, h in zip(keeps, gots, halves)]
        return keeps, gives

    def far_sends(self, keeps, gots):
        count = 1 << len(self.far)
        add = lambda r: [
            k[r : r + 1].astype(F32) + g[r : r + 1].astype(F32) for k, g in zip(keeps, gots)
        ]
        block = lambda r: jnp.concatenate(add(r), axis=2)
        if len(self.far) == 2:
            masks = self.far_masks()
            return block(0), [self.send(block(r).astype(LOW), "dp", masks[r]) for r in range(1, count)]
        keep = jnp.concatenate([block(r) for r in range(count)], axis=0)
        for axis, bit in reversed(self.far[1:]):
            half = keep.shape[0] // 2
            keep = keep[:half] + self.send(keep[half:].astype(LOW), axis, bit).astype(F32)
        return keep[:1], [self.send(keep[1:].astype(LOW), *self.far[0])]

    def far_sum(self, own, gots):
        return sum((got.astype(F32) for got in gots), own)[0]

    def far_first(self, keeps, gots):
        count = 1 << len(self.far)
        add = lambda r: jnp.concatenate(
            [k[r].astype(F32) + g[r].astype(F32) for k, g in zip(keeps, gots)], axis=2
        )
        keep, give = add(slice(0, count // 2)), add(slice(count // 2, None)).astype(LOW)
        return keep, self.send(give, *self.far[-1])

    def far_last(self, keep, got):
        for axis, bit in reversed(self.far[:-1]):
            half = keep.shape[0] // 2
            give = (keep[half:] + got[half:].astype(F32)).astype(LOW)
            keep = keep[:half] + got[:half].astype(F32)
            got = self.send(give, axis, bit)
        return keep, [got]

    def halve_wholes(self, wholes, rows):
        keeps, gives = [], []
        for whole, index in zip(wholes, self.origins()):
            blocks = jnp.take(whole.reshape(self.blocks, rows, -1), index, axis=0)
            keeps.append(blocks[: self.blocks // 2])
            gives.append(blocks[self.blocks // 2 :])
        return keeps, gives

    def across(self, mine):
        rows = mine[None]
        for axis, bit in self.group_bits:
            rows = jnp.concatenate([rows, self.send(rows, axis, bit)], axis=0)
        return rows

    def halves(self, first, later):
        mine = jnp.where(self.second, later, first)
        give = jnp.where(self.second, first, later)
        return jnp.concatenate(self.in_order(mine, self.swap(give)), axis=0)

    def pair_sum(self, keep, give):
        return keep + self.swap(give.astype(LOW)).astype(F32)

    def group_terms(self, total):
        for axis, bit in reversed(self.group_bits):
            middle = total.shape[0] // 2
            total = total[:middle] + self.send(total[middle:].astype(LOW), axis, bit).astype(F32)
        return total[0]

    def finished(self, keep, count):
        rows = keep.shape[0] // 2
        give = lax.dynamic_slice_in_dim(keep, (1 - self.half) * rows, rows, 0)
        got = self.swap(give)
        width = keep.shape[1] // count * 2
        return run_kernel(
            columns_kernel, [full_shape(rows, width)] * count, rows * width, [self.place], [keep, got]
        )


def column_halves(weights):
    half = weights[0].shape[1] // 2
    return [jnp.concatenate([w[:, i * half : (i + 1) * half] for w in weights], axis=1) for i in range(2)]


def unit_halves(weight, units):
    rows, columns = weight.shape
    split = weight.reshape(rows, columns // (2 * units), 2, units)
    return split[:, :, 0].reshape(rows, -1), split[:, :, 1].reshape(rows, -1)


def unit_whole(first, later, units):
    rows, columns = first.shape
    pieces = [part.reshape(rows, columns // units, 1, units) for part in (first, later)]
    return jnp.concatenate(pieces, axis=2).reshape(rows, 2 * columns)


def on_device(
    tokens,
    memory,
    text_length,
    patch_count,
    self_gain,
    self_query,
    self_key,
    self_value,
    self_out,
    cross_gain,
    cross_query,
    cross_key,
    cross_value,
    cross_out,
    mlp_gain,
    mlp_gate,
    mlp_up,
    mlp_down,
    output_grad,
):
    ring = Ring()
    place = ring.place
    width = tokens.shape[-1]
    half = width // 2
    units = mlp_down.shape[0]
    hidden_half = units * ring.blocks
    rows = self_query.shape[0]
    own = tokens.shape[1]
    own_patches = memory.shape[1]
    both = 2 * own
    keys = both * ring.groups
    patches = 2 * own_patches * ring.groups
    piece = 16
    packed = (2 * rows) % piece == 0 and units == HEAD_DIM and ring.blocks > 1
    pieces, down_pieces = 2 * rows // piece, units // piece
    pairs = ("dp", "hx")
    index_in = tuple(ring.arrivals()) if packed else ()
    index_out = tuple(ring.origins()) if packed else ()
    index_specs = [SMEM_SPEC] * len(index_in)
    block_rows = 2 * rows

    gain_columns = jnp.stack([self_gain, cross_gain, mlp_gain], axis=1)
    gain_columns = jnp.pad(gain_columns, ((0, 0), (0, PAIR_LANES - 3)))
    chains = ([self_query, gain_columns, self_out, cross_query], [self_key, self_value, cross_key, cross_value])
    splits = (half + PAIR_LANES, 2 * half)
    cut_all = 3 * half + PAIR_LANES
    packed_columns = (2 * hidden_half) * pieces + width * down_pieces
    widths_one = ([half, PAIR_LANES], [width])
    widths_two = ([half] * 2, [width])

    if packed:
        kinds = ["all" if w is gain_columns else "half" for w in chains[0] + chains[1]]
        mine, give = cut_shards(place, chains[0] + chains[1], kinds)
        blocks = jnp.concatenate(ring.in_order(mine, ring.swap(give)), axis=0)[None]
    else:
        sides = [
            jnp.concatenate(
                [w if w is gain_columns else column_halves([w])[i] for w in chains[0] + chains[1]],
                axis=1,
            )
            for i in range(2)
        ]
        blocks = ring.halves(*sides)[None]
    middle = own_patches // 2
    token_m = ring.across(tokens[0])
    patch_a = ring.across(memory[0, :middle])
    if packed:
        rest = after([mlp_gate, mlp_up, cross_out], blocks)
        mine, give = cut_shards(place, rest, ["units"] * 2 + ["half"])
        blocks_mlp = join_rows(place, mine, ring.swap(give), mlp_down, [], half, piece)[0]
    else:
        gate_halves, up_halves = unit_halves(mlp_gate, units), unit_halves(mlp_up, units)
        rest = [
            jnp.concatenate([gate_halves[i], up_halves[i], column_halves([cross_out])[i]], axis=1)
            for i in range(2)
        ]
        gate_up = lax.all_gather(ring.halves(*rest), pairs, axis=0, tiled=True)
        down_three = lax.all_gather(mlp_down, pairs, axis=0, tiled=True)
        out_two = gate_up[:, 2 * hidden_half :]
    blocks = ring.far_step(blocks, 0)
    blocks, token_m, memory = together(blocks, token_m, memory)
    if packed:
        mlp_weights = lax.all_gather(after(blocks_mlp, blocks), pairs, axis=0, tiled=True)
        mlp_weights = mlp_weights.reshape(ring.blocks, piece, -1)
    patch_b = ring.across(memory[0, middle:])
    for step in range(1, len(ring.far)):
        blocks = ring.far_step(blocks, step)
    blocks, patch_a, token_m = together(blocks, patch_a, token_m)
    parts = [blocks[:, :, :cut_all], blocks[:, :, cut_all:]]
    token_g = ring.swap(token_m)
    last = len(ring.tails[0]) - 1
    for step in range(last):
        got = ring.near_step(parts, step)
        parts = [jnp.concatenate(pair, axis=0) for pair in zip(parts, got)]
    parts, token_g, patch_b = together(parts, token_g, patch_b)
    parts_one = [part[:, :, :split] for part, split in zip(parts, splits)]
    parts_two = [part[:, :, split:] for part, split in zip(parts, splits)]
    near_one = ring.near_step(parts_one, last)
    patch_m = jnp.concatenate([patch_a, patch_b], axis=1)
    patch_g = ring.swap(patch_m)
    near_one, parts_two, patch_g = together(near_one, parts_two, patch_g)
    near_two = ring.near_step(parts_two, last)
    near_one = (parts_one[0], near_one[0], parts_one[1], near_one[1])
    arrivals = ring.arrivals()

    token_chunk = math.gcd(256, own)
    patch_chunk = math.gcd(256, own_patches)

    def chunk_starts(span, chunk, side_first):
        groups = ring.group ^ jnp.arange(ring.groups, dtype=jnp.int32)
        sides = ring.half ^ jnp.arange(2, dtype=jnp.int32)
        inner = jnp.arange(span // chunk, dtype=jnp.int32) * chunk
        if side_first:
            starts = groups[None, :, None] * 2 * span + sides[:, None, None] * span
        else:
            starts = groups[:, None, None] * 2 * span + sides[None, :, None] * span
        return (starts + inner).reshape(-1)

    fixed = jnp.stack([ring.group * both, ring.half])
    info_one = jnp.concatenate([text_length, fixed, chunk_starts(own, token_chunk, False)])
    info_two = jnp.concatenate([patch_count, fixed, chunk_starts(own_patches, patch_chunk, True)])

    head_shapes = [low_shape(both, half), low_shape(keys, half), low_shape(keys, half)]
    query_outs = [full_shape(8, width), low_shape(keys, width), *head_shapes]
    projections = [low_shape(width, w) for w in widths_one[0] + widths_one[1]]
    cost = keys * width * half
    if packed:
        outs = run_kernel(
            functools.partial(query_kernel, True),
            query_outs + projections,
            cost,
            index_in,
            [*near_one, token_m, token_g],
            late=True,
        )
        gain_rows, normed_one, query_heads, key_heads, value_heads = outs[:5]
        query_one, gain_cols, heads_one = outs[5:]
    else:
        query_one, gain_cols = to_whole(near_one[0], near_one[1], arrivals[0], widths_one[0])
        (heads_one,) = to_whole(near_one[2], near_one[3], arrivals[1], widths_one[1])
        gain_rows, normed_one, query_heads, key_heads, value_heads = run_kernel(
            functools.partial(query_kernel, False),
            query_outs,
            cost,
            [],
            [query_one, gain_cols, heads_one, token_m, token_g],
            late=True,
        )
    near_one = None
    grad_g = ring.swap(after(output_grad[0], query_heads))
    context_one, lse_one = attention_forward(
        info_one, query_heads, key_heads, value_heads, True, token_chunk
    )
    context_one, near_a, near_b, grad_g = together(context_one, *near_two, grad_g)
    context_one_g = ring.swap(context_one)
    out_one, query_two = to_whole(parts_two[0], near_a, arrivals[0], widths_two[0])
    out_one_g = ring.swap(out_one)
    patch_all = [part.reshape(-1, width) for part in (patch_m, patch_g)]
    memory_heads = [low_shape(patches, half)] * 2
    if packed:
        memory_keys, memory_values, heads_two = run_kernel(
            functools.partial(memory_kernel, True),
            memory_heads + [low_shape(width, width)],
            patches * width * half,
            index_in[1:],
            [parts_two[1], near_b, *patch_all],
            late=True,
        )
    else:
        (heads_two,) = to_whole(parts_two[1], near_b, arrivals[1], widths_two[1])
        memory_keys, memory_values = run_kernel(
            functools.partial(memory_kernel, False),
            memory_heads,
            patches * width * half,
            [],
            [heads_two, *patch_all],
            late=True,
        )
    context_one_g, memory_keys = together(context_one_g, memory_keys)
    hidden_one, normed_two, cross_heads = run_kernel(
        cross_query_kernel,
        [full_shape(both, width), low_shape(both, width), low_shape(both, half)],
        both * width * half,
        [place],
        [token_m[0], token_g[0], context_one, context_one_g, out_one, out_one_g, gain_rows, query_two],
        late=True,
    )
    if packed:
        out_two = from_pieces(after(mlp_weights, cross_heads), packed_columns, pieces, half)
    cross_heads, out_two = together(cross_heads, out_two)
    out_two_g = ring.swap(out_two)
    context_two, lse_two = attention_forward(
        info_two, cross_heads, memory_keys, memory_values, False, patch_chunk
    )
    context_two_g = ring.swap(context_two)
    if packed:
        hidden_two, part_low, down_keep, down_give, gain_three, mlp_terms = run_kernel(
            functools.partial(mlp_kernel, 512),
            [
                full_shape(both, width),
                low_shape(both, width),
                full_shape(own, width),
                low_shape(own, width),
                full_shape(width, PAIR_LANES),
                low_shape(ring.blocks, piece, packed_columns),
            ],
            2 * both * width * hidden_half,
            [place],
            [
                hidden_one,
                context_two,
                context_two_g,
                out_two,
                out_two_g,
                gain_rows,
                gain_cols,
                output_grad[0],
                grad_g,
            ],
            [
                pltpu.VMEM((ring.blocks, pieces, piece, hidden_half), LOW),
                pltpu.VMEM((ring.blocks, pieces, piece, hidden_half), LOW),
                pltpu.VMEM((ring.blocks, down_pieces, piece, width), LOW),
                pltpu.VMEM((both, width), LOW),
                pltpu.VMEM((width, both), LOW),
                pltpu.VMEM((both, width), LOW),
                pltpu.VMEM((both, width), F32),
                pltpu.VMEM((both, width), F32),
                pltpu.VMEM((width, PAIR_LANES), F32),
                pltpu.SemaphoreType.DMA((2 * pieces + down_pieces,)),
            ],
            [mlp_weights],
            late=True,
        )
        mlp_terms = mlp_terms.reshape(ring.blocks * piece, -1)
        mlp_sum = lax.psum_scatter(mlp_terms, pairs, scatter_dimension=0, tiled=True)
    else:
        joined = jnp.concatenate(ring.in_order(out_two, out_two_g), axis=1)
        swapped = jnp.concatenate([context_two_g[own:], context_two_g[:own]], axis=0)
        context = jnp.concatenate(ring.in_order(context_two, swapped), axis=1)
        hidden_two = hidden_one + dot_nn(context, joined)
        normed_three = (normalize(hidden_two)[0] * gain_rows[2:3]).astype(LOW)
        grad_low = jnp.concatenate([output_grad[0], grad_g], axis=0)
        gate_up = gate_up[:, : 2 * hidden_half]
        gate_three, up_three = gate_up[:, :hidden_half], gate_up[:, hidden_half:]
        active, slope = gelu_parts(dot_nn(normed_three, gate_three))
        up = dot_nn(normed_three, up_three)
        mixed = (active * up).astype(LOW)
        down_part = dot_nn(mixed, down_three)
        down_keep, down_give = down_part[:own], down_part[own:].astype(LOW)
        grad_mixed = dot_nt(grad_low, down_three)
        gate_low = (grad_mixed * up * slope).astype(LOW)
        up_low = (grad_mixed * active).astype(LOW)
        part_low = (dot_nt(gate_low, gate_three) + dot_nt(up_low, up_three)).astype(LOW)
        terms = jnp.concatenate(
            [dot_tn(normed_three, gate_low), dot_tn(normed_three, up_low)], axis=1
        )
        column = jnp.sum(terms * gate_up.astype(F32), axis=1, keepdims=True)
        gain_three = lane_column(column / gain_cols[:, 2:3].astype(F32), 2)
        gate_up = lax.psum_scatter(terms, pairs, scatter_dimension=0, tiled=True)
        mlp_ddown = lax.psum_scatter(
            dot_tn(mixed, grad_low), pairs, scatter_dimension=0, tiled=True
        )

    part_g = ring.swap(part_low)
    down_got = ring.swap(down_give)
    output = (hidden_two[:own] + down_keep + down_got.astype(F32)).astype(LOW)

    def branch(gain_at, hidden, mine, got, weight_m, weight_g, base):
        return run_kernel(
            functools.partial(branch_kernel, gain_at),
            [full_shape(both, width), low_shape(both, width), low_shape(both, half)],
            both * width * half,
            [place],
            [hidden, gain_rows, mine, got, weight_m, weight_g, *base],
            late=True,
        )

    dhidden_two, branch_two, dcontext_two = branch(
        2, hidden_two, part_low, part_g, out_two, out_two_g, [output_grad[0], grad_g]
    )
    dquery, dkey, dvalue = attention_backward(
        info_two,
        cross_heads,
        memory_keys,
        memory_values,
        context_two,
        dcontext_two,
        lse_two,
        False,
        patch_chunk,
    )
    (part_low,) = run_kernel(
        back_kernel, [low_shape(both, width)], both * width, [], [dquery, query_two]
    )
    part_g = ring.swap(part_low)

    count = ring.blocks // 2

    def grads(body, inputs, columns, gain_outs, cost):
        scratch = [pltpu.VMEM((width, c), LOW) for c in columns]
        acc = pltpu.VMEM((width, PAIR_LANES), F32)
        if packed:
            shapes = [low_shape(count, block_rows, c) for c in columns for _ in range(2)]
            outs = run_kernel(
                functools.partial(body, True),
                gain_outs + shapes,
                cost,
                [place, *index_out],
                inputs,
                scratch + [acc],
                late=True,
            )
            blocks = outs[len(gain_outs) :]
            return outs[: len(gain_outs)], blocks[0::2], blocks[1::2]
        wholes = [low_shape(width, c) for c in columns]
        outs = run_kernel(
            functools.partial(body, False), gain_outs + wholes, cost, [place], inputs, [acc], late=True
        )
        return outs[: len(gain_outs)], *ring.halve_wholes(outs[len(gain_outs) :], block_rows)

    patch_spans = [(side == 0, g) for side in range(2) for g in range(ring.groups)]
    patch_shape = (ring.groups, own_patches, width)
    memory_keep, memory_give = run_kernel(
        functools.partial(rows_back_kernel, patch_spans, False),
        [full_shape(*patch_shape), low_shape(*patch_shape)],
        patches * width,
        [],
        [dkey, dvalue, heads_two],
    )
    memory_total = ring.pair_sum(memory_keep, memory_give)
    part_g, memory_total = together(part_g, memory_total)
    memory_sent = ring.group_terms(memory_total)
    dhidden_one, branch_one, dcontext_one = branch(
        1, hidden_one, part_low, part_g, out_one, out_one_g, [dhidden_two]
    )
    (gain_two,), cross_keep, cross_give = grads(
        cross_grads_kernel,
        [
            context_two,
            context_two_g,
            branch_two,
            normed_two,
            dquery,
            *patch_all,
            dkey,
            dvalue,
            query_two,
            gain_cols,
            context_one,
            context_one_g,
            branch_one,
        ],
        (3 * half, 2 * half),
        [full_shape(width, PAIR_LANES)],
        (both + patches) * width * half,
    )
    cross_got = ring.near_sends(cross_give, last)
    cross_keep, dcontext_one = together(cross_keep, dcontext_one)

    dquery_one, dkey_one, dvalue_one = attention_backward(
        info_one,
        query_heads,
        key_heads,
        value_heads,
        context_one,
        dcontext_one,
        lse_one,
        True,
        token_chunk,
    )
    dquery_one, dkey_one, dvalue_one, cross_got, memory_grad = together(
        dquery_one, dkey_one, dvalue_one, cross_got, memory_sent
    )
    for step in reversed(range(1, last + 1)):
        cross_keep, cross_give = ring.near_sums(cross_keep, cross_got, step)
        cross_got = ring.near_sends(cross_give, step - 1)
    dquery_one, cross_give = together(dquery_one, cross_give)
    _, self_keep, self_give = grads(
        self_grads_kernel,
        [
            normed_one,
            dquery_one,
            dkey_one,
            dvalue_one,
            query_one,
            heads_one,
            gain_cols,
            gain_two,
            gain_three,
        ],
        (half + PAIR_LANES, 2 * half),
        [],
        (both + keys) * width * half,
    )
    self_give, cross_got = together(self_give, cross_got)
    self_got = ring.near_sends(self_give, last)
    cross_own, cross_far = ring.far_first(cross_keep, cross_got)
    dquery_one, dkey_one, dvalue_one = after((dquery_one, dkey_one, dvalue_one), self_give)
    token_spans = [(side == 0, g) for g in range(ring.groups) for side in range(2)]
    token_shape = (ring.groups, own, width)
    part_keep, part_give = run_kernel(
        functools.partial(rows_back_kernel, token_spans, True),
        [full_shape(*token_shape), low_shape(*token_shape)],
        keys * width,
        [],
        [dkey_one, dvalue_one, heads_one, dquery_one, query_one],
    )
    part_total = ring.pair_sum(part_keep, part_give)
    self_got, cross_far, part_total = together(self_got, cross_far, part_total)
    for step in reversed(range(1, last + 1)):
        self_keep, self_give = ring.near_sums(self_keep, self_got, step)
        self_got = ring.near_sends(self_give, step - 1)
    cross_own, cross_far = ring.far_last(cross_own, cross_far)
    self_got, cross_far, part_total = together(self_got, cross_far, part_total)
    self_own, self_far = ring.far_sends(self_keep, self_got)
    dnormed_one = ring.group_terms(part_total)
    plain, inverse = normalize(tokens[0].astype(F32))
    input_grad = dhidden_one[:own] + norm_back(plain, inverse, gain_rows[0:1], dnormed_one)

    if packed:
        mlp_rows = mlp_sum[:, : 2 * pieces * hidden_half].reshape(piece, 2, pieces, hidden_half)
        mlp_rows = mlp_rows.transpose(2, 0, 1, 3).reshape(2 * rows, 2 * hidden_half)
        mlp_give = lax.dynamic_slice_in_dim(mlp_rows, (1 - ring.half) * rows, rows, 0)
        mlp_dgate, mlp_dup, mlp_ddown = run_kernel(
            functools.partial(feed_forward_grads_kernel, pieces, units),
            [full_shape(rows, 2 * hidden_half)] * 2 + [full_shape(units, width)],
            rows * width,
            [place],
            [mlp_sum, ring.swap(mlp_give)],
        )
    else:
        (gate_up,) = ring.finished(gate_up, 1)
        gate_columns = [gate_up[:, i * hidden_half : (i + 1) * hidden_half] for i in range(4)]
        mlp_dgate = unit_whole(gate_columns[0], gate_columns[2], units)
        mlp_dup = unit_whole(gate_columns[1], gate_columns[3], units)
    cross_sum = ring.far_sum(cross_own, cross_far)
    cross_dout, cross_dquery, self_dout, cross_dkey, cross_dvalue = ring.finished(cross_sum, 5)
    self_far, mlp_dgate, mlp_dup, mlp_ddown, input_grad, cross_dout = together(
        self_far, mlp_dgate, mlp_dup, mlp_ddown, input_grad, cross_dout
    )
    self_sum = ring.far_sum(self_own, self_far)
    gain_block = self_sum[:, half : half + PAIR_LANES]
    gain_block = jnp.pad(gain_block, ((0, 0), (0, half - PAIR_LANES)))
    joined = jnp.concatenate(
        [self_sum[:, :half], self_sum[:, half + PAIR_LANES :], gain_block], axis=1
    )
    self_dquery, self_dvalue, self_dkey, gain_terms = ring.finished(joined, 4)
    dgains = gain_terms[:, :3] + gain_terms[:, half : half + 3]

    return (
        output[None],
        input_grad[None],
        memory_grad[None],
        dgains[:, 0],
        self_dquery,
        self_dkey,
        self_dvalue,
        self_dout,
        dgains[:, 1],
        cross_dquery,
        cross_dkey,
        cross_dvalue,
        cross_dout,
        dgains[:, 2],
        mlp_dgate,
        mlp_dup,
        mlp_ddown,
    )


def solution(mesh):
    charts, heads = mesh.devices.shape
    inner = Mesh(mesh.devices.reshape(charts, heads // 2, 2), ("dp", "hx", "hc"))
    every = ("dp", "hx", "hc")
    rows = P(every, None)
    vector = P(every)
    grid = P("dp", ("hx", "hc"), None)
    in_specs = (grid, grid, P("dp"), P("dp"))
    in_specs += (vector, rows, rows, rows, rows) * 2
    in_specs += (vector, rows, rows, rows, grid)
    out_specs = (grid, grid, grid)
    out_specs += (vector, rows, rows, rows, rows) * 2
    out_specs += (vector, rows, rows, rows)
    return jax.shard_map(
        on_device, mesh=inner, in_specs=in_specs, out_specs=out_specs, check_vma=False
    )
```

```python
import functools
import math

import jax
import jax.numpy as jnp
from jax import lax
from jax.experimental import pallas as pl
from jax.experimental.pallas import tpu as pltpu
from jax.sharding import Mesh
from jax.sharding import PartitionSpec as P

HEAD_DIM = 64
PAIR_LANES = 128
NEG_FILL = -1e30
EPS = 1e-06
F32 = jnp.float32
LOW = jnp.bfloat16


NT = (((1,), (1,)), ((), ()))
TN = (((0,), (0,)), ((), ()))


def dot_nt(left, right):
    return lax.dot_general(left, right, NT, preferred_element_type=F32)


def dot_tn(left, right):
    return lax.dot_general(left, right, TN, preferred_element_type=F32)


def dot_nn(left, right):
    return jnp.dot(left, right, preferred_element_type=F32)


FIXED = 3
SPANS = 4


def query_limits(info, queries, causal):
    last = info[0] - 1
    if not causal:
        return jnp.full((1, queries), last, jnp.int32), last
    lanes = lax.broadcasted_iota(jnp.int32, (1, queries), 1)
    span = queries // 2
    swapped = jnp.where(lanes < span, lanes + info[2] * span, lanes - info[2] * span)
    return jnp.minimum(info[1] + swapped, last), jnp.minimum(info[1] + queries - 1, last)


def key_places(info, chunk, span, queries, j):
    parts = chunk // span
    starts = [info[FIXED + j * parts + i] for i in range(parts)]
    inner = lax.broadcasted_iota(jnp.int32, (span, queries), 0)
    first = functools.reduce(jnp.minimum, starts)
    return jnp.concatenate([start + inner for start in starts], axis=0), first


def first_place(info, chunk, span, j):
    parts = chunk // span
    return functools.reduce(jnp.minimum, [info[FIXED + j * parts + i] for i in range(parts)])


def head_lanes(head):
    lanes = lax.broadcasted_iota(jnp.int32, (1, PAIR_LANES), 1)
    return (lanes // HEAD_DIM) == head


def fold(values, op):
    rows, columns = values.shape
    return op(values.reshape(rows // 8, 8, columns), axis=0)


def forward_kernel(causal, chunk, span, info, q_ref, k_ref, v_ref, c_ref, lse_ref, s_ref, m_ref, l_ref, a_ref):
    queries = q_ref.shape[0]
    chunks = k_ref.shape[0] // chunk
    scaling = 1.0 / math.sqrt(HEAD_DIM)
    limit, latest = query_limits(info, queries, causal)
    q_all = q_ref[...] * jnp.asarray(scaling, q_ref.dtype)
    q_heads = [jnp.where(head_lanes(h), q_all, jnp.zeros_like(q_all)) for h in range(2)]
    m_ref[...] = jnp.full(m_ref.shape, NEG_FILL, F32)
    l_ref[...] = jnp.zeros(l_ref.shape, F32)
    a_ref[...] = jnp.zeros(a_ref.shape, F32)

    @pl.loop(0, chunks)
    def _(j):
        @pl.when(first_place(info, chunk, span, j) <= latest)
        def _():
            rows = pl.ds(pl.multiple_of(j * chunk, chunk), chunk)
            keys = k_ref[rows, :]
            place, _ = key_places(info, chunk, span, queries, j)
            allowed = place <= limit
            for h in range(2):
                scores = jnp.where(allowed, dot_nt(keys, q_heads[h]), NEG_FILL)
                s_ref[h, rows, :] = scores
                m_ref[h] = jnp.maximum(m_ref[h], fold(scores, jnp.max))

    highest = [jnp.max(m_ref[h], axis=0, keepdims=True) for h in range(2)]

    @pl.loop(0, chunks)
    def _(j):
        @pl.when(first_place(info, chunk, span, j) <= latest)
        def _():
            rows = pl.ds(pl.multiple_of(j * chunk, chunk), chunk)
            values = v_ref[rows, :]
            for h in range(2):
                weight = jnp.exp(s_ref[h, rows, :] - highest[h])
                l_ref[h] = l_ref[h] + fold(weight, jnp.sum)
                a_ref[h] = a_ref[h] + dot_tn(values, weight.astype(LOW))

    parts = []
    for h in range(2):
        total = jnp.sum(l_ref[h], axis=0, keepdims=True)
        lse_ref[0, pl.ds(h, 1), :] = highest[h] + jnp.log(total)
        parts.append(a_ref[h, pl.ds(h * HEAD_DIM, HEAD_DIM), :] / total)
    c_ref[...] = jnp.concatenate(parts, axis=0).T.astype(c_ref.dtype)


def backward_kernel(causal, chunk, span, info, q_ref, k_ref, v_ref, c_ref, g_ref, lse_ref, dq_ref, dk_ref, dv_ref, a_ref):
    queries = q_ref.shape[0]
    chunks = k_ref.shape[0] // chunk
    scaling = 1.0 / math.sqrt(HEAD_DIM)
    limit, latest = query_limits(info, queries, causal)
    q_all = q_ref[...] * jnp.asarray(scaling, q_ref.dtype)
    g_all = g_ref[...]
    q_heads = [jnp.where(head_lanes(h), q_all, jnp.zeros_like(q_all)) for h in range(2)]
    g_heads = [jnp.where(head_lanes(h), g_all, jnp.zeros_like(g_all)) for h in range(2)]
    product = (c_ref[...].astype(F32) * g_all.astype(F32)).T
    centres = [
        jnp.sum(product[h * HEAD_DIM : (h + 1) * HEAD_DIM], axis=0, keepdims=True) for h in range(2)
    ]
    logs = [lse_ref[0, pl.ds(h, 1), :] for h in range(2)]
    a_ref[...] = jnp.zeros(a_ref.shape, F32)

    @pl.loop(0, chunks)
    def _(j):
        start = first_place(info, chunk, span, j)
        rows = pl.ds(pl.multiple_of(j * chunk, chunk), chunk)

        @pl.when(start <= latest)
        def _():
            keys = k_ref[rows, :]
            values = v_ref[rows, :]
            place, _ = key_places(info, chunk, span, queries, j)
            allowed = place <= limit
            dk = jnp.zeros((chunk, PAIR_LANES), F32)
            dv = jnp.zeros((chunk, PAIR_LANES), F32)
            for h in range(2):
                scores = jnp.where(allowed, dot_nt(keys, q_heads[h]), NEG_FILL)
                prob = jnp.exp(scores - logs[h])
                dprob = dot_nt(values, g_heads[h])
                dv = dv + dot_nn(prob.astype(LOW), g_heads[h])
                dscore = (prob * (dprob - centres[h])).astype(LOW)
                dk = dk + dot_nn(dscore, q_heads[h])
                a_ref[h] = a_ref[h] + dot_tn(keys, dscore)
            dk_ref[rows, :] = dk.astype(dk_ref.dtype)
            dv_ref[rows, :] = dv.astype(dv_ref.dtype)

        @pl.when(start > latest)
        def _():
            dk_ref[rows, :] = jnp.zeros((chunk, PAIR_LANES), dk_ref.dtype)
            dv_ref[rows, :] = jnp.zeros((chunk, PAIR_LANES), dv_ref.dtype)

    parts = [a_ref[h, pl.ds(h * HEAD_DIM, HEAD_DIM), :] for h in range(2)]
    dq_ref[...] = (jnp.concatenate(parts, axis=0).T * scaling).astype(dq_ref.dtype)


def lane_spec(rows):
    return pl.BlockSpec((rows, PAIR_LANES), lambda i, info: (0, i))


def stat_spec(queries):
    return pl.BlockSpec((1, 2, queries), lambda i, info: (i, 0, 0))


def attention_forward(info, queries, keys, values, causal, span):
    chunk = math.gcd(SPANS * span, keys.shape[0])
    rows, features = queries.shape
    key_rows = keys.shape[0]
    pairs = features // PAIR_LANES
    return pl.pallas_call(
        functools.partial(forward_kernel, causal, chunk, span),
        out_shape=(
            jax.ShapeDtypeStruct((rows, features), LOW),
            jax.ShapeDtypeStruct((pairs, 2, rows), F32),
        ),
        grid_spec=pltpu.PrefetchScalarGridSpec(
            num_scalar_prefetch=1,
            grid=(pairs,),
            in_specs=[lane_spec(rows), lane_spec(key_rows), lane_spec(key_rows)],
            out_specs=[lane_spec(rows), stat_spec(rows)],
            scratch_shapes=[
                pltpu.VMEM((2, key_rows, rows), F32),
                pltpu.VMEM((2, 8, rows), F32),
                pltpu.VMEM((2, 8, rows), F32),
                pltpu.VMEM((2, PAIR_LANES, rows), F32),
            ],
        ),
        compiler_params=pltpu.CompilerParams(vmem_limit_bytes=VMEM_LIMIT),
        cost_estimate=pl.CostEstimate(flops=rows, transcendentals=0, bytes_accessed=0),
    )(info, queries, keys, values)


def attention_backward(info, queries, keys, values, context, grads, lse, causal, span):
    chunk = math.gcd(SPANS * span, keys.shape[0])
    rows, features = queries.shape
    key_rows = keys.shape[0]
    pairs = features // PAIR_LANES
    return pl.pallas_call(
        functools.partial(backward_kernel, causal, chunk, span),
        out_shape=(
            jax.ShapeDtypeStruct((rows, features), LOW),
            jax.ShapeDtypeStruct((key_rows, features), LOW),
            jax.ShapeDtypeStruct((key_rows, features), LOW),
        ),
        grid_spec=pltpu.PrefetchScalarGridSpec(
            num_scalar_prefetch=1,
            grid=(pairs,),
            in_specs=[
                lane_spec(rows),
                lane_spec(key_rows),
                lane_spec(key_rows),
                lane_spec(rows),
                lane_spec(rows),
                stat_spec(rows),
            ],
            out_specs=[lane_spec(rows), lane_spec(key_rows), lane_spec(key_rows)],
            scratch_shapes=[pltpu.VMEM((2, PAIR_LANES, rows), F32)],
        ),
        compiler_params=pltpu.CompilerParams(vmem_limit_bytes=VMEM_LIMIT),
        cost_estimate=pl.CostEstimate(flops=rows, transcendentals=0, bytes_accessed=0),
    )(info, queries, keys, values, context, grads, lse)


SMEM_SPEC = pl.BlockSpec(memory_space=pltpu.SMEM)


def vmem_specs(number):
    return [pl.BlockSpec(memory_space=pltpu.VMEM)] * number


def cuts_of(widths):
    return [sum(widths[:i]) for i in range(len(widths))]


def place_blocks(index, first, later, targets):
    half, rows, _ = first.shape
    cuts = cuts_of([target.shape[1] for target in targets])

    @pl.loop(0, 2 * half)
    def _(step):
        at = index[step]
        place = pl.ds(pl.multiple_of(step * rows, rows), rows)

        def put(source, block):
            for cut, target in zip(cuts, targets):
                target[place, :] = source[block, :, pl.ds(cut, target.shape[1])]

        @pl.when(at < half)
        def _():
            put(first, at)

        @pl.when(at >= half)
        def _():
            put(later, at - half)


def send_order(index, whole, keep, give):
    half, rows, _ = keep.shape

    @pl.loop(0, half)
    def _(step):
        for side, target in enumerate((keep, give)):
            at = pl.ds(pl.multiple_of(index[step + side * half] * rows, rows), rows)
            target[step] = whole[at, :]


def whole_kernel(index, first, later, *targets):
    place_blocks(index, first, later, targets)


def to_whole(first, later, index, widths):
    half, rows, columns = first.shape
    count = 2 * half
    if rows % 16:
        blocks = jnp.concatenate([first, later], axis=0)
        whole = jnp.take(blocks, index, axis=0).reshape(count * rows, columns)
        return [whole[:, cut : cut + width] for cut, width in zip(cuts_of(widths), widths)]
    return run_kernel(
        whole_kernel,
        [low_shape(count * rows, width) for width in widths],
        count * rows * columns,
        [index],
        [first, later],
    )


class Stage:
    def __init__(self, loads, stores):
        self.loads, self.stores = loads, stores
        self.waited, self.sent = set(), set()

    def need(self, *numbers):
        for i in numbers or range(len(self.loads)):
            if i not in self.waited:
                self.waited.add(i)
                self.loads[i].wait()

    def done(self, *numbers):
        for i in numbers or range(len(self.stores)):
            if i not in self.sent:
                self.sent.add(i)
                self.stores[i].start()


def staged_kernel(body, late, sizes, *refs):
    parts, at = [], 0
    for size in sizes:
        parts.append(refs[at : at + size])
        at += size
    tables, arrays, streamed, outs, scratch, held_in, held_out, (in_sems, out_sems) = parts
    stage = Stage(
        [pltpu.make_async_copy(a, b, in_sems.at[i]) for i, (a, b) in enumerate(zip(arrays, held_in))],
        [pltpu.make_async_copy(a, b, out_sems.at[i]) for i, (a, b) in enumerate(zip(held_out, outs))],
    )
    for load in stage.loads:
        load.start()
    if late:
        body(stage, *tables, *held_in, *streamed, *held_out, *scratch)
    else:
        stage.need()
        body(*tables, *held_in, *streamed, *held_out, *scratch)
    stage.need()
    stage.done()
    for store in stage.stores:
        store.wait()


HBM_SPEC = pl.BlockSpec(memory_space=pltpu.HBM)


def run_kernel(body, out_shape, cost, tables, arrays, scratch=(), streamed=(), late=False):
    sizes = (len(tables), len(arrays), len(streamed), len(out_shape), len(scratch))
    sizes += (len(arrays), len(out_shape), 2)
    held = [pltpu.VMEM(x.shape, x.dtype) for x in [*arrays, *out_shape]]
    sems = [pltpu.SemaphoreType.DMA((len(arrays),)), pltpu.SemaphoreType.DMA((len(out_shape),))]
    return pl.pallas_call(
        functools.partial(staged_kernel, body, late, sizes),
        out_shape=out_shape,
        in_specs=[SMEM_SPEC] * len(tables) + [HBM_SPEC] * (len(arrays) + len(streamed)),
        out_specs=[HBM_SPEC] * len(out_shape),
        scratch_shapes=list(scratch) + held + sems,
        compiler_params=pltpu.CompilerParams(vmem_limit_bytes=VMEM_LIMIT),
        cost_estimate=pl.CostEstimate(flops=cost // 1000, transcendentals=0, bytes_accessed=0),
    )(*tables, *arrays, *streamed)


VMEM_LIMIT = 56 << 20


def low_shape(*shape):
    return jax.ShapeDtypeStruct(shape, LOW)


def full_shape(*shape):
    return jax.ShapeDtypeStruct(shape, F32)


def unit_tile(source, at, second):
    lanes = 2 * HEAD_DIM
    start = 2 * at * lanes + (HEAD_DIM if second else 0)
    return jnp.concatenate(
        [source[:, pl.ds(start, HEAD_DIM)], source[:, pl.ds(start + lanes, HEAD_DIM)]], axis=1
    )


def shards_kernel(kinds, place, *refs):
    sources, targets = refs[:-2], refs[-2:]

    def write(target, second):
        cut = 0
        for kind, source in zip(kinds, sources):
            columns = source.shape[1]
            if kind == "all":
                target[:, pl.ds(cut, columns)] = source[...]
                cut += columns
                continue
            if kind == "half":
                start = columns // 2 if second else 0
                target[:, pl.ds(cut, columns // 2)] = source[:, pl.ds(start, columns // 2)]
            else:
                for tile in range(columns // 256):
                    target[:, pl.ds(cut + 128 * tile, 128)] = unit_tile(source, tile, second)
            cut += columns // 2

    @pl.when(place[0] == 0)
    def _():
        write(targets[0], False)
        write(targets[1], True)

    @pl.when(place[0] != 0)
    def _():
        write(targets[0], True)
        write(targets[1], False)


def rows_kernel(widths, piece, place, mine, other, down, *targets):
    *widths, matrices, extra = widths
    rows = mine.shape[0]

    def write(upper, lower):
        cut = 0
        for target, width in zip(targets[:-1], widths):
            target[0, pl.ds(0, rows), :] = upper[:, pl.ds(cut, width)]
            target[0, pl.ds(rows, rows), :] = lower[:, pl.ds(cut, width)]
            cut += width
        packed = targets[-1]
        columns = (mine.shape[1] - cut - extra) // matrices
        step = 8
        base = matrices * (2 * rows // piece) * columns
        last = base + down.shape[1] * (down.shape[0] // piece)
        for start in range(0, 2 * rows, step):
            source = upper if start < rows else lower
            number, inner = start // piece, start % piece
            for matrix in range(matrices):
                place_at = (matrix * (2 * rows // piece) + number) * columns
                packed[pl.ds(inner, step), pl.ds(place_at, columns)] = source[
                    pl.ds(start % rows, step), pl.ds(cut + matrix * columns, columns)
                ]
            packed[pl.ds(inner, step), pl.ds(last + number * extra, extra)] = source[
                pl.ds(start % rows, step), pl.ds(cut + matrices * columns, extra)
            ]
        width = down.shape[1]
        for number in range(down.shape[0] // piece):
            packed[:, pl.ds(base + number * width, width)] = down[pl.ds(number * piece, piece), :]

    @pl.when(place[0] == 0)
    def _():
        write(mine, other)

    @pl.when(place[0] != 0)
    def _():
        write(other, mine)


def cut_shards(place, shards, kinds):
    rows = shards[0].shape[0]
    columns = sum(w.shape[1] if k == "all" else w.shape[1] // 2 for w, k in zip(shards, kinds))
    return run_kernel(
        functools.partial(shards_kernel, kinds), [low_shape(rows, columns)] * 2, rows * columns, [place], shards
    )


def join_rows(place, mine, other, down, widths, extra, piece):
    rows = 2 * mine.shape[0]
    rest = mine.shape[1] - sum(widths)
    packed = rest * (rows // piece) + down.shape[1] * (down.shape[0] // piece)
    return run_kernel(
        functools.partial(rows_kernel, [*widths, 2, extra], piece),
        [low_shape(1, rows, width) for width in widths] + [low_shape(piece, packed)],
        rows * rest,
        [place],
        [mine, other, down],
    )


def pieces_kernel(cut, source, target, held, sem):
    blocks, pieces, piece, columns = held.shape
    copies = [
        pltpu.make_async_copy(
            source.at[:, :, pl.ds(cut + i * columns, columns)], held.at[:, i], sem.at[i]
        )
        for i in range(pieces)
    ]
    for copy in copies:
        copy.start()
    for copy in copies:
        copy.wait()
    target[...] = held[...].reshape(target.shape)


def from_pieces(packed, cut, pieces, columns):
    blocks, piece, _ = packed.shape
    return pl.pallas_call(
        functools.partial(pieces_kernel, cut),
        out_shape=low_shape(blocks * pieces * piece, columns),
        in_specs=[HBM_SPEC],
        out_specs=pl.BlockSpec(memory_space=pltpu.VMEM),
        scratch_shapes=[
            pltpu.VMEM((blocks, pieces, piece, columns), LOW),
            pltpu.SemaphoreType.DMA((pieces,)),
        ],
        cost_estimate=pl.CostEstimate(flops=1000, transcendentals=0, bytes_accessed=0),
    )(packed)


def normalize(values):
    inverse = lax.rsqrt(jnp.mean(values * values, axis=-1, keepdims=True) + EPS)
    return values * inverse, inverse


def norm_back(normed, inverse, gain, grads):
    scaled = grads * gain
    return inverse * (scaled - normed * jnp.mean(scaled * normed, axis=-1, keepdims=True))


def gelu_parts(gate):
    factor = math.sqrt(2.0 / math.pi)
    inner = jnp.tanh(factor * (gate + 0.044715 * gate * gate * gate))
    value = 0.5 * gate * (1.0 + inner)
    slope = 0.5 * (1.0 + inner) + 0.5 * gate * (1.0 - inner * inner) * factor * (
        1.0 + 3.0 * 0.044715 * gate * gate
    )
    return value, slope


def head_slices(place, half):
    mine = pl.ds(pl.multiple_of(place[0] * half, half), half)
    other = pl.ds(pl.multiple_of((1 - place[0]) * half, half), half)
    return mine, other


def query_kernel(packed, stage, *refs):
    if packed:
        index_a, index_b, first_a, later_a, first_b, later_b, token_m, token_g = refs[:8]
        rows_ref, normed_ref, q_ref, k_ref, v_ref, wq, gain_cols, wkv = refs[8:]
        stage.need(0, 1)
        place_blocks(index_a, first_a, later_a, [wq, gain_cols])
        stage.done(5, 6)
        stage.need(2, 3)
        place_blocks(index_b, first_b, later_b, [wkv])
        stage.done(7)
    else:
        wq, gain_cols, wkv, token_m, token_g = refs[:5]
        rows_ref, normed_ref, q_ref, k_ref, v_ref = refs[5:]
    stage.need()
    gain_rows = gain_cols[...].astype(F32).T[0:8]
    rows_ref[...] = gain_rows
    groups, own, _ = token_m.shape
    half = q_ref.shape[1]
    for group in range(groups):
        for side, source in enumerate((token_m, token_g)):
            plain, _ = normalize(source[group].astype(F32))
            at = pl.ds((2 * group + side) * own, own)
            normed_ref[at, :] = (plain * gain_rows[0:1]).astype(LOW)
    stage.done(0, 1)
    q_ref[...] = dot_nn(normed_ref[pl.ds(0, 2 * own), :], wq[...]).astype(LOW)
    stage.done(2)
    value = dot_nn(normed_ref[...], wkv[...]).astype(LOW)
    k_ref[...] = value[:, :half]
    v_ref[...] = value[:, half:]


def add_context(place, target, base, c_m, c_g, w_m, w_g):
    rows, half = c_m.shape
    own = rows // 2
    mine, other = head_slices(place, half)
    for side in range(2):
        at = pl.ds(side * own, own)
        left = c_m[at, :]
        right = c_g[pl.ds((1 - side) * own, own), :]
        for weight, columns in ((w_m, mine), (w_g, other)):
            value = dot_nn(left, weight[mine, :]) + dot_nn(right, weight[other, :])
            target[at, columns] = base(side, columns) + value


def cross_query_kernel(stage, place, token_m, token_g, c_m, c_g, w_m, w_g, rows_ref, wq, h_ref, normed_ref, q_ref):
    tokens = (token_m, token_g)
    base = lambda side, columns: tokens[side][0, :, columns].astype(F32)
    stage.need(*range(7))
    add_context(place, h_ref, base, c_m, c_g, w_m, w_g)
    stage.done(0)
    plain, _ = normalize(h_ref[...])
    normed_ref[...] = (plain * rows_ref[1:2, :]).astype(LOW)
    stage.done(1)
    stage.need()
    q_ref[...] = dot_nn(normed_ref[...], wq[...]).astype(LOW)


def memory_kernel(packed, stage, *refs):
    if packed:
        index, first, later, patch_m, patch_g, k_ref, v_ref, wkv = refs
        stage.need(0, 1)
        place_blocks(index, first, later, [wkv])
        stage.done(2)
    else:
        wkv, patch_m, patch_g, k_ref, v_ref = refs
    stage.need()
    count = patch_m.shape[0]
    half = k_ref.shape[1]
    for side, source in enumerate((patch_m, patch_g)):
        value = dot_nn(source[...], wkv[...]).astype(LOW)
        k_ref[pl.ds(side * count, count), :] = value[:, :half]
        v_ref[pl.ds(side * count, count), :] = value[:, half:]


def lane_column(column, lane):
    lanes = lax.broadcasted_iota(jnp.int32, (1, PAIR_LANES), 1)
    return jnp.where(lanes == lane, column, 0.0)


def mlp_kernel(
    chunk,
    stage,
    place,
    h_in,
    c_m,
    c_g,
    out_m,
    out_g,
    rows_ref,
    cols_ref,
    g_m,
    g_g,
    w_ref,
    h_ref,
    part_ref,
    keep_ref,
    give_ref,
    gain_ref,
    grad_ref,
    gate_w,
    up_w,
    down_w,
    a_ref,
    t_ref,
    g_ref,
    p_acc,
    d_acc,
    r_acc,
    sems,
):
    blocks, pieces, piece, units = gate_w.shape
    down_pieces, width = down_w.shape[1], down_w.shape[3]
    total = blocks * pieces * piece
    own = g_m.shape[0]
    moves = []
    for number in range(pieces):
        moves.append((w_ref.at[:, :, pl.ds(number * units, units)], gate_w.at[:, number]))
    for number in range(pieces):
        moves.append((w_ref.at[:, :, pl.ds((pieces + number) * units, units)], up_w.at[:, number]))
    base = 2 * pieces * units
    for number in range(down_pieces):
        moves.append((w_ref.at[:, :, pl.ds(base + number * width, width)], down_w.at[:, number]))
    copies = [pltpu.make_async_copy(a, b, sems.at[i]) for i, (a, b) in enumerate(moves)]
    for copy in copies:
        copy.start()
    stage.need(*range(6))
    add_context(
        place, h_ref, lambda side, columns: h_in[pl.ds(side * own, own), columns], c_m, c_g, out_m, out_g
    )
    stage.done(0)
    plain, _ = normalize(h_ref[...])
    a_ref[...] = (plain * rows_ref[2:3, :]).astype(LOW)
    t_ref[...] = a_ref[...].T
    stage.need()
    g_ref[pl.ds(0, own), :] = g_m[...]
    g_ref[pl.ds(own, own), :] = g_g[...]
    p_acc[...] = jnp.zeros(p_acc.shape, F32)
    d_acc[...] = jnp.zeros(d_acc.shape, F32)
    r_acc[...] = jnp.zeros(r_acc.shape, F32)
    for copy in copies:
        copy.wait()

    per_block = down_pieces * piece
    step_blocks = chunk // per_block

    @pl.loop(0, units // chunk)
    def _(step):
        start = pl.multiple_of(step * chunk, chunk)
        a_in = a_ref[...]
        g_in = g_ref[...]
        columns = pl.ds(start, chunk)
        gate_part = gate_w[:, :, :, columns].reshape(total, chunk)
        up_part = up_w[:, :, :, columns].reshape(total, chunk)
        down_at = pl.ds(step * step_blocks, step_blocks)
        down_part = down_w[down_at].reshape(chunk, width)
        gate = dot_nn(a_in, gate_part)
        up = dot_nn(a_in, up_part)
        active, slope = gelu_parts(gate)
        mixed = (active * up).astype(LOW)
        grad = dot_nt(g_in, down_part)
        gate_low = (grad * up * slope).astype(LOW)
        up_low = (grad * active).astype(LOW)
        d_acc[...] += dot_nn(mixed, down_part)
        p_acc[...] += dot_nt(gate_low, gate_part) + dot_nt(up_low, up_part)
        dgate = dot_nn(t_ref[...], gate_low)
        dup = dot_nn(t_ref[...], up_low)
        gain_terms = dgate * gate_part.astype(F32) + dup * up_part.astype(F32)
        for lane in range(0, chunk, PAIR_LANES):
            r_acc[...] += gain_terms[:, lane : lane + PAIR_LANES]
        dgate = dgate.astype(LOW).reshape(blocks, pieces, piece, chunk)
        dup = dup.astype(LOW).reshape(blocks, pieces, piece, chunk)
        for number in range(pieces):
            gate_at = pl.multiple_of(number * units + start, chunk)
            up_at = pl.multiple_of((pieces + number) * units + start, chunk)
            grad_ref[:, :, pl.ds(gate_at, chunk)] = dgate[:, number]
            grad_ref[:, :, pl.ds(up_at, chunk)] = dup[:, number]
        ddown = dot_tn(mixed, g_in).astype(LOW).reshape(step_blocks, down_pieces, piece, width)
        for number in range(down_pieces):
            grad_ref[down_at, :, pl.ds(base + number * width, width)] = ddown[:, number]

    stage.done(5)
    part_ref[...] = p_acc[...].astype(LOW)
    stage.done(1)
    keep_ref[...] = d_acc[pl.ds(0, own), :]
    give_ref[...] = d_acc[pl.ds(own, own), :].astype(LOW)
    summed = jnp.sum(r_acc[...], axis=1, keepdims=True)
    gain_ref[...] = lane_column(summed / cols_ref[:, 2:3].astype(F32), 2)


def branch_kernel(gain_at, stage, place, *refs):
    h_ref, rows_ref, part_m, part_g, w_m, w_g = refs[:6]
    base, (d_ref, low_ref, c_ref) = refs[6:-3], refs[-3:]
    rows = h_ref.shape[0]
    own = rows // 2
    half = w_m.shape[1]
    mine, other = head_slices(place, half)
    stage.need(0, 1, 2, 3, *range(6, 6 + len(base)))
    for side in range(2):
        at = pl.ds(side * own, own)
        plain, inverse = normalize(h_ref[at, :])
        got = part_g[pl.ds((1 - side) * own, own), :]
        grads = part_m[at, :].astype(F32) + got.astype(F32)
        value = norm_back(plain, inverse, rows_ref[gain_at : gain_at + 1, :], grads)
        before = base[side][...].astype(F32) if len(base) == 2 else base[0][at, :]
        d_ref[at, :] = before + value
    stage.done(0)
    low_ref[...] = d_ref[...].astype(LOW)
    stage.done(1)
    stage.need()
    value = dot_nt(low_ref[:, mine], w_m[mine, :]) + dot_nt(low_ref[:, other], w_g[mine, :])
    c_ref[...] = value.astype(LOW)


def dot_rows(left, right):
    columns = left.shape[1]
    step = math.gcd(columns, 256)
    return [(i, dot_tn(left[:, i : i + step], right)) for i in range(0, columns, step)]


def out_grad(place, whole, cut, c_m, c_g, branch):
    rows, half = c_m.shape
    own = rows // 2
    mine, other = head_slices(place, half)
    grads = branch[:, mine]
    columns = pl.ds(cut, half)
    whole[mine, columns] = dot_tn(c_m[...], grads).astype(LOW)
    value = dot_tn(c_g[pl.ds(own, own), :], grads[:own]) + dot_tn(c_g[pl.ds(0, own), :], grads[own:])
    whole[other, columns] = value.astype(LOW)


def weight_grads(targets, lefts, rights, gain_acc=None):
    features = lefts[0].shape[1]
    step = math.gcd(features, 256)

    for number in range(features // step):
        at = pl.ds(number * step, step)
        turned = [left[:, at].T for left in lefts]
        for (whole, cut, weight), terms in zip(targets, rights):
            width = terms[0].shape[1]
            value = sum(dot_nn(left, right[...]) for left, right in zip(turned, terms))
            whole[at, pl.ds(cut, width)] = value.astype(LOW)
            if weight is not None:
                products = value * weight[at, :].astype(F32)
                gain_acc[at, :] += sum(
                    products[:, lane : lane + PAIR_LANES] for lane in range(0, width, PAIR_LANES)
                )


def cross_grads_kernel(packed, stage, place, *refs):
    index, refs = (refs[:2], refs[2:]) if packed else ((), refs)
    c_m, c_g, branch, normed, dq, patch_m, patch_g, dk, dv, wq, cols_ref = refs[:11]
    one_m, one_g, branch_one = refs[11:14]
    gain_ref, *outs, whole_a, whole_b, gain_acc = refs[14:]
    half = dq.shape[1]
    stage.need(0, 1, 2, 3, 4, 9, 10, 11, 12, 13)
    out_grad(place, whole_a, 2 * half, one_m, one_g, branch_one)
    count = patch_m.shape[0]
    gain_acc[...] = jnp.zeros(gain_acc.shape, F32)
    out_grad(place, whole_a, 0, c_m, c_g, branch)
    weight_grads([(whole_a, half, wq)], [normed], [[dq]], gain_acc)
    if packed:
        send_order(index[0], whole_a, outs[0], outs[1])
        stage.done(1, 2)
    summed = jnp.sum(gain_acc[...], axis=1, keepdims=True)
    gain_ref[...] = lane_column(summed / cols_ref[:, 1:2].astype(F32), 1)
    stage.need()
    halves = [[g.at[pl.ds(i * count, count), :] for i in range(2)] for g in (dk, dv)]
    weight_grads(
        [(whole_b, 0, None), (whole_b, half, None)], [patch_m, patch_g], halves
    )
    if packed:
        send_order(index[1], whole_b, outs[2], outs[3])


def self_grads_kernel(packed, stage, place, *refs):
    index, refs = (refs[:2], refs[2:]) if packed else ((), refs)
    normed, dq, dk, dv, wq, wkv, cols_ref, gain_two, gain_three = refs[:9]
    *outs, whole_a, whole_b, gain_acc = refs[9:]
    rows, half = dq.shape
    gain_acc[...] = jnp.zeros(gain_acc.shape, F32)
    stage.need(0, 3, 5)
    weight_grads([(whole_b, 0, wkv.at[:, pl.ds(half, half)])], [normed], [[dv]], gain_acc)
    stage.need(2)
    weight_grads([(whole_b, half, wkv.at[:, pl.ds(0, half)])], [normed], [[dk]], gain_acc)
    if packed:
        send_order(index[1], whole_b, outs[2], outs[3])
        stage.done(2, 3)
    stage.need()
    weight_grads([(whole_a, 0, wq)], [normed.at[pl.ds(0, rows), :]], [[dq]], gain_acc)
    summed = jnp.sum(gain_acc[...], axis=1, keepdims=True)
    gains = lane_column(summed / cols_ref[:, 0:1].astype(F32), 0) + gain_two[...] + gain_three[...]
    whole_a[:, pl.ds(half, PAIR_LANES)] = gains.astype(LOW)
    if packed:
        send_order(index[0], whole_a, outs[0], outs[1])


def back_kernel(grads, weight, out):
    out[...] = dot_nt(grads[...], weight[...]).astype(LOW)


def rows_back_kernel(spans, with_query, *refs):
    dk, dv, wkv = refs[:3]
    queries = refs[3:5] if with_query else None
    half = dk.shape[1]
    wk, wv = wkv.at[:, pl.ds(0, half)], wkv.at[:, pl.ds(half, half)]
    keep, give = refs[-2:]
    rows = dk.shape[0] // len(spans)
    for number, (mine, place) in enumerate(spans):
        at = pl.ds(number * rows, rows)
        value = dot_nt(dk[at, :], wk[...]) + dot_nt(dv[at, :], wv[...])
        if queries and number < 2:
            value = value + dot_nt(queries[0][at, :], queries[1][...])
        if mine:
            keep[place] = value
        else:
            give[place] = value.astype(LOW)


def feed_forward_grads_kernel(pieces, units, place, sums, got, gate_ref, up_ref, down_ref):
    piece = sums.shape[0]
    rows = got.shape[0]
    hidden = got.shape[1] // 2
    step = 8

    def write(second):
        for row in range(0, rows, step):
            at = row + (rows if second else 0)
            number, inner = at // piece, at % piece
            for matrix, target in enumerate((gate_ref, up_ref)):
                start = (matrix * pieces + number) * hidden
                mine = sums[pl.ds(inner, step), pl.ds(start, hidden)].astype(F32)
                other = got[pl.ds(row, step), pl.ds(matrix * hidden, hidden)].astype(F32)
                pair = (other, mine) if second else (mine, other)
                for unit in range(0, hidden, units):
                    tile = jnp.concatenate([part[:, unit : unit + units] for part in pair], axis=1)
                    target[pl.ds(row, step), pl.ds(2 * unit, 2 * units)] = tile

    @pl.when(place[0] == 0)
    def _():
        write(False)

    @pl.when(place[0] != 0)
    def _():
        write(True)

    base = 2 * pieces * hidden
    width = down_ref.shape[1]
    for number in range(down_ref.shape[0] // piece):
        down_ref[pl.ds(number * piece, piece), :] = sums[:, pl.ds(base + number * width, width)].astype(F32)


def columns_kernel(place, keep, got, *targets):
    rows = got.shape[0]

    def write(start, first, later):
        for number, target in enumerate(targets):
            half = target.shape[1] // 2
            columns = pl.ds(number * half, half)
            target[:, pl.ds(0, half)] = first(start, columns)
            target[:, pl.ds(half, half)] = later(start, columns)

    from_keep = lambda start, columns: keep[pl.ds(start, rows), columns]
    from_got = lambda start, columns: got[:, columns]

    @pl.when(place[0] == 0)
    def _():
        write(0, from_keep, from_got)

    @pl.when(place[0] != 0)
    def _():
        write(rows, from_got, from_keep)


def after(values, *others):
    return lax.optimization_barrier((values, *others))[0]


def together(*values):
    return lax.optimization_barrier(values)


class Ring:
    def __init__(self):
        self.charts = lax.axis_size("dp")
        self.groups = lax.axis_size("hx")
        self.half = lax.axis_index("hc").astype(jnp.int32)
        self.second = self.half == 1
        self.place = self.half[None]
        self.group = lax.axis_index("hx").astype(jnp.int32)
        self.block = lax.axis_index("dp").astype(jnp.int32) * self.groups + self.group
        self.blocks = self.charts * self.groups
        chart_bits = [("dp", 1 << i) for i in range(self.charts.bit_length() - 1)]
        self.group_bits = [("hx", 1 << i) for i in range(self.groups.bit_length() - 1)]
        self.far = chart_bits[:0:-1]
        near = chart_bits[:1]
        self.tails = (near + self.group_bits, self.group_bits + near)
        self.orders = tuple(self.far + tail for tail in self.tails)

    def send(self, values, axis, bit):
        size = self.charts if axis == "dp" else self.groups
        return lax.ppermute(values, axis, [(i, i ^ bit) for i in range(size)])

    def swap(self, values):
        return lax.ppermute(values, "hc", [(0, 1), (1, 0)])

    def in_order(self, mine, other):
        return jnp.where(self.second, other, mine), jnp.where(self.second, mine, other)

    def steps(self, order):
        return [bit * self.groups if axis == "dp" else bit for axis, bit in order]

    def arrivals(self):
        apart = self.block ^ jnp.arange(self.blocks, dtype=jnp.int32)
        indices = []
        for order in self.orders:
            index = jnp.zeros((self.blocks,), jnp.int32)
            for place, step in enumerate(self.steps(order)):
                index = index + jnp.where((apart & step) != 0, 1 << place, 0)
            indices.append(index)
        return indices

    def origins(self):
        indices = []
        for order in self.orders:
            masks = [0]
            for step in self.steps(order):
                masks = masks + [m ^ step for m in masks]
            indices.append(self.block ^ jnp.asarray(masks, jnp.int32))
        return indices

    def far_masks(self):
        masks = [0]
        for _, bit in self.far:
            masks = masks + [m | bit for m in masks]
        return masks

    def far_step(self, blocks, step):
        return jnp.concatenate([blocks, self.send(blocks, *self.far[step])], axis=0)

    def near_step(self, parts, step):
        return [self.send(part, *tail[step]) for part, tail in zip(parts, self.tails)]

    def near_sends(self, gives, place):
        return [self.send(give, *tail[place]) for give, tail in zip(gives, self.tails)]

    def near_sums(self, keeps, gots, place):
        halves = [got.shape[0] // 2 for got in gots]
        add = lambda k, g: (k.astype(F32) + g.astype(F32)).astype(LOW)
        gives = [add(k[h:], g[h:]) for k, g, h in zip(keeps, gots, halves)]
        keeps = [add(k[:h], g[:h]) for k, g, h in zip(keeps, gots, halves)]
        return keeps, gives

    def far_sends(self, keeps, gots):
        count = 1 << len(self.far)
        add = lambda r: [
            k[r : r + 1].astype(F32) + g[r : r + 1].astype(F32) for k, g in zip(keeps, gots)
        ]
        block = lambda r: jnp.concatenate(add(r), axis=2)
        if len(self.far) == 2:
            masks = self.far_masks()
            return block(0), [self.send(block(r).astype(LOW), "dp", masks[r]) for r in range(1, count)]
        keep = jnp.concatenate([block(r) for r in range(count)], axis=0)
        for axis, bit in reversed(self.far[1:]):
            half = keep.shape[0] // 2
            keep = keep[:half] + self.send(keep[half:].astype(LOW), axis, bit).astype(F32)
        return keep[:1], [self.send(keep[1:].astype(LOW), *self.far[0])]

    def far_sum(self, own, gots):
        return sum((got.astype(F32) for got in gots), own)[0]

    def far_first(self, keeps, gots):
        count = 1 << len(self.far)
        add = lambda r: jnp.concatenate(
            [k[r].astype(F32) + g[r].astype(F32) for k, g in zip(keeps, gots)], axis=2
        )
        keep, give = add(slice(0, count // 2)), add(slice(count // 2, None)).astype(LOW)
        return keep, self.send(give, *self.far[-1])

    def far_last(self, keep, got):
        for axis, bit in reversed(self.far[:-1]):
            half = keep.shape[0] // 2
            give = (keep[half:] + got[half:].astype(F32)).astype(LOW)
            keep = keep[:half] + got[:half].astype(F32)
            got = self.send(give, axis, bit)
        return keep, [got]

    def halve_wholes(self, wholes, rows):
        keeps, gives = [], []
        for whole, index in zip(wholes, self.origins()):
            blocks = jnp.take(whole.reshape(self.blocks, rows, -1), index, axis=0)
            keeps.append(blocks[: self.blocks // 2])
            gives.append(blocks[self.blocks // 2 :])
        return keeps, gives

    def across(self, mine):
        rows = mine[None]
        for axis, bit in self.group_bits:
            rows = jnp.concatenate([rows, self.send(rows, axis, bit)], axis=0)
        return rows

    def halves(self, first, later):
        mine = jnp.where(self.second, later, first)
        give = jnp.where(self.second, first, later)
        return jnp.concatenate(self.in_order(mine, self.swap(give)), axis=0)

    def pair_sum(self, keep, give):
        return keep + self.swap(give.astype(LOW)).astype(F32)

    def group_terms(self, total):
        for axis, bit in reversed(self.group_bits):
            middle = total.shape[0] // 2
            total = total[:middle] + self.send(total[middle:].astype(LOW), axis, bit).astype(F32)
        return total[0]

    def finished(self, keep, count):
        rows = keep.shape[0] // 2
        give = lax.dynamic_slice_in_dim(keep, (1 - self.half) * rows, rows, 0)
        got = self.swap(give)
        width = keep.shape[1] // count * 2
        return run_kernel(
            columns_kernel, [full_shape(rows, width)] * count, rows * width, [self.place], [keep, got]
        )


def column_halves(weights):
    half = weights[0].shape[1] // 2
    return [jnp.concatenate([w[:, i * half : (i + 1) * half] for w in weights], axis=1) for i in range(2)]


def unit_halves(weight, units):
    rows, columns = weight.shape
    split = weight.reshape(rows, columns // (2 * units), 2, units)
    return split[:, :, 0].reshape(rows, -1), split[:, :, 1].reshape(rows, -1)


def unit_whole(first, later, units):
    rows, columns = first.shape
    pieces = [part.reshape(rows, columns // units, 1, units) for part in (first, later)]
    return jnp.concatenate(pieces, axis=2).reshape(rows, 2 * columns)


def on_device(
    tokens,
    memory,
    text_length,
    patch_count,
    self_gain,
    self_query,
    self_key,
    self_value,
    self_out,
    cross_gain,
    cross_query,
    cross_key,
    cross_value,
    cross_out,
    mlp_gain,
    mlp_gate,
    mlp_up,
    mlp_down,
    output_grad,
):
    ring = Ring()
    place = ring.place
    width = tokens.shape[-1]
    half = width // 2
    units = mlp_down.shape[0]
    hidden_half = units * ring.blocks
    rows = self_query.shape[0]
    own = tokens.shape[1]
    own_patches = memory.shape[1]
    both = 2 * own
    keys = both * ring.groups
    patches = 2 * own_patches * ring.groups
    piece = 16
    packed = (2 * rows) % piece == 0 and units == HEAD_DIM and ring.blocks > 1
    pieces, down_pieces = 2 * rows // piece, units // piece
    pairs = ("dp", "hx")
    index_in = tuple(ring.arrivals()) if packed else ()
    index_out = tuple(ring.origins()) if packed else ()
    index_specs = [SMEM_SPEC] * len(index_in)
    block_rows = 2 * rows

    gain_columns = jnp.stack([self_gain, cross_gain, mlp_gain], axis=1)
    gain_columns = jnp.pad(gain_columns, ((0, 0), (0, PAIR_LANES - 3)))
    chains = ([self_query, gain_columns, self_out, cross_query], [self_key, self_value, cross_key, cross_value])
    splits = (half + PAIR_LANES, 2 * half)
    cut_all = 3 * half + PAIR_LANES
    packed_columns = (2 * hidden_half) * pieces + width * down_pieces
    widths_one = ([half, PAIR_LANES], [width])
    widths_two = ([half] * 2, [width])

    if packed:
        kinds = ["all" if w is gain_columns else "half" for w in chains[0] + chains[1]]
        mine, give = cut_shards(place, chains[0] + chains[1], kinds)
        blocks = jnp.concatenate(ring.in_order(mine, ring.swap(give)), axis=0)[None]
    else:
        sides = [
            jnp.concatenate(
                [w if w is gain_columns else column_halves([w])[i] for w in chains[0] + chains[1]],
                axis=1,
            )
            for i in range(2)
        ]
        blocks = ring.halves(*sides)[None]
    middle = own_patches // 2
    token_m = ring.across(tokens[0])
    patch_a = ring.across(memory[0, :middle])
    if packed:
        rest = after([mlp_gate, mlp_up, cross_out], blocks)
        mine, give = cut_shards(place, rest, ["units"] * 2 + ["half"])
        blocks_mlp = join_rows(place, mine, ring.swap(give), mlp_down, [], half, piece)[0]
    else:
        gate_halves, up_halves = unit_halves(mlp_gate, units), unit_halves(mlp_up, units)
        rest = [
            jnp.concatenate([gate_halves[i], up_halves[i], column_halves([cross_out])[i]], axis=1)
            for i in range(2)
        ]
        gate_up = lax.all_gather(ring.halves(*rest), pairs, axis=0, tiled=True)
        down_three = lax.all_gather(mlp_down, pairs, axis=0, tiled=True)
        out_two = gate_up[:, 2 * hidden_half :]
    blocks = ring.far_step(blocks, 0)
    blocks, token_m, memory = together(blocks, token_m, memory)
    if packed:
        mlp_weights = lax.all_gather(after(blocks_mlp, blocks), pairs, axis=0, tiled=True)
        mlp_weights = mlp_weights.reshape(ring.blocks, piece, -1)
    patch_b = ring.across(memory[0, middle:])
    for step in range(1, len(ring.far)):
        blocks = ring.far_step(blocks, step)
    blocks, patch_a, token_m = together(blocks, patch_a, token_m)
    parts = [blocks[:, :, :cut_all], blocks[:, :, cut_all:]]
    token_g = ring.swap(token_m)
    last = len(ring.tails[0]) - 1
    for step in range(last):
        got = ring.near_step(parts, step)
        parts = [jnp.concatenate(pair, axis=0) for pair in zip(parts, got)]
    parts, token_g, patch_b = together(parts, token_g, patch_b)
    parts_one = [part[:, :, :split] for part, split in zip(parts, splits)]
    parts_two = [part[:, :, split:] for part, split in zip(parts, splits)]
    near_one = ring.near_step(parts_one, last)
    patch_m = jnp.concatenate([patch_a, patch_b], axis=1)
    patch_g = ring.swap(patch_m)
    near_one, parts_two, patch_g = together(near_one, parts_two, patch_g)
    near_two = ring.near_step(parts_two, last)
    near_one = (parts_one[0], near_one[0], parts_one[1], near_one[1])
    arrivals = ring.arrivals()

    token_chunk = math.gcd(256, own)
    patch_chunk = math.gcd(256, own_patches)

    def chunk_starts(span, chunk, side_first):
        groups = ring.group ^ jnp.arange(ring.groups, dtype=jnp.int32)
        sides = ring.half ^ jnp.arange(2, dtype=jnp.int32)
        inner = jnp.arange(span // chunk, dtype=jnp.int32) * chunk
        if side_first:
            starts = groups[None, :, None] * 2 * span + sides[:, None, None] * span
        else:
            starts = groups[:, None, None] * 2 * span + sides[None, :, None] * span
        return (starts + inner).reshape(-1)

    fixed = jnp.stack([ring.group * both, ring.half])
    info_one = jnp.concatenate([text_length, fixed, chunk_starts(own, token_chunk, False)])
    info_two = jnp.concatenate([patch_count, fixed, chunk_starts(own_patches, patch_chunk, True)])

    head_shapes = [low_shape(both, half), low_shape(keys, half), low_shape(keys, half)]
    query_outs = [full_shape(8, width), low_shape(keys, width), *head_shapes]
    projections = [low_shape(width, w) for w in widths_one[0] + widths_one[1]]
    cost = keys * width * half
    if packed:
        outs = run_kernel(
            functools.partial(query_kernel, True),
            query_outs + projections,
            cost,
            index_in,
            [*near_one, token_m, token_g],
            late=True,
        )
        gain_rows, normed_one, query_heads, key_heads, value_heads = outs[:5]
        query_one, gain_cols, heads_one = outs[5:]
    else:
        query_one, gain_cols = to_whole(near_one[0], near_one[1], arrivals[0], widths_one[0])
        (heads_one,) = to_whole(near_one[2], near_one[3], arrivals[1], widths_one[1])
        gain_rows, normed_one, query_heads, key_heads, value_heads = run_kernel(
            functools.partial(query_kernel, False),
            query_outs,
            cost,
            [],
            [query_one, gain_cols, heads_one, token_m, token_g],
            late=True,
        )
    near_one = None
    grad_g = ring.swap(after(output_grad[0], query_heads))
    context_one, lse_one = attention_forward(
        info_one, query_heads, key_heads, value_heads, True, token_chunk
    )
    context_one, near_a, near_b, grad_g = together(context_one, *near_two, grad_g)
    context_one_g = ring.swap(context_one)
    out_one, query_two = to_whole(parts_two[0], near_a, arrivals[0], widths_two[0])
    out_one_g = ring.swap(out_one)
    patch_all = [part.reshape(-1, width) for part in (patch_m, patch_g)]
    memory_heads = [low_shape(patches, half)] * 2
    if packed:
        memory_keys, memory_values, heads_two = run_kernel(
            functools.partial(memory_kernel, True),
            memory_heads + [low_shape(width, width)],
            patches * width * half,
            index_in[1:],
            [parts_two[1], near_b, *patch_all],
            late=True,
        )
    else:
        (heads_two,) = to_whole(parts_two[1], near_b, arrivals[1], widths_two[1])
        memory_keys, memory_values = run_kernel(
            functools.partial(memory_kernel, False),
            memory_heads,
            patches * width * half,
            [],
            [heads_two, *patch_all],
            late=True,
        )
    context_one_g, memory_keys = together(context_one_g, memory_keys)
    hidden_one, normed_two, cross_heads = run_kernel(
        cross_query_kernel,
        [full_shape(both, width), low_shape(both, width), low_shape(both, half)],
        both * width * half,
        [place],
        [token_m, token_g, context_one, context_one_g, out_one, out_one_g, gain_rows, query_two],
        late=True,
    )
    if packed:
        out_two = from_pieces(after(mlp_weights, cross_heads), packed_columns, pieces, half)
    cross_heads, out_two = together(cross_heads, out_two)
    out_two_g = ring.swap(out_two)
    context_two, lse_two = attention_forward(
        info_two, cross_heads, memory_keys, memory_values, False, patch_chunk
    )
    context_two_g = ring.swap(context_two)
    if packed:
        hidden_two, part_low, down_keep, down_give, gain_three, mlp_terms = run_kernel(
            functools.partial(mlp_kernel, 1024),
            [
                full_shape(both, width),
                low_shape(both, width),
                full_shape(own, width),
                low_shape(own, width),
                full_shape(width, PAIR_LANES),
                low_shape(ring.blocks, piece, packed_columns),
            ],
            2 * both * width * hidden_half,
            [place],
            [
                hidden_one,
                context_two,
                context_two_g,
                out_two,
                out_two_g,
                gain_rows,
                gain_cols,
                output_grad[0],
                grad_g,
            ],
            [
                pltpu.VMEM((ring.blocks, pieces, piece, hidden_half), LOW),
                pltpu.VMEM((ring.blocks, pieces, piece, hidden_half), LOW),
                pltpu.VMEM((ring.blocks, down_pieces, piece, width), LOW),
                pltpu.VMEM((both, width), LOW),
                pltpu.VMEM((width, both), LOW),
                pltpu.VMEM((both, width), LOW),
                pltpu.VMEM((both, width), F32),
                pltpu.VMEM((both, width), F32),
                pltpu.VMEM((width, PAIR_LANES), F32),
                pltpu.SemaphoreType.DMA((2 * pieces + down_pieces,)),
            ],
            [mlp_weights],
            late=True,
        )
        mlp_terms = mlp_terms.reshape(ring.blocks * piece, -1)
        mlp_sum = lax.psum_scatter(mlp_terms, pairs, scatter_dimension=0, tiled=True)
    else:
        joined = jnp.concatenate(ring.in_order(out_two, out_two_g), axis=1)
        swapped = jnp.concatenate([context_two_g[own:], context_two_g[:own]], axis=0)
        context = jnp.concatenate(ring.in_order(context_two, swapped), axis=1)
        hidden_two = hidden_one + dot_nn(context, joined)
        normed_three = (normalize(hidden_two)[0] * gain_rows[2:3]).astype(LOW)
        grad_low = jnp.concatenate([output_grad[0], grad_g], axis=0)
        gate_up = gate_up[:, : 2 * hidden_half]
        gate_three, up_three = gate_up[:, :hidden_half], gate_up[:, hidden_half:]
        active, slope = gelu_parts(dot_nn(normed_three, gate_three))
        up = dot_nn(normed_three, up_three)
        mixed = (active * up).astype(LOW)
        down_part = dot_nn(mixed, down_three)
        down_keep, down_give = down_part[:own], down_part[own:].astype(LOW)
        grad_mixed = dot_nt(grad_low, down_three)
        gate_low = (grad_mixed * up * slope).astype(LOW)
        up_low = (grad_mixed * active).astype(LOW)
        part_low = (dot_nt(gate_low, gate_three) + dot_nt(up_low, up_three)).astype(LOW)
        terms = jnp.concatenate(
            [dot_tn(normed_three, gate_low), dot_tn(normed_three, up_low)], axis=1
        )
        column = jnp.sum(terms * gate_up.astype(F32), axis=1, keepdims=True)
        gain_three = lane_column(column / gain_cols[:, 2:3].astype(F32), 2)
        gate_up = lax.psum_scatter(terms, pairs, scatter_dimension=0, tiled=True)
        mlp_ddown = lax.psum_scatter(
            dot_tn(mixed, grad_low), pairs, scatter_dimension=0, tiled=True
        )

    part_g = ring.swap(part_low)
    down_got = ring.swap(down_give)
    output = (hidden_two[:own] + down_keep + down_got.astype(F32)).astype(LOW)

    def branch(gain_at, hidden, mine, got, weight_m, weight_g, base):
        return run_kernel(
            functools.partial(branch_kernel, gain_at),
            [full_shape(both, width), low_shape(both, width), low_shape(both, half)],
            both * width * half,
            [place],
            [hidden, gain_rows, mine, got, weight_m, weight_g, *base],
            late=True,
        )

    dhidden_two, branch_two, dcontext_two = branch(
        2, hidden_two, part_low, part_g, out_two, out_two_g, [output_grad[0], grad_g]
    )
    dquery, dkey, dvalue = attention_backward(
        info_two,
        cross_heads,
        memory_keys,
        memory_values,
        context_two,
        dcontext_two,
        lse_two,
        False,
        patch_chunk,
    )
    (part_low,) = run_kernel(
        back_kernel, [low_shape(both, width)], both * width, [], [dquery, query_two]
    )
    part_g = ring.swap(part_low)

    count = ring.blocks // 2

    def grads(body, inputs, columns, gain_outs, cost):
        scratch = [pltpu.VMEM((width, c), LOW) for c in columns]
        acc = pltpu.VMEM((width, PAIR_LANES), F32)
        if packed:
            shapes = [low_shape(count, block_rows, c) for c in columns for _ in range(2)]
            outs = run_kernel(
                functools.partial(body, True),
                gain_outs + shapes,
                cost,
                [place, *index_out],
                inputs,
                scratch + [acc],
                late=True,
            )
            blocks = outs[len(gain_outs) :]
            return outs[: len(gain_outs)], blocks[0::2], blocks[1::2]
        wholes = [low_shape(width, c) for c in columns]
        outs = run_kernel(
            functools.partial(body, False), gain_outs + wholes, cost, [place], inputs, [acc], late=True
        )
        return outs[: len(gain_outs)], *ring.halve_wholes(outs[len(gain_outs) :], block_rows)

    patch_spans = [(side == 0, g) for side in range(2) for g in range(ring.groups)]
    patch_shape = (ring.groups, own_patches, width)
    memory_keep, memory_give = run_kernel(
        functools.partial(rows_back_kernel, patch_spans, False),
        [full_shape(*patch_shape), low_shape(*patch_shape)],
        patches * width,
        [],
        [dkey, dvalue, heads_two],
    )
    memory_total = ring.pair_sum(memory_keep, memory_give)
    part_g, memory_total = together(part_g, memory_total)
    memory_sent = ring.group_terms(memory_total)
    dhidden_one, branch_one, dcontext_one = branch(
        1, hidden_one, part_low, part_g, out_one, out_one_g, [dhidden_two]
    )
    (gain_two,), cross_keep, cross_give = grads(
        cross_grads_kernel,
        [
            context_two,
            context_two_g,
            branch_two,
            normed_two,
            dquery,
            *patch_all,
            dkey,
            dvalue,
            query_two,
            gain_cols,
            context_one,
            context_one_g,
            branch_one,
        ],
        (3 * half, 2 * half),
        [full_shape(width, PAIR_LANES)],
        (both + patches) * width * half,
    )
    cross_got = ring.near_sends(cross_give, last)
    cross_keep, dcontext_one = together(cross_keep, dcontext_one)

    dquery_one, dkey_one, dvalue_one = attention_backward(
        info_one,
        query_heads,
        key_heads,
        value_heads,
        context_one,
        dcontext_one,
        lse_one,
        True,
        token_chunk,
    )
    dquery_one, dkey_one, dvalue_one, cross_got, memory_grad, output = together(
        dquery_one, dkey_one, dvalue_one, cross_got, memory_sent, output
    )
    for step in reversed(range(1, last + 1)):
        cross_keep, cross_give = ring.near_sums(cross_keep, cross_got, step)
        cross_got = ring.near_sends(cross_give, step - 1)
    dquery_one, cross_give = together(dquery_one, cross_give)
    _, self_keep, self_give = grads(
        self_grads_kernel,
        [
            normed_one,
            dquery_one,
            dkey_one,
            dvalue_one,
            query_one,
            heads_one,
            gain_cols,
            gain_two,
            gain_three,
        ],
        (half + PAIR_LANES, 2 * half),
        [],
        (both + keys) * width * half,
    )
    self_give, cross_got = together(self_give, cross_got)
    self_got = ring.near_sends(self_give, last)
    cross_own, cross_far = ring.far_first(cross_keep, cross_got)
    dquery_one, dkey_one, dvalue_one = after((dquery_one, dkey_one, dvalue_one), self_give)
    token_spans = [(side == 0, g) for g in range(ring.groups) for side in range(2)]
    token_shape = (ring.groups, own, width)
    part_keep, part_give = run_kernel(
        functools.partial(rows_back_kernel, token_spans, True),
        [full_shape(*token_shape), low_shape(*token_shape)],
        keys * width,
        [],
        [dkey_one, dvalue_one, heads_one, dquery_one, query_one],
    )
    part_total = ring.pair_sum(part_keep, part_give)
    self_got, part_total = together(self_got, part_total)
    for step in reversed(range(1, last + 1)):
        self_keep, self_give = ring.near_sums(self_keep, self_got, step)
        self_got = ring.near_sends(self_give, step - 1)
    dnormed_one = ring.group_terms(part_total)
    self_got, cross_far = together(self_got, cross_far)
    self_own, self_far = ring.far_sends(self_keep, self_got)
    cross_own, cross_far = ring.far_last(cross_own, cross_far)
    plain, inverse = normalize(tokens[0].astype(F32))
    input_grad = dhidden_one[:own] + norm_back(plain, inverse, gain_rows[0:1], dnormed_one)

    if packed:
        mlp_rows = mlp_sum[:, : 2 * pieces * hidden_half].reshape(piece, 2, pieces, hidden_half)
        mlp_rows = mlp_rows.transpose(2, 0, 1, 3).reshape(2 * rows, 2 * hidden_half)
        mlp_give = lax.dynamic_slice_in_dim(mlp_rows, (1 - ring.half) * rows, rows, 0)
        mlp_dgate, mlp_dup, mlp_ddown = run_kernel(
            functools.partial(feed_forward_grads_kernel, pieces, units),
            [full_shape(rows, 2 * hidden_half)] * 2 + [full_shape(units, width)],
            rows * width,
            [place],
            [mlp_sum, ring.swap(mlp_give)],
        )
    else:
        (gate_up,) = ring.finished(gate_up, 1)
        gate_columns = [gate_up[:, i * hidden_half : (i + 1) * hidden_half] for i in range(4)]
        mlp_dgate = unit_whole(gate_columns[0], gate_columns[2], units)
        mlp_dup = unit_whole(gate_columns[1], gate_columns[3], units)
    cross_sum = ring.far_sum(cross_own, cross_far)
    cross_dout, cross_dquery, self_dout, cross_dkey, cross_dvalue = ring.finished(cross_sum, 5)
    self_far, mlp_dgate, mlp_dup, mlp_ddown, input_grad = together(
        self_far, mlp_dgate, mlp_dup, mlp_ddown, input_grad
    )
    self_sum = ring.far_sum(self_own, self_far)
    gain_block = self_sum[:, half : half + PAIR_LANES]
    gain_block = jnp.pad(gain_block, ((0, 0), (0, half - PAIR_LANES)))
    joined = jnp.concatenate(
        [self_sum[:, :half], self_sum[:, half + PAIR_LANES :], gain_block], axis=1
    )
    self_dquery, self_dvalue, self_dkey, gain_terms = ring.finished(joined, 4)
    dgains = gain_terms[:, :3] + gain_terms[:, half : half + 3]

    return (
        output[None],
        input_grad[None],
        memory_grad[None],
        dgains[:, 0],
        self_dquery,
        self_dkey,
        self_dvalue,
        self_dout,
        dgains[:, 1],
        cross_dquery,
        cross_dkey,
        cross_dvalue,
        cross_dout,
        dgains[:, 2],
        mlp_dgate,
        mlp_dup,
        mlp_ddown,
    )


def solution(mesh):
    charts, heads = mesh.devices.shape
    inner = Mesh(mesh.devices.reshape(charts, heads // 2, 2), ("dp", "hx", "hc"))
    every = ("dp", "hx", "hc")
    rows = P(every, None)
    vector = P(every)
    grid = P("dp", ("hx", "hc"), None)
    in_specs = (grid, grid, P("dp"), P("dp"))
    in_specs += (vector, rows, rows, rows, rows) * 2
    in_specs += (vector, rows, rows, rows, grid)
    out_specs = (grid, grid, grid)
    out_specs += (vector, rows, rows, rows, rows) * 2
    out_specs += (vector, rows, rows, rows)
    return jax.shard_map(
        on_device, mesh=inner, in_specs=in_specs, out_specs=out_specs, check_vma=False
    )
```

```python
import functools
import math

import jax
import jax.numpy as jnp
from jax import lax
from jax.experimental import pallas as pl
from jax.experimental.pallas import tpu as pltpu
from jax.sharding import Mesh
from jax.sharding import PartitionSpec as P

HEAD_DIM = 64
PAIR_LANES = 128
NEG_FILL = -1e30
EPS = 1e-06
F32 = jnp.float32
LOW = jnp.bfloat16


NT = (((1,), (1,)), ((), ()))
TN = (((0,), (0,)), ((), ()))


def dot_nt(left, right):
    return lax.dot_general(left, right, NT, preferred_element_type=F32)


def dot_tn(left, right):
    return lax.dot_general(left, right, TN, preferred_element_type=F32)


def dot_nn(left, right):
    return jnp.dot(left, right, preferred_element_type=F32)


FIXED = 3
SPANS = 8


def query_limits(info, queries, causal):
    last = info[0] - 1
    if not causal:
        return jnp.full((1, queries), last, jnp.int32), last
    lanes = lax.broadcasted_iota(jnp.int32, (1, queries), 1)
    span = queries // 2
    swapped = jnp.where(lanes < span, lanes + info[2] * span, lanes - info[2] * span)
    return jnp.minimum(info[1] + swapped, last), jnp.minimum(info[1] + queries - 1, last)


def key_places(info, chunk, span, queries, j):
    parts = chunk // span
    starts = [info[FIXED + j * parts + i] for i in range(parts)]
    inner = lax.broadcasted_iota(jnp.int32, (span, queries), 0)
    first = functools.reduce(jnp.minimum, starts)
    return jnp.concatenate([start + inner for start in starts], axis=0), first


def first_place(info, chunk, span, j):
    parts = chunk // span
    return functools.reduce(jnp.minimum, [info[FIXED + j * parts + i] for i in range(parts)])


def head_lanes(head):
    lanes = lax.broadcasted_iota(jnp.int32, (1, PAIR_LANES), 1)
    return (lanes // HEAD_DIM) == head


def fold(values, op):
    rows, columns = values.shape
    return op(values.reshape(rows // 8, 8, columns), axis=0)


def forward_kernel(causal, chunk, span, info, q_ref, k_ref, v_ref, c_ref, lse_ref, s_ref, m_ref, l_ref, a_ref):
    queries = q_ref.shape[0]
    chunks = k_ref.shape[0] // chunk
    scaling = 1.0 / math.sqrt(HEAD_DIM)
    limit, latest = query_limits(info, queries, causal)
    q_all = q_ref[...] * jnp.asarray(scaling, q_ref.dtype)
    q_heads = [jnp.where(head_lanes(h), q_all, jnp.zeros_like(q_all)) for h in range(2)]
    m_ref[...] = jnp.full(m_ref.shape, NEG_FILL, F32)
    l_ref[...] = jnp.zeros(l_ref.shape, F32)
    a_ref[...] = jnp.zeros(a_ref.shape, F32)

    @pl.loop(0, chunks)
    def _(j):
        @pl.when(first_place(info, chunk, span, j) <= latest)
        def _():
            rows = pl.ds(pl.multiple_of(j * chunk, chunk), chunk)
            keys = k_ref[rows, :]
            place, _ = key_places(info, chunk, span, queries, j)
            allowed = place <= limit
            for h in range(2):
                scores = jnp.where(allowed, dot_nt(keys, q_heads[h]), NEG_FILL)
                s_ref[h, rows, :] = scores
                m_ref[h] = jnp.maximum(m_ref[h], fold(scores, jnp.max))

    highest = [jnp.max(m_ref[h], axis=0, keepdims=True) for h in range(2)]

    @pl.loop(0, chunks)
    def _(j):
        @pl.when(first_place(info, chunk, span, j) <= latest)
        def _():
            rows = pl.ds(pl.multiple_of(j * chunk, chunk), chunk)
            values = v_ref[rows, :]
            for h in range(2):
                weight = jnp.exp(s_ref[h, rows, :] - highest[h])
                l_ref[h] = l_ref[h] + fold(weight, jnp.sum)
                a_ref[h] = a_ref[h] + dot_tn(values, weight.astype(LOW))

    parts = []
    for h in range(2):
        total = jnp.sum(l_ref[h], axis=0, keepdims=True)
        lse_ref[0, pl.ds(h, 1), :] = highest[h] + jnp.log(total)
        parts.append(a_ref[h, pl.ds(h * HEAD_DIM, HEAD_DIM), :] / total)
    c_ref[...] = jnp.concatenate(parts, axis=0).T.astype(c_ref.dtype)


def backward_kernel(causal, chunk, span, info, q_ref, k_ref, v_ref, c_ref, g_ref, lse_ref, dq_ref, dk_ref, dv_ref, a_ref):
    queries = q_ref.shape[0]
    chunks = k_ref.shape[0] // chunk
    scaling = 1.0 / math.sqrt(HEAD_DIM)
    limit, latest = query_limits(info, queries, causal)
    q_all = q_ref[...] * jnp.asarray(scaling, q_ref.dtype)
    g_all = g_ref[...]
    q_heads = [jnp.where(head_lanes(h), q_all, jnp.zeros_like(q_all)) for h in range(2)]
    g_heads = [jnp.where(head_lanes(h), g_all, jnp.zeros_like(g_all)) for h in range(2)]
    product = (c_ref[...].astype(F32) * g_all.astype(F32)).T
    centres = [
        jnp.sum(product[h * HEAD_DIM : (h + 1) * HEAD_DIM], axis=0, keepdims=True) for h in range(2)
    ]
    logs = [lse_ref[0, pl.ds(h, 1), :] for h in range(2)]
    a_ref[...] = jnp.zeros(a_ref.shape, F32)

    @pl.loop(0, chunks)
    def _(j):
        start = first_place(info, chunk, span, j)
        rows = pl.ds(pl.multiple_of(j * chunk, chunk), chunk)

        @pl.when(start <= latest)
        def _():
            keys = k_ref[rows, :]
            values = v_ref[rows, :]
            place, _ = key_places(info, chunk, span, queries, j)
            allowed = place <= limit
            dk = jnp.zeros((chunk, PAIR_LANES), F32)
            dv = jnp.zeros((chunk, PAIR_LANES), F32)
            for h in range(2):
                scores = jnp.where(allowed, dot_nt(keys, q_heads[h]), NEG_FILL)
                prob = jnp.exp(scores - logs[h])
                dprob = dot_nt(values, g_heads[h])
                dv = dv + dot_nn(prob.astype(LOW), g_heads[h])
                dscore = (prob * (dprob - centres[h])).astype(LOW)
                dk = dk + dot_nn(dscore, q_heads[h])
                a_ref[h] = a_ref[h] + dot_tn(keys, dscore)
            dk_ref[rows, :] = dk.astype(dk_ref.dtype)
            dv_ref[rows, :] = dv.astype(dv_ref.dtype)

        @pl.when(start > latest)
        def _():
            dk_ref[rows, :] = jnp.zeros((chunk, PAIR_LANES), dk_ref.dtype)
            dv_ref[rows, :] = jnp.zeros((chunk, PAIR_LANES), dv_ref.dtype)

    parts = [a_ref[h, pl.ds(h * HEAD_DIM, HEAD_DIM), :] for h in range(2)]
    dq_ref[...] = (jnp.concatenate(parts, axis=0).T * scaling).astype(dq_ref.dtype)


def lane_spec(rows):
    return pl.BlockSpec((rows, PAIR_LANES), lambda i, info: (0, i))


def stat_spec(queries):
    return pl.BlockSpec((1, 2, queries), lambda i, info: (i, 0, 0))


def attention_forward(info, queries, keys, values, causal, span):
    chunk = math.gcd(SPANS * span, keys.shape[0])
    rows, features = queries.shape
    key_rows = keys.shape[0]
    pairs = features // PAIR_LANES
    return pl.pallas_call(
        functools.partial(forward_kernel, causal, chunk, span),
        out_shape=(
            jax.ShapeDtypeStruct((rows, features), LOW),
            jax.ShapeDtypeStruct((pairs, 2, rows), F32),
        ),
        grid_spec=pltpu.PrefetchScalarGridSpec(
            num_scalar_prefetch=1,
            grid=(pairs,),
            in_specs=[lane_spec(rows), lane_spec(key_rows), lane_spec(key_rows)],
            out_specs=[lane_spec(rows), stat_spec(rows)],
            scratch_shapes=[
                pltpu.VMEM((2, key_rows, rows), F32),
                pltpu.VMEM((2, 8, rows), F32),
                pltpu.VMEM((2, 8, rows), F32),
                pltpu.VMEM((2, PAIR_LANES, rows), F32),
            ],
        ),
        compiler_params=pltpu.CompilerParams(vmem_limit_bytes=VMEM_LIMIT),
        cost_estimate=pl.CostEstimate(flops=rows, transcendentals=0, bytes_accessed=0),
    )(info, queries, keys, values)


def attention_backward(info, queries, keys, values, context, grads, lse, causal, span):
    chunk = math.gcd(SPANS * span, keys.shape[0])
    rows, features = queries.shape
    key_rows = keys.shape[0]
    pairs = features // PAIR_LANES
    return pl.pallas_call(
        functools.partial(backward_kernel, causal, chunk, span),
        out_shape=(
            jax.ShapeDtypeStruct((rows, features), LOW),
            jax.ShapeDtypeStruct((key_rows, features), LOW),
            jax.ShapeDtypeStruct((key_rows, features), LOW),
        ),
        grid_spec=pltpu.PrefetchScalarGridSpec(
            num_scalar_prefetch=1,
            grid=(pairs,),
            in_specs=[
                lane_spec(rows),
                lane_spec(key_rows),
                lane_spec(key_rows),
                lane_spec(rows),
                lane_spec(rows),
                stat_spec(rows),
            ],
            out_specs=[lane_spec(rows), lane_spec(key_rows), lane_spec(key_rows)],
            scratch_shapes=[pltpu.VMEM((2, PAIR_LANES, rows), F32)],
        ),
        compiler_params=pltpu.CompilerParams(vmem_limit_bytes=VMEM_LIMIT),
        cost_estimate=pl.CostEstimate(flops=rows, transcendentals=0, bytes_accessed=0),
    )(info, queries, keys, values, context, grads, lse)


SMEM_SPEC = pl.BlockSpec(memory_space=pltpu.SMEM)


def vmem_specs(number):
    return [pl.BlockSpec(memory_space=pltpu.VMEM)] * number


def cuts_of(widths):
    return [sum(widths[:i]) for i in range(len(widths))]


def place_blocks(index, first, later, targets):
    half, rows, _ = first.shape
    cuts = cuts_of([target.shape[1] for target in targets])

    @pl.loop(0, 2 * half)
    def _(step):
        at = index[step]
        place = pl.ds(pl.multiple_of(step * rows, rows), rows)

        def put(source, block):
            for cut, target in zip(cuts, targets):
                target[place, :] = source[block, :, pl.ds(cut, target.shape[1])]

        @pl.when(at < half)
        def _():
            put(first, at)

        @pl.when(at >= half)
        def _():
            put(later, at - half)


def send_order(index, whole, keep, give):
    half, rows, _ = keep.shape

    @pl.loop(0, half)
    def _(step):
        for side, target in enumerate((keep, give)):
            at = pl.ds(pl.multiple_of(index[step + side * half] * rows, rows), rows)
            target[step] = whole[at, :]


def whole_kernel(index, first, later, *targets):
    place_blocks(index, first, later, targets)


def to_whole(first, later, index, widths):
    half, rows, columns = first.shape
    count = 2 * half
    if rows % 16:
        blocks = jnp.concatenate([first, later], axis=0)
        whole = jnp.take(blocks, index, axis=0).reshape(count * rows, columns)
        return [whole[:, cut : cut + width] for cut, width in zip(cuts_of(widths), widths)]
    return run_kernel(
        whole_kernel,
        [low_shape(count * rows, width) for width in widths],
        count * rows * columns,
        [index],
        [first, later],
    )


class Stage:
    def __init__(self, loads, stores):
        self.loads, self.stores = loads, stores
        self.waited, self.sent = set(), set()

    def need(self, *numbers):
        for i in numbers or range(len(self.loads)):
            if i not in self.waited:
                self.waited.add(i)
                self.loads[i].wait()

    def done(self, *numbers):
        for i in numbers or range(len(self.stores)):
            if i not in self.sent:
                self.sent.add(i)
                self.stores[i].start()


def staged_kernel(body, late, sizes, *refs):
    parts, at = [], 0
    for size in sizes:
        parts.append(refs[at : at + size])
        at += size
    tables, arrays, streamed, outs, scratch, held_in, held_out, (in_sems, out_sems) = parts
    stage = Stage(
        [pltpu.make_async_copy(a, b, in_sems.at[i]) for i, (a, b) in enumerate(zip(arrays, held_in))],
        [pltpu.make_async_copy(a, b, out_sems.at[i]) for i, (a, b) in enumerate(zip(held_out, outs))],
    )
    for load in stage.loads:
        load.start()
    if late:
        body(stage, *tables, *held_in, *streamed, *held_out, *scratch)
    else:
        stage.need()
        body(*tables, *held_in, *streamed, *held_out, *scratch)
    stage.need()
    stage.done()
    for store in stage.stores:
        store.wait()


HBM_SPEC = pl.BlockSpec(memory_space=pltpu.HBM)


def run_kernel(body, out_shape, cost, tables, arrays, scratch=(), streamed=(), late=False):
    sizes = (len(tables), len(arrays), len(streamed), len(out_shape), len(scratch))
    sizes += (len(arrays), len(out_shape), 2)
    held = [pltpu.VMEM(x.shape, x.dtype) for x in [*arrays, *out_shape]]
    sems = [pltpu.SemaphoreType.DMA((len(arrays),)), pltpu.SemaphoreType.DMA((len(out_shape),))]
    return pl.pallas_call(
        functools.partial(staged_kernel, body, late, sizes),
        out_shape=out_shape,
        in_specs=[SMEM_SPEC] * len(tables) + [HBM_SPEC] * (len(arrays) + len(streamed)),
        out_specs=[HBM_SPEC] * len(out_shape),
        scratch_shapes=list(scratch) + held + sems,
        compiler_params=pltpu.CompilerParams(vmem_limit_bytes=VMEM_LIMIT),
        cost_estimate=pl.CostEstimate(flops=cost // 1000, transcendentals=0, bytes_accessed=0),
    )(*tables, *arrays, *streamed)


VMEM_LIMIT = 56 << 20


def low_shape(*shape):
    return jax.ShapeDtypeStruct(shape, LOW)


def full_shape(*shape):
    return jax.ShapeDtypeStruct(shape, F32)


def unit_tile(source, at, second):
    lanes = 2 * HEAD_DIM
    start = 2 * at * lanes + (HEAD_DIM if second else 0)
    return jnp.concatenate(
        [source[:, pl.ds(start, HEAD_DIM)], source[:, pl.ds(start + lanes, HEAD_DIM)]], axis=1
    )


def shards_kernel(kinds, place, *refs):
    sources, targets = refs[:-2], refs[-2:]

    def write(target, second):
        cut = 0
        for kind, source in zip(kinds, sources):
            columns = source.shape[1]
            if kind == "all":
                target[:, pl.ds(cut, columns)] = source[...]
                cut += columns
                continue
            if kind == "half":
                start = columns // 2 if second else 0
                target[:, pl.ds(cut, columns // 2)] = source[:, pl.ds(start, columns // 2)]
            else:
                for tile in range(columns // 256):
                    target[:, pl.ds(cut + 128 * tile, 128)] = unit_tile(source, tile, second)
            cut += columns // 2

    @pl.when(place[0] == 0)
    def _():
        write(targets[0], False)
        write(targets[1], True)

    @pl.when(place[0] != 0)
    def _():
        write(targets[0], True)
        write(targets[1], False)


def rows_kernel(widths, piece, place, mine, other, down, *targets):
    *widths, matrices, extra = widths
    rows = mine.shape[0]

    def write(upper, lower):
        cut = 0
        for target, width in zip(targets[:-1], widths):
            target[0, pl.ds(0, rows), :] = upper[:, pl.ds(cut, width)]
            target[0, pl.ds(rows, rows), :] = lower[:, pl.ds(cut, width)]
            cut += width
        packed = targets[-1]
        columns = (mine.shape[1] - cut - extra) // matrices
        step = 8
        base = matrices * (2 * rows // piece) * columns
        last = base + down.shape[1] * (down.shape[0] // piece)
        for start in range(0, 2 * rows, step):
            source = upper if start < rows else lower
            number, inner = start // piece, start % piece
            for matrix in range(matrices):
                place_at = (matrix * (2 * rows // piece) + number) * columns
                packed[pl.ds(inner, step), pl.ds(place_at, columns)] = source[
                    pl.ds(start % rows, step), pl.ds(cut + matrix * columns, columns)
                ]
            packed[pl.ds(inner, step), pl.ds(last + number * extra, extra)] = source[
                pl.ds(start % rows, step), pl.ds(cut + matrices * columns, extra)
            ]
        width = down.shape[1]
        for number in range(down.shape[0] // piece):
            packed[:, pl.ds(base + number * width, width)] = down[pl.ds(number * piece, piece), :]

    @pl.when(place[0] == 0)
    def _():
        write(mine, other)

    @pl.when(place[0] != 0)
    def _():
        write(other, mine)


def cut_shards(place, shards, kinds):
    rows = shards[0].shape[0]
    columns = sum(w.shape[1] if k == "all" else w.shape[1] // 2 for w, k in zip(shards, kinds))
    return run_kernel(
        functools.partial(shards_kernel, kinds), [low_shape(rows, columns)] * 2, rows * columns, [place], shards
    )


def join_rows(place, mine, other, down, widths, extra, piece):
    rows = 2 * mine.shape[0]
    rest = mine.shape[1] - sum(widths)
    packed = rest * (rows // piece) + down.shape[1] * (down.shape[0] // piece)
    return run_kernel(
        functools.partial(rows_kernel, [*widths, 2, extra], piece),
        [low_shape(1, rows, width) for width in widths] + [low_shape(piece, packed)],
        rows * rest,
        [place],
        [mine, other, down],
    )


def pieces_kernel(cut, source, target, held, sem):
    blocks, pieces, piece, columns = held.shape
    copies = [
        pltpu.make_async_copy(
            source.at[:, :, pl.ds(cut + i * columns, columns)], held.at[:, i], sem.at[i]
        )
        for i in range(pieces)
    ]
    for copy in copies:
        copy.start()
    for copy in copies:
        copy.wait()
    target[...] = held[...].reshape(target.shape)


def from_pieces(packed, cut, pieces, columns):
    blocks, piece, _ = packed.shape
    return pl.pallas_call(
        functools.partial(pieces_kernel, cut),
        out_shape=low_shape(blocks * pieces * piece, columns),
        in_specs=[HBM_SPEC],
        out_specs=pl.BlockSpec(memory_space=pltpu.VMEM),
        scratch_shapes=[
            pltpu.VMEM((blocks, pieces, piece, columns), LOW),
            pltpu.SemaphoreType.DMA((pieces,)),
        ],
        cost_estimate=pl.CostEstimate(flops=1000, transcendentals=0, bytes_accessed=0),
    )(packed)


def normalize(values):
    inverse = lax.rsqrt(jnp.mean(values * values, axis=-1, keepdims=True) + EPS)
    return values * inverse, inverse


def norm_back(normed, inverse, gain, grads):
    scaled = grads * gain
    return inverse * (scaled - normed * jnp.mean(scaled * normed, axis=-1, keepdims=True))


def gelu_parts(gate):
    factor = math.sqrt(2.0 / math.pi)
    inner = jnp.tanh(factor * (gate + 0.044715 * gate * gate * gate))
    value = 0.5 * gate * (1.0 + inner)
    slope = 0.5 * (1.0 + inner) + 0.5 * gate * (1.0 - inner * inner) * factor * (
        1.0 + 3.0 * 0.044715 * gate * gate
    )
    return value, slope


def head_slices(place, half):
    mine = pl.ds(pl.multiple_of(place[0] * half, half), half)
    other = pl.ds(pl.multiple_of((1 - place[0]) * half, half), half)
    return mine, other


def query_kernel(packed, stage, *refs):
    if packed:
        index_a, index_b, first_a, later_a, first_b, later_b, token_m, token_g = refs[:8]
        rows_ref, normed_ref, q_ref, k_ref, v_ref, wq, gain_cols, wkv = refs[8:]
        stage.need(0, 1)
        place_blocks(index_a, first_a, later_a, [wq, gain_cols])
        stage.done(5, 6)
        stage.need(2, 3)
        place_blocks(index_b, first_b, later_b, [wkv])
        stage.done(7)
    else:
        wq, gain_cols, wkv, token_m, token_g = refs[:5]
        rows_ref, normed_ref, q_ref, k_ref, v_ref = refs[5:]
    stage.need()
    gain_rows = gain_cols[...].astype(F32).T[0:8]
    rows_ref[...] = gain_rows
    groups, own, _ = token_m.shape
    half = q_ref.shape[1]
    for group in range(groups):
        for side, source in enumerate((token_m, token_g)):
            plain, _ = normalize(source[group].astype(F32))
            at = pl.ds((2 * group + side) * own, own)
            normed_ref[at, :] = (plain * gain_rows[0:1]).astype(LOW)
    stage.done(0, 1)
    q_ref[...] = dot_nn(normed_ref[pl.ds(0, 2 * own), :], wq[...]).astype(LOW)
    stage.done(2)
    value = dot_nn(normed_ref[...], wkv[...]).astype(LOW)
    k_ref[...] = value[:, :half]
    v_ref[...] = value[:, half:]


def add_context(place, target, base, c_m, c_g, w_m, w_g):
    rows, half = c_m.shape
    own = rows // 2
    mine, other = head_slices(place, half)
    for side in range(2):
        at = pl.ds(side * own, own)
        left = c_m[at, :]
        right = c_g[pl.ds((1 - side) * own, own), :]
        for weight, columns in ((w_m, mine), (w_g, other)):
            value = dot_nn(left, weight[mine, :]) + dot_nn(right, weight[other, :])
            target[at, columns] = base(side, columns) + value


def cross_query_kernel(stage, place, token_m, token_g, c_m, c_g, w_m, w_g, rows_ref, wq, h_ref, normed_ref, q_ref):
    tokens = (token_m, token_g)
    base = lambda side, columns: tokens[side][0, :, columns].astype(F32)
    stage.need(*range(7))
    add_context(place, h_ref, base, c_m, c_g, w_m, w_g)
    stage.done(0)
    plain, _ = normalize(h_ref[...])
    normed_ref[...] = (plain * rows_ref[1:2, :]).astype(LOW)
    stage.done(1)
    stage.need()
    q_ref[...] = dot_nn(normed_ref[...], wq[...]).astype(LOW)


def memory_kernel(packed, stage, *refs):
    if packed:
        index, first, later, patch_m, patch_g, k_ref, v_ref, wkv = refs
        stage.need(0, 1)
        place_blocks(index, first, later, [wkv])
        stage.done(2)
    else:
        wkv, patch_m, patch_g, k_ref, v_ref = refs
    stage.need()
    count = patch_m.shape[0]
    half = k_ref.shape[1]
    for side, source in enumerate((patch_m, patch_g)):
        value = dot_nn(source[...], wkv[...]).astype(LOW)
        k_ref[pl.ds(side * count, count), :] = value[:, :half]
        v_ref[pl.ds(side * count, count), :] = value[:, half:]


def lane_column(column, lane):
    lanes = lax.broadcasted_iota(jnp.int32, (1, PAIR_LANES), 1)
    return jnp.where(lanes == lane, column, 0.0)


def mlp_kernel(
    chunk,
    stage,
    place,
    h_in,
    c_m,
    c_g,
    out_m,
    out_g,
    rows_ref,
    cols_ref,
    g_m,
    g_g,
    w_ref,
    h_ref,
    part_ref,
    keep_ref,
    give_ref,
    gain_ref,
    grad_ref,
    gate_w,
    up_w,
    down_w,
    a_ref,
    t_ref,
    g_ref,
    p_acc,
    d_acc,
    r_acc,
    sems,
):
    blocks, pieces, piece, units = gate_w.shape
    down_pieces, width = down_w.shape[1], down_w.shape[3]
    total = blocks * pieces * piece
    own = g_m.shape[0]
    moves = []
    for number in range(pieces):
        moves.append((w_ref.at[:, :, pl.ds(number * units, units)], gate_w.at[:, number]))
    for number in range(pieces):
        moves.append((w_ref.at[:, :, pl.ds((pieces + number) * units, units)], up_w.at[:, number]))
    base = 2 * pieces * units
    for number in range(down_pieces):
        moves.append((w_ref.at[:, :, pl.ds(base + number * width, width)], down_w.at[:, number]))
    copies = [pltpu.make_async_copy(a, b, sems.at[i]) for i, (a, b) in enumerate(moves)]
    for copy in copies:
        copy.start()
    stage.need(*range(6))
    add_context(
        place, h_ref, lambda side, columns: h_in[pl.ds(side * own, own), columns], c_m, c_g, out_m, out_g
    )
    stage.done(0)
    plain, _ = normalize(h_ref[...])
    a_ref[...] = (plain * rows_ref[2:3, :]).astype(LOW)
    t_ref[...] = a_ref[...].T
    stage.need()
    g_ref[pl.ds(0, own), :] = g_m[...]
    g_ref[pl.ds(own, own), :] = g_g[...]
    p_acc[...] = jnp.zeros(p_acc.shape, F32)
    d_acc[...] = jnp.zeros(d_acc.shape, F32)
    r_acc[...] = jnp.zeros(r_acc.shape, F32)
    for copy in copies:
        copy.wait()

    per_block = down_pieces * piece
    step_blocks = chunk // per_block

    @pl.loop(0, units // chunk)
    def _(step):
        start = pl.multiple_of(step * chunk, chunk)
        a_in = a_ref[...]
        g_in = g_ref[...]
        columns = pl.ds(start, chunk)
        gate_part = gate_w[:, :, :, columns].reshape(total, chunk)
        up_part = up_w[:, :, :, columns].reshape(total, chunk)
        down_at = pl.ds(step * step_blocks, step_blocks)
        down_part = down_w[down_at].reshape(chunk, width)
        gate = dot_nn(a_in, gate_part)
        up = dot_nn(a_in, up_part)
        active, slope = gelu_parts(gate)
        mixed = (active * up).astype(LOW)
        grad = dot_nt(g_in, down_part)
        gate_low = (grad * up * slope).astype(LOW)
        up_low = (grad * active).astype(LOW)
        d_acc[...] += dot_nn(mixed, down_part)
        p_acc[...] += dot_nt(gate_low, gate_part) + dot_nt(up_low, up_part)
        dgate = dot_nn(t_ref[...], gate_low)
        dup = dot_nn(t_ref[...], up_low)
        gain_terms = dgate * gate_part.astype(F32) + dup * up_part.astype(F32)
        for lane in range(0, chunk, PAIR_LANES):
            r_acc[...] += gain_terms[:, lane : lane + PAIR_LANES]
        dgate = dgate.astype(LOW).reshape(blocks, pieces, piece, chunk)
        dup = dup.astype(LOW).reshape(blocks, pieces, piece, chunk)
        for number in range(pieces):
            gate_at = pl.multiple_of(number * units + start, chunk)
            up_at = pl.multiple_of((pieces + number) * units + start, chunk)
            grad_ref[:, :, pl.ds(gate_at, chunk)] = dgate[:, number]
            grad_ref[:, :, pl.ds(up_at, chunk)] = dup[:, number]
        ddown = dot_tn(mixed, g_in).astype(LOW).reshape(step_blocks, down_pieces, piece, width)
        for number in range(down_pieces):
            grad_ref[down_at, :, pl.ds(base + number * width, width)] = ddown[:, number]

    stage.done(5)
    part_ref[...] = p_acc[...].astype(LOW)
    stage.done(1)
    keep_ref[...] = d_acc[pl.ds(0, own), :]
    give_ref[...] = d_acc[pl.ds(own, own), :].astype(LOW)
    summed = jnp.sum(r_acc[...], axis=1, keepdims=True)
    gain_ref[...] = lane_column(summed / cols_ref[:, 2:3].astype(F32), 2)


def branch_kernel(gain_at, stage, place, *refs):
    h_ref, rows_ref, part_m, part_g, w_m, w_g = refs[:6]
    base, (d_ref, low_ref, c_ref) = refs[6:-3], refs[-3:]
    rows = h_ref.shape[0]
    own = rows // 2
    half = w_m.shape[1]
    mine, other = head_slices(place, half)
    stage.need(0, 1, 2, 3, *range(6, 6 + len(base)))
    for side in range(2):
        at = pl.ds(side * own, own)
        plain, inverse = normalize(h_ref[at, :])
        got = part_g[pl.ds((1 - side) * own, own), :]
        grads = part_m[at, :].astype(F32) + got.astype(F32)
        value = norm_back(plain, inverse, rows_ref[gain_at : gain_at + 1, :], grads)
        before = base[side][...].astype(F32) if len(base) == 2 else base[0][at, :]
        d_ref[at, :] = before + value
    stage.done(0)
    low_ref[...] = d_ref[...].astype(LOW)
    stage.done(1)
    stage.need()
    value = dot_nt(low_ref[:, mine], w_m[mine, :]) + dot_nt(low_ref[:, other], w_g[mine, :])
    c_ref[...] = value.astype(LOW)


def dot_rows(left, right):
    columns = left.shape[1]
    step = math.gcd(columns, 256)
    return [(i, dot_tn(left[:, i : i + step], right)) for i in range(0, columns, step)]


def out_grad(place, whole, cut, c_m, c_g, branch):
    rows, half = c_m.shape
    own = rows // 2
    mine, other = head_slices(place, half)
    grads = branch[:, mine]
    columns = pl.ds(cut, half)
    whole[mine, columns] = dot_tn(c_m[...], grads).astype(LOW)
    value = dot_tn(c_g[pl.ds(own, own), :], grads[:own]) + dot_tn(c_g[pl.ds(0, own), :], grads[own:])
    whole[other, columns] = value.astype(LOW)


def weight_grads(targets, lefts, rights, gain_acc=None):
    features = lefts[0].shape[1]
    step = math.gcd(features, 256)

    for number in range(features // step):
        at = pl.ds(number * step, step)
        turned = [left[:, at].T for left in lefts]
        for (whole, cut, weight), terms in zip(targets, rights):
            width = terms[0].shape[1]
            value = sum(dot_nn(left, right[...]) for left, right in zip(turned, terms))
            whole[at, pl.ds(cut, width)] = value.astype(LOW)
            if weight is not None:
                products = value * weight[at, :].astype(F32)
                gain_acc[at, :] += sum(
                    products[:, lane : lane + PAIR_LANES] for lane in range(0, width, PAIR_LANES)
                )


def cross_grads_kernel(packed, stage, place, *refs):
    index, refs = (refs[:2], refs[2:]) if packed else ((), refs)
    c_m, c_g, branch, normed, dq, patch_m, patch_g, dk, dv, wq, cols_ref = refs[:11]
    one_m, one_g, branch_one = refs[11:14]
    gain_ref, *outs, whole_a, whole_b, gain_acc = refs[14:]
    half = dq.shape[1]
    stage.need(0, 1, 2, 3, 4, 9, 10, 11, 12, 13)
    out_grad(place, whole_a, 2 * half, one_m, one_g, branch_one)
    count = patch_m.shape[0]
    gain_acc[...] = jnp.zeros(gain_acc.shape, F32)
    out_grad(place, whole_a, 0, c_m, c_g, branch)
    weight_grads([(whole_a, half, wq)], [normed], [[dq]], gain_acc)
    if packed:
        send_order(index[0], whole_a, outs[0], outs[1])
        stage.done(1, 2)
    summed = jnp.sum(gain_acc[...], axis=1, keepdims=True)
    gain_ref[...] = lane_column(summed / cols_ref[:, 1:2].astype(F32), 1)
    stage.need()
    halves = [[g.at[pl.ds(i * count, count), :] for i in range(2)] for g in (dk, dv)]
    weight_grads(
        [(whole_b, 0, None), (whole_b, half, None)], [patch_m, patch_g], halves
    )
    if packed:
        send_order(index[1], whole_b, outs[2], outs[3])


def self_grads_kernel(packed, stage, place, *refs):
    index, refs = (refs[:2], refs[2:]) if packed else ((), refs)
    normed, dq, dk, dv, wq, wkv, cols_ref, gain_two, gain_three = refs[:9]
    *outs, whole_a, whole_b, gain_acc = refs[9:]
    rows, half = dq.shape
    gain_acc[...] = jnp.zeros(gain_acc.shape, F32)
    stage.need(0, 3, 5)
    weight_grads([(whole_b, 0, wkv.at[:, pl.ds(half, half)])], [normed], [[dv]], gain_acc)
    stage.need(2)
    weight_grads([(whole_b, half, wkv.at[:, pl.ds(0, half)])], [normed], [[dk]], gain_acc)
    if packed:
        send_order(index[1], whole_b, outs[2], outs[3])
        stage.done(2, 3)
    stage.need()
    weight_grads([(whole_a, 0, wq)], [normed.at[pl.ds(0, rows), :]], [[dq]], gain_acc)
    summed = jnp.sum(gain_acc[...], axis=1, keepdims=True)
    gains = lane_column(summed / cols_ref[:, 0:1].astype(F32), 0) + gain_two[...] + gain_three[...]
    whole_a[:, pl.ds(half, PAIR_LANES)] = gains.astype(LOW)
    if packed:
        send_order(index[0], whole_a, outs[0], outs[1])


def back_kernel(grads, weight, out):
    out[...] = dot_nt(grads[...], weight[...]).astype(LOW)


def rows_back_kernel(spans, with_query, *refs):
    dk, dv, wkv = refs[:3]
    queries = refs[3:5] if with_query else None
    half = dk.shape[1]
    wk, wv = wkv.at[:, pl.ds(0, half)], wkv.at[:, pl.ds(half, half)]
    keep, give = refs[-2:]
    rows = dk.shape[0] // len(spans)
    for number, (mine, place) in enumerate(spans):
        at = pl.ds(number * rows, rows)
        value = dot_nt(dk[at, :], wk[...]) + dot_nt(dv[at, :], wv[...])
        if queries and number < 2:
            value = value + dot_nt(queries[0][at, :], queries[1][...])
        if mine:
            keep[place] = value
        else:
            give[place] = value.astype(LOW)


def feed_forward_grads_kernel(pieces, units, place, sums, got, gate_ref, up_ref, down_ref):
    piece = sums.shape[0]
    rows = got.shape[0]
    hidden = got.shape[1] // 2
    step = 8

    def write(second):
        for row in range(0, rows, step):
            at = row + (rows if second else 0)
            number, inner = at // piece, at % piece
            for matrix, target in enumerate((gate_ref, up_ref)):
                start = (matrix * pieces + number) * hidden
                mine = sums[pl.ds(inner, step), pl.ds(start, hidden)].astype(F32)
                other = got[pl.ds(row, step), pl.ds(matrix * hidden, hidden)].astype(F32)
                pair = (other, mine) if second else (mine, other)
                for unit in range(0, hidden, units):
                    tile = jnp.concatenate([part[:, unit : unit + units] for part in pair], axis=1)
                    target[pl.ds(row, step), pl.ds(2 * unit, 2 * units)] = tile

    @pl.when(place[0] == 0)
    def _():
        write(False)

    @pl.when(place[0] != 0)
    def _():
        write(True)

    base = 2 * pieces * hidden
    width = down_ref.shape[1]
    for number in range(down_ref.shape[0] // piece):
        down_ref[pl.ds(number * piece, piece), :] = sums[:, pl.ds(base + number * width, width)].astype(F32)


def columns_kernel(place, keep, got, *targets):
    rows = got.shape[0]

    def write(start, first, later):
        for number, target in enumerate(targets):
            half = target.shape[1] // 2
            columns = pl.ds(number * half, half)
            target[:, pl.ds(0, half)] = first(start, columns)
            target[:, pl.ds(half, half)] = later(start, columns)

    from_keep = lambda start, columns: keep[pl.ds(start, rows), columns]
    from_got = lambda start, columns: got[:, columns]

    @pl.when(place[0] == 0)
    def _():
        write(0, from_keep, from_got)

    @pl.when(place[0] != 0)
    def _():
        write(rows, from_got, from_keep)


def after(values, *others):
    return lax.optimization_barrier((values, *others))[0]


def together(*values):
    return lax.optimization_barrier(values)


class Ring:
    def __init__(self):
        self.charts = lax.axis_size("dp")
        self.groups = lax.axis_size("hx")
        self.half = lax.axis_index("hc").astype(jnp.int32)
        self.second = self.half == 1
        self.place = self.half[None]
        self.group = lax.axis_index("hx").astype(jnp.int32)
        self.block = lax.axis_index("dp").astype(jnp.int32) * self.groups + self.group
        self.blocks = self.charts * self.groups
        chart_bits = [("dp", 1 << i) for i in range(self.charts.bit_length() - 1)]
        self.group_bits = [("hx", 1 << i) for i in range(self.groups.bit_length() - 1)]
        self.far = chart_bits[:0:-1]
        near = chart_bits[:1]
        self.tails = (near + self.group_bits, self.group_bits + near)
        self.orders = tuple(self.far + tail for tail in self.tails)

    def send(self, values, axis, bit):
        size = self.charts if axis == "dp" else self.groups
        return lax.ppermute(values, axis, [(i, i ^ bit) for i in range(size)])

    def swap(self, values):
        return lax.ppermute(values, "hc", [(0, 1), (1, 0)])

    def in_order(self, mine, other):
        return jnp.where(self.second, other, mine), jnp.where(self.second, mine, other)

    def steps(self, order):
        return [bit * self.groups if axis == "dp" else bit for axis, bit in order]

    def arrivals(self):
        apart = self.block ^ jnp.arange(self.blocks, dtype=jnp.int32)
        indices = []
        for order in self.orders:
            index = jnp.zeros((self.blocks,), jnp.int32)
            for place, step in enumerate(self.steps(order)):
                index = index + jnp.where((apart & step) != 0, 1 << place, 0)
            indices.append(index)
        return indices

    def origins(self):
        indices = []
        for order in self.orders:
            masks = [0]
            for step in self.steps(order):
                masks = masks + [m ^ step for m in masks]
            indices.append(self.block ^ jnp.asarray(masks, jnp.int32))
        return indices

    def far_masks(self):
        masks = [0]
        for _, bit in self.far:
            masks = masks + [m | bit for m in masks]
        return masks

    def far_step(self, blocks, step):
        return jnp.concatenate([blocks, self.send(blocks, *self.far[step])], axis=0)

    def near_step(self, parts, step):
        return [self.send(part, *tail[step]) for part, tail in zip(parts, self.tails)]

    def near_sends(self, gives, place):
        return [self.send(give, *tail[place]) for give, tail in zip(gives, self.tails)]

    def near_sums(self, keeps, gots, place):
        halves = [got.shape[0] // 2 for got in gots]
        add = lambda k, g: (k.astype(F32) + g.astype(F32)).astype(LOW)
        gives = [add(k[h:], g[h:]) for k, g, h in zip(keeps, gots, halves)]
        keeps = [add(k[:h], g[:h]) for k, g, h in zip(keeps, gots, halves)]
        return keeps, gives

    def far_sends(self, keeps, gots):
        count = 1 << len(self.far)
        add = lambda r: [
            k[r : r + 1].astype(F32) + g[r : r + 1].astype(F32) for k, g in zip(keeps, gots)
        ]
        block = lambda r: jnp.concatenate(add(r), axis=2)
        if len(self.far) == 2:
            masks = self.far_masks()
            return block(0), [self.send(block(r).astype(LOW), "dp", masks[r]) for r in range(1, count)]
        keep = jnp.concatenate([block(r) for r in range(count)], axis=0)
        for axis, bit in reversed(self.far[1:]):
            half = keep.shape[0] // 2
            keep = keep[:half] + self.send(keep[half:].astype(LOW), axis, bit).astype(F32)
        return keep[:1], [self.send(keep[1:].astype(LOW), *self.far[0])]

    def far_sum(self, own, gots):
        return sum((got.astype(F32) for got in gots), own)[0]

    def far_first(self, keeps, gots):
        count = 1 << len(self.far)
        add = lambda r: jnp.concatenate(
            [k[r].astype(F32) + g[r].astype(F32) for k, g in zip(keeps, gots)], axis=2
        )
        keep, give = add(slice(0, count // 2)), add(slice(count // 2, None)).astype(LOW)
        return keep, self.send(give, *self.far[-1])

    def far_last(self, keep, got):
        for axis, bit in reversed(self.far[:-1]):
            half = keep.shape[0] // 2
            give = (keep[half:] + got[half:].astype(F32)).astype(LOW)
            keep = keep[:half] + got[:half].astype(F32)
            got = self.send(give, axis, bit)
        return keep, [got]

    def halve_wholes(self, wholes, rows):
        keeps, gives = [], []
        for whole, index in zip(wholes, self.origins()):
            blocks = jnp.take(whole.reshape(self.blocks, rows, -1), index, axis=0)
            keeps.append(blocks[: self.blocks // 2])
            gives.append(blocks[self.blocks // 2 :])
        return keeps, gives

    def across(self, mine):
        rows = mine[None]
        for axis, bit in self.group_bits:
            rows = jnp.concatenate([rows, self.send(rows, axis, bit)], axis=0)
        return rows

    def halves(self, first, later):
        mine = jnp.where(self.second, later, first)
        give = jnp.where(self.second, first, later)
        return jnp.concatenate(self.in_order(mine, self.swap(give)), axis=0)

    def pair_sum(self, keep, give):
        return keep + self.swap(give.astype(LOW)).astype(F32)

    def group_terms(self, total):
        for axis, bit in reversed(self.group_bits):
            middle = total.shape[0] // 2
            total = total[:middle] + self.send(total[middle:].astype(LOW), axis, bit).astype(F32)
        return total[0]

    def finished(self, keep, count):
        rows = keep.shape[0] // 2
        give = lax.dynamic_slice_in_dim(keep, (1 - self.half) * rows, rows, 0)
        got = self.swap(give)
        width = keep.shape[1] // count * 2
        return run_kernel(
            columns_kernel, [full_shape(rows, width)] * count, rows * width, [self.place], [keep, got]
        )


def column_halves(weights):
    half = weights[0].shape[1] // 2
    return [jnp.concatenate([w[:, i * half : (i + 1) * half] for w in weights], axis=1) for i in range(2)]


def unit_halves(weight, units):
    rows, columns = weight.shape
    split = weight.reshape(rows, columns // (2 * units), 2, units)
    return split[:, :, 0].reshape(rows, -1), split[:, :, 1].reshape(rows, -1)


def unit_whole(first, later, units):
    rows, columns = first.shape
    pieces = [part.reshape(rows, columns // units, 1, units) for part in (first, later)]
    return jnp.concatenate(pieces, axis=2).reshape(rows, 2 * columns)


def on_device(
    tokens,
    memory,
    text_length,
    patch_count,
    self_gain,
    self_query,
    self_key,
    self_value,
    self_out,
    cross_gain,
    cross_query,
    cross_key,
    cross_value,
    cross_out,
    mlp_gain,
    mlp_gate,
    mlp_up,
    mlp_down,
    output_grad,
):
    ring = Ring()
    place = ring.place
    width = tokens.shape[-1]
    half = width // 2
    units = mlp_down.shape[0]
    hidden_half = units * ring.blocks
    rows = self_query.shape[0]
    own = tokens.shape[1]
    own_patches = memory.shape[1]
    both = 2 * own
    keys = both * ring.groups
    patches = 2 * own_patches * ring.groups
    piece = 16
    packed = (2 * rows) % piece == 0 and units == HEAD_DIM and ring.blocks > 1
    pieces, down_pieces = 2 * rows // piece, units // piece
    pairs = ("dp", "hx")
    index_in = tuple(ring.arrivals()) if packed else ()
    index_out = tuple(ring.origins()) if packed else ()
    index_specs = [SMEM_SPEC] * len(index_in)
    block_rows = 2 * rows

    gain_columns = jnp.stack([self_gain, cross_gain, mlp_gain], axis=1)
    gain_columns = jnp.pad(gain_columns, ((0, 0), (0, PAIR_LANES - 3)))
    chains = ([self_query, gain_columns, self_out, cross_query], [self_key, self_value, cross_key, cross_value])
    splits = (half + PAIR_LANES, 2 * half)
    cut_all = 3 * half + PAIR_LANES
    packed_columns = (2 * hidden_half) * pieces + width * down_pieces
    widths_one = ([half, PAIR_LANES], [width])
    widths_two = ([half] * 2, [width])

    if packed:
        kinds = ["all" if w is gain_columns else "half" for w in chains[0] + chains[1]]
        mine, give = cut_shards(place, chains[0] + chains[1], kinds)
        blocks = jnp.concatenate(ring.in_order(mine, ring.swap(give)), axis=0)[None]
    else:
        sides = [
            jnp.concatenate(
                [w if w is gain_columns else column_halves([w])[i] for w in chains[0] + chains[1]],
                axis=1,
            )
            for i in range(2)
        ]
        blocks = ring.halves(*sides)[None]
    middle = own_patches // 2
    token_m = ring.across(tokens[0])
    patch_a = ring.across(memory[0, :middle])
    if packed:
        rest = after([mlp_gate, mlp_up, cross_out], blocks)
        mine, give = cut_shards(place, rest, ["units"] * 2 + ["half"])
        blocks_mlp = join_rows(place, mine, ring.swap(give), mlp_down, [], half, piece)[0]
    else:
        gate_halves, up_halves = unit_halves(mlp_gate, units), unit_halves(mlp_up, units)
        rest = [
            jnp.concatenate([gate_halves[i], up_halves[i], column_halves([cross_out])[i]], axis=1)
            for i in range(2)
        ]
        gate_up = lax.all_gather(ring.halves(*rest), pairs, axis=0, tiled=True)
        down_three = lax.all_gather(mlp_down, pairs, axis=0, tiled=True)
        out_two = gate_up[:, 2 * hidden_half :]
    blocks = ring.far_step(blocks, 0)
    blocks, token_m, memory = together(blocks, token_m, memory)
    if packed:
        mlp_weights = lax.all_gather(after(blocks_mlp, blocks), pairs, axis=0, tiled=True)
        mlp_weights = mlp_weights.reshape(ring.blocks, piece, -1)
    patch_b = ring.across(memory[0, middle:])
    for step in range(1, len(ring.far)):
        blocks = ring.far_step(blocks, step)
    blocks, patch_a, token_m = together(blocks, patch_a, token_m)
    parts = [blocks[:, :, :cut_all], blocks[:, :, cut_all:]]
    token_g = ring.swap(token_m)
    last = len(ring.tails[0]) - 1
    for step in range(last):
        got = ring.near_step(parts, step)
        parts = [jnp.concatenate(pair, axis=0) for pair in zip(parts, got)]
    parts, token_g, patch_b = together(parts, token_g, patch_b)
    parts_one = [part[:, :, :split] for part, split in zip(parts, splits)]
    parts_two = [part[:, :, split:] for part, split in zip(parts, splits)]
    near_one = ring.near_step(parts_one, last)
    patch_m = jnp.concatenate([patch_a, patch_b], axis=1)
    patch_g = ring.swap(patch_m)
    near_one, parts_two, patch_g = together(near_one, parts_two, patch_g)
    near_two = ring.near_step(parts_two, last)
    near_one = (parts_one[0], near_one[0], parts_one[1], near_one[1])
    arrivals = ring.arrivals()

    token_chunk = math.gcd(256, own)
    patch_chunk = math.gcd(256, own_patches)

    def chunk_starts(span, chunk, side_first):
        groups = ring.group ^ jnp.arange(ring.groups, dtype=jnp.int32)
        sides = ring.half ^ jnp.arange(2, dtype=jnp.int32)
        inner = jnp.arange(span // chunk, dtype=jnp.int32) * chunk
        if side_first:
            starts = groups[None, :, None] * 2 * span + sides[:, None, None] * span
        else:
            starts = groups[:, None, None] * 2 * span + sides[None, :, None] * span
        return (starts + inner).reshape(-1)

    fixed = jnp.stack([ring.group * both, ring.half])
    info_one = jnp.concatenate([text_length, fixed, chunk_starts(own, token_chunk, False)])
    info_two = jnp.concatenate([patch_count, fixed, chunk_starts(own_patches, patch_chunk, True)])

    head_shapes = [low_shape(both, half), low_shape(keys, half), low_shape(keys, half)]
    query_outs = [full_shape(8, width), low_shape(keys, width), *head_shapes]
    projections = [low_shape(width, w) for w in widths_one[0] + widths_one[1]]
    cost = keys * width * half
    if packed:
        outs = run_kernel(
            functools.partial(query_kernel, True),
            query_outs + projections,
            cost,
            index_in,
            [*near_one, token_m, token_g],
            late=True,
        )
        gain_rows, normed_one, query_heads, key_heads, value_heads = outs[:5]
        query_one, gain_cols, heads_one = outs[5:]
    else:
        query_one, gain_cols = to_whole(near_one[0], near_one[1], arrivals[0], widths_one[0])
        (heads_one,) = to_whole(near_one[2], near_one[3], arrivals[1], widths_one[1])
        gain_rows, normed_one, query_heads, key_heads, value_heads = run_kernel(
            functools.partial(query_kernel, False),
            query_outs,
            cost,
            [],
            [query_one, gain_cols, heads_one, token_m, token_g],
            late=True,
        )
    near_one = None
    grad_g = ring.swap(after(output_grad[0], query_heads))
    context_one, lse_one = attention_forward(
        info_one, query_heads, key_heads, value_heads, True, token_chunk
    )
    context_one, near_a, near_b, grad_g = together(context_one, *near_two, grad_g)
    context_one_g = ring.swap(context_one)
    out_one, query_two = to_whole(parts_two[0], near_a, arrivals[0], widths_two[0])
    out_one_g = ring.swap(out_one)
    patch_all = [part.reshape(-1, width) for part in (patch_m, patch_g)]
    memory_heads = [low_shape(patches, half)] * 2
    if packed:
        memory_keys, memory_values, heads_two = run_kernel(
            functools.partial(memory_kernel, True),
            memory_heads + [low_shape(width, width)],
            patches * width * half,
            index_in[1:],
            [parts_two[1], near_b, *patch_all],
            late=True,
        )
    else:
        (heads_two,) = to_whole(parts_two[1], near_b, arrivals[1], widths_two[1])
        memory_keys, memory_values = run_kernel(
            functools.partial(memory_kernel, False),
            memory_heads,
            patches * width * half,
            [],
            [heads_two, *patch_all],
            late=True,
        )
    context_one_g, memory_keys = together(context_one_g, memory_keys)
    hidden_one, normed_two, cross_heads = run_kernel(
        cross_query_kernel,
        [full_shape(both, width), low_shape(both, width), low_shape(both, half)],
        both * width * half,
        [place],
        [token_m, token_g, context_one, context_one_g, out_one, out_one_g, gain_rows, query_two],
        late=True,
    )
    if packed:
        out_two = from_pieces(after(mlp_weights, cross_heads), packed_columns, pieces, half)
    cross_heads, out_two = together(cross_heads, out_two)
    out_two_g = ring.swap(out_two)
    context_two, lse_two = attention_forward(
        info_two, cross_heads, memory_keys, memory_values, False, patch_chunk
    )
    context_two_g = ring.swap(context_two)
    if packed:
        hidden_two, part_low, down_keep, down_give, gain_three, mlp_terms = run_kernel(
            functools.partial(mlp_kernel, 1024),
            [
                full_shape(both, width),
                low_shape(both, width),
                full_shape(own, width),
                low_shape(own, width),
                full_shape(width, PAIR_LANES),
                low_shape(ring.blocks, piece, packed_columns),
            ],
            2 * both * width * hidden_half,
            [place],
            [
                hidden_one,
                context_two,
                context_two_g,
                out_two,
                out_two_g,
                gain_rows,
                gain_cols,
                output_grad[0],
                grad_g,
            ],
            [
                pltpu.VMEM((ring.blocks, pieces, piece, hidden_half), LOW),
                pltpu.VMEM((ring.blocks, pieces, piece, hidden_half), LOW),
                pltpu.VMEM((ring.blocks, down_pieces, piece, width), LOW),
                pltpu.VMEM((both, width), LOW),
                pltpu.VMEM((width, both), LOW),
                pltpu.VMEM((both, width), LOW),
                pltpu.VMEM((both, width), F32),
                pltpu.VMEM((both, width), F32),
                pltpu.VMEM((width, PAIR_LANES), F32),
                pltpu.SemaphoreType.DMA((2 * pieces + down_pieces,)),
            ],
            [mlp_weights],
            late=True,
        )
        mlp_terms = mlp_terms.reshape(ring.blocks * piece, -1)
        mlp_sum = lax.psum_scatter(mlp_terms, pairs, scatter_dimension=0, tiled=True)
    else:
        joined = jnp.concatenate(ring.in_order(out_two, out_two_g), axis=1)
        swapped = jnp.concatenate([context_two_g[own:], context_two_g[:own]], axis=0)
        context = jnp.concatenate(ring.in_order(context_two, swapped), axis=1)
        hidden_two = hidden_one + dot_nn(context, joined)
        normed_three = (normalize(hidden_two)[0] * gain_rows[2:3]).astype(LOW)
        grad_low = jnp.concatenate([output_grad[0], grad_g], axis=0)
        gate_up = gate_up[:, : 2 * hidden_half]
        gate_three, up_three = gate_up[:, :hidden_half], gate_up[:, hidden_half:]
        active, slope = gelu_parts(dot_nn(normed_three, gate_three))
        up = dot_nn(normed_three, up_three)
        mixed = (active * up).astype(LOW)
        down_part = dot_nn(mixed, down_three)
        down_keep, down_give = down_part[:own], down_part[own:].astype(LOW)
        grad_mixed = dot_nt(grad_low, down_three)
        gate_low = (grad_mixed * up * slope).astype(LOW)
        up_low = (grad_mixed * active).astype(LOW)
        part_low = (dot_nt(gate_low, gate_three) + dot_nt(up_low, up_three)).astype(LOW)
        terms = jnp.concatenate(
            [dot_tn(normed_three, gate_low), dot_tn(normed_three, up_low)], axis=1
        )
        column = jnp.sum(terms * gate_up.astype(F32), axis=1, keepdims=True)
        gain_three = lane_column(column / gain_cols[:, 2:3].astype(F32), 2)
        gate_up = lax.psum_scatter(terms, pairs, scatter_dimension=0, tiled=True)
        mlp_ddown = lax.psum_scatter(
            dot_tn(mixed, grad_low), pairs, scatter_dimension=0, tiled=True
        )

    part_g = ring.swap(part_low)
    down_got = ring.swap(down_give)
    output = (hidden_two[:own] + down_keep + down_got.astype(F32)).astype(LOW)

    def branch(gain_at, hidden, mine, got, weight_m, weight_g, base):
        return run_kernel(
            functools.partial(branch_kernel, gain_at),
            [full_shape(both, width), low_shape(both, width), low_shape(both, half)],
            both * width * half,
            [place],
            [hidden, gain_rows, mine, got, weight_m, weight_g, *base],
            late=True,
        )

    dhidden_two, branch_two, dcontext_two = branch(
        2, hidden_two, part_low, part_g, out_two, out_two_g, [output_grad[0], grad_g]
    )
    dquery, dkey, dvalue = attention_backward(
        info_two,
        cross_heads,
        memory_keys,
        memory_values,
        context_two,
        dcontext_two,
        lse_two,
        False,
        patch_chunk,
    )
    (part_low,) = run_kernel(
        back_kernel, [low_shape(both, width)], both * width, [], [dquery, query_two]
    )
    part_g = ring.swap(part_low)

    count = ring.blocks // 2

    def grads(body, inputs, columns, gain_outs, cost, order=1):
        scratch = [pltpu.VMEM((width, c), LOW) for c in columns]
        acc = pltpu.VMEM((width, PAIR_LANES), F32)
        if packed:
            shapes = [low_shape(count, block_rows, c) for c in columns for _ in range(2)]
            outs = run_kernel(
                functools.partial(body, True),
                gain_outs + shapes,
                cost,
                [place, *index_out[::order]],
                inputs,
                scratch + [acc],
                late=True,
            )
            blocks = outs[len(gain_outs) :]
            return outs[: len(gain_outs)], blocks[0::2][::order], blocks[1::2][::order]
        wholes = [low_shape(width, c) for c in columns]
        outs = run_kernel(
            functools.partial(body, False), gain_outs + wholes, cost, [place], inputs, [acc], late=True
        )
        return outs[: len(gain_outs)], *ring.halve_wholes(outs[len(gain_outs) :][::order], block_rows)

    patch_spans = [(side == 0, g) for side in range(2) for g in range(ring.groups)]
    patch_shape = (ring.groups, own_patches, width)
    memory_keep, memory_give = run_kernel(
        functools.partial(rows_back_kernel, patch_spans, False),
        [full_shape(*patch_shape), low_shape(*patch_shape)],
        patches * width,
        [],
        [dkey, dvalue, heads_two],
    )
    memory_total = ring.pair_sum(memory_keep, memory_give)
    part_g, memory_total = together(part_g, memory_total)
    memory_sent = ring.group_terms(memory_total)
    dhidden_one, branch_one, dcontext_one = branch(
        1, hidden_one, part_low, part_g, out_one, out_one_g, [dhidden_two]
    )
    (gain_two,), cross_keep, cross_give = grads(
        cross_grads_kernel,
        [
            context_two,
            context_two_g,
            branch_two,
            normed_two,
            dquery,
            *patch_all,
            dkey,
            dvalue,
            query_two,
            gain_cols,
            context_one,
            context_one_g,
            branch_one,
        ],
        (3 * half, 2 * half),
        [full_shape(width, PAIR_LANES)],
        (both + patches) * width * half,
        -1,
    )
    cross_got = ring.near_sends(cross_give, last)
    cross_keep, dcontext_one = together(cross_keep, dcontext_one)

    dquery_one, dkey_one, dvalue_one = attention_backward(
        info_one,
        query_heads,
        key_heads,
        value_heads,
        context_one,
        dcontext_one,
        lse_one,
        True,
        token_chunk,
    )
    dquery_one, dkey_one, dvalue_one, cross_got, memory_grad, output = together(
        dquery_one, dkey_one, dvalue_one, cross_got, memory_sent, output
    )
    for step in reversed(range(1, last + 1)):
        cross_keep, cross_give = ring.near_sums(cross_keep, cross_got, step)
        cross_got = ring.near_sends(cross_give, step - 1)
    dquery_one, cross_give = together(dquery_one, cross_give)
    _, self_keep, self_give = grads(
        self_grads_kernel,
        [
            normed_one,
            dquery_one,
            dkey_one,
            dvalue_one,
            query_one,
            heads_one,
            gain_cols,
            gain_two,
            gain_three,
        ],
        (half + PAIR_LANES, 2 * half),
        [],
        (both + keys) * width * half,
    )
    self_give, cross_got = together(self_give, cross_got)
    self_got = ring.near_sends(self_give, last)
    cross_own, cross_far = ring.far_first(cross_keep, cross_got)
    dquery_one, dkey_one, dvalue_one = after((dquery_one, dkey_one, dvalue_one), self_give)
    token_spans = [(side == 0, g) for g in range(ring.groups) for side in range(2)]
    token_shape = (ring.groups, own, width)
    part_keep, part_give = run_kernel(
        functools.partial(rows_back_kernel, token_spans, True),
        [full_shape(*token_shape), low_shape(*token_shape)],
        keys * width,
        [],
        [dkey_one, dvalue_one, heads_one, dquery_one, query_one],
    )
    part_total = ring.pair_sum(part_keep, part_give)
    self_got, part_total = together(self_got, part_total)
    for step in reversed(range(1, last + 1)):
        self_keep, self_give = ring.near_sums(self_keep, self_got, step)
        self_got = ring.near_sends(self_give, step - 1)
    dnormed_one = ring.group_terms(part_total)
    self_got, cross_far = together(self_got, cross_far)
    self_own, self_far = ring.far_sends(self_keep, self_got)
    cross_own, cross_far = ring.far_last(cross_own, cross_far)
    plain, inverse = normalize(tokens[0].astype(F32))
    input_grad = dhidden_one[:own] + norm_back(plain, inverse, gain_rows[0:1], dnormed_one)

    if packed:
        mlp_rows = mlp_sum[:, : 2 * pieces * hidden_half].reshape(piece, 2, pieces, hidden_half)
        mlp_rows = mlp_rows.transpose(2, 0, 1, 3).reshape(2 * rows, 2 * hidden_half)
        mlp_give = lax.dynamic_slice_in_dim(mlp_rows, (1 - ring.half) * rows, rows, 0)
        mlp_dgate, mlp_dup, mlp_ddown = run_kernel(
            functools.partial(feed_forward_grads_kernel, pieces, units),
            [full_shape(rows, 2 * hidden_half)] * 2 + [full_shape(units, width)],
            rows * width,
            [place],
            [mlp_sum, ring.swap(mlp_give)],
        )
    else:
        (gate_up,) = ring.finished(gate_up, 1)
        gate_columns = [gate_up[:, i * hidden_half : (i + 1) * hidden_half] for i in range(4)]
        mlp_dgate = unit_whole(gate_columns[0], gate_columns[2], units)
        mlp_dup = unit_whole(gate_columns[1], gate_columns[3], units)
    self_far, cross_far, mlp_dgate, mlp_dup, mlp_ddown, input_grad, memory_grad = together(
        self_far, cross_far, mlp_dgate, mlp_dup, mlp_ddown, input_grad, memory_grad
    )
    cross_sum = ring.far_sum(cross_own, cross_far)
    self_sum = ring.far_sum(self_own, self_far)
    gain_block = self_sum[:, half : half + PAIR_LANES]
    gain_block = jnp.pad(gain_block, ((0, 0), (0, half - PAIR_LANES)))
    joined = jnp.concatenate(
        [cross_sum, self_sum[:, :half], self_sum[:, half + PAIR_LANES :], gain_block], axis=1
    )
    cross_dkey, cross_dvalue, cross_dout, cross_dquery, self_dout, *rest = ring.finished(joined, 9)
    self_dquery, self_dvalue, self_dkey, gain_terms = rest
    dgains = gain_terms[:, :3] + gain_terms[:, half : half + 3]

    return (
        output[None],
        input_grad[None],
        memory_grad[None],
        dgains[:, 0],
        self_dquery,
        self_dkey,
        self_dvalue,
        self_dout,
        dgains[:, 1],
        cross_dquery,
        cross_dkey,
        cross_dvalue,
        cross_dout,
        dgains[:, 2],
        mlp_dgate,
        mlp_dup,
        mlp_ddown,
    )


def solution(mesh):
    charts, heads = mesh.devices.shape
    inner = Mesh(mesh.devices.reshape(charts, heads // 2, 2), ("dp", "hx", "hc"))
    every = ("dp", "hx", "hc")
    rows = P(every, None)
    vector = P(every)
    grid = P("dp", ("hx", "hc"), None)
    in_specs = (grid, grid, P("dp"), P("dp"))
    in_specs += (vector, rows, rows, rows, rows) * 2
    in_specs += (vector, rows, rows, rows, grid)
    out_specs = (grid, grid, grid)
    out_specs += (vector, rows, rows, rows, rows) * 2
    out_specs += (vector, rows, rows, rows)
    return jax.shard_map(
        on_device, mesh=inner, in_specs=in_specs, out_specs=out_specs, check_vma=False
    )
```

```python
import functools
import math

import jax
import jax.numpy as jnp
from jax import lax
from jax.experimental import pallas as pl
from jax.experimental.pallas import tpu as pltpu
from jax.sharding import Mesh
from jax.sharding import PartitionSpec as P

HEAD_DIM = 64
PAIR_LANES = 128
NEG_FILL = -1e30
EPS = 1e-06
F32 = jnp.float32
LOW = jnp.bfloat16


NT = (((1,), (1,)), ((), ()))
TN = (((0,), (0,)), ((), ()))


def dot_nt(left, right):
    return lax.dot_general(left, right, NT, preferred_element_type=F32)


def dot_tn(left, right):
    return lax.dot_general(left, right, TN, preferred_element_type=F32)


def dot_nn(left, right):
    return jnp.dot(left, right, preferred_element_type=F32)


FIXED = 3
SPANS = 8


def query_limits(info, queries, causal):
    last = info[0] - 1
    if not causal:
        return jnp.full((1, queries), last, jnp.int32), last
    lanes = lax.broadcasted_iota(jnp.int32, (1, queries), 1)
    span = queries // 2
    swapped = jnp.where(lanes < span, lanes + info[2] * span, lanes - info[2] * span)
    return jnp.minimum(info[1] + swapped, last), jnp.minimum(info[1] + queries - 1, last)


def key_places(info, chunk, span, queries, j):
    parts = chunk // span
    starts = [info[FIXED + j * parts + i] for i in range(parts)]
    inner = lax.broadcasted_iota(jnp.int32, (span, queries), 0)
    first = functools.reduce(jnp.minimum, starts)
    return jnp.concatenate([start + inner for start in starts], axis=0), first


def first_place(info, chunk, span, j):
    parts = chunk // span
    return functools.reduce(jnp.minimum, [info[FIXED + j * parts + i] for i in range(parts)])


def head_lanes(head):
    lanes = lax.broadcasted_iota(jnp.int32, (1, PAIR_LANES), 1)
    return (lanes // HEAD_DIM) == head


def fold(values, op):
    rows, columns = values.shape
    return op(values.reshape(rows // 8, 8, columns), axis=0)


def forward_kernel(causal, chunk, span, info, q_ref, k_ref, v_ref, c_ref, lse_ref, s_ref, m_ref, l_ref, a_ref):
    queries = q_ref.shape[0]
    chunks = k_ref.shape[0] // chunk
    scaling = 1.0 / math.sqrt(HEAD_DIM)
    limit, latest = query_limits(info, queries, causal)
    q_all = q_ref[...] * jnp.asarray(scaling, q_ref.dtype)
    q_heads = [jnp.where(head_lanes(h), q_all, jnp.zeros_like(q_all)) for h in range(2)]
    m_ref[...] = jnp.full(m_ref.shape, NEG_FILL, F32)
    l_ref[...] = jnp.zeros(l_ref.shape, F32)
    a_ref[...] = jnp.zeros(a_ref.shape, F32)

    @pl.loop(0, chunks)
    def _(j):
        @pl.when(first_place(info, chunk, span, j) <= latest)
        def _():
            rows = pl.ds(pl.multiple_of(j * chunk, chunk), chunk)
            keys = k_ref[rows, :]
            place, _ = key_places(info, chunk, span, queries, j)
            allowed = place <= limit
            for h in range(2):
                scores = jnp.where(allowed, dot_nt(keys, q_heads[h]), NEG_FILL)
                s_ref[h, rows, :] = scores
                m_ref[h] = jnp.maximum(m_ref[h], fold(scores, jnp.max))

    highest = [jnp.max(m_ref[h], axis=0, keepdims=True) for h in range(2)]

    @pl.loop(0, chunks)
    def _(j):
        @pl.when(first_place(info, chunk, span, j) <= latest)
        def _():
            rows = pl.ds(pl.multiple_of(j * chunk, chunk), chunk)
            values = v_ref[rows, :]
            for h in range(2):
                weight = jnp.exp(s_ref[h, rows, :] - highest[h])
                l_ref[h] = l_ref[h] + fold(weight, jnp.sum)
                a_ref[h] = a_ref[h] + dot_tn(values, weight.astype(LOW))

    parts = []
    for h in range(2):
        total = jnp.sum(l_ref[h], axis=0, keepdims=True)
        lse_ref[0, pl.ds(h, 1), :] = highest[h] + jnp.log(total)
        parts.append(a_ref[h, pl.ds(h * HEAD_DIM, HEAD_DIM), :] / total)
    c_ref[...] = jnp.concatenate(parts, axis=0).T.astype(c_ref.dtype)


def backward_kernel(causal, chunk, span, info, q_ref, k_ref, v_ref, c_ref, g_ref, lse_ref, dq_ref, dk_ref, dv_ref, a_ref):
    queries = q_ref.shape[0]
    chunks = k_ref.shape[0] // chunk
    scaling = 1.0 / math.sqrt(HEAD_DIM)
    limit, latest = query_limits(info, queries, causal)
    q_all = q_ref[...] * jnp.asarray(scaling, q_ref.dtype)
    g_all = g_ref[...]
    q_heads = [jnp.where(head_lanes(h), q_all, jnp.zeros_like(q_all)) for h in range(2)]
    g_heads = [jnp.where(head_lanes(h), g_all, jnp.zeros_like(g_all)) for h in range(2)]
    product = (c_ref[...].astype(F32) * g_all.astype(F32)).T
    centres = [
        jnp.sum(product[h * HEAD_DIM : (h + 1) * HEAD_DIM], axis=0, keepdims=True) for h in range(2)
    ]
    logs = [lse_ref[0, pl.ds(h, 1), :] for h in range(2)]
    a_ref[...] = jnp.zeros(a_ref.shape, F32)

    @pl.loop(0, chunks)
    def _(j):
        start = first_place(info, chunk, span, j)
        rows = pl.ds(pl.multiple_of(j * chunk, chunk), chunk)

        @pl.when(start <= latest)
        def _():
            keys = k_ref[rows, :]
            values = v_ref[rows, :]
            place, _ = key_places(info, chunk, span, queries, j)
            allowed = place <= limit
            dk = jnp.zeros((chunk, PAIR_LANES), F32)
            dv = jnp.zeros((chunk, PAIR_LANES), F32)
            for h in range(2):
                scores = jnp.where(allowed, dot_nt(keys, q_heads[h]), NEG_FILL)
                prob = jnp.exp(scores - logs[h])
                dprob = dot_nt(values, g_heads[h])
                dv = dv + dot_nn(prob.astype(LOW), g_heads[h])
                dscore = (prob * (dprob - centres[h])).astype(LOW)
                dk = dk + dot_nn(dscore, q_heads[h])
                a_ref[h] = a_ref[h] + dot_tn(keys, dscore)
            dk_ref[rows, :] = dk.astype(dk_ref.dtype)
            dv_ref[rows, :] = dv.astype(dv_ref.dtype)

        @pl.when(start > latest)
        def _():
            dk_ref[rows, :] = jnp.zeros((chunk, PAIR_LANES), dk_ref.dtype)
            dv_ref[rows, :] = jnp.zeros((chunk, PAIR_LANES), dv_ref.dtype)

    parts = [a_ref[h, pl.ds(h * HEAD_DIM, HEAD_DIM), :] for h in range(2)]
    dq_ref[...] = (jnp.concatenate(parts, axis=0).T * scaling).astype(dq_ref.dtype)


def lane_spec(rows):
    return pl.BlockSpec((rows, PAIR_LANES), lambda i, info: (0, i))


def stat_spec(queries):
    return pl.BlockSpec((1, 2, queries), lambda i, info: (i, 0, 0))


def attention_forward(info, queries, keys, values, causal, span):
    chunk = math.gcd(SPANS * span, keys.shape[0])
    rows, features = queries.shape
    key_rows = keys.shape[0]
    pairs = features // PAIR_LANES
    return pl.pallas_call(
        functools.partial(forward_kernel, causal, chunk, span),
        out_shape=(
            jax.ShapeDtypeStruct((rows, features), LOW),
            jax.ShapeDtypeStruct((pairs, 2, rows), F32),
        ),
        grid_spec=pltpu.PrefetchScalarGridSpec(
            num_scalar_prefetch=1,
            grid=(pairs,),
            in_specs=[lane_spec(rows), lane_spec(key_rows), lane_spec(key_rows)],
            out_specs=[lane_spec(rows), stat_spec(rows)],
            scratch_shapes=[
                pltpu.VMEM((2, key_rows, rows), F32),
                pltpu.VMEM((2, 8, rows), F32),
                pltpu.VMEM((2, 8, rows), F32),
                pltpu.VMEM((2, PAIR_LANES, rows), F32),
            ],
        ),
        compiler_params=pltpu.CompilerParams(vmem_limit_bytes=VMEM_LIMIT),
        cost_estimate=pl.CostEstimate(flops=rows, transcendentals=0, bytes_accessed=0),
    )(info, queries, keys, values)


def attention_backward(info, queries, keys, values, context, grads, lse, causal, span):
    chunk = math.gcd(SPANS * span, keys.shape[0])
    rows, features = queries.shape
    key_rows = keys.shape[0]
    pairs = features // PAIR_LANES
    return pl.pallas_call(
        functools.partial(backward_kernel, causal, chunk, span),
        out_shape=(
            jax.ShapeDtypeStruct((rows, features), LOW),
            jax.ShapeDtypeStruct((key_rows, features), LOW),
            jax.ShapeDtypeStruct((key_rows, features), LOW),
        ),
        grid_spec=pltpu.PrefetchScalarGridSpec(
            num_scalar_prefetch=1,
            grid=(pairs,),
            in_specs=[
                lane_spec(rows),
                lane_spec(key_rows),
                lane_spec(key_rows),
                lane_spec(rows),
                lane_spec(rows),
                stat_spec(rows),
            ],
            out_specs=[lane_spec(rows), lane_spec(key_rows), lane_spec(key_rows)],
            scratch_shapes=[pltpu.VMEM((2, PAIR_LANES, rows), F32)],
        ),
        compiler_params=pltpu.CompilerParams(vmem_limit_bytes=VMEM_LIMIT),
        cost_estimate=pl.CostEstimate(flops=rows, transcendentals=0, bytes_accessed=0),
    )(info, queries, keys, values, context, grads, lse)


SMEM_SPEC = pl.BlockSpec(memory_space=pltpu.SMEM)


def vmem_specs(number):
    return [pl.BlockSpec(memory_space=pltpu.VMEM)] * number


def cuts_of(widths):
    return [sum(widths[:i]) for i in range(len(widths))]


def place_blocks(index, first, later, targets):
    half, rows, _ = first.shape
    cuts = cuts_of([target.shape[1] for target in targets])

    @pl.loop(0, 2 * half)
    def _(step):
        at = index[step]
        place = pl.ds(pl.multiple_of(step * rows, rows), rows)

        def put(source, block):
            for cut, target in zip(cuts, targets):
                target[place, :] = source[block, :, pl.ds(cut, target.shape[1])]

        @pl.when(at < half)
        def _():
            put(first, at)

        @pl.when(at >= half)
        def _():
            put(later, at - half)


def send_order(index, whole, keep, give):
    half, rows, _ = keep.shape

    @pl.loop(0, half)
    def _(step):
        for side, target in enumerate((keep, give)):
            at = pl.ds(pl.multiple_of(index[step + side * half] * rows, rows), rows)
            target[step] = whole[at, :]


def whole_kernel(index, first, later, *targets):
    place_blocks(index, first, later, targets)


def to_whole(first, later, index, widths):
    half, rows, columns = first.shape
    count = 2 * half
    if rows % 16:
        blocks = jnp.concatenate([first, later], axis=0)
        whole = jnp.take(blocks, index, axis=0).reshape(count * rows, columns)
        return [whole[:, cut : cut + width] for cut, width in zip(cuts_of(widths), widths)]
    return run_kernel(
        whole_kernel,
        [low_shape(count * rows, width) for width in widths],
        count * rows * columns,
        [index],
        [first, later],
    )


class Stage:
    def __init__(self, loads, stores):
        self.loads, self.stores = loads, stores
        self.waited, self.sent = set(), set()

    def need(self, *numbers):
        for i in numbers or range(len(self.loads)):
            if i not in self.waited:
                self.waited.add(i)
                self.loads[i].wait()

    def done(self, *numbers):
        for i in numbers or range(len(self.stores)):
            if i not in self.sent:
                self.sent.add(i)
                self.stores[i].start()


def staged_kernel(body, late, sizes, *refs):
    parts, at = [], 0
    for size in sizes:
        parts.append(refs[at : at + size])
        at += size
    tables, arrays, streamed, outs, scratch, held_in, held_out, (in_sems, out_sems) = parts
    stage = Stage(
        [pltpu.make_async_copy(a, b, in_sems.at[i]) for i, (a, b) in enumerate(zip(arrays, held_in))],
        [pltpu.make_async_copy(a, b, out_sems.at[i]) for i, (a, b) in enumerate(zip(held_out, outs))],
    )
    for load in stage.loads:
        load.start()
    if late:
        body(stage, *tables, *held_in, *streamed, *held_out, *scratch)
    else:
        stage.need()
        body(*tables, *held_in, *streamed, *held_out, *scratch)
    stage.need()
    stage.done()
    for store in stage.stores:
        store.wait()


HBM_SPEC = pl.BlockSpec(memory_space=pltpu.HBM)


def run_kernel(body, out_shape, cost, tables, arrays, scratch=(), streamed=(), late=False):
    sizes = (len(tables), len(arrays), len(streamed), len(out_shape), len(scratch))
    sizes += (len(arrays), len(out_shape), 2)
    held = [pltpu.VMEM(x.shape, x.dtype) for x in [*arrays, *out_shape]]
    sems = [pltpu.SemaphoreType.DMA((len(arrays),)), pltpu.SemaphoreType.DMA((len(out_shape),))]
    return pl.pallas_call(
        functools.partial(staged_kernel, body, late, sizes),
        out_shape=out_shape,
        in_specs=[SMEM_SPEC] * len(tables) + [HBM_SPEC] * (len(arrays) + len(streamed)),
        out_specs=[HBM_SPEC] * len(out_shape),
        scratch_shapes=list(scratch) + held + sems,
        compiler_params=pltpu.CompilerParams(vmem_limit_bytes=VMEM_LIMIT),
        cost_estimate=pl.CostEstimate(flops=cost // 1000, transcendentals=0, bytes_accessed=0),
    )(*tables, *arrays, *streamed)


VMEM_LIMIT = 56 << 20


def low_shape(*shape):
    return jax.ShapeDtypeStruct(shape, LOW)


def full_shape(*shape):
    return jax.ShapeDtypeStruct(shape, F32)


def unit_tile(source, at, second):
    lanes = 2 * HEAD_DIM
    start = 2 * at * lanes + (HEAD_DIM if second else 0)
    return jnp.concatenate(
        [source[:, pl.ds(start, HEAD_DIM)], source[:, pl.ds(start + lanes, HEAD_DIM)]], axis=1
    )


def shards_kernel(kinds, place, *refs):
    sources, targets = refs[:-2], refs[-2:]

    def write(target, second):
        cut = 0
        for kind, source in zip(kinds, sources):
            columns = source.shape[1]
            if kind == "all":
                target[:, pl.ds(cut, columns)] = source[...]
                cut += columns
                continue
            if kind == "half":
                start = columns // 2 if second else 0
                target[:, pl.ds(cut, columns // 2)] = source[:, pl.ds(start, columns // 2)]
            else:
                for tile in range(columns // 256):
                    target[:, pl.ds(cut + 128 * tile, 128)] = unit_tile(source, tile, second)
            cut += columns // 2

    @pl.when(place[0] == 0)
    def _():
        write(targets[0], False)
        write(targets[1], True)

    @pl.when(place[0] != 0)
    def _():
        write(targets[0], True)
        write(targets[1], False)


def rows_kernel(widths, piece, place, mine, other, down, *targets):
    *widths, matrices, extra = widths
    rows = mine.shape[0]

    def write(upper, lower):
        cut = 0
        for target, width in zip(targets[:-1], widths):
            target[0, pl.ds(0, rows), :] = upper[:, pl.ds(cut, width)]
            target[0, pl.ds(rows, rows), :] = lower[:, pl.ds(cut, width)]
            cut += width
        packed = targets[-1]
        columns = (mine.shape[1] - cut - extra) // matrices
        step = 8
        base = matrices * (2 * rows // piece) * columns
        last = base + down.shape[1] * (down.shape[0] // piece)
        for start in range(0, 2 * rows, step):
            source = upper if start < rows else lower
            number, inner = start // piece, start % piece
            for matrix in range(matrices):
                place_at = (matrix * (2 * rows // piece) + number) * columns
                packed[pl.ds(inner, step), pl.ds(place_at, columns)] = source[
                    pl.ds(start % rows, step), pl.ds(cut + matrix * columns, columns)
                ]
            packed[pl.ds(inner, step), pl.ds(last + number * extra, extra)] = source[
                pl.ds(start % rows, step), pl.ds(cut + matrices * columns, extra)
            ]
        width = down.shape[1]
        for number in range(down.shape[0] // piece):
            packed[:, pl.ds(base + number * width, width)] = down[pl.ds(number * piece, piece), :]

    @pl.when(place[0] == 0)
    def _():
        write(mine, other)

    @pl.when(place[0] != 0)
    def _():
        write(other, mine)


def cut_shards(place, shards, kinds):
    rows = shards[0].shape[0]
    columns = sum(w.shape[1] if k == "all" else w.shape[1] // 2 for w, k in zip(shards, kinds))
    return run_kernel(
        functools.partial(shards_kernel, kinds), [low_shape(rows, columns)] * 2, rows * columns, [place], shards
    )


def join_rows(place, mine, other, down, widths, extra, piece):
    rows = 2 * mine.shape[0]
    rest = mine.shape[1] - sum(widths)
    packed = rest * (rows // piece) + down.shape[1] * (down.shape[0] // piece)
    return run_kernel(
        functools.partial(rows_kernel, [*widths, 2, extra], piece),
        [low_shape(1, rows, width) for width in widths] + [low_shape(piece, packed)],
        rows * rest,
        [place],
        [mine, other, down],
    )


def pieces_kernel(cut, source, target, held, sem):
    blocks, pieces, piece, columns = held.shape
    copies = [
        pltpu.make_async_copy(
            source.at[:, :, pl.ds(cut + i * columns, columns)], held.at[:, i], sem.at[i]
        )
        for i in range(pieces)
    ]
    for copy in copies:
        copy.start()
    for copy in copies:
        copy.wait()
    target[...] = held[...].reshape(target.shape)


def from_pieces(packed, cut, pieces, columns):
    blocks, piece, _ = packed.shape
    return pl.pallas_call(
        functools.partial(pieces_kernel, cut),
        out_shape=low_shape(blocks * pieces * piece, columns),
        in_specs=[HBM_SPEC],
        out_specs=pl.BlockSpec(memory_space=pltpu.VMEM),
        scratch_shapes=[
            pltpu.VMEM((blocks, pieces, piece, columns), LOW),
            pltpu.SemaphoreType.DMA((pieces,)),
        ],
        cost_estimate=pl.CostEstimate(flops=1000, transcendentals=0, bytes_accessed=0),
    )(packed)


def normalize(values):
    inverse = lax.rsqrt(jnp.mean(values * values, axis=-1, keepdims=True) + EPS)
    return values * inverse, inverse


def norm_back(normed, inverse, gain, grads):
    scaled = grads * gain
    return inverse * (scaled - normed * jnp.mean(scaled * normed, axis=-1, keepdims=True))


def gelu_parts(gate):
    factor = math.sqrt(2.0 / math.pi)
    inner = jnp.tanh(factor * (gate + 0.044715 * gate * gate * gate))
    value = 0.5 * gate * (1.0 + inner)
    slope = 0.5 * (1.0 + inner) + 0.5 * gate * (1.0 - inner * inner) * factor * (
        1.0 + 3.0 * 0.044715 * gate * gate
    )
    return value, slope


def head_slices(place, half):
    mine = pl.ds(pl.multiple_of(place[0] * half, half), half)
    other = pl.ds(pl.multiple_of((1 - place[0]) * half, half), half)
    return mine, other


def query_kernel(packed, stage, *refs):
    if packed:
        index_a, index_b, first_a, later_a, first_b, later_b, token_m, token_g = refs[:8]
        rows_ref, normed_ref, q_ref, k_ref, v_ref, wq, gain_cols, wkv = refs[8:]
        stage.need(0, 1)
        place_blocks(index_a, first_a, later_a, [wq, gain_cols])
        stage.done(5, 6)
        stage.need(2, 3)
        place_blocks(index_b, first_b, later_b, [wkv])
        stage.done(7)
    else:
        wq, gain_cols, wkv, token_m, token_g = refs[:5]
        rows_ref, normed_ref, q_ref, k_ref, v_ref = refs[5:]
    stage.need()
    gain_rows = gain_cols[...].astype(F32).T[0:8]
    rows_ref[...] = gain_rows
    groups, own, _ = token_m.shape
    half = q_ref.shape[1]
    for group in range(groups):
        for side, source in enumerate((token_m, token_g)):
            plain, _ = normalize(source[group].astype(F32))
            at = pl.ds((2 * group + side) * own, own)
            normed_ref[at, :] = (plain * gain_rows[0:1]).astype(LOW)
    stage.done(0, 1)
    q_ref[...] = dot_nn(normed_ref[pl.ds(0, 2 * own), :], wq[...]).astype(LOW)
    stage.done(2)
    value = dot_nn(normed_ref[...], wkv[...]).astype(LOW)
    k_ref[...] = value[:, :half]
    v_ref[...] = value[:, half:]


def add_context(place, target, base, c_m, c_g, w_m, w_g):
    rows, half = c_m.shape
    own = rows // 2
    mine, other = head_slices(place, half)
    for side in range(2):
        at = pl.ds(side * own, own)
        left = c_m[at, :]
        right = c_g[pl.ds((1 - side) * own, own), :]
        for weight, columns in ((w_m, mine), (w_g, other)):
            value = dot_nn(left, weight[mine, :]) + dot_nn(right, weight[other, :])
            target[at, columns] = base(side, columns) + value


def cross_query_kernel(stage, place, token_m, token_g, c_m, c_g, w_m, w_g, rows_ref, wq, h_ref, normed_ref, q_ref):
    tokens = (token_m, token_g)
    base = lambda side, columns: tokens[side][0, :, columns].astype(F32)
    stage.need(*range(7))
    add_context(place, h_ref, base, c_m, c_g, w_m, w_g)
    stage.done(0)
    plain, _ = normalize(h_ref[...])
    normed_ref[...] = (plain * rows_ref[1:2, :]).astype(LOW)
    stage.done(1)
    stage.need()
    q_ref[...] = dot_nn(normed_ref[...], wq[...]).astype(LOW)


def memory_kernel(packed, stage, *refs):
    if packed:
        index, first, later, patch_m, patch_g, k_ref, v_ref, wkv = refs
        stage.need(0, 1)
        place_blocks(index, first, later, [wkv])
        stage.done(2)
    else:
        wkv, patch_m, patch_g, k_ref, v_ref = refs
    stage.need()
    count = patch_m.shape[0]
    half = k_ref.shape[1]
    for side, source in enumerate((patch_m, patch_g)):
        value = dot_nn(source[...], wkv[...]).astype(LOW)
        k_ref[pl.ds(side * count, count), :] = value[:, :half]
        v_ref[pl.ds(side * count, count), :] = value[:, half:]


def lane_column(column, lane):
    lanes = lax.broadcasted_iota(jnp.int32, (1, PAIR_LANES), 1)
    return jnp.where(lanes == lane, column, 0.0)


def mlp_kernel(
    chunk,
    stage,
    place,
    h_in,
    c_m,
    c_g,
    out_m,
    out_g,
    rows_ref,
    cols_ref,
    g_m,
    g_g,
    w_ref,
    h_ref,
    part_ref,
    keep_ref,
    give_ref,
    gain_ref,
    grad_ref,
    gate_w,
    up_w,
    down_w,
    a_ref,
    t_ref,
    g_ref,
    p_acc,
    d_acc,
    r_acc,
    sems,
):
    blocks, pieces, piece, units = gate_w.shape
    down_pieces, width = down_w.shape[1], down_w.shape[3]
    total = blocks * pieces * piece
    own = g_m.shape[0]
    moves = []
    for number in range(pieces):
        moves.append((w_ref.at[:, :, pl.ds(number * units, units)], gate_w.at[:, number]))
    for number in range(pieces):
        moves.append((w_ref.at[:, :, pl.ds((pieces + number) * units, units)], up_w.at[:, number]))
    base = 2 * pieces * units
    for number in range(down_pieces):
        moves.append((w_ref.at[:, :, pl.ds(base + number * width, width)], down_w.at[:, number]))
    copies = [pltpu.make_async_copy(a, b, sems.at[i]) for i, (a, b) in enumerate(moves)]
    for copy in copies:
        copy.start()
    stage.need(*range(6))
    add_context(
        place, h_ref, lambda side, columns: h_in[pl.ds(side * own, own), columns], c_m, c_g, out_m, out_g
    )
    stage.done(0)
    plain, _ = normalize(h_ref[...])
    a_ref[...] = (plain * rows_ref[2:3, :]).astype(LOW)
    t_ref[...] = a_ref[...].T
    stage.need()
    g_ref[pl.ds(0, own), :] = g_m[...]
    g_ref[pl.ds(own, own), :] = g_g[...]
    p_acc[...] = jnp.zeros(p_acc.shape, F32)
    d_acc[...] = jnp.zeros(d_acc.shape, F32)
    r_acc[...] = jnp.zeros(r_acc.shape, F32)
    for copy in copies:
        copy.wait()

    per_block = down_pieces * piece
    step_blocks = chunk // per_block

    @pl.loop(0, units // chunk)
    def _(step):
        start = pl.multiple_of(step * chunk, chunk)
        a_in = a_ref[...]
        g_in = g_ref[...]
        columns = pl.ds(start, chunk)
        gate_part = gate_w[:, :, :, columns].reshape(total, chunk)
        up_part = up_w[:, :, :, columns].reshape(total, chunk)
        down_at = pl.ds(step * step_blocks, step_blocks)
        down_part = down_w[down_at].reshape(chunk, width)
        gate = dot_nn(a_in, gate_part)
        up = dot_nn(a_in, up_part)
        active, slope = gelu_parts(gate)
        mixed = (active * up).astype(LOW)
        grad = dot_nt(g_in, down_part)
        gate_low = (grad * up * slope).astype(LOW)
        up_low = (grad * active).astype(LOW)
        d_acc[...] += dot_nn(mixed, down_part)
        p_acc[...] += dot_nt(gate_low, gate_part) + dot_nt(up_low, up_part)
        dgate = dot_nn(t_ref[...], gate_low)
        dup = dot_nn(t_ref[...], up_low)
        gain_terms = dgate * gate_part.astype(F32) + dup * up_part.astype(F32)
        for lane in range(0, chunk, PAIR_LANES):
            r_acc[...] += gain_terms[:, lane : lane + PAIR_LANES]
        dgate = dgate.astype(LOW).reshape(blocks, pieces, piece, chunk)
        dup = dup.astype(LOW).reshape(blocks, pieces, piece, chunk)
        for number in range(pieces):
            gate_at = pl.multiple_of(number * units + start, chunk)
            up_at = pl.multiple_of((pieces + number) * units + start, chunk)
            grad_ref[:, :, pl.ds(gate_at, chunk)] = dgate[:, number]
            grad_ref[:, :, pl.ds(up_at, chunk)] = dup[:, number]
        ddown = dot_tn(mixed, g_in).astype(LOW).reshape(step_blocks, down_pieces, piece, width)
        for number in range(down_pieces):
            grad_ref[down_at, :, pl.ds(base + number * width, width)] = ddown[:, number]

    stage.done(5)
    part_ref[...] = p_acc[...].astype(LOW)
    stage.done(1)
    keep_ref[...] = d_acc[pl.ds(0, own), :]
    give_ref[...] = d_acc[pl.ds(own, own), :].astype(LOW)
    summed = jnp.sum(r_acc[...], axis=1, keepdims=True)
    gain_ref[...] = lane_column(summed / cols_ref[:, 2:3].astype(F32), 2)


def branch_kernel(gain_at, stage, place, *refs):
    h_ref, rows_ref, part_m, part_g, w_m, w_g = refs[:6]
    base, (d_ref, low_ref, c_ref) = refs[6:-3], refs[-3:]
    rows = h_ref.shape[0]
    own = rows // 2
    half = w_m.shape[1]
    mine, other = head_slices(place, half)
    stage.need(0, 1, 2, 3, *range(6, 6 + len(base)))
    for side in range(2):
        at = pl.ds(side * own, own)
        plain, inverse = normalize(h_ref[at, :])
        got = part_g[pl.ds((1 - side) * own, own), :]
        grads = part_m[at, :].astype(F32) + got.astype(F32)
        value = norm_back(plain, inverse, rows_ref[gain_at : gain_at + 1, :], grads)
        before = base[side][...].astype(F32) if len(base) == 2 else base[0][at, :]
        d_ref[at, :] = before + value
    stage.done(0)
    low_ref[...] = d_ref[...].astype(LOW)
    stage.done(1)
    stage.need()
    value = dot_nt(low_ref[:, mine], w_m[mine, :]) + dot_nt(low_ref[:, other], w_g[mine, :])
    c_ref[...] = value.astype(LOW)


def dot_rows(left, right):
    columns = left.shape[1]
    step = math.gcd(columns, 256)
    return [(i, dot_tn(left[:, i : i + step], right)) for i in range(0, columns, step)]


def out_grad(place, whole, cut, c_m, c_g, branch):
    rows, half = c_m.shape
    own = rows // 2
    mine, other = head_slices(place, half)
    grads = branch[:, mine]
    columns = pl.ds(cut, half)
    whole[mine, columns] = dot_tn(c_m[...], grads).astype(LOW)
    value = dot_tn(c_g[pl.ds(own, own), :], grads[:own]) + dot_tn(c_g[pl.ds(0, own), :], grads[own:])
    whole[other, columns] = value.astype(LOW)


def weight_grads(targets, lefts, rights, gain_acc=None):
    features = lefts[0].shape[1]
    step = math.gcd(features, 256)

    for number in range(features // step):
        at = pl.ds(number * step, step)
        turned = [left[:, at].T for left in lefts]
        for (whole, cut, weight), terms in zip(targets, rights):
            width = terms[0].shape[1]
            value = sum(dot_nn(left, right[...]) for left, right in zip(turned, terms))
            whole[at, pl.ds(cut, width)] = value.astype(LOW)
            if weight is not None:
                products = value * weight[at, :].astype(F32)
                gain_acc[at, :] += sum(
                    products[:, lane : lane + PAIR_LANES] for lane in range(0, width, PAIR_LANES)
                )


def cross_grads_kernel(packed, stage, place, *refs):
    index, refs = (refs[:2], refs[2:]) if packed else ((), refs)
    c_m, c_g, branch, normed, dq, patch_m, patch_g, dk, dv, wq, cols_ref = refs[:11]
    one_m, one_g, branch_one = refs[11:14]
    gain_ref, *outs, whole_a, whole_b, gain_acc = refs[14:]
    half = dq.shape[1]
    stage.need(0, 1, 2, 3, 4, 9, 10, 11, 12, 13)
    out_grad(place, whole_a, 2 * half, one_m, one_g, branch_one)
    count = patch_m.shape[0]
    gain_acc[...] = jnp.zeros(gain_acc.shape, F32)
    out_grad(place, whole_a, 0, c_m, c_g, branch)
    weight_grads([(whole_a, half, wq)], [normed], [[dq]], gain_acc)
    if packed:
        send_order(index[0], whole_a, outs[0], outs[1])
        stage.done(1, 2)
    summed = jnp.sum(gain_acc[...], axis=1, keepdims=True)
    gain_ref[...] = lane_column(summed / cols_ref[:, 1:2].astype(F32), 1)
    stage.need()
    halves = [[g.at[pl.ds(i * count, count), :] for i in range(2)] for g in (dk, dv)]
    weight_grads(
        [(whole_b, 0, None), (whole_b, half, None)], [patch_m, patch_g], halves
    )
    if packed:
        send_order(index[1], whole_b, outs[2], outs[3])


def self_grads_kernel(packed, stage, place, *refs):
    index, refs = (refs[:2], refs[2:]) if packed else ((), refs)
    normed, dq, dk, dv, wq, wkv, cols_ref, gain_two, gain_three = refs[:9]
    *outs, whole_a, whole_b, gain_acc = refs[9:]
    rows, half = dq.shape
    gain_acc[...] = jnp.zeros(gain_acc.shape, F32)
    stage.need(0, 3, 5)
    weight_grads([(whole_b, 0, wkv.at[:, pl.ds(half, half)])], [normed], [[dv]], gain_acc)
    stage.need(2)
    weight_grads([(whole_b, half, wkv.at[:, pl.ds(0, half)])], [normed], [[dk]], gain_acc)
    if packed:
        send_order(index[1], whole_b, outs[2], outs[3])
        stage.done(2, 3)
    stage.need()
    weight_grads([(whole_a, 0, wq)], [normed.at[pl.ds(0, rows), :]], [[dq]], gain_acc)
    summed = jnp.sum(gain_acc[...], axis=1, keepdims=True)
    gains = lane_column(summed / cols_ref[:, 0:1].astype(F32), 0) + gain_two[...] + gain_three[...]
    whole_a[:, pl.ds(half, PAIR_LANES)] = gains.astype(LOW)
    if packed:
        send_order(index[0], whole_a, outs[0], outs[1])


def back_kernel(grads, weight, out):
    out[...] = dot_nt(grads[...], weight[...]).astype(LOW)


def rows_back_kernel(spans, with_query, *refs):
    dk, dv, wkv = refs[:3]
    queries = refs[3:5] if with_query else None
    half = dk.shape[1]
    wk, wv = wkv.at[:, pl.ds(0, half)], wkv.at[:, pl.ds(half, half)]
    keep, give = refs[-2:]
    rows = dk.shape[0] // len(spans)
    for number, (mine, place) in enumerate(spans):
        at = pl.ds(number * rows, rows)
        value = dot_nt(dk[at, :], wk[...]) + dot_nt(dv[at, :], wv[...])
        if queries and number < 2:
            value = value + dot_nt(queries[0][at, :], queries[1][...])
        if mine:
            keep[place] = value
        else:
            give[place] = value.astype(LOW)


def feed_forward_grads_kernel(pieces, units, place, sums, got, gate_ref, up_ref, down_ref):
    piece = sums.shape[0]
    rows = got.shape[0]
    hidden = got.shape[1] // 2
    step = 8

    def write(second):
        for row in range(0, rows, step):
            at = row + (rows if second else 0)
            number, inner = at // piece, at % piece
            for matrix, target in enumerate((gate_ref, up_ref)):
                start = (matrix * pieces + number) * hidden
                mine = sums[pl.ds(inner, step), pl.ds(start, hidden)].astype(F32)
                other = got[pl.ds(row, step), pl.ds(matrix * hidden, hidden)].astype(F32)
                pair = (other, mine) if second else (mine, other)
                for unit in range(0, hidden, units):
                    tile = jnp.concatenate([part[:, unit : unit + units] for part in pair], axis=1)
                    target[pl.ds(row, step), pl.ds(2 * unit, 2 * units)] = tile

    @pl.when(place[0] == 0)
    def _():
        write(False)

    @pl.when(place[0] != 0)
    def _():
        write(True)

    base = 2 * pieces * hidden
    width = down_ref.shape[1]
    for number in range(down_ref.shape[0] // piece):
        down_ref[pl.ds(number * piece, piece), :] = sums[:, pl.ds(base + number * width, width)].astype(F32)


def columns_kernel(place, keep, got, *targets):
    rows = got.shape[0]

    def write(start, first, later):
        for number, target in enumerate(targets):
            half = target.shape[1] // 2
            columns = pl.ds(number * half, half)
            target[:, pl.ds(0, half)] = first(start, columns)
            target[:, pl.ds(half, half)] = later(start, columns)

    from_keep = lambda start, columns: keep[pl.ds(start, rows), columns]
    from_got = lambda start, columns: got[:, columns]

    @pl.when(place[0] == 0)
    def _():
        write(0, from_keep, from_got)

    @pl.when(place[0] != 0)
    def _():
        write(rows, from_got, from_keep)


def after(values, *others):
    return lax.optimization_barrier((values, *others))[0]


def together(*values):
    return lax.optimization_barrier(values)


class Ring:
    def __init__(self):
        self.charts = lax.axis_size("dp")
        self.groups = lax.axis_size("hx")
        self.half = lax.axis_index("hc").astype(jnp.int32)
        self.second = self.half == 1
        self.place = self.half[None]
        self.group = lax.axis_index("hx").astype(jnp.int32)
        self.block = lax.axis_index("dp").astype(jnp.int32) * self.groups + self.group
        self.blocks = self.charts * self.groups
        chart_bits = [("dp", 1 << i) for i in range(self.charts.bit_length() - 1)]
        self.group_bits = [("hx", 1 << i) for i in range(self.groups.bit_length() - 1)]
        self.far = chart_bits[:0:-1]
        near = chart_bits[:1]
        self.tails = (near + self.group_bits, self.group_bits + near)
        self.orders = tuple(self.far + tail for tail in self.tails)

    def send(self, values, axis, bit):
        size = self.charts if axis == "dp" else self.groups
        return lax.ppermute(values, axis, [(i, i ^ bit) for i in range(size)])

    def swap(self, values):
        return lax.ppermute(values, "hc", [(0, 1), (1, 0)])

    def in_order(self, mine, other):
        return jnp.where(self.second, other, mine), jnp.where(self.second, mine, other)

    def steps(self, order):
        return [bit * self.groups if axis == "dp" else bit for axis, bit in order]

    def arrivals(self):
        apart = self.block ^ jnp.arange(self.blocks, dtype=jnp.int32)
        indices = []
        for order in self.orders:
            index = jnp.zeros((self.blocks,), jnp.int32)
            for place, step in enumerate(self.steps(order)):
                index = index + jnp.where((apart & step) != 0, 1 << place, 0)
            indices.append(index)
        return indices

    def origins(self):
        indices = []
        for order in self.orders:
            masks = [0]
            for step in self.steps(order):
                masks = masks + [m ^ step for m in masks]
            indices.append(self.block ^ jnp.asarray(masks, jnp.int32))
        return indices

    def far_masks(self):
        masks = [0]
        for _, bit in self.far:
            masks = masks + [m | bit for m in masks]
        return masks

    def far_step(self, blocks, step):
        return jnp.concatenate([blocks, self.send(blocks, *self.far[step])], axis=0)

    def near_step(self, parts, step):
        return [self.send(part, *tail[step]) for part, tail in zip(parts, self.tails)]

    def near_sends(self, gives, place):
        return [self.send(give, *tail[place]) for give, tail in zip(gives, self.tails)]

    def near_sums(self, keeps, gots, place):
        halves = [got.shape[0] // 2 for got in gots]
        add = lambda k, g: (k.astype(F32) + g.astype(F32)).astype(LOW)
        gives = [add(k[h:], g[h:]) for k, g, h in zip(keeps, gots, halves)]
        keeps = [add(k[:h], g[:h]) for k, g, h in zip(keeps, gots, halves)]
        return keeps, gives

    def far_sends(self, keeps, gots):
        count = 1 << len(self.far)
        add = lambda r: [
            k[r : r + 1].astype(F32) + g[r : r + 1].astype(F32) for k, g in zip(keeps, gots)
        ]
        block = lambda r: jnp.concatenate(add(r), axis=2)
        if len(self.far) == 2:
            masks = self.far_masks()
            return block(0), [self.send(block(r).astype(LOW), "dp", masks[r]) for r in range(1, count)]
        keep = jnp.concatenate([block(r) for r in range(count)], axis=0)
        for axis, bit in reversed(self.far[1:]):
            half = keep.shape[0] // 2
            keep = keep[:half] + self.send(keep[half:].astype(LOW), axis, bit).astype(F32)
        return keep[:1], [self.send(keep[1:].astype(LOW), *self.far[0])]

    def far_sum(self, own, gots):
        return sum((got.astype(F32) for got in gots), own)[0]

    def far_first(self, keeps, gots):
        count = 1 << len(self.far)
        add = lambda r: jnp.concatenate(
            [k[r].astype(F32) + g[r].astype(F32) for k, g in zip(keeps, gots)], axis=2
        )
        keep, give = add(slice(0, count // 2)), add(slice(count // 2, None)).astype(LOW)
        return keep, self.send(give, *self.far[-1])

    def far_last(self, keep, got):
        for axis, bit in reversed(self.far[:-1]):
            half = keep.shape[0] // 2
            give = (keep[half:] + got[half:].astype(F32)).astype(LOW)
            keep = keep[:half] + got[:half].astype(F32)
            got = self.send(give, axis, bit)
        return keep, [got]

    def halve_wholes(self, wholes, rows):
        keeps, gives = [], []
        for whole, index in zip(wholes, self.origins()):
            blocks = jnp.take(whole.reshape(self.blocks, rows, -1), index, axis=0)
            keeps.append(blocks[: self.blocks // 2])
            gives.append(blocks[self.blocks // 2 :])
        return keeps, gives

    def across(self, mine):
        rows = mine[None]
        for axis, bit in self.group_bits:
            rows = jnp.concatenate([rows, self.send(rows, axis, bit)], axis=0)
        return rows

    def halves(self, first, later):
        mine = jnp.where(self.second, later, first)
        give = jnp.where(self.second, first, later)
        return jnp.concatenate(self.in_order(mine, self.swap(give)), axis=0)

    def pair_sum(self, keep, give):
        return keep + self.swap(give.astype(LOW)).astype(F32)

    def group_terms(self, total):
        for axis, bit in reversed(self.group_bits):
            middle = total.shape[0] // 2
            total = total[:middle] + self.send(total[middle:].astype(LOW), axis, bit).astype(F32)
        return total[0]

    def finished(self, keep, count):
        rows = keep.shape[0] // 2
        give = lax.dynamic_slice_in_dim(keep, (1 - self.half) * rows, rows, 0)
        got = self.swap(give)
        width = keep.shape[1] // count * 2
        return run_kernel(
            columns_kernel, [full_shape(rows, width)] * count, rows * width, [self.place], [keep, got]
        )


def column_halves(weights):
    half = weights[0].shape[1] // 2
    return [jnp.concatenate([w[:, i * half : (i + 1) * half] for w in weights], axis=1) for i in range(2)]


def unit_halves(weight, units):
    rows, columns = weight.shape
    split = weight.reshape(rows, columns // (2 * units), 2, units)
    return split[:, :, 0].reshape(rows, -1), split[:, :, 1].reshape(rows, -1)


def unit_whole(first, later, units):
    rows, columns = first.shape
    pieces = [part.reshape(rows, columns // units, 1, units) for part in (first, later)]
    return jnp.concatenate(pieces, axis=2).reshape(rows, 2 * columns)


def on_device(
    tokens,
    memory,
    text_length,
    patch_count,
    self_gain,
    self_query,
    self_key,
    self_value,
    self_out,
    cross_gain,
    cross_query,
    cross_key,
    cross_value,
    cross_out,
    mlp_gain,
    mlp_gate,
    mlp_up,
    mlp_down,
    output_grad,
):
    ring = Ring()
    place = ring.place
    width = tokens.shape[-1]
    half = width // 2
    units = mlp_down.shape[0]
    hidden_half = units * ring.blocks
    rows = self_query.shape[0]
    own = tokens.shape[1]
    own_patches = memory.shape[1]
    both = 2 * own
    keys = both * ring.groups
    patches = 2 * own_patches * ring.groups
    piece = 16
    packed = (2 * rows) % piece == 0 and units == HEAD_DIM and ring.blocks > 1
    pieces, down_pieces = 2 * rows // piece, units // piece
    pairs = ("dp", "hx")
    index_in = tuple(ring.arrivals()) if packed else ()
    index_out = tuple(ring.origins()) if packed else ()
    index_specs = [SMEM_SPEC] * len(index_in)
    block_rows = 2 * rows

    gain_columns = jnp.stack([self_gain, cross_gain, mlp_gain], axis=1)
    gain_columns = jnp.pad(gain_columns, ((0, 0), (0, PAIR_LANES - 3)))
    chains = ([self_query, gain_columns, self_out, cross_query], [self_key, self_value, cross_key, cross_value])
    splits = (half + PAIR_LANES, 2 * half)
    cut_all = 3 * half + PAIR_LANES
    packed_columns = (2 * hidden_half) * pieces + width * down_pieces
    widths_one = ([half, PAIR_LANES], [width])
    widths_two = ([half] * 2, [width])

    if packed:
        kinds = ["all" if w is gain_columns else "half" for w in chains[0] + chains[1]]
        mine, give = cut_shards(place, chains[0] + chains[1], kinds)
        blocks = jnp.concatenate(ring.in_order(mine, ring.swap(give)), axis=0)[None]
    else:
        sides = [
            jnp.concatenate(
                [w if w is gain_columns else column_halves([w])[i] for w in chains[0] + chains[1]],
                axis=1,
            )
            for i in range(2)
        ]
        blocks = ring.halves(*sides)[None]
    middle = own_patches // 2
    token_m = ring.across(tokens[0])
    patch_a = ring.across(memory[0, :middle])
    if packed:
        rest = after([mlp_gate, mlp_up, cross_out], blocks)
        mine, give = cut_shards(place, rest, ["units"] * 2 + ["half"])
        blocks_mlp = join_rows(place, mine, ring.swap(give), mlp_down, [], half, piece)[0]
    else:
        gate_halves, up_halves = unit_halves(mlp_gate, units), unit_halves(mlp_up, units)
        rest = [
            jnp.concatenate([gate_halves[i], up_halves[i], column_halves([cross_out])[i]], axis=1)
            for i in range(2)
        ]
        gate_up = lax.all_gather(ring.halves(*rest), pairs, axis=0, tiled=True)
        down_three = lax.all_gather(mlp_down, pairs, axis=0, tiled=True)
        out_two = gate_up[:, 2 * hidden_half :]
    blocks = ring.far_step(blocks, 0)
    blocks, token_m, memory = together(blocks, token_m, memory)
    if packed:
        mlp_weights = lax.all_gather(after(blocks_mlp, blocks), pairs, axis=0, tiled=True)
        mlp_weights = mlp_weights.reshape(ring.blocks, piece, -1)
    patch_b = ring.across(memory[0, middle:])
    for step in range(1, len(ring.far)):
        blocks = ring.far_step(blocks, step)
    blocks, patch_a, token_m = together(blocks, patch_a, token_m)
    parts = [blocks[:, :, :cut_all], blocks[:, :, cut_all:]]
    token_g = ring.swap(token_m)
    last = len(ring.tails[0]) - 1
    for step in range(last):
        got = ring.near_step(parts, step)
        parts = [jnp.concatenate(pair, axis=0) for pair in zip(parts, got)]
    parts, token_g, patch_b = together(parts, token_g, patch_b)
    parts_one = [part[:, :, :split] for part, split in zip(parts, splits)]
    parts_two = [part[:, :, split:] for part, split in zip(parts, splits)]
    near_one = ring.near_step(parts_one, last)
    patch_m = jnp.concatenate([patch_a, patch_b], axis=1)
    patch_g = ring.swap(patch_m)
    near_one, parts_two, patch_g = together(near_one, parts_two, patch_g)
    near_two = ring.near_step(parts_two, last)
    near_one = (parts_one[0], near_one[0], parts_one[1], near_one[1])
    arrivals = ring.arrivals()

    token_chunk = math.gcd(256, own)
    patch_chunk = math.gcd(256, own_patches)

    def chunk_starts(span, chunk, side_first):
        groups = ring.group ^ jnp.arange(ring.groups, dtype=jnp.int32)
        sides = ring.half ^ jnp.arange(2, dtype=jnp.int32)
        inner = jnp.arange(span // chunk, dtype=jnp.int32) * chunk
        if side_first:
            starts = groups[None, :, None] * 2 * span + sides[:, None, None] * span
        else:
            starts = groups[:, None, None] * 2 * span + sides[None, :, None] * span
        return (starts + inner).reshape(-1)

    fixed = jnp.stack([ring.group * both, ring.half])
    info_one = jnp.concatenate([text_length, fixed, chunk_starts(own, token_chunk, False)])
    info_two = jnp.concatenate([patch_count, fixed, chunk_starts(own_patches, patch_chunk, True)])

    head_shapes = [low_shape(both, half), low_shape(keys, half), low_shape(keys, half)]
    query_outs = [full_shape(8, width), low_shape(keys, width), *head_shapes]
    projections = [low_shape(width, w) for w in widths_one[0] + widths_one[1]]
    cost = keys * width * half
    if packed:
        outs = run_kernel(
            functools.partial(query_kernel, True),
            query_outs + projections,
            cost,
            index_in,
            [*near_one, token_m, token_g],
            late=True,
        )
        gain_rows, normed_one, query_heads, key_heads, value_heads = outs[:5]
        query_one, gain_cols, heads_one = outs[5:]
    else:
        query_one, gain_cols = to_whole(near_one[0], near_one[1], arrivals[0], widths_one[0])
        (heads_one,) = to_whole(near_one[2], near_one[3], arrivals[1], widths_one[1])
        gain_rows, normed_one, query_heads, key_heads, value_heads = run_kernel(
            functools.partial(query_kernel, False),
            query_outs,
            cost,
            [],
            [query_one, gain_cols, heads_one, token_m, token_g],
            late=True,
        )
    near_one = None
    grad_g = ring.swap(after(output_grad[0], query_heads))
    context_one, lse_one = attention_forward(
        info_one, query_heads, key_heads, value_heads, True, token_chunk
    )
    context_one, near_a, near_b, grad_g = together(context_one, *near_two, grad_g)
    context_one_g = ring.swap(context_one)
    out_one, query_two = to_whole(parts_two[0], near_a, arrivals[0], widths_two[0])
    out_one_g = ring.swap(out_one)
    patch_all = [part.reshape(-1, width) for part in (patch_m, patch_g)]
    memory_heads = [low_shape(patches, half)] * 2
    if packed:
        memory_keys, memory_values, heads_two = run_kernel(
            functools.partial(memory_kernel, True),
            memory_heads + [low_shape(width, width)],
            patches * width * half,
            index_in[1:],
            [parts_two[1], near_b, *patch_all],
            late=True,
        )
    else:
        (heads_two,) = to_whole(parts_two[1], near_b, arrivals[1], widths_two[1])
        memory_keys, memory_values = run_kernel(
            functools.partial(memory_kernel, False),
            memory_heads,
            patches * width * half,
            [],
            [heads_two, *patch_all],
            late=True,
        )
    context_one_g, memory_keys = together(context_one_g, memory_keys)
    hidden_one, normed_two, cross_heads = run_kernel(
        cross_query_kernel,
        [full_shape(both, width), low_shape(both, width), low_shape(both, half)],
        both * width * half,
        [place],
        [token_m, token_g, context_one, context_one_g, out_one, out_one_g, gain_rows, query_two],
        late=True,
    )
    if packed:
        out_two = from_pieces(after(mlp_weights, cross_heads), packed_columns, pieces, half)
    cross_heads, out_two = together(cross_heads, out_two)
    out_two_g = ring.swap(out_two)
    context_two, lse_two = attention_forward(
        info_two, cross_heads, memory_keys, memory_values, False, patch_chunk
    )
    context_two_g = ring.swap(context_two)
    if packed:
        hidden_two, part_low, down_keep, down_give, gain_three, mlp_terms = run_kernel(
            functools.partial(mlp_kernel, 1024),
            [
                full_shape(both, width),
                low_shape(both, width),
                full_shape(own, width),
                low_shape(own, width),
                full_shape(width, PAIR_LANES),
                low_shape(ring.blocks, piece, packed_columns),
            ],
            2 * both * width * hidden_half,
            [place],
            [
                hidden_one,
                context_two,
                context_two_g,
                out_two,
                out_two_g,
                gain_rows,
                gain_cols,
                output_grad[0],
                grad_g,
            ],
            [
                pltpu.VMEM((ring.blocks, pieces, piece, hidden_half), LOW),
                pltpu.VMEM((ring.blocks, pieces, piece, hidden_half), LOW),
                pltpu.VMEM((ring.blocks, down_pieces, piece, width), LOW),
                pltpu.VMEM((both, width), LOW),
                pltpu.VMEM((width, both), LOW),
                pltpu.VMEM((both, width), LOW),
                pltpu.VMEM((both, width), F32),
                pltpu.VMEM((both, width), F32),
                pltpu.VMEM((width, PAIR_LANES), F32),
                pltpu.SemaphoreType.DMA((2 * pieces + down_pieces,)),
            ],
            [mlp_weights],
            late=True,
        )
        mlp_terms = mlp_terms.reshape(ring.blocks * piece, -1)
        mlp_sum = lax.psum_scatter(mlp_terms, pairs, scatter_dimension=0, tiled=True)
    else:
        joined = jnp.concatenate(ring.in_order(out_two, out_two_g), axis=1)
        swapped = jnp.concatenate([context_two_g[own:], context_two_g[:own]], axis=0)
        context = jnp.concatenate(ring.in_order(context_two, swapped), axis=1)
        hidden_two = hidden_one + dot_nn(context, joined)
        normed_three = (normalize(hidden_two)[0] * gain_rows[2:3]).astype(LOW)
        grad_low = jnp.concatenate([output_grad[0], grad_g], axis=0)
        gate_up = gate_up[:, : 2 * hidden_half]
        gate_three, up_three = gate_up[:, :hidden_half], gate_up[:, hidden_half:]
        active, slope = gelu_parts(dot_nn(normed_three, gate_three))
        up = dot_nn(normed_three, up_three)
        mixed = (active * up).astype(LOW)
        down_part = dot_nn(mixed, down_three)
        down_keep, down_give = down_part[:own], down_part[own:].astype(LOW)
        grad_mixed = dot_nt(grad_low, down_three)
        gate_low = (grad_mixed * up * slope).astype(LOW)
        up_low = (grad_mixed * active).astype(LOW)
        part_low = (dot_nt(gate_low, gate_three) + dot_nt(up_low, up_three)).astype(LOW)
        terms = jnp.concatenate(
            [dot_tn(normed_three, gate_low), dot_tn(normed_three, up_low)], axis=1
        )
        column = jnp.sum(terms * gate_up.astype(F32), axis=1, keepdims=True)
        gain_three = lane_column(column / gain_cols[:, 2:3].astype(F32), 2)
        gate_up = lax.psum_scatter(terms, pairs, scatter_dimension=0, tiled=True)
        mlp_ddown = lax.psum_scatter(
            dot_tn(mixed, grad_low), pairs, scatter_dimension=0, tiled=True
        )

    part_g = ring.swap(part_low)
    down_got = ring.swap(down_give)
    output = (hidden_two[:own] + down_keep + down_got.astype(F32)).astype(LOW)

    def branch(gain_at, hidden, mine, got, weight_m, weight_g, base):
        return run_kernel(
            functools.partial(branch_kernel, gain_at),
            [full_shape(both, width), low_shape(both, width), low_shape(both, half)],
            both * width * half,
            [place],
            [hidden, gain_rows, mine, got, weight_m, weight_g, *base],
            late=True,
        )

    dhidden_two, branch_two, dcontext_two = branch(
        2, hidden_two, part_low, part_g, out_two, out_two_g, [output_grad[0], grad_g]
    )
    dquery, dkey, dvalue = attention_backward(
        info_two,
        cross_heads,
        memory_keys,
        memory_values,
        context_two,
        dcontext_two,
        lse_two,
        False,
        patch_chunk,
    )
    (part_low,) = run_kernel(
        back_kernel, [low_shape(both, width)], both * width, [], [dquery, query_two]
    )
    part_g = ring.swap(part_low)

    count = ring.blocks // 2

    def grads(body, inputs, columns, gain_outs, cost, order=1):
        scratch = [pltpu.VMEM((width, c), LOW) for c in columns]
        acc = pltpu.VMEM((width, PAIR_LANES), F32)
        if packed:
            shapes = [low_shape(count, block_rows, c) for c in columns for _ in range(2)]
            outs = run_kernel(
                functools.partial(body, True),
                gain_outs + shapes,
                cost,
                [place, *index_out[::order]],
                inputs,
                scratch + [acc],
                late=True,
            )
            blocks = outs[len(gain_outs) :]
            return outs[: len(gain_outs)], blocks[0::2][::order], blocks[1::2][::order]
        wholes = [low_shape(width, c) for c in columns]
        outs = run_kernel(
            functools.partial(body, False), gain_outs + wholes, cost, [place], inputs, [acc], late=True
        )
        return outs[: len(gain_outs)], *ring.halve_wholes(outs[len(gain_outs) :][::order], block_rows)

    patch_spans = [(side == 0, g) for side in range(2) for g in range(ring.groups)]
    patch_shape = (ring.groups, own_patches, width)
    memory_keep, memory_give = run_kernel(
        functools.partial(rows_back_kernel, patch_spans, False),
        [full_shape(*patch_shape), low_shape(*patch_shape)],
        patches * width,
        [],
        [dkey, dvalue, heads_two],
    )
    memory_total = ring.pair_sum(memory_keep, memory_give)
    part_g, memory_total = together(part_g, memory_total)
    memory_sent = ring.group_terms(memory_total)
    dhidden_one, branch_one, dcontext_one = branch(
        1, hidden_one, part_low, part_g, out_one, out_one_g, [dhidden_two]
    )
    (gain_two,), cross_keep, cross_give = grads(
        cross_grads_kernel,
        [
            context_two,
            context_two_g,
            branch_two,
            normed_two,
            dquery,
            *patch_all,
            dkey,
            dvalue,
            query_two,
            gain_cols,
            context_one,
            context_one_g,
            branch_one,
        ],
        (3 * half, 2 * half),
        [full_shape(width, PAIR_LANES)],
        (both + patches) * width * half,
        -1,
    )
    cross_got = ring.near_sends(cross_give, last)
    cross_keep, dcontext_one = together(cross_keep, dcontext_one)

    dquery_one, dkey_one, dvalue_one = attention_backward(
        info_one,
        query_heads,
        key_heads,
        value_heads,
        context_one,
        dcontext_one,
        lse_one,
        True,
        token_chunk,
    )
    dquery_one, dkey_one, dvalue_one, cross_got, memory_grad, output = together(
        dquery_one, dkey_one, dvalue_one, cross_got, memory_sent, output
    )
    for step in reversed(range(1, last + 1)):
        cross_keep, cross_give = ring.near_sums(cross_keep, cross_got, step)
        cross_got = ring.near_sends(cross_give, step - 1)
    dquery_one, cross_give = together(dquery_one, cross_give)
    _, self_keep, self_give = grads(
        self_grads_kernel,
        [
            normed_one,
            dquery_one,
            dkey_one,
            dvalue_one,
            query_one,
            heads_one,
            gain_cols,
            gain_two,
            gain_three,
        ],
        (half + PAIR_LANES, 2 * half),
        [],
        (both + keys) * width * half,
    )
    self_give, cross_got = together(self_give, cross_got)
    self_got = ring.near_sends(self_give, last)
    cross_own, cross_far = ring.far_first(cross_keep, cross_got)
    dquery_one, dkey_one, dvalue_one = after((dquery_one, dkey_one, dvalue_one), self_give)
    token_spans = [(side == 0, g) for g in range(ring.groups) for side in range(2)]
    token_shape = (ring.groups, own, width)
    part_keep, part_give = run_kernel(
        functools.partial(rows_back_kernel, token_spans, True),
        [full_shape(*token_shape), low_shape(*token_shape)],
        keys * width,
        [],
        [dkey_one, dvalue_one, heads_one, dquery_one, query_one],
    )
    part_total = ring.pair_sum(part_keep, part_give)
    self_got, part_total = together(self_got, part_total)
    for step in reversed(range(1, last + 1)):
        self_keep, self_give = ring.near_sums(self_keep, self_got, step)
        self_got = ring.near_sends(self_give, step - 1)
    dnormed_one = ring.group_terms(part_total)
    self_got, cross_far = together(self_got, cross_far)
    self_own, self_far = ring.far_sends(self_keep, self_got)
    cross_own, cross_far = ring.far_last(cross_own, cross_far)
    plain, inverse = normalize(tokens[0].astype(F32))
    input_grad = dhidden_one[:own] + norm_back(plain, inverse, gain_rows[0:1], dnormed_one)

    if packed:
        mlp_sum, input_grad = together(mlp_sum, input_grad)
        mlp_rows = mlp_sum[:, : 2 * pieces * hidden_half].reshape(piece, 2, pieces, hidden_half)
        mlp_rows = mlp_rows.transpose(2, 0, 1, 3).reshape(2 * rows, 2 * hidden_half)
        mlp_give = lax.dynamic_slice_in_dim(mlp_rows, (1 - ring.half) * rows, rows, 0)
        mlp_dgate, mlp_dup, mlp_ddown = run_kernel(
            functools.partial(feed_forward_grads_kernel, pieces, units),
            [full_shape(rows, 2 * hidden_half)] * 2 + [full_shape(units, width)],
            rows * width,
            [place],
            [mlp_sum, ring.swap(mlp_give)],
        )
    else:
        (gate_up,) = ring.finished(gate_up, 1)
        gate_columns = [gate_up[:, i * hidden_half : (i + 1) * hidden_half] for i in range(4)]
        mlp_dgate = unit_whole(gate_columns[0], gate_columns[2], units)
        mlp_dup = unit_whole(gate_columns[1], gate_columns[3], units)
    self_far, cross_far, mlp_dgate, mlp_dup, mlp_ddown, input_grad, memory_grad = together(
        self_far, cross_far, mlp_dgate, mlp_dup, mlp_ddown, input_grad, memory_grad
    )
    cross_sum = ring.far_sum(cross_own, cross_far)
    self_sum = ring.far_sum(self_own, self_far)
    gain_block = self_sum[:, half : half + PAIR_LANES]
    gain_block = jnp.pad(gain_block, ((0, 0), (0, half - PAIR_LANES)))
    joined = jnp.concatenate(
        [cross_sum, self_sum[:, :half], self_sum[:, half + PAIR_LANES :], gain_block], axis=1
    )
    cross_dkey, cross_dvalue, cross_dout, cross_dquery, self_dout, *rest = ring.finished(joined, 9)
    self_dquery, self_dvalue, self_dkey, gain_terms = rest
    dgains = gain_terms[:, :3] + gain_terms[:, half : half + 3]

    return (
        output[None],
        input_grad[None],
        memory_grad[None],
        dgains[:, 0],
        self_dquery,
        self_dkey,
        self_dvalue,
        self_dout,
        dgains[:, 1],
        cross_dquery,
        cross_dkey,
        cross_dvalue,
        cross_dout,
        dgains[:, 2],
        mlp_dgate,
        mlp_dup,
        mlp_ddown,
    )


def solution(mesh):
    charts, heads = mesh.devices.shape
    inner = Mesh(mesh.devices.reshape(charts, heads // 2, 2), ("dp", "hx", "hc"))
    every = ("dp", "hx", "hc")
    rows = P(every, None)
    vector = P(every)
    grid = P("dp", ("hx", "hc"), None)
    in_specs = (grid, grid, P("dp"), P("dp"))
    in_specs += (vector, rows, rows, rows, rows) * 2
    in_specs += (vector, rows, rows, rows, grid)
    out_specs = (grid, grid, grid)
    out_specs += (vector, rows, rows, rows, rows) * 2
    out_specs += (vector, rows, rows, rows)
    return jax.shard_map(
        on_device, mesh=inner, in_specs=in_specs, out_specs=out_specs, check_vma=False
    )
```
